32 devices in a mesh: expert: 4 (over y, x), context: 4 (over z), dp: 2 (over core).
Axes of the slice: x: 2, y: 2, z: 4, core: 2. Of those that a mesh axis runs over, the one named last changes fastest.
Arguments:
- tokens: bfloat16 [8, 1024, 1024], P(('expert', 'dp'), 'context'), may hold values from -6 to 6
- attn_scale: bfloat16 [1024], replicated, may hold values from 0.5 to 1.5
- w_query: bfloat16 [1024, 1024], replicated, may hold values from -0.1875 to 0.1875
- w_key: bfloat16 [1024, 512], replicated, may hold values from -0.1875 to 0.1875
- w_value: bfloat16 [1024, 512], replicated, may hold values from -0.1875 to 0.1875
- w_out: bfloat16 [1024, 1024], replicated, may hold values from -2 to 2
- moe_scale: bfloat16 [1024], replicated, may hold values from 0.5 to 1.5
- w_router: bfloat16 [1024, 16], replicated, may hold values from -0.09375 to 0.09375
- w_gate: bfloat16 [16, 1024, 512], P('expert'), may hold values from -0.1875 to 0.1875
- w_up: bfloat16 [16, 1024, 512], P('expert'), may hold values from -0.1875 to 0.1875
- w_down: bfloat16 [16, 512, 1024], P('expert'), may hold values from -2 to 2
- segment_ids: int32 [8, 1024], P(('expert', 'dp'), 'context'), may hold values from 0 to 2, as said below
- expert_choice: int32 [8, 1024, 8], P(('expert', 'dp'), 'context'), may hold values from 0 to 15, all different within a row
- slot_order: int32 [8, 4, 2048], P(('expert', 'dp'), 'context'), may hold values from 0 to 2047, each once within a row
- out_grad: bfloat16 [8, 1024, 1024], P(('expert', 'dp'), 'context'), may hold values from -6 to 6
Outputs:
- layer_out: float32 [8, 1024, 1024], P(('expert', 'dp'), 'context')
- input_grad: float32 [8, 1024, 1024], P(('expert', 'dp'), 'context')
- attn_scale_grad: float32 [1024], P(('expert', 'context', 'dp'))
- moe_scale_grad: float32 [1024], P(('expert', 'context', 'dp'))
- query_grad: float32 [1024, 1024], P(('expert', 'context', 'dp'))
- key_grad: float32 [1024, 512], P(('expert', 'context', 'dp'))
- value_grad: float32 [1024, 512], P(('expert', 'context', 'dp'))
- out_proj_grad: float32 [1024, 1024], P(('expert', 'context', 'dp'))
- router_grad: float32 [1024, 16], P(('expert', 'context', 'dp'))
- gate_grad: float32 [16, 1024, 512], P('expert', ('context', 'dp'))
- up_grad: float32 [16, 1024, 512], P('expert', ('context', 'dp'))
- down_grad: float32 [16, 512, 1024], P('expert', ('context', 'dp'))
The draws below stay inside these ranges and needn't reach their ends.
Inputs may be any that keep to these rules, and one draw needn't show every extreme that they name: `segment_ids`: along each sequence the ids rise from 0 to 2 in steps of one; document 1 begins within the first 256 positions and ends within the last 256. `expert_choice`: A token names 8 different experts. `slot_order`: each row of 2048 entries holds every pair index of its block once.
All inputs are finite; a program needn't handle non-finite values.
Results may differ from the reference program's by a relative error of at most 0.018.
Values may be sent and summed in bfloat16 or wider, within the bound.
A program may use at most 192 MiB of HBM per device.

```python
import jax
import jax.numpy as jnp
from jax import lax

D = 1024
HEADS = 16
KV_HEADS = 8
HEAD_DIM = 64
FFE = 512
TOPK = 8
CTX_TOK = 256
EXPERTS = 16
LEN = 1024
SEQS = 8
CAPACITY = 144
N_CONTEXT = 4


def draw_segment_ids(key, part):
    first_key, second_key = jax.random.split(jax.random.fold_in(key, 17))
    begins = jax.random.randint(first_key, (SEQS, 1), 1, CTX_TOK)
    finishes = LEN - jax.random.randint(second_key, (SEQS, 1), 1, CTX_TOK)
    places = jnp.arange(LEN, dtype=jnp.int32)[None, :]
    return (places >= begins).astype(jnp.int32) + (places >= finishes).astype(jnp.int32)


def block_levels(key, extent, pieces, low, top_value):
    gain, own = 1.0, jax.random.fold_in(key, 6)
    for axis_at, blocks in pieces:
        heights = jnp.exp(jax.random.uniform(jax.random.fold_in(own, axis_at), (blocks,), jnp.float32, low / len(pieces), top_value / len(pieces)))
        gain = gain * jnp.repeat(heights, extent[axis_at] // blocks).reshape([-1 if axis == axis_at else 1 for axis in range(len(extent))])
    return gain


def different_ones(rng, rows, count, top, lift):
    ranking = jax.random.permutation(jax.random.fold_in(rng, 1), count)
    pull = ranking
    for power in range(3):
        pull = pull * pull // count
    pull = pull * lift // count
    lots = jax.random.randint(jax.random.fold_in(rng, 2), (rows, count), 0, 4096) + pull
    sure = jax.random.permutation(jax.random.fold_in(rng, 3), rows)[jnp.arange(count) % rows]
    lots = jnp.where(jnp.arange(rows)[:, None] == sure[None, :], 1 << 14, lots)
    priority = lots * count + jnp.arange(count)
    return lax.top_k(priority.astype(jnp.int32), top)[1].astype(jnp.int32)


def centred(own_key, dims, spread, most, pieces=(), held_as=jnp.bfloat16):
    values = spread * jax.random.normal(own_key, dims, jnp.float32)
    if pieces:
        values = values * block_levels(own_key, dims, pieces, -0.22, 0.18)
    return jnp.clip(values, -most, most).astype(held_as)


def setup_inputs(seed: int = 0) -> dict:
    streams_of = jax.random.split(jax.random.key(seed), 16)
    return {
        "tokens": centred(streams_of[0], (SEQS, LEN, D), 1.0, 6.0, ((0, 8), (1, 4))),
        "attn_scale": jnp.clip(1.0 + 0.1 * jax.random.normal(streams_of[1], (D,), jnp.float32), 0.5, 1.5).astype(jnp.bfloat16),
        "w_query": centred(streams_of[2], (D, HEADS * HEAD_DIM), D ** -0.5, 0.1875),
        "w_key": centred(streams_of[3], (D, KV_HEADS * HEAD_DIM), D ** -0.5, 0.1875),
        "w_value": centred(streams_of[4], (D, KV_HEADS * HEAD_DIM), D ** -0.5, 0.1875),
        "w_out": centred(streams_of[5], (HEADS * HEAD_DIM, D), (HEADS * HEAD_DIM // 128) ** -0.5, 2.0),
        "moe_scale": jnp.clip(1.0 + 0.1 * jax.random.normal(streams_of[6], (D,), jnp.float32), 0.5, 1.5).astype(jnp.bfloat16),
        "w_router": centred(streams_of[7], (D, EXPERTS), (4 * D) ** -0.5, 0.09375),
        "w_gate": centred(streams_of[8], (EXPERTS, D, FFE), D ** -0.5, 0.1875, ((0, 4),)),
        "w_up": centred(streams_of[9], (EXPERTS, D, FFE), D ** -0.5, 0.1875, ((0, 4),)),
        "w_down": centred(streams_of[10], (EXPERTS, FFE, D), (max(FFE // 64, 1)) ** -0.5, 2.0, ((0, 4),)),
        "segment_ids": draw_segment_ids(jax.random.fold_in(streams_of[15], 71), 0),
        "expert_choice": different_ones(streams_of[12], SEQS * LEN, EXPERTS, TOPK, 4096).reshape((SEQS, LEN, TOPK)),
        "slot_order": jax.vmap(lambda own: jax.random.permutation(own, CTX_TOK * TOPK))(jax.random.split(streams_of[13], SEQS * N_CONTEXT)).reshape((SEQS, N_CONTEXT, CTX_TOK * TOPK)).astype(jnp.int32),
        "out_grad": centred(streams_of[14], (SEQS, LEN, D), 1.0, 6.0, ((0, 8), (1, 4))),
    }


epsilon = 1e-06
rope_base = 10000.0
negative_large = -1e+30

@jax.custom_vjp
def low(v):
    return lax.optimization_barrier(v.astype(jnp.bfloat16)).astype(jnp.float32)

@jax.custom_vjp
def low_back(v):
    return v

def low_keep(v):
    return (low(v), None)

def low_pass(kept, grad):
    return (grad,)

def back_keep(v):
    return (v, None)

def back_low(kept, grad):
    return (low(grad),)
low.defvjp(low_keep, low_pass)
low_back.defvjp(back_keep, back_low)

def matmul(left_side, right_side):
    return jnp.dot(left_side, right_side, precision=lax.Precision.HIGHEST, preferred_element_type=jnp.float32)

def norm_apply(values, scale_gain):
    return values * lax.rsqrt(lax.optimization_barrier(jnp.mean(values * values, axis=-1, keepdims=True)) + epsilon) * scale_gain

def rope_tables(positions, head_width):
    halves = head_width // 2
    inverse_freq = rope_base ** (-2.0 * jnp.arange(halves, dtype=jnp.float32) / head_width)
    angles = positions.astype(jnp.float32)[:, None] * inverse_freq[None, :]
    return (jnp.cos(angles)[:, None, :], jnp.sin(angles)[:, None, :])

def rotate(values, cosine_table, sine_table):
    halves = values.shape[-1] // 2
    first_half = values[..., :halves]
    second_half = values[..., halves:]
    return jnp.concatenate([first_half * cosine_table - second_half * sine_table, second_half * cosine_table + first_half * sine_table], axis=-1)

def expert_block(block_rows, chosen, turn_order, w_router, w_gate, w_up, w_down):
    logits = low_back(matmul(block_rows, w_router))
    router_soft = jax.nn.softmax(logits, axis=-1)
    gate_values = jnp.take_along_axis(router_soft, chosen, axis=1)
    flat_expert = chosen.reshape(-1)
    ordered = flat_expert[turn_order]
    hit_table = (ordered[:, None] == jnp.arange(EXPERTS, dtype=jnp.int32)[None, :]).astype(jnp.int32)
    earlier = jnp.cumsum(hit_table, axis=0) - hit_table
    ranked = lax.optimization_barrier(jnp.sum(earlier * hit_table, axis=1))
    slot_index = jnp.zeros(flat_expert.shape, jnp.int32).at[turn_order].set(ranked)
    destination = jnp.where(slot_index < CAPACITY, flat_expert * CAPACITY + slot_index, EXPERTS * CAPACITY)
    owner_token = jnp.arange(flat_expert.shape[0], dtype=jnp.int32) // TOPK
    padded = jnp.concatenate([block_rows, jnp.zeros((1, D), jnp.float32)], axis=0)
    slot_token = jnp.full((EXPERTS * CAPACITY + 1,), CTX_TOK, jnp.int32).at[destination].set(owner_token)[:EXPERTS * CAPACITY]
    buffer = low_back(padded[slot_token].reshape(EXPERTS, CAPACITY, D))
    gate_pre = low_back(jnp.einsum('ecd,edf->ecf', buffer, w_gate, precision=lax.Precision.HIGHEST))
    up_pre = low_back(jnp.einsum('ecd,edf->ecf', buffer, w_up, precision=lax.Precision.HIGHEST))
    hidden = low(jax.nn.silu(gate_pre) * up_pre)
    produced = low(low_back(jnp.einsum('ecf,efd->ecd', hidden, w_down, precision=lax.Precision.HIGHEST)))
    out_rows = jnp.concatenate([produced.reshape(EXPERTS * CAPACITY, D), jnp.zeros((1, D), jnp.float32)], axis=0)
    pair_out = out_rows[destination].reshape(CTX_TOK, TOPK, D)
    return lax.optimization_barrier(jnp.sum(gate_values[:, :, None] * pair_out, axis=1))

def layer_one(params, inputs):
    attn_scale, w_query, w_key, w_value, w_out, moe_scale, w_router, w_gate, w_up, w_down = params
    tokens_seq, seg_ids, chosen, turn_order = inputs
    group_size = HEADS // KV_HEADS
    first_normed = low(norm_apply(tokens_seq, attn_scale))
    positions = jnp.arange(LEN, dtype=jnp.int32)
    cosine_table, sine_table = rope_tables(positions, HEAD_DIM)
    query_pre = low_back(matmul(first_normed, w_query)).reshape(LEN, HEADS, HEAD_DIM)
    queries = low(rotate(query_pre, cosine_table, sine_table)).reshape(LEN, KV_HEADS, group_size, HEAD_DIM)
    key_pre = low_back(matmul(first_normed, w_key)).reshape(LEN, KV_HEADS, HEAD_DIM)
    key_rot = low(rotate(key_pre, cosine_table, sine_table))
    values = low(low_back(matmul(first_normed, w_value))).reshape(LEN, KV_HEADS, HEAD_DIM)
    scores = low_back(jnp.einsum('qhgd,khd->hgqk', queries, key_rot, precision=lax.Precision.HIGHEST) * HEAD_DIM ** (-0.5))
    allowed = (seg_ids[:, None] == seg_ids[None, :]) & (positions[None, :] <= positions[:, None])
    soft_low = low(jax.nn.softmax(jnp.where(allowed, scores, negative_large), axis=-1))
    attn_mixed = low(low_back(jnp.einsum('hgqk,khd->qhgd', soft_low, values, precision=lax.Precision.HIGHEST)))
    attn_mixed = attn_mixed.reshape(LEN, HEADS * HEAD_DIM)
    middle = tokens_seq + low_back(matmul(attn_mixed, w_out))
    second = low(norm_apply(middle, moe_scale))
    routed = jax.vmap(expert_block, in_axes=(0, 0, 0, None, None, None, None))(second.reshape(N_CONTEXT, CTX_TOK, D), chosen.reshape(N_CONTEXT, CTX_TOK, TOPK), turn_order, w_router, w_gate, w_up, w_down)
    return middle + routed.reshape(LEN, D)

def reference(tokens, attn_scale, w_query, w_key, w_value, w_out, moe_scale, w_router, w_gate, w_up, w_down, segment_ids, expert_choice, slot_order, out_grad):
    floats = tuple((argument.astype(jnp.float32) for argument in (tokens, attn_scale, w_query, w_key, w_value, w_out, moe_scale, w_router, w_gate, w_up, w_down)))

    def forward(inputs_all, *params):

        def per_sequence(items):
            return layer_one(params, items)
        return lax.map(jax.checkpoint(per_sequence), (inputs_all, segment_ids, expert_choice, slot_order))
    result, pullback = jax.vjp(forward, *floats)
    gradients = pullback(out_grad.astype(jnp.float32))
    return (result, gradients[0], gradients[1], gradients[6], gradients[2], gradients[3], gradients[4], gradients[5], gradients[7], gradients[8], gradients[9], gradients[10])
```

```python
import functools

import jax
import jax.numpy as jnp
from jax import lax
from jax.experimental import pallas as pl
from jax.experimental.pallas import tpu as pltpu
from jax.sharding import PartitionSpec as P

HEAD_DIM = 64
MESH = pl.DeviceIdType.MESH

epsilon = 1e-06
rope_base = 10000.0
negative_large = -1e30
block_limit = 512
bf16 = jnp.bfloat16
f32 = jnp.float32


def gather_kernel(axis, size, count, *refs):
    ins, outs = refs[:count], refs[count : 2 * count]
    send_sem, recv_sem, own_sem = refs[2 * count :]
    me = lax.axis_index(axis)
    barrier = pltpu.get_barrier_semaphore()
    for step in range(1, size):
        pl.semaphore_signal(
            barrier, inc=1, device_id={axis: lax.rem(me + step, size)}, device_id_type=MESH
        )
    pl.semaphore_wait(barrier, size - 1)
    copies = []
    for step in range(1, size):
        for k in range(count):
            copies.append(
                pltpu.make_async_remote_copy(
                    src_ref=ins[k],
                    dst_ref=outs[k].at[me],
                    send_sem=send_sem.at[k, step],
                    recv_sem=recv_sem.at[k, step],
                    device_id={axis: lax.rem(me + step, size)},
                    device_id_type=MESH,
                )
            )
            copies[-1].start()
    own = [
        pltpu.make_async_copy(ins[k], outs[k].at[me], own_sem.at[k]) for k in range(count)
    ]
    for copy in own:
        copy.start()
    for copy in own + copies:
        copy.wait()


def gather_all(arrays, axis, size, cid, name):
    count = len(arrays)
    return pl.pallas_call(
        functools.partial(gather_kernel, axis, size, count),
        out_shape=tuple(jax.ShapeDtypeStruct((size,) + a.shape, a.dtype) for a in arrays),
        in_specs=[pl.BlockSpec(memory_space=pl.ANY)] * count,
        out_specs=tuple([pl.BlockSpec(memory_space=pl.ANY)] * count),
        scratch_shapes=[
            pltpu.SemaphoreType.DMA((count, size)),
            pltpu.SemaphoreType.DMA((count, size)),
            pltpu.SemaphoreType.DMA((count,)),
        ],
        compiler_params=pltpu.CompilerParams(collective_id=cid, has_side_effects=True),
        name=name,
    )(*arrays)


def scatter_kernel(axis, size, sums, cats, *refs):
    count = sums + cats
    ins, outs = refs[:count], refs[count : 2 * count]
    bufs = refs[2 * count : 2 * count + sums]
    own_bufs = refs[2 * count + sums : 2 * count + 2 * sums]
    send_sem, recv_sem, own_sem = refs[2 * count + 2 * sums :]
    me = lax.axis_index(axis)
    barrier = pltpu.get_barrier_semaphore()
    for step in range(1, size):
        pl.semaphore_signal(
            barrier, inc=1, device_id={axis: lax.rem(me + step, size)}, device_id_type=MESH
        )
    pl.semaphore_wait(barrier, size - 1)
    copies = []
    for step in range(1, size):
        other = lax.rem(me + step, size)
        for k in range(count):
            copies.append(
                pltpu.make_async_remote_copy(
                    src_ref=ins[k].at[other],
                    dst_ref=bufs[k].at[step - 1] if k < sums else outs[k].at[me],
                    send_sem=send_sem.at[k, step],
                    recv_sem=recv_sem.at[k, step],
                    device_id={axis: other},
                    device_id_type=MESH,
                )
            )
            copies[-1].start()
    own = [
        pltpu.make_async_copy(
            ins[k].at[me], own_bufs[k] if k < sums else outs[k].at[me], own_sem.at[k]
        )
        for k in range(count)
    ]
    for copy in own:
        copy.start()
    for copy in own + copies:
        copy.wait()
    for k in range(sums):
        rows = outs[k].shape[0]
        step_rows = 16

        @pl.loop(0, rows // step_rows)
        def _(i):
            at = pl.ds(pl.multiple_of(i * step_rows, step_rows), step_rows)
            total = own_bufs[k][at, :].astype(f32)
            for step in range(size - 1):
                total = total + bufs[k][step, at, :].astype(f32)
            outs[k][at, :] = total.astype(outs[k].dtype)


def scatter_all(sum_arrays, sum_types, cat_arrays, axis, size, cid, name):
    arrays = list(sum_arrays) + list(cat_arrays)
    sums, cats = len(sum_arrays), len(cat_arrays)
    out_shape = [
        jax.ShapeDtypeStruct(a.shape[1:], t) for a, t in zip(sum_arrays, sum_types)
    ] + [jax.ShapeDtypeStruct(a.shape, a.dtype) for a in cat_arrays]
    return pl.pallas_call(
        functools.partial(scatter_kernel, axis, size, sums, cats),
        out_shape=tuple(out_shape),
        in_specs=[pl.BlockSpec(memory_space=pl.ANY)] * (sums + cats),
        out_specs=tuple(
            [pl.BlockSpec(memory_space=pltpu.VMEM)] * sums
            + [pl.BlockSpec(memory_space=pl.ANY)] * cats
        ),
        scratch_shapes=[
            pltpu.VMEM((size - 1,) + a.shape[1:], a.dtype) for a in sum_arrays
        ]
        + [pltpu.VMEM(a.shape[1:], a.dtype) for a in sum_arrays]
        + [
            pltpu.SemaphoreType.DMA((sums + cats, size)),
            pltpu.SemaphoreType.DMA((sums + cats, size)),
            pltpu.SemaphoreType.DMA((sums + cats,)),
        ],
        compiler_params=pltpu.CompilerParams(
            collective_id=cid, has_side_effects=True, vmem_limit_bytes=24 << 20
        ),
        name=name,
    )(*arrays)


def take(array, index, axis=0):
    return lax.dynamic_index_in_dim(array, index, axis, keepdims=False)


def core_sum(pieces, axis_index, size):
    total = take(pieces, axis_index).astype(f32)
    for step in range(1, size):
        gone = take(pieces, lax.rem(axis_index + step, size))
        got = lax.ppermute(gone, "dp", [(i, (i + step) % size) for i in range(size)])
        total = total + got.astype(f32)
    return total.astype(bf16)


def line_sum(pieces, me, size):
    up = down = None
    for step in range(size - 1):
        up_piece = take(pieces, jnp.clip(size - 1 - step + me, 0, size - 1)).astype(f32)
        down_piece = take(pieces, jnp.clip(step - (size - 1 - me), 0, size - 1)).astype(f32)
        if step:
            up_piece = up_piece + up.astype(f32)
            down_piece = down_piece + down.astype(f32)
        pairs = [(i, i + 1) for i in range(step + 1)]
        up = lax.ppermute(up_piece.astype(bf16), "context", pairs)
        down = lax.ppermute(
            down_piece.astype(bf16),
            "context",
            [(size - 1 - a, size - 1 - b) for a, b in pairs],
        )
    return take(pieces, me).astype(f32) + up.astype(f32) + down.astype(f32)


def norm_forward(values, scale_gain):
    inverse = lax.rsqrt(jnp.mean(values * values, axis=-1, keepdims=True) + epsilon)
    normed = values * inverse
    return (normed * scale_gain, normed, inverse)


def norm_backward(upstream, normed, inverse, scale_gain):
    scaled = upstream * scale_gain
    gain_grad = jnp.sum(upstream * normed, axis=0)
    inner_mean = jnp.mean(scaled * normed, axis=-1, keepdims=True)
    return (inverse * (scaled - normed * inner_mean), gain_grad)


def rope_tables(positions, head_width):
    halves = head_width // 2
    inverse_freq = rope_base ** (-2.0 * jnp.arange(halves, dtype=f32) / head_width)
    angles = positions.astype(f32)[:, None] * inverse_freq[None, :]
    return (jnp.cos(angles)[:, None, :], jnp.sin(angles)[:, None, :])


def rotate(values, cosine_table, sine_table):
    halves = values.shape[-1] // 2
    first_half = values[..., :halves]
    second_half = values[..., halves:]
    return jnp.concatenate(
        [
            first_half * cosine_table - second_half * sine_table,
            second_half * cosine_table + first_half * sine_table,
        ],
        axis=-1,
    )


def rotate_back(upstream, cosine_table, sine_table):
    return rotate(upstream, cosine_table, -sine_table)


def slot_table(chosen, turn_order, experts_all, capacity):
    tokens, top_count = chosen.shape
    pair_count = tokens * top_count
    turns = jnp.arange(pair_count, dtype=jnp.int32)
    owner = (turn_order // top_count)[:, None] == jnp.arange(tokens, dtype=jnp.int32)[None, :]
    which = (turn_order % top_count)[:, None] == jnp.arange(top_count, dtype=jnp.int32)[None, :]
    high = jnp.where(which, (turns // 256)[:, None], 0)
    low = jnp.where(which, (turns % 256)[:, None], 0)
    both = jnp.concatenate([high, low], axis=1).astype(bf16)
    found = lax.dot_general(
        owner.astype(bf16), both, (((0,), (0,)), ((), ())), preferred_element_type=f32
    )
    turn_of = found[:, :top_count] * 256.0 + found[:, top_count:]
    picks = chosen[:, :, None] == jnp.arange(experts_all, dtype=jnp.int32)[None, None, :]
    far = float(2 * pair_count)
    turn_at = far + jnp.sum(jnp.where(picks, turn_of[:, :, None] - far, 0.0), axis=1)
    turn_row = turn_at.T
    rank = jnp.sum((turn_row[:, :, None] < turn_row[:, None, :]).astype(f32), axis=1)
    return jnp.where((turn_row < far) & (rank < capacity), rank, -1.0)


def body(
    sizes,
    tokens,
    attn_scale,
    w_query,
    w_key,
    w_value,
    w_out,
    moe_scale,
    w_router,
    w_gate,
    w_up,
    w_down,
    segment_ids,
    expert_choice,
    slot_order,
    out_grad,
):
    ne, nz, nd = sizes
    my_expert = lax.axis_index("expert")
    my_ctx = lax.axis_index("context")
    my_dp = lax.axis_index("dp")
    local_rows = tokens.shape[1]
    model_width = tokens.shape[2]
    head_width = HEAD_DIM
    query_heads = w_query.shape[1] // head_width
    kv_heads = w_key.shape[1] // head_width
    kv_width = kv_heads * head_width
    group_size = query_heads // kv_heads
    factor = head_width ** (-0.5)
    seq_len = local_rows * nz
    experts_all = w_router.shape[1]
    local_experts = w_gate.shape[0]
    top_count = expert_choice.shape[2]
    pair_count = local_rows * top_count
    capacity = (pair_count * 9 + 8 * experts_all - 1) // (8 * experts_all)

    positions = my_ctx * local_rows + jnp.arange(local_rows, dtype=jnp.int32)
    cosine_table, sine_table = rope_tables(positions, head_width)
    residual_in = tokens[0].astype(f32)
    seg_local = segment_ids[0]
    attn_gain = attn_scale.astype(f32)
    moe_gain = moe_scale.astype(f32)

    grad_all = lax.all_gather(out_grad[0], "expert", axis=0)
    slots = slot_table(expert_choice[0], slot_order[0, 0], experts_all, capacity)

    first_out, first_normed, first_inverse = norm_forward(residual_in, attn_gain)
    first_low = first_out.astype(bf16)
    query_pre = jnp.dot(first_low, w_query, preferred_element_type=f32)
    key_pre = jnp.dot(first_low, w_key, preferred_element_type=f32)
    value_low = jnp.dot(first_low, w_value, preferred_element_type=f32).astype(bf16)
    query_rot = rotate(
        query_pre.reshape(local_rows, query_heads, head_width), cosine_table, sine_table
    ).astype(bf16)
    query_rot = query_rot.reshape(local_rows, kv_heads, group_size, head_width)
    key_rot = rotate(
        key_pre.reshape(local_rows, kv_heads, head_width), cosine_table, sine_table
    ).astype(bf16)
    key_rot = key_rot.reshape(local_rows, kv_width)
    key_all, value_all, seg_all = (
        lax.all_gather(key_rot, "context", axis=0, tiled=True),
        lax.all_gather(value_low, "context", axis=0, tiled=True),
        lax.all_gather(seg_local, "context", axis=0, tiled=True),
    )
    block_rows = min(block_limit, seq_len)
    block_count = seq_len // block_rows
    numbers = jnp.arange(block_count, dtype=jnp.int32)

    def take_block(array, number):
        return lax.dynamic_slice_in_dim(array, number * block_rows, block_rows, 0)

    def scores_for(number):
        key_block = take_block(key_all, number).reshape(block_rows, kv_heads, head_width)
        key_pos = number * block_rows + jnp.arange(block_rows, dtype=jnp.int32)
        scores = (
            jnp.einsum("qhgd,khd->hgqk", query_rot, key_block, preferred_element_type=f32) * factor
        )
        allowed = (seg_local[:, None] == take_block(seg_all, number)[None, :]) & (
            key_pos[None, :] <= positions[:, None]
        )
        return (scores, allowed, key_block)

    def stat_step(state_carry, number):
        running_top, running_total = state_carry
        scores, allowed, unused = scores_for(number)
        masked = jnp.where(allowed, scores, negative_large)
        new_top = jnp.maximum(running_top, jnp.max(masked, axis=-1))
        kept_exp = jnp.where(allowed, jnp.exp(masked - new_top[..., None]), 0.0)
        running_total = running_total * jnp.exp(running_top - new_top) + jnp.sum(kept_exp, axis=-1)
        return ((new_top, running_total), None)

    stat_shape = (kv_heads, group_size, local_rows)
    (final_top, final_total), unused = lax.scan(
        stat_step,
        (jnp.full(stat_shape, negative_large, f32), jnp.zeros(stat_shape, f32)),
        numbers,
    )
    log_total = final_top + jnp.log(final_total)

    def out_step(accumulated, number):
        scores, allowed, unused = scores_for(number)
        soft_low = jnp.where(allowed, jnp.exp(scores - log_total[..., None]), 0.0).astype(bf16)
        value_block = take_block(value_all, number).reshape(block_rows, kv_heads, head_width)
        return (
            accumulated
            + jnp.einsum("hgqk,khd->qhgd", soft_low, value_block, preferred_element_type=f32),
            None,
        )

    attn_full, unused = lax.scan(
        out_step, jnp.zeros((local_rows, kv_heads, group_size, head_width), f32), numbers
    )
    attn_low = attn_full.reshape(local_rows, query_heads * head_width).astype(bf16)
    middle = residual_in + jnp.dot(attn_low, w_out, preferred_element_type=f32)
    second_out, second_normed, second_inverse = norm_forward(middle, moe_gain)
    second_low = second_out.astype(bf16)
    logits = jnp.dot(second_low, w_router, preferred_element_type=f32)
    router_soft = jax.nn.softmax(logits, axis=-1)
    tables = jnp.stack([slots, router_soft.T])

    rows_all, tables_all = gather_all([second_low, tables], "expert", ne, 1, "rows_gather")
    mine = lax.dynamic_slice_in_dim(tables_all, my_expert * local_experts, local_experts, 2)
    slot_mine, gate_mine = mine[:, 0], mine[:, 1]
    hits = slot_mine[:, :, None, :] == jnp.arange(capacity, dtype=f32)[None, None, :, None]
    gate_slot = jnp.sum(jnp.where(hits, gate_mine[:, :, None, :], 0.0), axis=-1)
    hits_low = hits.astype(bf16)
    rows_in = jnp.einsum("xest,xtd->xesd", hits_low, rows_all, preferred_element_type=f32).astype(
        bf16
    )
    grads_in = jnp.einsum("xest,xtd->xesd", hits_low, grad_all, preferred_element_type=f32)
    received = (gate_slot[..., None] * grads_in).astype(bf16)
    gate_pre = jnp.einsum("secd,edf->secf", rows_in, w_gate, preferred_element_type=f32)
    up_pre = jnp.einsum("secd,edf->secf", rows_in, w_up, preferred_element_type=f32)
    sigmoid_gate = jax.nn.sigmoid(gate_pre)
    silu_gate = gate_pre * sigmoid_gate
    hidden = (silu_gate * up_pre).astype(bf16)
    produced = jnp.einsum("secf,efd->secd", hidden, w_down, preferred_element_type=f32)
    pair_grad = jnp.sum(grads_in * produced, axis=-1)
    soft_part = jnp.sum(jnp.where(hits, pair_grad[..., None], 0.0), axis=2)
    weighed = (gate_slot[..., None] * produced).astype(bf16)
    out_part = jnp.einsum("xest,xesd->xtd", hits_low, weighed, preferred_element_type=f32).astype(
        bf16
    )
    hidden_back = jnp.einsum("secd,efd->secf", received, w_down, preferred_element_type=f32)
    gate_back = (
        hidden_back * up_pre * sigmoid_gate * (1.0 + gate_pre * (1.0 - sigmoid_gate))
    ).astype(bf16)
    up_back = (hidden_back * silu_gate).astype(bf16)
    dispatch_back = (
        jnp.einsum("secf,edf->secd", gate_back, w_gate, preferred_element_type=f32)
        + jnp.einsum("secf,edf->secd", up_back, w_up, preferred_element_type=f32)
    ).astype(bf16)
    back_part = jnp.einsum(
        "xest,xesd->xtd", hits_low, dispatch_back, preferred_element_type=f32
    ).astype(bf16)
    second_sum, soft_all = scatter_all(
        [back_part], [f32], [soft_part], "expert", ne, 2, "rows_return"
    )
    out_sum = lax.psum_scatter(out_part, "expert", scatter_dimension=0, tiled=False)
    layer_out = middle + out_sum.astype(f32)

    gate_wgrad = jnp.einsum("secd,secf->edf", rows_in, gate_back, preferred_element_type=f32)
    up_wgrad = jnp.einsum("secd,secf->edf", rows_in, up_back, preferred_element_type=f32)
    down_wgrad = jnp.einsum("secf,secd->efd", hidden, received, preferred_element_type=f32)

    def expert_pieces(wgrad):
        e, r, c = wgrad.shape
        return wgrad.astype(bf16).reshape(e, nz, nd, r // (nz * nd), c)

    def expert_sum(wgrad):
        pieces = expert_pieces(wgrad)
        held = core_sum(jnp.moveaxis(pieces, 2, 0), my_dp, nd)
        return line_sum(jnp.moveaxis(held, 1, 0), my_ctx, nz)

    gate_shard, up_shard, down_shard = (
        expert_sum(gate_wgrad),
        expert_sum(up_wgrad),
        expert_sum(down_wgrad),
    )

    grad_top = out_grad[0].astype(f32)
    pick_table = (
        expert_choice[0][:, :, None] == jnp.arange(experts_all, dtype=jnp.int32)[None, None, :]
    )
    soft_back = soft_all.reshape(experts_all, local_rows).T
    logit_back = (
        router_soft * (soft_back - jnp.sum(router_soft * soft_back, axis=-1, keepdims=True))
    ).astype(bf16)
    second_back = second_sum + jnp.dot(logit_back, w_router.T, preferred_element_type=f32)
    router_wgrad = jnp.dot(second_low.T, logit_back, preferred_element_type=f32)
    middle_norm_back, moe_gain_grad = norm_backward(
        second_back, second_normed, second_inverse, moe_gain
    )
    middle_grad = grad_top + middle_norm_back
    branch_back = middle_grad.astype(bf16)
    out_wgrad = jnp.dot(attn_low.T, branch_back, preferred_element_type=f32)
    attn_back = jnp.dot(branch_back, w_out.T, preferred_element_type=f32).astype(bf16)
    attn_back = attn_back.reshape(local_rows, kv_heads, group_size, head_width)
    delta = jnp.einsum("qhgd,qhgd->hgq", attn_back.astype(f32), attn_full)

    def grad_step(query_acc, number):
        scores, allowed, key_block = scores_for(number)
        value_block = take_block(value_all, number).reshape(block_rows, kv_heads, head_width)
        soft = jnp.where(allowed, jnp.exp(scores - log_total[..., None]), 0.0)
        soft_low = soft.astype(bf16)
        value_part = jnp.einsum("hgqk,qhgd->khd", soft_low, attn_back, preferred_element_type=f32)
        soft_grad = jnp.einsum("qhgd,khd->hgqk", attn_back, value_block, preferred_element_type=f32)
        score_back = (soft * (soft_grad - delta[..., None])).astype(bf16)
        query_acc = (
            query_acc
            + jnp.einsum("hgqk,khd->qhgd", score_back, key_block, preferred_element_type=f32)
            * factor
        )
        key_part = (
            jnp.einsum("hgqk,qhgd->khd", score_back, query_rot, preferred_element_type=f32) * factor
        )
        return (query_acc, (key_part, value_part))

    qrot_back, (key_parts, value_parts) = lax.scan(
        grad_step, jnp.zeros((local_rows, kv_heads, group_size, head_width), f32), numbers
    )
    kv_parts = jnp.concatenate(
        [key_parts.reshape(seq_len, kv_width), value_parts.reshape(seq_len, kv_width)], axis=1
    ).astype(bf16)
    (own_kv,) = scatter_all(
        [kv_parts.reshape(nz, local_rows, 2 * kv_width)], [f32], [], "context", nz, 3, "kv_return"
    )
    own_key_back, own_value_back = own_kv[:, :kv_width], own_kv[:, kv_width:]
    query_back = rotate_back(
        qrot_back.reshape(local_rows, query_heads, head_width), cosine_table, sine_table
    )
    query_back = query_back.reshape(local_rows, query_heads * head_width).astype(bf16)
    key_back = rotate_back(
        own_key_back.reshape(local_rows, kv_heads, head_width), cosine_table, sine_table
    )
    key_back = key_back.reshape(local_rows, kv_width).astype(bf16)
    value_back = own_value_back.astype(bf16)
    query_wgrad = jnp.dot(first_low.T, query_back, preferred_element_type=f32)
    key_wgrad = jnp.dot(first_low.T, key_back, preferred_element_type=f32)
    value_wgrad = jnp.dot(first_low.T, value_back, preferred_element_type=f32)
    first_back = (
        jnp.dot(query_back, w_query.T, preferred_element_type=f32)
        + jnp.dot(key_back, w_key.T, preferred_element_type=f32)
        + jnp.dot(value_back, w_value.T, preferred_element_type=f32)
    )
    input_norm_back, attn_gain_grad = norm_backward(
        first_back, first_normed, first_inverse, attn_gain
    )
    input_grad = middle_grad + input_norm_back

    small = jnp.concatenate(
        [router_wgrad, attn_gain_grad[:, None], moe_gain_grad[:, None]], axis=1
    )
    small_width = -(-small.shape[1] // 128) * 128
    small = jnp.pad(small, ((0, 0), (0, small_width - small.shape[1])))
    packed = jnp.concatenate(
        [
            query_wgrad.astype(bf16),
            key_wgrad.astype(bf16),
            value_wgrad.astype(bf16),
            out_wgrad.astype(bf16),
            small.astype(bf16),
        ],
        axis=1,
    )
    width = packed.shape[1]
    rows = model_width // (ne * nz * nd)
    pieces = packed.reshape(ne, nz, nd, rows, width)
    held = core_sum(jnp.moveaxis(pieces, 2, 0), my_dp, nd)
    (held,) = scatter_all(
        [held.reshape(ne, nz * rows, width)], [bf16], [], "expert", ne, 4, "grads_plane"
    )
    (total,) = scatter_all(
        [held.reshape(nz, rows, width)], [f32], [], "context", nz, 5, "grads_line"
    )
    at = [0]
    for part in (query_wgrad, key_wgrad, value_wgrad, out_wgrad, router_wgrad):
        at.append(at[-1] + part.shape[1])
    query_shard, key_shard, value_shard, out_shard, router_shard = (
        total[:, a:b] for a, b in zip(at[:-1], at[1:])
    )
    attn_gain_shard = total[:, at[-1]]
    moe_gain_shard = total[:, at[-1] + 1]
    return (
        layer_out[None],
        input_grad[None],
        attn_gain_shard,
        moe_gain_shard,
        query_shard,
        key_shard,
        value_shard,
        out_shard,
        router_shard,
        gate_shard,
        up_shard,
        down_shard,
    )


def solution(mesh):
    sizes = (mesh.shape["expert"], mesh.shape["context"], mesh.shape["dp"])
    in_specs = (
        P(("expert", "dp"), "context", None),
        P(),
        P(),
        P(),
        P(),
        P(),
        P(),
        P(),
        P("expert", None, None),
        P("expert", None, None),
        P("expert", None, None),
        P(("expert", "dp"), "context"),
        P(("expert", "dp"), "context", None),
        P(("expert", "dp"), "context", None),
        P(("expert", "dp"), "context", None),
    )
    out_specs = (
        P(("expert", "dp"), "context", None),
        P(("expert", "dp"), "context", None),
        P(("expert", "context", "dp")),
        P(("expert", "context", "dp")),
        P(("expert", "context", "dp"), None),
        P(("expert", "context", "dp"), None),
        P(("expert", "context", "dp"), None),
        P(("expert", "context", "dp"), None),
        P(("expert", "context", "dp"), None),
        P("expert", ("context", "dp"), None),
        P("expert", ("context", "dp"), None),
        P("expert", ("context", "dp"), None),
    )
    return jax.shard_map(
        functools.partial(body, sizes),
        mesh=mesh,
        in_specs=in_specs,
        out_specs=out_specs,
        check_vma=False,
    )
```

```python
import functools

import jax
import jax.numpy as jnp
from jax import lax
from jax.experimental import pallas as pl
from jax.experimental.pallas import tpu as pltpu
from jax.sharding import PartitionSpec as P

HEAD_DIM = 64
MESH = pl.DeviceIdType.MESH

epsilon = 1e-06
rope_base = 10000.0
negative_large = -1e30
bf16 = jnp.bfloat16
f32 = jnp.float32


def gather_kernel(axis, size, count, *refs):
    ins, outs = refs[:count], refs[count : 2 * count]
    send_sem, recv_sem, own_sem = refs[2 * count :]
    me = lax.axis_index(axis)
    barrier = pltpu.get_barrier_semaphore()
    for step in range(1, size):
        pl.semaphore_signal(
            barrier, inc=1, device_id={axis: lax.rem(me + step, size)}, device_id_type=MESH
        )
    pl.semaphore_wait(barrier, size - 1)
    copies = []
    for step in range(1, size):
        for k in range(count):
            copies.append(
                pltpu.make_async_remote_copy(
                    src_ref=ins[k],
                    dst_ref=outs[k].at[me],
                    send_sem=send_sem.at[k, step],
                    recv_sem=recv_sem.at[k, step],
                    device_id={axis: lax.rem(me + step, size)},
                    device_id_type=MESH,
                )
            )
            copies[-1].start()
    own = [
        pltpu.make_async_copy(ins[k], outs[k].at[me], own_sem.at[k]) for k in range(count)
    ]
    for copy in own:
        copy.start()
    for copy in own + copies:
        copy.wait()


def gather_all(arrays, axis, size, cid, name):
    count = len(arrays)
    return pl.pallas_call(
        functools.partial(gather_kernel, axis, size, count),
        out_shape=tuple(jax.ShapeDtypeStruct((size,) + a.shape, a.dtype) for a in arrays),
        in_specs=[pl.BlockSpec(memory_space=pl.ANY)] * count,
        out_specs=tuple([pl.BlockSpec(memory_space=pl.ANY)] * count),
        scratch_shapes=[
            pltpu.SemaphoreType.DMA((count, size)),
            pltpu.SemaphoreType.DMA((count, size)),
            pltpu.SemaphoreType.DMA((count,)),
        ],
        compiler_params=pltpu.CompilerParams(collective_id=cid, has_side_effects=True),
        name=name,
    )(*arrays)


def scatter_kernel(axis, size, sums, cats, *refs):
    count = sums + cats
    ins, outs = refs[:count], refs[count : 2 * count]
    bufs = refs[2 * count : 2 * count + sums]
    own_bufs = refs[2 * count + sums : 2 * count + 2 * sums]
    send_sem, recv_sem, own_sem = refs[2 * count + 2 * sums :]
    me = lax.axis_index(axis)
    barrier = pltpu.get_barrier_semaphore()
    for step in range(1, size):
        pl.semaphore_signal(
            barrier, inc=1, device_id={axis: lax.rem(me + step, size)}, device_id_type=MESH
        )
    pl.semaphore_wait(barrier, size - 1)
    copies = []
    for step in range(1, size):
        other = lax.rem(me + step, size)
        for k in range(count):
            copies.append(
                pltpu.make_async_remote_copy(
                    src_ref=ins[k].at[other],
                    dst_ref=bufs[k].at[step - 1] if k < sums else outs[k].at[me],
                    send_sem=send_sem.at[k, step],
                    recv_sem=recv_sem.at[k, step],
                    device_id={axis: other},
                    device_id_type=MESH,
                )
            )
            copies[-1].start()
    own = [
        pltpu.make_async_copy(
            ins[k].at[me], own_bufs[k] if k < sums else outs[k].at[me], own_sem.at[k]
        )
        for k in range(count)
    ]
    for copy in own:
        copy.start()
    for copy in own + copies:
        copy.wait()
    for k in range(sums):
        rows = outs[k].shape[0]
        step_rows = 16

        @pl.loop(0, rows // step_rows)
        def _(i):
            at = pl.ds(pl.multiple_of(i * step_rows, step_rows), step_rows)
            total = own_bufs[k][at, :].astype(f32)
            for step in range(size - 1):
                total = total + bufs[k][step, at, :].astype(f32)
            outs[k][at, :] = total.astype(outs[k].dtype)


def scatter_all(sum_arrays, sum_types, cat_arrays, axis, size, cid, name):
    arrays = list(sum_arrays) + list(cat_arrays)
    sums, cats = len(sum_arrays), len(cat_arrays)
    out_shape = [
        jax.ShapeDtypeStruct(a.shape[1:], t) for a, t in zip(sum_arrays, sum_types)
    ] + [jax.ShapeDtypeStruct(a.shape, a.dtype) for a in cat_arrays]
    return pl.pallas_call(
        functools.partial(scatter_kernel, axis, size, sums, cats),
        out_shape=tuple(out_shape),
        in_specs=[pl.BlockSpec(memory_space=pl.ANY)] * (sums + cats),
        out_specs=tuple(
            [pl.BlockSpec(memory_space=pltpu.VMEM)] * sums
            + [pl.BlockSpec(memory_space=pl.ANY)] * cats
        ),
        scratch_shapes=[
            pltpu.VMEM((size - 1,) + a.shape[1:], a.dtype) for a in sum_arrays
        ]
        + [pltpu.VMEM(a.shape[1:], a.dtype) for a in sum_arrays]
        + [
            pltpu.SemaphoreType.DMA((sums + cats, size)),
            pltpu.SemaphoreType.DMA((sums + cats, size)),
            pltpu.SemaphoreType.DMA((sums + cats,)),
        ],
        compiler_params=pltpu.CompilerParams(
            collective_id=cid, has_side_effects=True, vmem_limit_bytes=24 << 20
        ),
        name=name,
    )(*arrays)


def take(array, index, axis=0):
    return lax.dynamic_index_in_dim(array, index, axis, keepdims=False)


def core_sum(pieces, axis_index, size):
    total = take(pieces, axis_index).astype(f32)
    for step in range(1, size):
        gone = take(pieces, lax.rem(axis_index + step, size))
        got = lax.ppermute(gone, "dp", [(i, (i + step) % size) for i in range(size)])
        total = total + got.astype(f32)
    return total.astype(bf16)


def nt(a, b):
    return lax.dot_general(a, b, (((1,), (1,)), ((), ())), preferred_element_type=f32)


def tn(a, b):
    return lax.dot_general(a, b, (((0,), (0,)), ((), ())), preferred_element_type=f32)


def nn(a, b):
    return jnp.dot(a, b, preferred_element_type=f32)


def experts_kernel(
    sizes,
    cap,
    x_ref,
    og_ref,
    tab_ref,
    wg_ref,
    wu_ref,
    wd_ref,
    grads_ref,
    outp_ref,
    backp_ref,
    soft_ref,
    x_s,
    og_s,
    sg_s,
    gate_s,
    hit_s,
    out_acc,
    back_acc,
):
    ne, nz, nd = sizes
    e = pl.program_id(0)
    local = pl.num_programs(0)
    me = lax.axis_index("expert")
    tokens = x_ref.shape[1]
    half = wg_ref.shape[2]

    @pl.when(e == 0)
    def _():
        out_acc[...] = jnp.zeros_like(out_acc)
        back_acc[...] = jnp.zeros_like(back_acc)

    row_id = lax.broadcasted_iota(jnp.int32, (cap, tokens), 0).astype(f32)
    for src in range(ne):
        at = pl.ds(src * cap, cap)
        hits = tab_ref[src, 0, pl.ds(me * local + e, 1), :] == row_id
        gate_row = tab_ref[src, 1, pl.ds(me * local + e, 1), :]
        gate = jnp.sum(jnp.where(hits, gate_row, 0.0), axis=1, keepdims=True)
        low = jnp.where(hits, 1.0, 0.0).astype(bf16)
        hit_s[at, :] = low
        gate_s[at, :] = jnp.broadcast_to(gate, (cap, 128))
        x_s[at, :] = nn(low, x_ref[src]).astype(bf16)
        og = nn(low, og_ref[src])
        og_s[at, :] = og.astype(bf16)
        sg_s[at, :] = (og * gate).astype(bf16)
    wg, wu, wd = wg_ref[0], wu_ref[0], wd_ref[0]
    x, sg = x_s[...], sg_s[...]
    gate_pre = nn(x, wg)
    up_pre = nn(x, wu)
    sig = jax.nn.sigmoid(gate_pre)
    silu = gate_pre * sig
    hidden = (silu * up_pre).astype(bf16)
    hidden_back = nt(sg, wd)
    gate_back = (hidden_back * up_pre * sig * (1.0 + gate_pre * (1.0 - sig))).astype(bf16)
    up_back = (hidden_back * silu).astype(bf16)
    produced = nn(hidden, wd)
    pair = jnp.sum(og_s[...].astype(f32) * produced, axis=1, keepdims=True)
    weighed = (produced * gate_s[:, :1]).astype(bf16)
    back = (nt(gate_back, wg) + nt(up_back, wu)).astype(bf16)
    for src in range(ne):
        a, b = src * cap, (src + 1) * cap
        low = hit_s[a:b, :]
        out_acc[src] += tn(low, weighed[a:b])
        back_acc[src] += tn(low, back[a:b])
        soft_ref[src, pl.ds(e, 1), :] = jnp.sum(
            low.astype(f32) * pair[a:b], axis=0, keepdims=True
        )
    gate_rows = wg.shape[0] // (nz * nd)
    down_rows = wd.shape[0] // (nz * nd)
    shape = (nz, nd, gate_rows, half)
    grads_ref[0, :, :, :gate_rows, :half] = tn(x, gate_back).astype(bf16).reshape(shape)
    grads_ref[0, :, :, :gate_rows, half:] = tn(x, up_back).astype(bf16).reshape(shape)
    grads_ref[0, :, :, gate_rows:, :] = (
        tn(hidden, sg).astype(bf16).reshape(nz, nd, down_rows, wd.shape[1])
    )

    @pl.when(e == local - 1)
    def _():
        outp_ref[...] = out_acc[...].astype(bf16)
        backp_ref[...] = back_acc[...].astype(bf16)


def experts(sizes, cap, rows_all, grad_all, tables_all, w_gate, w_up, w_down):
    ne, nz, nd = sizes
    local, width, hid = w_gate.shape
    tokens = rows_all.shape[1]
    piece = (width // (nz * nd)) + (hid // (nz * nd))
    whole = pl.BlockSpec(memory_space=pltpu.VMEM)
    per = lambda shape: pl.BlockSpec((1,) + shape, lambda e: (e,) + (0,) * len(shape))
    return pl.pallas_call(
        functools.partial(experts_kernel, sizes, cap),
        grid=(local,),
        out_shape=(
            jax.ShapeDtypeStruct((local, nz, nd, piece, width), bf16),
            jax.ShapeDtypeStruct((ne, tokens, width), bf16),
            jax.ShapeDtypeStruct((ne, tokens, width), bf16),
            jax.ShapeDtypeStruct((ne, local, tokens), f32),
        ),
        in_specs=[whole, whole, whole, per((width, hid)), per((width, hid)), per((hid, width))],
        out_specs=(per((nz, nd, piece, width)), whole, whole, whole),
        scratch_shapes=[
            pltpu.VMEM((ne * cap, width), bf16),
            pltpu.VMEM((ne * cap, width), bf16),
            pltpu.VMEM((ne * cap, width), bf16),
            pltpu.VMEM((ne * cap, 128), f32),
            pltpu.VMEM((ne * cap, tokens), bf16),
            pltpu.VMEM((ne, tokens, width), f32),
            pltpu.VMEM((ne, tokens, width), f32),
        ],
        compiler_params=pltpu.CompilerParams(vmem_limit_bytes=56 << 20),
        name="experts",
    )(rows_all, grad_all, tables_all, w_gate, w_up, w_down)


def lane_half(shape, which):
    lanes = lax.broadcasted_iota(jnp.int32, shape, 1)
    return (lanes >= HEAD_DIM) if which else (lanes < HEAD_DIM)


def column_of(row):
    n = row.shape[1]
    rows = lax.broadcasted_iota(jnp.int32, (n, n), 0)
    cols = lax.broadcasted_iota(jnp.int32, (n, n), 1)
    return jnp.sum(jnp.where(rows == cols, row, 0.0), axis=1, keepdims=True)


def mask_bias(seg_ref, block, me, tokens):
    key_seg = column_of(seg_ref[block, :1, :])
    same = key_seg == seg_ref[me, :1, :]
    rows = lax.broadcasted_iota(jnp.int32, (tokens, tokens), 0) + block * tokens
    cols = lax.broadcasted_iota(jnp.int32, (tokens, tokens), 1) + me * tokens
    return jnp.where(same & (rows <= cols), 0.0, negative_large)


def attend_kernel(nz, q_ref, kv_ref, seg_ref, at_ref, lse_ref, kv_all, seg_all, acc, top, total, bias_s,
                  own_sem, kv_send, kv_recv, seg_send, seg_recv):
    me = lax.axis_index("context")
    tokens = kv_ref.shape[0]
    width = kv_ref.shape[1] // 2
    slices = width // 128
    barrier = pltpu.get_barrier_semaphore()

    @pl.when(me > 0)
    def _():
        pl.semaphore_signal(barrier, inc=1, device_id={"context": me - 1}, device_id_type=MESH)

    @pl.when(me < nz - 1)
    def _():
        pl.semaphore_signal(barrier, inc=1, device_id={"context": me + 1}, device_id_type=MESH)

    pl.semaphore_wait(
        barrier, jnp.where(me > 0, 1, 0) + jnp.where(me < nz - 1, 1, 0)
    )

    def up(slot):
        return [
            pltpu.make_async_remote_copy(
                src_ref=ref.at[slot],
                dst_ref=ref.at[slot],
                send_sem=send.at[slot],
                recv_sem=recv.at[slot],
                device_id={"context": me + 1},
                device_id_type=MESH,
            )
            for ref, send, recv in ((kv_all, kv_send, kv_recv), (seg_all, seg_send, seg_recv))
        ]

    own = [
        pltpu.make_async_copy(kv_ref, kv_all.at[me], own_sem.at[0]),
        pltpu.make_async_copy(seg_ref, seg_all.at[me], own_sem.at[1]),
    ]
    for copy in own:
        copy.start()
    for copy in own:
        copy.wait()

    @pl.when(me < nz - 1)
    def _():
        for copy in up(me):
            copy.start()

    acc[...] = jnp.zeros_like(acc)
    top[...] = jnp.full_like(top, -3e38)
    total[...] = jnp.zeros_like(total)

    def block(j):
        bias = mask_bias(seg_all, j, me, tokens)
        bias_s[:, :tokens] = bias
        bias_s[:, tokens:] = bias

        @pl.loop(0, slices)
        def _(t):
            k_at = pl.ds(pl.multiple_of(t * 128, 128), 128)
            v_at = pl.ds(pl.multiple_of(width + t * 128, 128), 128)
            keys = kv_all[j, :, k_at]
            vals = kv_all[j, :, v_at]
            for half in (0, 1):
                keep = lane_half((tokens, 128), half)
                zero = jnp.zeros_like(keys)
                scores = nt(jnp.where(keep, keys, zero), q_ref[t]) + bias_s[...]
                old = top[t, half : half + 1, :]
                new = jnp.maximum(old, jnp.max(scores, axis=0, keepdims=True))
                scale = jnp.exp(old - new)
                soft = jnp.exp(scores - new)
                top[t, half : half + 1, :] = new
                total[t, half : half + 1, :] = total[t, half : half + 1, :] * scale + jnp.sum(
                    soft, axis=0, keepdims=True
                )
                mixed = tn(jnp.where(keep, vals, zero), soft.astype(bf16))
                a, b = half * HEAD_DIM, (half + 1) * HEAD_DIM
                acc[t, a:b, :] = acc[t, a:b, :] * scale + mixed[a:b]

    block(me)
    for step in range(1, nz):
        j = me - step

        @pl.when(j >= 0)
        def _():
            for copy in up(j):
                copy.wait_recv()

            @pl.when(me < nz - 1)
            def _():
                for copy in up(j):
                    copy.start()

            block(j)

    for t in range(slices):
        lse_ref[t] = top[t] + jnp.log(total[t])
        for half in (0, 1):
            a, b = half * HEAD_DIM, (half + 1) * HEAD_DIM
            at_ref[2 * t + half] = (acc[t, a:b, :] / total[t, half : half + 1, :]).astype(bf16)
    for step in range(nz):
        j = me - step

        @pl.when((j >= 0) & (me < nz - 1))
        def _():
            for copy in up(j):
                copy.wait_send()


def attend(nz, q, kv, seg, cid):
    tokens = kv.shape[0]
    slices, wide, _ = q.shape
    vm = pl.BlockSpec(memory_space=pltpu.VMEM)
    return pl.pallas_call(
        functools.partial(attend_kernel, nz),
        out_shape=(
            jax.ShapeDtypeStruct((2 * slices, HEAD_DIM, wide), bf16),
            jax.ShapeDtypeStruct((slices, 2, wide), f32),
            jax.ShapeDtypeStruct((nz,) + kv.shape, bf16),
            jax.ShapeDtypeStruct((nz,) + seg.shape, f32),
        ),
        in_specs=[vm, pl.BlockSpec(memory_space=pl.ANY), pl.BlockSpec(memory_space=pl.ANY)],
        out_specs=(vm, vm, vm, vm),
        scratch_shapes=[
            pltpu.VMEM((slices, 128, wide), f32),
            pltpu.VMEM((slices, 2, wide), f32),
            pltpu.VMEM((slices, 2, wide), f32),
            pltpu.VMEM((tokens, wide), f32),
            pltpu.SemaphoreType.DMA((2,)),
            pltpu.SemaphoreType.DMA((nz,)),
            pltpu.SemaphoreType.DMA((nz,)),
            pltpu.SemaphoreType.DMA((nz,)),
            pltpu.SemaphoreType.DMA((nz,)),
        ],
        compiler_params=pltpu.CompilerParams(
            collective_id=cid, has_side_effects=True, vmem_limit_bytes=30 << 20
        ),
        name="attend",
    )(q, kv, seg)


def add_rows(dst, dst_at, src, src_at, rows):
    step = 16

    @pl.loop(0, rows // step)
    def _(i):
        at = pl.ds(pl.multiple_of(i * step, step), step)
        dst[dst_at + (at, slice(None))] = (
            dst[dst_at + (at, slice(None))].astype(f32) + src[src_at + (at, slice(None))].astype(f32)
        ).astype(bf16)


class Pieces:
    def __init__(self, nz, nd, grads, held, from_dp, from_low, from_high, sems):
        self.nz, self.nd, self.grads, self.held = nz, nd, grads, held
        self.from_dp, self.from_low, self.from_high = from_dp, from_low, from_high
        self.own_sem, self.dp_send, self.dp_recv, self.send, self.recv = sems
        self.me, self.dp = lax.axis_index("context"), lax.axis_index("dp")
        self.chunks, self.rows = grads.shape[0], grads.shape[3]

    @staticmethod
    def scratch(nz, nd, chunks, rows, width):
        return [
            pltpu.VMEM((chunks, nz, rows, width), bf16),
            pltpu.VMEM((nd - 1, chunks, nz, rows, width), bf16),
            pltpu.VMEM((chunks, nz, rows, width), bf16),
            pltpu.VMEM((chunks, nz, rows, width), bf16),
            pltpu.SemaphoreType.DMA((chunks,)),
            pltpu.SemaphoreType.DMA((chunks, nd)),
            pltpu.SemaphoreType.DMA((chunks, nd)),
            pltpu.SemaphoreType.DMA((2, chunks, nz)),
            pltpu.SemaphoreType.DMA((2, chunks, nz)),
        ]

    def own(self, k):
        return pltpu.make_async_copy(
            self.grads.at[k, :, self.dp], self.held.at[k], self.own_sem.at[k]
        )

    def dp_copy(self, k, step):
        other = lax.rem(self.dp + step, self.nd)
        return pltpu.make_async_remote_copy(
            src_ref=self.grads.at[k, :, other],
            dst_ref=self.from_dp.at[step - 1, k],
            send_sem=self.dp_send.at[k, step],
            recv_sem=self.dp_recv.at[k, step],
            device_id={"dp": other},
            device_id_type=MESH,
        )

    def hop(self, k, s, upward):
        way = 0 if upward else 1
        return pltpu.make_async_remote_copy(
            src_ref=self.held.at[k, s],
            dst_ref=(self.from_low if upward else self.from_high).at[k, s],
            send_sem=self.send.at[way, k, s],
            recv_sem=self.recv.at[way, k, s],
            device_id={"context": self.me + 1 if upward else self.me - 1},
            device_id_type=MESH,
        )

    def greet(self, barrier):
        for step in range(1, self.nd):
            pl.semaphore_signal(
                barrier,
                inc=1,
                device_id={"dp": lax.rem(self.dp + step, self.nd)},
                device_id_type=MESH,
            )

    def begin(self):
        for k in range(self.chunks):
            self.own(k).start()
            for step in range(1, self.nd):
                self.dp_copy(k, step).start()

    def cores(self, k):
        self.own(k).wait()
        for step in range(1, self.nd):
            self.dp_copy(k, step).wait_recv()
            for s in range(self.nz):
                add_rows(self.held, (k, s), self.from_dp, (step - 1, k, s), self.rows)

        @pl.when(self.me == 0)
        def _():
            for s in reversed(range(1, self.nz)):
                self.hop(k, s, True).start()

        @pl.when(self.me == self.nz - 1)
        def _():
            for s in range(self.nz - 1):
                self.hop(k, s, False).start()

    def line(self, k, i):
        nz, me = self.nz, self.me
        s = nz - 1 - i

        @pl.when((me > 0) & (me <= s))
        def _():
            self.hop(k, s, True).wait_recv()
            add_rows(self.held, (k, s), self.from_low, (k, s), self.rows)

            @pl.when(me < s)
            def _():
                self.hop(k, s, True).start()

        @pl.when((me < nz - 1) & (me >= i))
        def _():
            self.hop(k, i, False).wait_recv()
            add_rows(self.held, (k, i), self.from_high, (k, i), self.rows)

            @pl.when(me > i)
            def _():
                self.hop(k, i, False).start()

    def finish(self, k, out, out_k):
        step = 16

        @pl.loop(0, self.rows // step)
        def _(i):
            at = pl.ds(pl.multiple_of(i * step, step), step)
            out[out_k, at, :] = self.held[k, self.me, at, :].astype(f32)

        for step_dp in range(1, self.nd):
            self.dp_copy(k, step_dp).wait_send()
        for s in range(self.nz):

            @pl.when(self.me < s)
            def _():
                self.hop(k, s, True).wait_send()

            @pl.when(self.me > s)
            def _():
                self.hop(k, s, False).wait_send()


def attend_back_kernel(nz, nd, q_ref, kv_all, seg_all, lse_ref, do_ref, at_ref, grads_ref,
                       dq_ref, dkv_ref, shard_ref, part, came, own_kv, bias_s, delta,
                       send_sem, recv_sem, held, from_dp, from_low, from_high, *sems):
    me = lax.axis_index("context")
    tokens = kv_all.shape[1]
    width = kv_all.shape[2] // 2
    slices = width // 128
    pieces = Pieces(nz, nd, grads_ref, held, from_dp, from_low, from_high, sems)
    barrier = pltpu.get_barrier_semaphore()
    for step in range(1, nz):
        pl.semaphore_signal(
            barrier, inc=1, device_id={"context": lax.rem(me + step, nz)}, device_id_type=MESH
        )
    pieces.greet(barrier)
    pl.semaphore_wait(barrier, nz - 1 + nd - 1)
    pieces.begin()

    dq_ref[...] = jnp.zeros_like(dq_ref)
    for t in range(slices):
        for half in (0, 1):
            a, b = half * HEAD_DIM, (half + 1) * HEAD_DIM
            delta[t, half : half + 1, :] = jnp.sum(
                do_ref[t, a:b, :].astype(f32) * at_ref[2 * t + half].astype(f32),
                axis=0,
                keepdims=True,
            )

    def block(j, store):
        bias = mask_bias(seg_all, j, me, tokens)
        bias_s[:, :tokens] = bias
        bias_s[:, tokens:] = bias

        @pl.loop(0, slices)
        def _(t):
            k_at = pl.ds(pl.multiple_of(t * 128, 128), 128)
            v_at = pl.ds(pl.multiple_of(width + t * 128, 128), 128)
            keys = kv_all[j, :, k_at]
            vals = kv_all[j, :, v_at]
            dks, dvs = [], []
            for half in (0, 1):
                keep = lane_half((tokens, 128), half)
                zero = jnp.zeros_like(keys)
                keys_half = jnp.where(keep, keys, zero)
                scores = nt(keys_half, q_ref[t]) + bias_s[...]
                soft = jnp.exp(scores - lse_ref[t, half : half + 1, :])
                soft_grad = nn(jnp.where(keep, vals, zero), do_ref[t])
                back = (soft * (soft_grad - delta[t, half : half + 1, :])).astype(bf16)
                dvs.append(nt(soft.astype(bf16), do_ref[t]))
                dks.append(nn(back, q_ref[t]))
                dq_ref[t] += tn(keys_half, back)
            low = lane_half((tokens, 128), 0)
            store(k_at, jnp.where(low, dks[0], dks[1]))
            store(v_at, jnp.where(low, dvs[0], dvs[1]))

    def give(j):
        return pltpu.make_async_remote_copy(
            src_ref=part.at[j],
            dst_ref=came.at[me],
            send_sem=send_sem.at[j],
            recv_sem=recv_sem.at[me],
            device_id={"context": j},
            device_id_type=MESH,
        )

    for j in range(nz - 1):

        @pl.when(j < me)
        def _():
            def store(at, value):
                part[j, :, at] = value.astype(bf16)

            block(j, store)
            give(j).start()

        if j < pieces.chunks:
            pieces.cores(j)
    for k in range(nz - 1, pieces.chunks):
        pieces.cores(k)

    def store_own(at, value):
        own_kv[:, at] = value

    block(me, store_own)
    for j in range(1, nz):

        @pl.when(me < j)
        def _():
            pltpu.make_async_remote_copy(
                src_ref=part.at[0],
                dst_ref=came.at[j],
                send_sem=send_sem.at[0],
                recv_sem=recv_sem.at[j],
                device_id={"context": j},
                device_id_type=MESH,
            ).wait_recv()

            @pl.loop(0, tokens // 16)
            def _(i):
                at = pl.ds(pl.multiple_of(i * 16, 16), 16)
                own_kv[at, :] += came[j, at, :].astype(f32)

    dkv_ref[...] = own_kv[...]
    for k in range(pieces.chunks):
        for i in range(nz):
            pieces.line(k, i)
    for k in range(pieces.chunks):
        pieces.finish(k, shard_ref, k)
    for j in range(nz - 1):

        @pl.when(j < me)
        def _():
            give(j).wait_send()


def attend_back(nz, nd, q, kv_all, seg_all, lse, do, at, grads, cid):
    tokens = kv_all.shape[1]
    slices, wide, _ = q.shape
    chunks, _, _, rows, width = grads.shape
    vm = pl.BlockSpec(memory_space=pltpu.VMEM)
    return pl.pallas_call(
        functools.partial(attend_back_kernel, nz, nd),
        out_shape=(
            jax.ShapeDtypeStruct((slices, 128, wide), f32),
            jax.ShapeDtypeStruct(kv_all.shape[1:], f32),
            jax.ShapeDtypeStruct((chunks, rows, width), f32),
        ),
        in_specs=[vm] * 6 + [pl.BlockSpec(memory_space=pl.ANY)],
        out_specs=(vm, vm, vm),
        scratch_shapes=[
            pltpu.VMEM(kv_all.shape, bf16),
            pltpu.VMEM(kv_all.shape, bf16),
            pltpu.VMEM(kv_all.shape[1:], f32),
            pltpu.VMEM((tokens, wide), f32),
            pltpu.VMEM((slices, 2, wide), f32),
            pltpu.SemaphoreType.DMA((nz,)),
            pltpu.SemaphoreType.DMA((nz,)),
        ]
        + Pieces.scratch(nz, nd, chunks, rows, width),
        compiler_params=pltpu.CompilerParams(
            collective_id=cid, has_side_effects=True, vmem_limit_bytes=58 << 20
        ),
        name="attend_back",
    )(q, kv_all, seg_all, lse, do, at, grads)


def norm_forward(values, scale_gain):
    inverse = lax.rsqrt(jnp.mean(values * values, axis=-1, keepdims=True) + epsilon)
    normed = values * inverse
    return (normed * scale_gain, normed, inverse)


def norm_backward(upstream, normed, inverse, scale_gain):
    scaled = upstream * scale_gain
    gain_grad = jnp.sum(upstream * normed, axis=0)
    inner_mean = jnp.mean(scaled * normed, axis=-1, keepdims=True)
    return (inverse * (scaled - normed * inner_mean), gain_grad)


def rope_tables(positions, head_width):
    halves = head_width // 2
    inverse_freq = rope_base ** (-2.0 * jnp.arange(halves, dtype=f32) / head_width)
    angles = positions.astype(f32)[:, None] * inverse_freq[None, :]
    return (jnp.cos(angles)[:, None, :], jnp.sin(angles)[:, None, :])


def rotate(values, cosine_table, sine_table):
    halves = values.shape[-1] // 2
    first_half = values[..., :halves]
    second_half = values[..., halves:]
    return jnp.concatenate(
        [
            first_half * cosine_table - second_half * sine_table,
            second_half * cosine_table + first_half * sine_table,
        ],
        axis=-1,
    )


def rotate_back(upstream, cosine_table, sine_table):
    return rotate(upstream, cosine_table, -sine_table)


def slot_table(chosen, turn_order, experts_all, capacity):
    tokens, top_count = chosen.shape
    pair_count = tokens * top_count
    turns = jnp.arange(pair_count, dtype=jnp.int32)
    owner = (turn_order // top_count)[:, None] == jnp.arange(tokens, dtype=jnp.int32)[None, :]
    which = (turn_order % top_count)[:, None] == jnp.arange(top_count, dtype=jnp.int32)[None, :]
    high = jnp.where(which, (turns // 256)[:, None], 0)
    low = jnp.where(which, (turns % 256)[:, None], 0)
    both = jnp.concatenate([high, low], axis=1).astype(bf16)
    found = lax.dot_general(
        owner.astype(bf16), both, (((0,), (0,)), ((), ())), preferred_element_type=f32
    )
    turn_of = found[:, :top_count] * 256.0 + found[:, top_count:]
    picks = chosen[:, :, None] == jnp.arange(experts_all, dtype=jnp.int32)[None, None, :]
    far = float(2 * pair_count)
    turn_at = far + jnp.sum(jnp.where(picks, turn_of[:, :, None] - far, 0.0), axis=1)
    turn_row = turn_at.T
    rank = jnp.sum((turn_row[:, :, None] < turn_row[:, None, :]).astype(f32), axis=1)
    return jnp.where((turn_row < far) & (rank < capacity), rank, -1.0)


def body(
    sizes,
    tokens,
    attn_scale,
    w_query,
    w_key,
    w_value,
    w_out,
    moe_scale,
    w_router,
    w_gate,
    w_up,
    w_down,
    segment_ids,
    expert_choice,
    slot_order,
    out_grad,
):
    ne, nz, nd = sizes
    my_expert = lax.axis_index("expert")
    my_ctx = lax.axis_index("context")
    my_dp = lax.axis_index("dp")
    local_rows = tokens.shape[1]
    model_width = tokens.shape[2]
    head_width = HEAD_DIM
    query_heads = w_query.shape[1] // head_width
    kv_heads = w_key.shape[1] // head_width
    kv_width = kv_heads * head_width
    group_size = query_heads // kv_heads
    factor = head_width ** (-0.5)
    experts_all = w_router.shape[1]
    local_experts = w_gate.shape[0]
    top_count = expert_choice.shape[2]
    pair_count = local_rows * top_count
    capacity = (pair_count * 9 + 8 * experts_all - 1) // (8 * experts_all)

    positions = my_ctx * local_rows + jnp.arange(local_rows, dtype=jnp.int32)
    cosine_table, sine_table = rope_tables(positions, head_width)
    residual_in = tokens[0].astype(f32)
    seg_local = segment_ids[0]
    attn_gain = attn_scale.astype(f32)
    moe_gain = moe_scale.astype(f32)

    grad_all = lax.all_gather(out_grad[0], "expert", axis=0)
    slots = slot_table(expert_choice[0], slot_order[0, 0], experts_all, capacity)

    first_out, first_normed, first_inverse = norm_forward(residual_in, attn_gain)
    first_low = first_out.astype(bf16)
    query_pre = jnp.dot(first_low, w_query, preferred_element_type=f32)
    key_pre = jnp.dot(first_low, w_key, preferred_element_type=f32)
    value_low = jnp.dot(first_low, w_value, preferred_element_type=f32).astype(bf16)
    query_rot = rotate(
        query_pre.reshape(local_rows, query_heads, head_width), cosine_table, sine_table
    ).astype(bf16)
    slices = kv_heads // 2
    query_in = (
        (query_rot * factor)
        .astype(bf16)
        .reshape(local_rows, slices, 2, group_size, head_width)
        .transpose(1, 3, 0, 2, 4)
        .reshape(slices, group_size * local_rows, 2 * head_width)
    )
    key_rot = rotate(
        key_pre.reshape(local_rows, kv_heads, head_width), cosine_table, sine_table
    ).astype(bf16)
    kv_own = jnp.concatenate([key_rot.reshape(local_rows, kv_width), value_low], axis=1)
    seg_own = jnp.broadcast_to(seg_local.astype(f32)[None, :], (8, local_rows))
    heads, log_total, kv_all, seg_all = attend(nz, query_in, kv_own, seg_own, 6)
    attn_turned = (
        heads.reshape(kv_heads, head_width, group_size, local_rows)
        .transpose(0, 2, 1, 3)
        .reshape(query_heads * head_width, local_rows)
    )
    middle = residual_in + tn(attn_turned, w_out)
    second_out, second_normed, second_inverse = norm_forward(middle, moe_gain)
    second_low = second_out.astype(bf16)
    logits = jnp.dot(second_low, w_router, preferred_element_type=f32)
    router_soft = jax.nn.softmax(logits, axis=-1)
    tables = jnp.stack([slots, router_soft.T])

    rows_all, tables_all = gather_all([second_low, tables], "expert", ne, 1, "rows_gather")
    expert_grads, out_part, back_part, soft_part = experts(
        sizes, capacity, rows_all, grad_all, tables_all, w_gate, w_up, w_down
    )
    second_sum, soft_all = scatter_all(
        [back_part], [f32], [soft_part], "expert", ne, 2, "rows_return"
    )
    out_sum = lax.psum_scatter(out_part, "expert", scatter_dimension=0, tiled=False)
    layer_out = middle + out_sum.astype(f32)

    grad_top = out_grad[0].astype(f32)
    soft_back = soft_all.reshape(experts_all, local_rows).T
    logit_back = (
        router_soft * (soft_back - jnp.sum(router_soft * soft_back, axis=-1, keepdims=True))
    ).astype(bf16)
    second_back = second_sum + jnp.dot(logit_back, w_router.T, preferred_element_type=f32)
    router_wgrad = jnp.dot(second_low.T, logit_back, preferred_element_type=f32)
    middle_norm_back, moe_gain_grad = norm_backward(
        second_back, second_normed, second_inverse, moe_gain
    )
    middle_grad = grad_top + middle_norm_back
    branch_back = middle_grad.astype(bf16)
    out_wgrad = nn(attn_turned, branch_back)
    attn_back = (
        nt(w_out, branch_back)
        .astype(bf16)
        .reshape(slices, 2, group_size, head_width, local_rows)
        .transpose(0, 1, 3, 2, 4)
        .reshape(slices, 2 * head_width, group_size * local_rows)
    )
    query_turned, own_kv, expert_shards = attend_back(
        nz, nd, query_in, kv_all, seg_all, log_total, attn_back, heads, expert_grads, 3
    )
    gate_rows = model_width // (nz * nd)
    hidden_width = w_gate.shape[2]
    gate_shard = expert_shards[:, :gate_rows, :hidden_width]
    up_shard = expert_shards[:, :gate_rows, hidden_width:]
    down_shard = expert_shards[:, gate_rows:, :]
    qrot_back = (
        query_turned.reshape(slices, 2, head_width, group_size, local_rows).transpose(4, 0, 1, 3, 2)
        * factor
    )
    own_key_back, own_value_back = own_kv[:, :kv_width], own_kv[:, kv_width:]
    query_back = rotate_back(
        qrot_back.reshape(local_rows, query_heads, head_width), cosine_table, sine_table
    )
    query_back = query_back.reshape(local_rows, query_heads * head_width).astype(bf16)
    key_back = rotate_back(
        own_key_back.reshape(local_rows, kv_heads, head_width), cosine_table, sine_table
    )
    key_back = key_back.reshape(local_rows, kv_width).astype(bf16)
    value_back = own_value_back.astype(bf16)
    query_wgrad = jnp.dot(first_low.T, query_back, preferred_element_type=f32)
    key_wgrad = jnp.dot(first_low.T, key_back, preferred_element_type=f32)
    value_wgrad = jnp.dot(first_low.T, value_back, preferred_element_type=f32)
    first_back = (
        jnp.dot(query_back, w_query.T, preferred_element_type=f32)
        + jnp.dot(key_back, w_key.T, preferred_element_type=f32)
        + jnp.dot(value_back, w_value.T, preferred_element_type=f32)
    )
    input_norm_back, attn_gain_grad = norm_backward(
        first_back, first_normed, first_inverse, attn_gain
    )
    input_grad = middle_grad + input_norm_back

    small = jnp.concatenate(
        [router_wgrad, attn_gain_grad[:, None], moe_gain_grad[:, None]], axis=1
    )
    small_width = -(-small.shape[1] // 128) * 128
    small = jnp.pad(small, ((0, 0), (0, small_width - small.shape[1])))
    packed = jnp.concatenate(
        [
            query_wgrad.astype(bf16),
            key_wgrad.astype(bf16),
            value_wgrad.astype(bf16),
            out_wgrad.astype(bf16),
            small.astype(bf16),
        ],
        axis=1,
    )
    width = packed.shape[1]
    rows = model_width // (ne * nz * nd)
    pieces = packed.reshape(ne, nz, nd, rows, width)
    held = core_sum(jnp.moveaxis(pieces, 2, 0), my_dp, nd)
    (held,) = scatter_all(
        [held.reshape(ne, nz * rows, width)], [bf16], [], "expert", ne, 4, "grads_plane"
    )
    (total,) = scatter_all(
        [held.reshape(nz, rows, width)], [f32], [], "context", nz, 5, "grads_line"
    )
    at = [0]
    for part in (query_wgrad, key_wgrad, value_wgrad, out_wgrad, router_wgrad):
        at.append(at[-1] + part.shape[1])
    query_shard, key_shard, value_shard, out_shard, router_shard = (
        total[:, a:b] for a, b in zip(at[:-1], at[1:])
    )
    attn_gain_shard = total[:, at[-1]]
    moe_gain_shard = total[:, at[-1] + 1]
    return (
        layer_out[None],
        input_grad[None],
        attn_gain_shard,
        moe_gain_shard,
        query_shard,
        key_shard,
        value_shard,
        out_shard,
        router_shard,
        gate_shard,
        up_shard,
        down_shard,
    )


def solution(mesh):
    sizes = (mesh.shape["expert"], mesh.shape["context"], mesh.shape["dp"])
    in_specs = (
        P(("expert", "dp"), "context", None),
        P(),
        P(),
        P(),
        P(),
        P(),
        P(),
        P(),
        P("expert", None, None),
        P("expert", None, None),
        P("expert", None, None),
        P(("expert", "dp"), "context"),
        P(("expert", "dp"), "context", None),
        P(("expert", "dp"), "context", None),
        P(("expert", "dp"), "context", None),
    )
    out_specs = (
        P(("expert", "dp"), "context", None),
        P(("expert", "dp"), "context", None),
        P(("expert", "context", "dp")),
        P(("expert", "context", "dp")),
        P(("expert", "context", "dp"), None),
        P(("expert", "context", "dp"), None),
        P(("expert", "context", "dp"), None),
        P(("expert", "context", "dp"), None),
        P(("expert", "context", "dp"), None),
        P("expert", ("context", "dp"), None),
        P("expert", ("context", "dp"), None),
        P("expert", ("context", "dp"), None),
    )
    return jax.shard_map(
        functools.partial(body, sizes),
        mesh=mesh,
        in_specs=in_specs,
        out_specs=out_specs,
        check_vma=False,
    )
```

```python
import functools

import jax
import jax.numpy as jnp
from jax import lax
from jax.experimental import pallas as pl
from jax.experimental.pallas import tpu as pltpu
from jax.sharding import PartitionSpec as P

HEAD_DIM = 64
MESH = pl.DeviceIdType.MESH

epsilon = 1e-06
rope_base = 10000.0
negative_large = -1e30
bf16 = jnp.bfloat16
f32 = jnp.float32


def gather_kernel(axis, size, count, *refs):
    ins, outs = refs[:count], refs[count : 2 * count]
    send_sem, recv_sem, own_sem = refs[2 * count :]
    me = lax.axis_index(axis)
    barrier = pltpu.get_barrier_semaphore()
    for step in range(1, size):
        pl.semaphore_signal(
            barrier, inc=1, device_id={axis: lax.rem(me + step, size)}, device_id_type=MESH
        )
    pl.semaphore_wait(barrier, size - 1)
    copies = []
    for step in range(1, size):
        for k in range(count):
            copies.append(
                pltpu.make_async_remote_copy(
                    src_ref=ins[k],
                    dst_ref=outs[k].at[me],
                    send_sem=send_sem.at[k, step],
                    recv_sem=recv_sem.at[k, step],
                    device_id={axis: lax.rem(me + step, size)},
                    device_id_type=MESH,
                )
            )
            copies[-1].start()
    own = [
        pltpu.make_async_copy(ins[k], outs[k].at[me], own_sem.at[k]) for k in range(count)
    ]
    for copy in own:
        copy.start()
    for copy in own + copies:
        copy.wait()


def gather_all(arrays, axis, size, cid, name):
    count = len(arrays)
    return pl.pallas_call(
        functools.partial(gather_kernel, axis, size, count),
        out_shape=tuple(jax.ShapeDtypeStruct((size,) + a.shape, a.dtype) for a in arrays),
        in_specs=[pl.BlockSpec(memory_space=pl.ANY)] * count,
        out_specs=tuple([pl.BlockSpec(memory_space=pl.ANY)] * count),
        scratch_shapes=[
            pltpu.SemaphoreType.DMA((count, size)),
            pltpu.SemaphoreType.DMA((count, size)),
            pltpu.SemaphoreType.DMA((count,)),
        ],
        compiler_params=pltpu.CompilerParams(collective_id=cid, has_side_effects=True),
        name=name,
    )(*arrays)


def nt(a, b):
    return lax.dot_general(a, b, (((1,), (1,)), ((), ())), preferred_element_type=f32)


def tn(a, b):
    return lax.dot_general(a, b, (((0,), (0,)), ((), ())), preferred_element_type=f32)


def nn(a, b):
    return jnp.dot(a, b, preferred_element_type=f32)


def add_rows(dst, dst_at, src, src_at, rows):
    step = 16

    @pl.loop(0, rows // step)
    def _(i):
        at = pl.ds(pl.multiple_of(i * step, step), step)
        dst[dst_at + (at, slice(None))] = (
            dst[dst_at + (at, slice(None))].astype(f32) + src[src_at + (at, slice(None))].astype(f32)
        ).astype(bf16)


def experts_kernel(
    sizes,
    cap,
    x_ref,
    og_ref,
    tab_ref,
    wg_ref,
    wu_ref,
    wd_ref,
    held_ref,
    outp_ref,
    backp_ref,
    soft_ref,
    x_s,
    og_s,
    sg_s,
    gate_s,
    hit_s,
    out_acc,
    back_acc,
    made,
    from_dp,
    dp_send,
    dp_recv,
):
    ne, nz, nd = sizes
    e = pl.program_id(0)
    local = pl.num_programs(0)
    me = lax.axis_index("expert")
    dp = lax.axis_index("dp")
    tokens = x_ref.shape[1]
    half = wg_ref.shape[2]

    @pl.when(e == 0)
    def _():
        barrier = pltpu.get_barrier_semaphore()
        for step in range(1, nd):
            pl.semaphore_signal(
                barrier, inc=1, device_id={"dp": lax.rem(dp + step, nd)}, device_id_type=MESH
            )
        pl.semaphore_wait(barrier, nd - 1)
        out_acc[...] = jnp.zeros_like(out_acc)
        back_acc[...] = jnp.zeros_like(back_acc)

    row_id = lax.broadcasted_iota(jnp.int32, (cap, tokens), 0).astype(f32)
    for src in range(ne):
        at = pl.ds(src * cap, cap)
        hits = tab_ref[src, 0, pl.ds(me * local + e, 1), :] == row_id
        gate_row = tab_ref[src, 1, pl.ds(me * local + e, 1), :]
        gate = jnp.sum(jnp.where(hits, gate_row, 0.0), axis=1, keepdims=True)
        low = jnp.where(hits, 1.0, 0.0).astype(bf16)
        hit_s[at, :] = low
        gate_s[at, :] = jnp.broadcast_to(gate, (cap, 128))
        x_s[at, :] = nn(low, x_ref[src]).astype(bf16)
        og = nn(low, og_ref[src])
        og_s[at, :] = og.astype(bf16)
        sg_s[at, :] = (og * gate).astype(bf16)
    wg, wu, wd = wg_ref[0], wu_ref[0], wd_ref[0]
    x, sg = x_s[...], sg_s[...]
    gate_pre = nn(x, wg)
    up_pre = nn(x, wu)
    sig = jax.nn.sigmoid(gate_pre)
    silu = gate_pre * sig
    hidden = (silu * up_pre).astype(bf16)
    hidden_back = nt(sg, wd)
    gate_back = (hidden_back * up_pre * sig * (1.0 + gate_pre * (1.0 - sig))).astype(bf16)
    up_back = (hidden_back * silu).astype(bf16)
    produced = nn(hidden, wd)
    pair = jnp.sum(og_s[...].astype(f32) * produced, axis=1, keepdims=True)
    weighed = (produced * gate_s[:, :1]).astype(bf16)
    back = (nt(gate_back, wg) + nt(up_back, wu)).astype(bf16)
    for src in range(ne):
        a, b = src * cap, (src + 1) * cap
        low = hit_s[a:b, :]
        out_acc[src] += tn(low, weighed[a:b])
        back_acc[src] += tn(low, back[a:b])
        soft_ref[src, pl.ds(e, 1), :] = jnp.sum(
            low.astype(f32) * pair[a:b], axis=0, keepdims=True
        )
    gate_rows = wg.shape[0] // (nz * nd)
    down_rows = wd.shape[0] // (nz * nd)
    shape = (nz, nd, gate_rows, half)

    def cores(k, step):
        other = lax.rem(dp + step, nd)
        return pltpu.make_async_remote_copy(
            src_ref=made.at[:, other],
            dst_ref=from_dp.at[step - 1, k],
            send_sem=dp_send.at[k, step],
            recv_sem=dp_recv.at[k, step],
            device_id={"dp": other},
            device_id_type=MESH,
        )

    def add_cores(k):
        for step in range(1, nd):
            cores(k, step).wait_recv()
            for z in range(nz):
                add_rows(held_ref, (k, z), from_dp, (step - 1, k, z), gate_rows + down_rows)

    @pl.when(e > 0)
    def _():
        for step in range(1, nd):
            cores(e - 1, step).wait_send()

    made[:, :, :gate_rows, :half] = tn(x, gate_back).astype(bf16).reshape(shape)
    made[:, :, :gate_rows, half:] = tn(x, up_back).astype(bf16).reshape(shape)
    made[:, :, gate_rows:, :] = (
        tn(hidden, sg).astype(bf16).reshape(nz, nd, down_rows, wd.shape[1])
    )
    for step in range(1, nd):
        cores(e, step).start()
    held_ref[e] = made[:, dp]

    @pl.when(e > 0)
    def _():
        add_cores(e - 1)

    @pl.when(e == local - 1)
    def _():
        outp_ref[...] = out_acc[...].astype(bf16)
        backp_ref[...] = back_acc[...].astype(bf16)
        add_cores(e)
        for step in range(1, nd):
            cores(e, step).wait_send()


def experts(sizes, cap, rows_all, grad_all, tables_all, w_gate, w_up, w_down):
    ne, nz, nd = sizes
    local, width, hid = w_gate.shape
    tokens = rows_all.shape[1]
    piece = (width // (nz * nd)) + (hid // (nz * nd))
    whole = pl.BlockSpec(memory_space=pltpu.VMEM)
    per = lambda shape: pl.BlockSpec((1,) + shape, lambda e: (e,) + (0,) * len(shape))
    return pl.pallas_call(
        functools.partial(experts_kernel, sizes, cap),
        grid=(local,),
        out_shape=(
            jax.ShapeDtypeStruct((local, nz, piece, width), bf16),
            jax.ShapeDtypeStruct((ne, tokens, width), bf16),
            jax.ShapeDtypeStruct((ne, tokens, width), bf16),
            jax.ShapeDtypeStruct((ne, local, tokens), f32),
        ),
        in_specs=[whole, whole, whole, per((width, hid)), per((width, hid)), per((hid, width))],
        out_specs=(whole, whole, whole, whole),
        scratch_shapes=[
            pltpu.VMEM((ne * cap, width), bf16),
            pltpu.VMEM((ne * cap, width), bf16),
            pltpu.VMEM((ne * cap, width), bf16),
            pltpu.VMEM((ne * cap, 128), f32),
            pltpu.VMEM((ne * cap, tokens), bf16),
            pltpu.VMEM((ne, tokens, width), f32),
            pltpu.VMEM((ne, tokens, width), f32),
            pltpu.VMEM((nz, nd, piece, width), bf16),
            pltpu.VMEM((nd - 1, local, nz, piece, width), bf16),
            pltpu.SemaphoreType.DMA((local, nd)),
            pltpu.SemaphoreType.DMA((local, nd)),
        ],
        compiler_params=pltpu.CompilerParams(
            collective_id=2, has_side_effects=True, vmem_limit_bytes=60 << 20
        ),
        name="experts",
    )(rows_all, grad_all, tables_all, w_gate, w_up, w_down)


def lane_half(shape, which):
    lanes = lax.broadcasted_iota(jnp.int32, shape, 1)
    return (lanes >= HEAD_DIM) if which else (lanes < HEAD_DIM)


def column_of(row):
    n = row.shape[1]
    rows = lax.broadcasted_iota(jnp.int32, (n, n), 0)
    cols = lax.broadcasted_iota(jnp.int32, (n, n), 1)
    return jnp.sum(jnp.where(rows == cols, row, 0.0), axis=1, keepdims=True)


def mask_bias(seg_ref, block, me, tokens):
    key_seg = column_of(seg_ref[block, :1, :])
    same = key_seg == seg_ref[me, :1, :]
    rows = lax.broadcasted_iota(jnp.int32, (tokens, tokens), 0) + block * tokens
    cols = lax.broadcasted_iota(jnp.int32, (tokens, tokens), 1) + me * tokens
    return jnp.where(same & (rows <= cols), 0.0, negative_large)


def attend_kernel(nz, q_ref, kv_ref, seg_ref, at_ref, lse_ref, kv_all, seg_all, acc, top, total, bias_s,
                  own_sem, kv_send, kv_recv, seg_send, seg_recv):
    me = lax.axis_index("context")
    tokens = kv_ref.shape[0]
    width = kv_ref.shape[1] // 2
    slices = width // 128
    barrier = pltpu.get_barrier_semaphore()

    @pl.when(me > 0)
    def _():
        pl.semaphore_signal(barrier, inc=1, device_id={"context": me - 1}, device_id_type=MESH)

    @pl.when(me < nz - 1)
    def _():
        pl.semaphore_signal(barrier, inc=1, device_id={"context": me + 1}, device_id_type=MESH)

    pl.semaphore_wait(
        barrier, jnp.where(me > 0, 1, 0) + jnp.where(me < nz - 1, 1, 0)
    )

    def up(slot):
        return [
            pltpu.make_async_remote_copy(
                src_ref=ref.at[slot],
                dst_ref=ref.at[slot],
                send_sem=send.at[slot],
                recv_sem=recv.at[slot],
                device_id={"context": me + 1},
                device_id_type=MESH,
            )
            for ref, send, recv in ((kv_all, kv_send, kv_recv), (seg_all, seg_send, seg_recv))
        ]

    own = [
        pltpu.make_async_copy(kv_ref, kv_all.at[me], own_sem.at[0]),
        pltpu.make_async_copy(seg_ref, seg_all.at[me], own_sem.at[1]),
    ]
    for copy in own:
        copy.start()
    for copy in own:
        copy.wait()

    @pl.when(me < nz - 1)
    def _():
        for copy in up(me):
            copy.start()

    acc[...] = jnp.zeros_like(acc)
    top[...] = jnp.full_like(top, -3e38)
    total[...] = jnp.zeros_like(total)

    def block(j):
        bias = mask_bias(seg_all, j, me, tokens)
        bias_s[:, :tokens] = bias
        bias_s[:, tokens:] = bias

        @pl.loop(0, slices)
        def _(t):
            k_at = pl.ds(pl.multiple_of(t * 128, 128), 128)
            v_at = pl.ds(pl.multiple_of(width + t * 128, 128), 128)
            keys = kv_all[j, :, k_at]
            vals = kv_all[j, :, v_at]
            for half in (0, 1):
                keep = lane_half((tokens, 128), half)
                zero = jnp.zeros_like(keys)
                scores = nt(jnp.where(keep, keys, zero), q_ref[t]) + bias_s[...]
                old = top[t, half : half + 1, :]
                new = jnp.maximum(old, jnp.max(scores, axis=0, keepdims=True))
                scale = jnp.exp(old - new)
                soft = jnp.exp(scores - new)
                top[t, half : half + 1, :] = new
                total[t, half : half + 1, :] = total[t, half : half + 1, :] * scale + jnp.sum(
                    soft, axis=0, keepdims=True
                )
                mixed = tn(jnp.where(keep, vals, zero), soft.astype(bf16))
                a, b = half * HEAD_DIM, (half + 1) * HEAD_DIM
                acc[t, a:b, :] = acc[t, a:b, :] * scale + mixed[a:b]

    block(me)
    for step in range(1, nz):
        j = me - step

        @pl.when(j >= 0)
        def _():
            for copy in up(j):
                copy.wait_recv()

            @pl.when(me < nz - 1)
            def _():
                for copy in up(j):
                    copy.start()

            block(j)

    for t in range(slices):
        lse_ref[t] = top[t] + jnp.log(total[t])
        for half in (0, 1):
            a, b = half * HEAD_DIM, (half + 1) * HEAD_DIM
            at_ref[2 * t + half] = (acc[t, a:b, :] / total[t, half : half + 1, :]).astype(bf16)
    for step in range(nz):
        j = me - step

        @pl.when((j >= 0) & (me < nz - 1))
        def _():
            for copy in up(j):
                copy.wait_send()


def attend(nz, q, kv, seg, cid):
    tokens = kv.shape[0]
    slices, wide, _ = q.shape
    vm = pl.BlockSpec(memory_space=pltpu.VMEM)
    return pl.pallas_call(
        functools.partial(attend_kernel, nz),
        out_shape=(
            jax.ShapeDtypeStruct((2 * slices, HEAD_DIM, wide), bf16),
            jax.ShapeDtypeStruct((slices, 2, wide), f32),
            jax.ShapeDtypeStruct((nz,) + kv.shape, bf16),
            jax.ShapeDtypeStruct((nz,) + seg.shape, f32),
        ),
        in_specs=[vm, pl.BlockSpec(memory_space=pl.ANY), pl.BlockSpec(memory_space=pl.ANY)],
        out_specs=(vm, vm, vm, vm),
        scratch_shapes=[
            pltpu.VMEM((slices, 128, wide), f32),
            pltpu.VMEM((slices, 2, wide), f32),
            pltpu.VMEM((slices, 2, wide), f32),
            pltpu.VMEM((tokens, wide), f32),
            pltpu.SemaphoreType.DMA((2,)),
            pltpu.SemaphoreType.DMA((nz,)),
            pltpu.SemaphoreType.DMA((nz,)),
            pltpu.SemaphoreType.DMA((nz,)),
            pltpu.SemaphoreType.DMA((nz,)),
        ],
        compiler_params=pltpu.CompilerParams(
            collective_id=cid, has_side_effects=True, vmem_limit_bytes=30 << 20
        ),
        name="attend",
    )(q, kv, seg)


class Line:
    def __init__(self, nz, held, came, send, recv):
        self.nz, self.held, self.came, self.send, self.recv = nz, held, came, send, recv
        self.me = lax.axis_index("context")
        self.chunks, _, self.rows, self.width = held.shape
        self.count = self.chunks * (nz - 1)
        self.slots = self.count + nz - 1

    @staticmethod
    def scratch(nz, chunks, rows, width):
        return [
            pltpu.VMEM((chunks, nz, rows, width), bf16),
            pltpu.VMEM((chunks, nz + 1, rows, width), bf16),
            pltpu.SemaphoreType.DMA((2, chunks, nz)),
            pltpu.SemaphoreType.DMA((2, chunks, nz)),
        ]

    def hop(self, way, k, s):
        return pltpu.make_async_remote_copy(
            src_ref=self.held.at[k, s],
            dst_ref=self.came.at[k, s + 1 - way],
            send_sem=self.send.at[way, k, s],
            recv_sem=self.recv.at[way, k, s],
            device_id={"context": self.me - 1 if way else self.me + 1},
            device_id_type=MESH,
        )

    def slot(self, i):
        nz, me = self.nz, self.me
        for way in (0, 1):
            place = nz - 1 - me if way else me
            m = i - place
            k = lax.div(m, nz - 1)
            part = m - k * (nz - 1)
            s = part if way else nz - 1 - part
            far = me - s if way else s - me
            ok = (m >= 0) & (m < self.count) & (far >= 0)

            @pl.when(ok & (place > 0))
            def _():
                self.hop(way, k, s).wait_recv()
                add_rows(self.held, (k, s), self.came, (k, s + 1 - way), self.rows)

            @pl.when(ok & (far > 0))
            def _():
                @pl.when(part > 0)
                def _():
                    self.hop(way, k, s - 1 if way else s + 1).wait_send()

                @pl.when((part == 0) & (k > 0))
                def _():
                    self.hop(way, k - 1, me - 1 if way else me + 1).wait_send()

                self.hop(way, k, s).start()

    def finish(self, out):
        step = 16
        for k in range(self.chunks):

            @pl.loop(0, self.rows // step)
            def _(i):
                at = pl.ds(pl.multiple_of(i * step, step), step)
                out[k, at, :] = self.held[k, self.me, at, :].astype(f32)

        @pl.when(self.me < self.nz - 1)
        def _():
            self.hop(0, self.chunks - 1, self.me + 1).wait_send()

        @pl.when(self.me > 0)
        def _():
            self.hop(1, self.chunks - 1, self.me - 1).wait_send()


class Spread:
    def __init__(self, sizes, made, from_dp, held, from_ex, line, from_z, send, recv):
        self.sizes, self.made, self.from_dp, self.held = sizes, made, from_dp, held
        self.from_ex, self.line, self.from_z, self.send, self.recv = from_ex, line, from_z, send, recv
        self.places = tuple(lax.axis_index(a) for a in ("dp", "expert", "context"))

    @staticmethod
    def scratch(sizes, rows, width):
        ne, nz, nd = sizes
        most = max(sizes)
        return [
            pltpu.VMEM((nd - 1, ne, nz, rows, width), bf16),
            pltpu.VMEM((ne, nz, rows, width), bf16),
            pltpu.VMEM((ne - 1, nz, rows, width), bf16),
            pltpu.VMEM((nz, rows, width), bf16),
            pltpu.VMEM((nz - 1, rows, width), bf16),
            pltpu.SemaphoreType.DMA((3, most)),
            pltpu.SemaphoreType.DMA((3, most)),
        ]

    def copy(self, stage, step):
        ne, nz, nd = self.sizes
        axis, size = (("dp", nd), ("expert", ne), ("context", nz))[stage]
        other = lax.rem(self.places[stage] + step, size)
        src = (
            self.made.at[:, :, other]
            if stage == 0
            else self.held.at[other] if stage == 1 else self.line.at[other]
        )
        dst = (self.from_dp, self.from_ex, self.from_z)[stage].at[step - 1]
        return pltpu.make_async_remote_copy(
            src_ref=src,
            dst_ref=dst,
            send_sem=self.send.at[stage, step],
            recv_sem=self.recv.at[stage, step],
            device_id={axis: other},
            device_id_type=MESH,
        )

    def others(self, stage):
        ne, nz, nd = self.sizes
        return range(1, (nd, ne, nz)[stage])

    def over_dp(self):
        for step in self.others(0):
            self.copy(0, step).start()

    def made_free(self):
        for step in self.others(0):
            self.copy(0, step).wait_send()

    def over_expert(self):
        ne, nz, _ = self.sizes
        for step in self.others(0):
            self.copy(0, step).wait_recv()

        @pl.loop(0, ne * nz)
        def _(i):
            a = lax.div(i, nz)
            b = i - a * nz
            total = self.made[a, b, self.places[0]].astype(f32)
            for step in self.others(0):
                total = total + self.from_dp[step - 1, a, b].astype(f32)
            self.held[a, b] = total.astype(bf16)

        for step in self.others(1):
            self.copy(1, step).start()

    def over_context(self):
        nz = self.sizes[1]
        for step in self.others(1):
            self.copy(1, step).wait_recv()

        @pl.loop(0, nz)
        def _(b):
            total = self.held[self.places[1], b].astype(f32)
            for step in self.others(1):
                total = total + self.from_ex[step - 1, b].astype(f32)
            self.line[b] = total.astype(bf16)

        for step in self.others(2):
            self.copy(2, step).start()

    def finish(self, out):
        for step in self.others(2):
            self.copy(2, step).wait_recv()
        total = self.line[self.places[2]].astype(f32)
        for step in self.others(2):
            total = total + self.from_z[step - 1].astype(f32)
        out[...] = total
        for stage in (1, 2):
            for step in self.others(stage):
                self.copy(stage, step).wait_send()


HBM_INS = ("held_in", "back_in", "out_in", "soft_in", "w_query", "w_key", "w_value", "w_out")
VMEM_INS = (
    "q", "kv_all", "seg_all", "lse", "heads", "middle", "tokens", "grad_top", "second_low",
    "first_low", "router_turned", "w_router_turned", "attn_gain", "moe_gain", "turn_q", "turn_k",
)
OUTS = ("layer_out", "input_grad", "query_out", "kv_out", "proj_out", "small_out", "expert_out")


def tail_kernel(sizes, names, *refs):
    r = dict(zip(names, refs))
    ne, nz, nd = sizes
    ex, me, dp = (lax.axis_index(a) for a in ("expert", "context", "dp"))
    tokens, width = r["tokens"].shape
    kv_width = r["kv_all"].shape[2] // 2
    slices = kv_width // 128
    group = width // ne

    barrier = pltpu.get_barrier_semaphore()
    for axis, place, size in (("expert", ex, ne), ("context", me, nz), ("dp", dp, nd)):
        for step in range(1, size):
            pl.semaphore_signal(
                barrier, inc=1, device_id={axis: lax.rem(place + step, size)}, device_id_type=MESH
            )
    pl.semaphore_wait(barrier, ne + nz + nd - 3)

    line = Line(nz, r["held"], r["came"], r["line_send"], r["line_recv"])
    sums = {
        kind: Spread(sizes, r["small_made" if kind == "small" else "made"],
                     *(r[kind + str(i)] for i in range(7)))
        for kind in ("proj", "query", "kv", "small")
    }

    held_copies = [
        pltpu.make_async_copy(r["held_in"].at[k], r["held"].at[k], r["held_sem"].at[k])
        for k in range(line.chunks)
    ]
    for copy in held_copies:
        copy.start()

    def rows_copy(kind, step):
        other = lax.rem(ex + step, ne)
        at = {"back": 0, "out": 1, "soft": 2}[kind]
        return pltpu.make_async_remote_copy(
            src_ref=r[kind + "_in"].at[other],
            dst_ref=r["soft_all"].at[ex] if kind == "soft" else r[kind + "_came"].at[step - 1],
            send_sem=r["rows_send"].at[at, step],
            recv_sem=r["rows_recv"].at[at, step],
            device_id={"expert": other},
            device_id_type=MESH,
        )

    for kind in ("soft", "back"):
        for step in range(1, ne):
            rows_copy(kind, step).start()
    loads = [
        pltpu.make_async_copy(r["back_in"].at[ex], r["back_own"], r["load_sem"].at[0]),
        pltpu.make_async_copy(r["soft_in"].at[ex], r["soft_all"].at[ex], r["load_sem"].at[1]),
        pltpu.make_async_copy(r["out_in"].at[ex], r["out_own"], r["load_sem"].at[2]),
        pltpu.make_async_copy(r["w_out"], r["w_out_v"], r["load_sem"].at[3]),
        pltpu.make_async_copy(r["w_query"], r["w_query_v"], r["load_sem"].at[4]),
        pltpu.make_async_copy(r["w_key"], r["w_key_v"], r["load_sem"].at[5]),
        pltpu.make_async_copy(r["w_value"], r["w_value_v"], r["load_sem"].at[6]),
    ]
    for copy in loads:
        copy.start()
    for copy in held_copies:
        copy.wait()
    line.slot(0)
    for copy in loads:
        copy.wait()
    for t in range(2 * slices):
        for ab in (0, 1):
            h = 2 * t + ab
            r["attn_turned"][h * HEAD_DIM : (h + 1) * HEAD_DIM, :] = r["heads"][
                t, :, ab * tokens : (ab + 1) * tokens
            ]
    line.slot(1)
    line.slot(2)

    for kind in ("soft", "back"):
        for step in range(1, ne):
            rows_copy(kind, step).wait_recv()
    for step in range(1, ne):
        rows_copy("out", step).start()
    soft_back = jnp.concatenate([r["soft_all"][i] for i in range(ne)], axis=0)
    router_soft = r["router_turned"][...]
    logit_back = (
        router_soft * (soft_back - jnp.sum(router_soft * soft_back, axis=0, keepdims=True))
    ).astype(bf16)
    second_back = r["back_own"][...].astype(f32) + tn(logit_back, r["w_router_turned"][...])
    for step in range(1, ne):
        second_back = second_back + r["back_came"][step - 1].astype(f32)
    middle = r["middle"][...]
    inverse = lax.rsqrt(jnp.mean(middle * middle, axis=-1, keepdims=True) + epsilon)
    normed = middle * inverse
    scaled = second_back * r["moe_gain"][...]
    moe_gain_grad = jnp.sum(second_back * normed, axis=0, keepdims=True)
    middle_grad = r["grad_top"][...].astype(f32) + inverse * (
        scaled - normed * jnp.mean(scaled * normed, axis=-1, keepdims=True)
    )
    r["middle_grad"][...] = middle_grad
    r["branch"][...] = middle_grad.astype(bf16)
    experts_all = logit_back.shape[0]
    r["small_rows"][...] = jnp.zeros_like(r["small_rows"])
    r["small_rows"][:experts_all, :] = nn(logit_back, r["second_low"][...])
    r["small_rows"][experts_all : experts_all + 1, :] = moe_gain_grad

    @pl.loop(0, slices)
    def _(t):
        at = pl.ds(pl.multiple_of(t * 256, 256), 256)
        turned = nt(r["w_out_v"][at, :], r["branch"][...]).astype(bf16)
        for half in (0, 1):
            a, b = half * HEAD_DIM, (half + 1) * HEAD_DIM
            for ab in (0, 1):
                c = (2 * half + ab) * HEAD_DIM
                r["do"][t, a:b, ab * tokens : (ab + 1) * tokens] = turned[c : c + HEAD_DIM]
            r["delta"][t, half : half + 1, :] = jnp.sum(
                r["do"][t, a:b, :].astype(f32) * r["heads"][2 * t + half].astype(f32),
                axis=0,
                keepdims=True,
            )

    @pl.loop(0, ne)
    def _(g):
        at = pl.ds(pl.multiple_of(g * group, group), group)
        grad = nn(r["attn_turned"][at, :], r["branch"][...])
        r["made"][g] = grad.reshape((nz, nd, group // (nz * nd), width)).astype(bf16)

    sums["proj"].over_dp()
    line.slot(3)

    r["dq"][...] = jnp.zeros_like(r["dq"])
    bias_s = r["bias"]

    def block(j, store):
        bias = mask_bias(r["seg_all"], j, me, tokens)
        bias_s[:, :tokens] = bias
        bias_s[:, tokens:] = bias

        @pl.loop(0, slices)
        def _(t):
            k_at = pl.ds(pl.multiple_of(t * 128, 128), 128)
            v_at = pl.ds(pl.multiple_of(kv_width + t * 128, 128), 128)
            keys = r["kv_all"][j, :, k_at]
            vals = r["kv_all"][j, :, v_at]
            dks, dvs = [], []
            for half in (0, 1):
                keep = lane_half((tokens, 128), half)
                zero = jnp.zeros_like(keys)
                keys_half = jnp.where(keep, keys, zero)
                scores = nt(keys_half, r["q"][t]) + bias_s[...]
                soft = jnp.exp(scores - r["lse"][t, half : half + 1, :])
                soft_grad = nn(jnp.where(keep, vals, zero), r["do"][t])
                back = (soft * (soft_grad - r["delta"][t, half : half + 1, :])).astype(bf16)
                dvs.append(nt(soft.astype(bf16), r["do"][t]))
                dks.append(nn(back, r["q"][t]))
                r["dq"][t] += tn(keys_half, back)
            low = lane_half((tokens, 128), 0)
            store(k_at, jnp.where(low, dks[0], dks[1]))
            store(v_at, jnp.where(low, dvs[0], dvs[1]))

    def give(j):
        return pltpu.make_async_remote_copy(
            src_ref=r["kv_part"].at[j],
            dst_ref=r["kv_came"].at[me],
            send_sem=r["kv_send"].at[j],
            recv_sem=r["kv_recv"].at[me],
            device_id={"context": j},
            device_id_type=MESH,
        )

    for j in range(nz - 1):

        @pl.when(j < me)
        def _():
            def store(at, value):
                r["kv_part"][j, :, at] = value.astype(bf16)

            block(j, store)
            give(j).start()

        line.slot(4 + j)
        if j == 0:
            sums["proj"].over_expert()

    def store_own(at, value):
        r["own_kv"][:, at] = value

    block(me, store_own)
    sums["proj"].over_context()

    cos_q, sin_q = r["turn_q"][0], r["turn_q"][1]
    quarter = HEAD_DIM // 2
    for t in range(slices):
        for half in (0, 1):
            a = half * HEAD_DIM
            first = r["dq"][t, a : a + quarter, :]
            second = r["dq"][t, a + quarter : a + 2 * quarter, :]
            turned = jnp.concatenate(
                [first * cos_q + second * sin_q, second * cos_q - first * sin_q], axis=0
            )
            pair = jnp.concatenate([turned[:, :tokens], turned[:, tokens:]], axis=0)
            at = (2 * t + half) * 128
            r["back_s"][:, at : at + 128] = pair.T.astype(bf16)

    def make(a, b):
        @pl.loop(0, ne)
        def _(g):
            at = pl.ds(pl.multiple_of(g * group, group), group)
            grad = tn(r["first_low"][:, at], r["back_s"][:, a:b])
            r["made"][g] = grad.reshape((nz, nd, group // (nz * nd), b - a)).astype(bf16)

    sums["proj"].made_free()
    make(0, width)
    sums["query"].over_dp()
    line.slot(4 + nz - 1)

    for j in range(1, nz):

        @pl.when(me < j)
        def _():
            pltpu.make_async_remote_copy(
                src_ref=r["kv_part"].at[0],
                dst_ref=r["kv_came"].at[j],
                send_sem=r["kv_send"].at[0],
                recv_sem=r["kv_recv"].at[j],
                device_id={"context": j},
                device_id_type=MESH,
            ).wait_recv()

            @pl.loop(0, tokens // 16)
            def _(i):
                at = pl.ds(pl.multiple_of(i * 16, 16), 16)
                r["own_kv"][at, :] += r["kv_came"][j, at, :].astype(f32)

    sums["query"].over_expert()
    cos_k, sin_k = r["turn_k"][0], r["turn_k"][1]
    first_lanes = lax.rem(lax.broadcasted_iota(jnp.int32, (tokens, 128), 1), HEAD_DIM) < quarter
    for t in range(slices):
        grad = r["own_kv"][:, t * 128 : (t + 1) * 128]
        swapped = jnp.where(
            first_lanes, pltpu.roll(grad, 128 - quarter, 1), pltpu.roll(grad, quarter, 1)
        )
        r["back_s"][:, width + t * 128 : width + (t + 1) * 128] = (
            grad * cos_k + swapped * sin_k
        ).astype(bf16)
    r["back_s"][:, width + kv_width :] = r["own_kv"][:, kv_width:].astype(bf16)
    sums["query"].made_free()
    make(width, width + 2 * kv_width)
    sums["kv"].over_dp()
    line.slot(4 + nz)

    first_back = nt(r["back_s"][:, :width], r["w_query_v"][...])
    first_back = first_back + nt(r["back_s"][:, width : width + kv_width], r["w_key_v"][...])
    first_back = first_back + nt(r["back_s"][:, width + kv_width :], r["w_value_v"][...])
    values = r["tokens"][...].astype(f32)
    inverse = lax.rsqrt(jnp.mean(values * values, axis=-1, keepdims=True) + epsilon)
    normed = values * inverse
    scaled = first_back * r["attn_gain"][...]
    r["small_rows"][experts_all + 1 : experts_all + 2, :] = jnp.sum(
        first_back * normed, axis=0, keepdims=True
    )
    r["input_grad"][...] = r["middle_grad"][...] + inverse * (
        scaled - normed * jnp.mean(scaled * normed, axis=-1, keepdims=True)
    )
    small_turned = r["small_rows"][...].T
    r["small_made"][...] = small_turned.reshape(r["small_made"].shape).astype(bf16)
    sums["small"].over_dp()
    sums["kv"].over_expert()
    sums["small"].over_expert()
    sums["query"].over_context()
    line.slot(4 + nz + 1)

    for step in range(1, ne):
        rows_copy("out", step).wait_recv()

    @pl.loop(0, tokens // 16)
    def _(i):
        at = pl.ds(pl.multiple_of(i * 16, 16), 16)
        total = r["middle"][at, :] + r["out_own"][at, :].astype(f32)
        for step in range(1, ne):
            total = total + r["out_came"][step - 1, at, :].astype(f32)
        r["layer_out"][at, :] = total

    line.slot(4 + nz + 2)
    sums["kv"].over_context()
    sums["small"].over_context()
    for i in range(4 + nz + 3, line.slots):
        line.slot(i)
    sums["kv"].made_free()
    sums["small"].made_free()
    for kind in ("proj", "query", "kv", "small"):
        sums[kind].finish(r[kind + "_out"])
    line.finish(r["expert_out"])
    for kind in ("soft", "back", "out"):
        for step in range(1, ne):
            rows_copy(kind, step).wait_send()
    for j in range(nz - 1):

        @pl.when(j < me)
        def _():
            give(j).wait_send()


def tail(sizes, cid, ins):
    ne, nz, nd = sizes
    tokens, width = ins["tokens"].shape
    slices, wide, _ = ins["q"].shape
    chunks, _, piece, _ = ins["held_in"].shape
    kv_shape = ins["kv_all"].shape
    rows = width // (ne * nz * nd)
    vm = pl.BlockSpec(memory_space=pltpu.VMEM)
    hbm = pl.BlockSpec(memory_space=pl.ANY)
    outs = (
        jax.ShapeDtypeStruct((tokens, width), f32),
        jax.ShapeDtypeStruct((tokens, width), f32),
        jax.ShapeDtypeStruct((rows, width), f32),
        jax.ShapeDtypeStruct((rows, kv_shape[2]), f32),
        jax.ShapeDtypeStruct((rows, width), f32),
        jax.ShapeDtypeStruct((rows, 128), f32),
        jax.ShapeDtypeStruct((chunks, piece, width), f32),
    )
    dma = pltpu.SemaphoreType.DMA
    scratch = dict(
        back_own=pltpu.VMEM((tokens, width), bf16),
        back_came=pltpu.VMEM((ne - 1, tokens, width), bf16),
        out_own=pltpu.VMEM((tokens, width), bf16),
        out_came=pltpu.VMEM((ne - 1, tokens, width), bf16),
        soft_all=pltpu.VMEM(ins["soft_in"].shape, f32),
        w_out_v=pltpu.VMEM(ins["w_out"].shape, bf16),
        w_query_v=pltpu.VMEM(ins["w_query"].shape, bf16),
        w_key_v=pltpu.VMEM(ins["w_key"].shape, bf16),
        w_value_v=pltpu.VMEM(ins["w_value"].shape, bf16),
        attn_turned=pltpu.VMEM((width, tokens), bf16),
        middle_grad=pltpu.VMEM((tokens, width), f32),
        branch=pltpu.VMEM((tokens, width), bf16),
        small_rows=pltpu.VMEM((128, width), f32),
        do=pltpu.VMEM((slices, 128, wide), bf16),
        delta=pltpu.VMEM((slices, 2, wide), f32),
        bias=pltpu.VMEM((tokens, wide), f32),
        dq=pltpu.VMEM((slices, 128, wide), f32),
        kv_part=pltpu.VMEM((nz - 1,) + kv_shape[1:], bf16),
        kv_came=pltpu.VMEM(kv_shape, bf16),
        own_kv=pltpu.VMEM(kv_shape[1:], f32),
        back_s=pltpu.VMEM((tokens, width + kv_shape[2]), bf16),
        made=pltpu.VMEM((ne, nz, nd, rows, width), bf16),
        small_made=pltpu.VMEM((ne, nz, nd, rows, 128), bf16),
        rows_send=dma((3, ne)),
        rows_recv=dma((3, ne)),
        load_sem=dma((7,)),
        held_sem=dma((chunks,)),
        kv_send=dma((nz,)),
        kv_recv=dma((nz,)),
    )
    scratch.update(
        zip(("held", "came", "line_send", "line_recv"), Line.scratch(nz, chunks, piece, width))
    )
    for kind, cols in (("proj", width), ("query", width), ("kv", kv_shape[2]), ("small", 128)):
        scratch.update(
            (kind + str(i), ref) for i, ref in enumerate(Spread.scratch(sizes, rows, cols))
        )
    names = HBM_INS + VMEM_INS + OUTS + tuple(scratch)
    return pl.pallas_call(
        functools.partial(tail_kernel, sizes, names),
        out_shape=outs,
        in_specs=[hbm] * len(HBM_INS) + [vm] * len(VMEM_INS),
        out_specs=(vm,) * len(OUTS),
        scratch_shapes=list(scratch.values()),
        compiler_params=pltpu.CompilerParams(
            collective_id=cid, has_side_effects=True, vmem_limit_bytes=63 << 20
        ),
        name="tail",
    )(*(ins[name] for name in HBM_INS + VMEM_INS))


def norm_forward(values, scale_gain):
    inverse = lax.rsqrt(jnp.mean(values * values, axis=-1, keepdims=True) + epsilon)
    normed = values * inverse
    return (normed * scale_gain, normed, inverse)


def rope_tables(positions, head_width):
    halves = head_width // 2
    inverse_freq = rope_base ** (-2.0 * jnp.arange(halves, dtype=f32) / head_width)
    angles = positions.astype(f32)[:, None] * inverse_freq[None, :]
    return (jnp.cos(angles)[:, None, :], jnp.sin(angles)[:, None, :])


def rotate(values, cosine_table, sine_table):
    halves = values.shape[-1] // 2
    first_half = values[..., :halves]
    second_half = values[..., halves:]
    return jnp.concatenate(
        [
            first_half * cosine_table - second_half * sine_table,
            second_half * cosine_table + first_half * sine_table,
        ],
        axis=-1,
    )


def slot_table(chosen, turn_order, experts_all, capacity):
    tokens, top_count = chosen.shape
    pair_count = tokens * top_count
    turns = jnp.arange(pair_count, dtype=jnp.int32)
    owner = (turn_order // top_count)[:, None] == jnp.arange(tokens, dtype=jnp.int32)[None, :]
    which = (turn_order % top_count)[:, None] == jnp.arange(top_count, dtype=jnp.int32)[None, :]
    high = jnp.where(which, (turns // 256)[:, None], 0)
    low = jnp.where(which, (turns % 256)[:, None], 0)
    both = jnp.concatenate([high, low], axis=1).astype(bf16)
    found = lax.dot_general(
        owner.astype(bf16), both, (((0,), (0,)), ((), ())), preferred_element_type=f32
    )
    turn_of = found[:, :top_count] * 256.0 + found[:, top_count:]
    picks = chosen[:, :, None] == jnp.arange(experts_all, dtype=jnp.int32)[None, None, :]
    far = float(2 * pair_count)
    turn_at = far + jnp.sum(jnp.where(picks, turn_of[:, :, None] - far, 0.0), axis=1)
    turn_row = turn_at.T
    rank = jnp.sum((turn_row[:, :, None] < turn_row[:, None, :]).astype(f32), axis=1)
    return jnp.where((turn_row < far) & (rank < capacity), rank, -1.0)


def body(
    sizes,
    tokens,
    attn_scale,
    w_query,
    w_key,
    w_value,
    w_out,
    moe_scale,
    w_router,
    w_gate,
    w_up,
    w_down,
    segment_ids,
    expert_choice,
    slot_order,
    out_grad,
):
    ne, nz, nd = sizes
    my_expert = lax.axis_index("expert")
    my_ctx = lax.axis_index("context")
    my_dp = lax.axis_index("dp")
    local_rows = tokens.shape[1]
    model_width = tokens.shape[2]
    head_width = HEAD_DIM
    query_heads = w_query.shape[1] // head_width
    kv_heads = w_key.shape[1] // head_width
    kv_width = kv_heads * head_width
    group_size = query_heads // kv_heads
    factor = head_width ** (-0.5)
    experts_all = w_router.shape[1]
    local_experts = w_gate.shape[0]
    top_count = expert_choice.shape[2]
    pair_count = local_rows * top_count
    capacity = (pair_count * 9 + 8 * experts_all - 1) // (8 * experts_all)

    positions = my_ctx * local_rows + jnp.arange(local_rows, dtype=jnp.int32)
    cosine_table, sine_table = rope_tables(positions, head_width)
    residual_in = tokens[0].astype(f32)
    seg_local = segment_ids[0]
    attn_gain = attn_scale.astype(f32)
    moe_gain = moe_scale.astype(f32)

    grad_all = lax.all_gather(out_grad[0], "expert", axis=0)
    slots = slot_table(expert_choice[0], slot_order[0, 0], experts_all, capacity)

    first_out, first_normed, first_inverse = norm_forward(residual_in, attn_gain)
    first_low = first_out.astype(bf16)
    query_pre = jnp.dot(first_low, w_query, preferred_element_type=f32)
    key_pre = jnp.dot(first_low, w_key, preferred_element_type=f32)
    value_low = jnp.dot(first_low, w_value, preferred_element_type=f32).astype(bf16)
    query_rot = rotate(
        query_pre.reshape(local_rows, query_heads, head_width), cosine_table, sine_table
    ).astype(bf16)
    slices = kv_heads // 2
    query_in = (
        (query_rot * factor)
        .astype(bf16)
        .reshape(local_rows, slices, 2, group_size, head_width)
        .transpose(1, 3, 0, 2, 4)
        .reshape(slices, group_size * local_rows, 2 * head_width)
    )
    key_rot = rotate(
        key_pre.reshape(local_rows, kv_heads, head_width), cosine_table, sine_table
    ).astype(bf16)
    kv_own = jnp.concatenate([key_rot.reshape(local_rows, kv_width), value_low], axis=1)
    seg_own = jnp.broadcast_to(seg_local.astype(f32)[None, :], (8, local_rows))
    heads, log_total, kv_all, seg_all = attend(nz, query_in, kv_own, seg_own, 6)
    attn_turned = (
        heads.reshape(kv_heads, head_width, group_size, local_rows)
        .transpose(0, 2, 1, 3)
        .reshape(query_heads * head_width, local_rows)
    )
    middle = residual_in + tn(attn_turned, w_out)
    second_out, second_normed, second_inverse = norm_forward(middle, moe_gain)
    second_low = second_out.astype(bf16)
    logits = jnp.dot(second_low, w_router, preferred_element_type=f32)
    router_soft = jax.nn.softmax(logits, axis=-1)
    tables = jnp.stack([slots, router_soft.T])

    rows_all, tables_all = gather_all([second_low, tables], "expert", ne, 1, "rows_gather")
    held_grads, out_part, back_part, soft_part = experts(
        sizes, capacity, rows_all, grad_all, tables_all, w_gate, w_up, w_down
    )
    cos_flat, sin_flat = cosine_table[:, 0, :], sine_table[:, 0, :]
    turn_q = jnp.stack([jnp.tile(table.T, (1, group_size)) for table in (cos_flat, sin_flat)])
    turn_k = jnp.stack(
        [
            jnp.tile(cos_flat, (1, 4)),
            jnp.tile(jnp.concatenate([sin_flat, -sin_flat], axis=1), (1, 2)),
        ]
    )
    layer_out, input_grad, query_shard, kv_shard, out_shard, small_shard, expert_shards = tail(
        sizes,
        3,
        dict(
            held_in=held_grads,
            back_in=back_part,
            out_in=out_part,
            soft_in=soft_part,
            w_query=w_query,
            w_key=w_key,
            w_value=w_value,
            w_out=w_out,
            q=query_in,
            kv_all=kv_all,
            seg_all=seg_all,
            lse=log_total,
            heads=heads,
            middle=middle,
            tokens=tokens[0],
            grad_top=out_grad[0],
            second_low=second_low,
            first_low=first_low,
            router_turned=router_soft.T,
            w_router_turned=w_router.T,
            attn_gain=attn_gain[None],
            moe_gain=moe_gain[None],
            turn_q=turn_q * factor,
            turn_k=turn_k,
        ),
    )
    key_shard, value_shard = kv_shard[:, :kv_width], kv_shard[:, kv_width:]
    router_shard = small_shard[:, :experts_all]
    moe_gain_shard = small_shard[:, experts_all]
    attn_gain_shard = small_shard[:, experts_all + 1]
    gate_rows = model_width // (nz * nd)
    hidden_width = w_gate.shape[2]
    gate_shard = expert_shards[:, :gate_rows, :hidden_width]
    up_shard = expert_shards[:, :gate_rows, hidden_width:]
    down_shard = expert_shards[:, gate_rows:, :]
    return (
        layer_out[None],
        input_grad[None],
        attn_gain_shard,
        moe_gain_shard,
        query_shard,
        key_shard,
        value_shard,
        out_shard,
        router_shard,
        gate_shard,
        up_shard,
        down_shard,
    )


def solution(mesh):
    sizes = (mesh.shape["expert"], mesh.shape["context"], mesh.shape["dp"])
    in_specs = (
        P(("expert", "dp"), "context", None),
        P(),
        P(),
        P(),
        P(),
        P(),
        P(),
        P(),
        P("expert", None, None),
        P("expert", None, None),
        P("expert", None, None),
        P(("expert", "dp"), "context"),
        P(("expert", "dp"), "context", None),
        P(("expert", "dp"), "context", None),
        P(("expert", "dp"), "context", None),
    )
    out_specs = (
        P(("expert", "dp"), "context", None),
        P(("expert", "dp"), "context", None),
        P(("expert", "context", "dp")),
        P(("expert", "context", "dp")),
        P(("expert", "context", "dp"), None),
        P(("expert", "context", "dp"), None),
        P(("expert", "context", "dp"), None),
        P(("expert", "context", "dp"), None),
        P(("expert", "context", "dp"), None),
        P("expert", ("context", "dp"), None),
        P("expert", ("context", "dp"), None),
        P("expert", ("context", "dp"), None),
    )
    return jax.shard_map(
        functools.partial(body, sizes),
        mesh=mesh,
        in_specs=in_specs,
        out_specs=out_specs,
        check_vma=False,
    )
```

```python
import functools
import types

import jax
import jax.numpy as jnp
import numpy as np
from jax import lax
from jax.experimental import pallas as pl
from jax.experimental.pallas import tpu as pltpu
from jax.sharding import PartitionSpec as P

HEAD_DIM = 64
MESH = pl.DeviceIdType.MESH

epsilon = 1e-06
rope_base = 10000.0
negative_large = -1e30
bf16 = jnp.bfloat16
f32 = jnp.float32


def nt(a, b):
    return lax.dot_general(a, b, (((1,), (1,)), ((), ())), preferred_element_type=f32)


def tn(a, b):
    return lax.dot_general(a, b, (((0,), (0,)), ((), ())), preferred_element_type=f32)


def nn(a, b):
    return jnp.dot(a, b, preferred_element_type=f32)


def add_rows(dst, dst_at, src, src_at, rows):
    step = 16

    @pl.loop(0, rows // step)
    def _(i):
        at = pl.ds(pl.multiple_of(i * step, step), step)
        dst[dst_at + (at, slice(None))] = (
            dst[dst_at + (at, slice(None))].astype(f32) + src[src_at + (at, slice(None))].astype(f32)
        ).astype(bf16)


def lane_half(shape, which):
    lanes = lax.broadcasted_iota(jnp.int32, shape, 1)
    return (lanes >= HEAD_DIM) if which else (lanes < HEAD_DIM)


def column_of(row):
    n = row.shape[1]
    rows = lax.broadcasted_iota(jnp.int32, (n, n), 0)
    cols = lax.broadcasted_iota(jnp.int32, (n, n), 1)
    return jnp.sum(jnp.where(rows == cols, row, 0.0), axis=1, keepdims=True)


def mask_bias(seg_ref, block, me, tokens):
    key_seg = column_of(seg_ref[block, :1, :])
    same = key_seg == seg_ref[me, :1, :]
    rows = lax.broadcasted_iota(jnp.int32, (tokens, tokens), 0) + block * tokens
    cols = lax.broadcasted_iota(jnp.int32, (tokens, tokens), 1) + me * tokens
    return jnp.where(same & (rows <= cols), 0.0, negative_large)


def named(defs, refs):
    counts = [d.num_leaves for d in defs]
    at = [sum(counts[:i]) for i in range(len(counts) + 1)]
    trees = [jax.tree.unflatten(d, refs[at[i] : at[i + 1]]) for i, d in enumerate(defs)]
    r = types.SimpleNamespace(**{k: v for tree in trees for k, v in tree.items()})
    read, (copies, sem) = trees[1], trees[3]["read"]
    r.loads = [
        pltpu.make_async_copy(read[k], copies[k], sem.at[i]) for i, k in enumerate(sorted(read))
    ]
    for k in read:
        setattr(r, k, copies[k])
    return r


def call_named(kernel, kept, read, outs, scratch, cid, limit, kept_outs):
    vm = pl.BlockSpec(memory_space=pltpu.VMEM)
    hbm = pl.BlockSpec(memory_space=pl.ANY)
    scratch["read"] = (
        {k: pltpu.VMEM(v.shape, v.dtype) for k, v in read.items()},
        pltpu.SemaphoreType.DMA((len(read),)),
    )
    flats, defs = zip(*(jax.tree.flatten(t) for t in (kept, read, outs, scratch)))
    out_specs = jax.tree.leaves(
        {k: jax.tree.map(lambda _: hbm if k in kept_outs else vm, v) for k, v in outs.items()}
    )
    results = pl.pallas_call(
        functools.partial(kernel, defs),
        out_shape=tuple(flats[2]),
        in_specs=[hbm] * (len(flats[0]) + len(flats[1])),
        out_specs=tuple(out_specs),
        scratch_shapes=flats[3],
        compiler_params=pltpu.CompilerParams(
            collective_id=cid, has_side_effects=True, vmem_limit_bytes=limit
        ),
        name=kernel.func.__name__,
    )(*flats[0], *flats[1])
    return types.SimpleNamespace(**jax.tree.unflatten(defs[2], results))


def slot_table(chosen, order, experts_all, capacity):
    top_count, tokens = chosen.shape
    pairs = order.shape[1]
    shift = top_count.bit_length() - 1
    if top_count != 1 << shift:
        raise ValueError("top count")
    owner = jnp.where(
        (order >> shift) == lax.broadcasted_iota(jnp.int32, (tokens, pairs), 0), 1.0, 0.0
    ).astype(bf16)
    which = (order & (top_count - 1)) == lax.broadcasted_iota(jnp.int32, (top_count, pairs), 0)
    turns = lax.broadcasted_iota(jnp.int32, (top_count, pairs), 1)
    high, low = (
        nt(jnp.where(which, part.astype(f32), 0.0).astype(bf16), owner)
        for part in (turns >> 8, turns & 255)
    )
    turn_of = high * 256.0 + low
    far = float(2 * pairs)
    ids = lax.broadcasted_iota(jnp.int32, (128, tokens), 0)
    turn_row = jnp.full((128, tokens), far, f32)
    for k in range(top_count):
        turn_row = jnp.where(chosen[k : k + 1, :] == ids, turn_of[k : k + 1, :], turn_row)
    turn_at = turn_row.T
    for e in range(experts_all):
        row = turn_row[e : e + 1, :]
        rank = jnp.sum(jnp.where(turn_at[:, e : e + 1] < row, 1.0, 0.0), axis=0, keepdims=True)
        yield jnp.where((row < far) & (rank < capacity), rank, -1.0)


def front_kernel(sizes, capacity, defs, *refs):
    r = named(defs, refs)
    ne, nz, nd = sizes
    ex, me = lax.axis_index("expert"), lax.axis_index("context")
    tokens, width = r.tokens.shape
    kv_width = r.w_key.shape[1]
    slices = kv_width // 128
    quarter = HEAD_DIM // 2

    barrier = pltpu.get_barrier_semaphore()
    for step in range(1, ne):
        pl.semaphore_signal(
            barrier, inc=1, device_id={"expert": lax.rem(ex + step, ne)}, device_id_type=MESH
        )

    @pl.when(me > 0)
    def _():
        pl.semaphore_signal(barrier, inc=1, device_id={"context": me - 1}, device_id_type=MESH)

    @pl.when(me < nz - 1)
    def _():
        pl.semaphore_signal(barrier, inc=1, device_id={"context": me + 1}, device_id_type=MESH)

    loads = [
        pltpu.make_async_copy(src, dst, r.load_sem.at[i])
        for i, (src, dst) in enumerate(
            (
                (r.w_key, r.w_key_v),
                (r.w_value, r.w_value_v),
                (r.w_query, r.w_query_v),
                (r.w_out, r.w_out_v),
                (r.grad_top, r.grad_all.at[ex]),
            )
        )
    ]
    for copy in r.loads + loads:
        copy.start()
    pl.semaphore_wait(
        barrier, ne - 1 + jnp.where(me > 0, 1, 0) + jnp.where(me < nz - 1, 1, 0)
    )

    def spread(kind, step):
        src = (r.grad_top, r.tables_s, r.second_s)[kind]
        dst = (r.grad_all, r.tables_all, r.rows_all)[kind]
        return pltpu.make_async_remote_copy(
            src_ref=src,
            dst_ref=dst.at[ex],
            send_sem=r.spread_send.at[kind, step],
            recv_sem=r.spread_recv.at[kind, step],
            device_id={"expert": lax.rem(ex + step, ne)},
            device_id_type=MESH,
        )

    def up(slot):
        return [
            pltpu.make_async_remote_copy(
                src_ref=ref.at[slot],
                dst_ref=ref.at[slot],
                send_sem=r.up_send.at[i, slot],
                recv_sem=r.up_recv.at[i, slot],
                device_id={"context": me + 1},
                device_id_type=MESH,
            )
            for i, ref in enumerate((r.kv_s, r.seg_s))
        ]

    for step in range(1, ne):
        spread(0, step).start()

    for copy in r.loads:
        copy.wait()

    values = r.tokens[...].astype(f32)
    inverse = lax.rsqrt(jnp.mean(values * values, axis=-1, keepdims=True) + epsilon)
    first = (values * inverse * r.gains[:1, :].astype(f32)).astype(bf16)
    r.first_s[...] = first
    cos_b, sin_b = r.base[0, pl.ds(me, 1), :], r.base[1, pl.ds(me, 1), :]
    cos_i, sin_i = r.inner[0], r.inner[1]
    cosine = cos_i * cos_b - sin_i * sin_b
    sine = sin_i * cos_b + cos_i * sin_b
    first_lanes = lax.rem(lax.broadcasted_iota(jnp.int32, (tokens, 128), 1), HEAD_DIM) < quarter
    sine = jnp.where(first_lanes, sine, -sine)
    r.turn_s[0] = cosine
    r.turn_s[1] = sine

    def rotate(x):
        swapped = jnp.where(
            first_lanes, pltpu.roll(x, 128 - quarter, 1), pltpu.roll(x, quarter, 1)
        )
        return x * cosine - swapped * sine

    loads[0].wait()
    keys = nn(first, r.w_key_v[...])
    for t in range(slices):
        at = slice(t * 128, (t + 1) * 128)
        r.kv_s[me, :, at] = rotate(keys[:, at]).astype(bf16)
    loads[1].wait()
    r.kv_s[me, :, kv_width:] = nn(first, r.w_value_v[...]).astype(bf16)
    r.seg_s[me] = jnp.broadcast_to(r.seg[...].astype(f32), (8, tokens))

    @pl.when(me < nz - 1)
    def _():
        for copy in up(me):
            copy.start()

    loads[2].wait()
    factor = HEAD_DIM ** (-0.5)
    low = lane_half((tokens, 128), 0)
    for t in range(slices):
        two = nn(first, r.w_query_v[:, t * 256 : (t + 1) * 256])
        left, right = rotate(two[:, :128]), rotate(two[:, 128:])
        even = jnp.where(low, left, pltpu.roll(right, HEAD_DIM, 1))
        odd = jnp.where(low, pltpu.roll(left, HEAD_DIM, 1), right)
        r.q_s[t, :tokens, :] = (even * factor).astype(bf16)
        r.q_s[t, tokens:, :] = (odd * factor).astype(bf16)
    experts_all = r.tables_s.shape[1]
    for e, row in enumerate(slot_table(r.chosen[...], r.order[...], experts_all, capacity)):
        r.tables_s[0, e : e + 1, :] = row

    r.acc[...] = jnp.zeros_like(r.acc)
    r.top[...] = jnp.full_like(r.top, -3e38)
    r.total[...] = jnp.zeros_like(r.total)

    def block(j):
        bias = mask_bias(r.seg_s, j, me, tokens)
        r.bias[:, :tokens] = bias
        r.bias[:, tokens:] = bias

        @pl.loop(0, slices)
        def _(t):
            k_at = pl.ds(pl.multiple_of(t * 128, 128), 128)
            v_at = pl.ds(pl.multiple_of(kv_width + t * 128, 128), 128)
            keys = r.kv_s[j, :, k_at]
            vals = r.kv_s[j, :, v_at]
            for half in (0, 1):
                keep = lane_half((tokens, 128), half)
                zero = jnp.zeros_like(keys)
                scores = nt(jnp.where(keep, keys, zero), r.q_s[t]) + r.bias[...]
                old = r.top[t, half : half + 1, :]
                new = jnp.maximum(old, jnp.max(scores, axis=0, keepdims=True))
                scale = jnp.exp(old - new)
                soft = jnp.exp(scores - new)
                r.top[t, half : half + 1, :] = new
                r.total[t, half : half + 1, :] = r.total[t, half : half + 1, :] * scale + jnp.sum(
                    soft, axis=0, keepdims=True
                )
                mixed = tn(jnp.where(keep, vals, zero), soft.astype(bf16))
                a, b = half * HEAD_DIM, (half + 1) * HEAD_DIM
                r.acc[t, a:b, :] = r.acc[t, a:b, :] * scale + mixed[a:b]

    block(me)
    for step in range(1, nz):
        j = me - step

        @pl.when(j >= 0)
        def _():
            for copy in up(j):
                copy.wait_recv()

            @pl.when(me < nz - 1)
            def _():
                for copy in up(j):
                    copy.start()

            block(j)

    for t in range(slices):
        r.lse_s[t] = r.top[t] + jnp.log(r.total[t])
        for half in (0, 1):
            a, b = half * HEAD_DIM, (half + 1) * HEAD_DIM
            head = (r.acc[t, a:b, :] / r.total[t, half : half + 1, :]).astype(bf16)
            r.heads_s[2 * t + half] = head
            for ab in (0, 1):
                h = (4 * t + 2 * half + ab) * HEAD_DIM
                r.attn_turned[h : h + HEAD_DIM, :] = head[:, ab * tokens : (ab + 1) * tokens]

    loads[3].wait()
    middle = r.tokens[...].astype(f32) + tn(r.attn_turned[...], r.w_out_v[...])
    r.middle_s[...] = middle
    inverse = lax.rsqrt(jnp.mean(middle * middle, axis=-1, keepdims=True) + epsilon)
    second = (middle * inverse * r.gains[1:, :].astype(f32)).astype(bf16)
    r.second_s[...] = second
    for step in range(1, ne):
        spread(2, step).start()
    logits = nt(r.w_router_turned[...], second)
    grown = jnp.exp(logits - jnp.max(logits, axis=0, keepdims=True))
    r.tables_s[1] = grown / jnp.sum(grown, axis=0, keepdims=True)
    for step in range(1, ne):
        spread(1, step).start()
    stores = [
        pltpu.make_async_copy(src, dst, r.store_sem.at[i])
        for i, (src, dst) in enumerate(
            (
                (r.second_s, r.rows_all.at[ex]),
                (r.tables_s, r.tables_all.at[ex]),
                (r.q_s, r.q),
                (r.kv_s, r.kv_all),
                (r.seg_s, r.seg_all),
                (r.lse_s, r.lse),
                (r.heads_s, r.heads),
                (r.middle_s, r.middle),
                (r.second_s, r.second_low),
                (r.first_s, r.first_low),
                (r.turn_s, r.turn),
            )
        )
    ]
    for copy in stores:
        copy.start()
    for copy in stores:
        copy.wait()
    loads[4].wait()
    for kind in range(3):
        for step in range(1, ne):
            spread(kind, step).wait()
    for step in range(nz):
        j = me - step

        @pl.when((j >= 0) & (me < nz - 1))
        def _():
            for copy in up(j):
                copy.wait_send()


def front(sizes, cid, capacity, hbm_ins, vmem_ins):
    ne, nz, nd = sizes
    ins = types.SimpleNamespace(**hbm_ins, **vmem_ins)
    tokens, width = ins.tokens.shape
    kv_width = ins.w_key.shape[1]
    slices, wide = kv_width // 128, 2 * tokens
    experts_all = ins.w_router_turned.shape[0]
    shape = jax.ShapeDtypeStruct
    vmem, dma = pltpu.VMEM, pltpu.SemaphoreType.DMA
    sized = dict(
        q=((slices, wide, 128), bf16),
        kv=((nz, tokens, 2 * kv_width), bf16),
        seg=((nz, 8, tokens), f32),
        lse=((slices, 2, wide), f32),
        heads=((2 * slices, HEAD_DIM, wide), bf16),
        middle=((tokens, width), f32),
        second=((tokens, width), bf16),
        first=((tokens, width), bf16),
        turn=((2, tokens, 128), f32),
        tables=((2, experts_all, tokens), f32),
    )
    outs = dict(
        rows_all=shape((ne, tokens, width), bf16),
        grad_all=shape((ne, tokens, width), bf16),
        tables_all=shape((ne, 2, experts_all, tokens), f32),
        q=shape(*sized["q"]),
        kv_all=shape(*sized["kv"]),
        seg_all=shape(*sized["seg"]),
        lse=shape(*sized["lse"]),
        heads=shape(*sized["heads"]),
        middle=shape(*sized["middle"]),
        second_low=shape(*sized["second"]),
        first_low=shape(*sized["first"]),
        turn=shape(*sized["turn"]),
    )
    scratch = dict(
        w_query_v=vmem(ins.w_query.shape, bf16),
        w_key_v=vmem(ins.w_key.shape, bf16),
        w_value_v=vmem(ins.w_value.shape, bf16),
        w_out_v=vmem(ins.w_out.shape, bf16),
        attn_turned=vmem((width, tokens), bf16),
        acc=vmem((slices, 128, wide), f32),
        top=vmem((slices, 2, wide), f32),
        total=vmem((slices, 2, wide), f32),
        bias=vmem((tokens, wide), f32),
        load_sem=dma((5,)),
        store_sem=dma((11,)),
        spread_send=dma((3, ne)),
        spread_recv=dma((3, ne)),
        up_send=dma((2, nz)),
        up_recv=dma((2, nz)),
        **{k + "_s": vmem(*v) for k, v in sized.items()},
    )
    return call_named(
        functools.partial(front_kernel, sizes, capacity),
        hbm_ins, vmem_ins, outs, scratch, cid, 60 << 20, tuple(outs),
    )


class Line:
    def __init__(self, nz, held, came, send, recv):
        if nz < 3:
            raise ValueError("context")
        self.nz, self.held, self.came, self.send, self.recv = nz, held, came, send, recv
        self.me = lax.axis_index("context")

    @staticmethod
    def scratch(nz, chunks, rows, width):
        return [
            pltpu.VMEM((chunks, nz, rows, width), bf16),
            pltpu.VMEM((chunks, nz, rows, width), bf16),
            pltpu.SemaphoreType.DMA((chunks, nz)),
            pltpu.SemaphoreType.DMA((chunks, nz)),
        ]

    def copy(self, k, s, target, slot):
        return pltpu.make_async_remote_copy(
            src_ref=self.held.at[k, s],
            dst_ref=self.came.at[k, slot],
            send_sem=self.send.at[k, s],
            recv_sem=self.recv.at[k, slot],
            device_id={"context": target},
            device_id_type=MESH,
        )

    def route(self, place, s):
        last = self.nz - 1
        if (place, s) == (0, last):
            return 1, 1
        if (place, s) == (last, 0):
            return last - 1, last - 1
        return s, place

    def merged(self, place, s):
        return (place, s) in ((1, self.nz - 1), (self.nz - 2, 0))

    def start(self, k, place, pieces):
        for s in pieces:
            self.copy(k, s, *self.route(place, s)).start()

    def first(self, k):
        last = self.nz - 1
        for place in range(self.nz):

            @pl.when(self.me == place)
            def _():
                if place in (0, last):
                    self.start(k, place, [last - place])
                else:
                    self.start(
                        k, place,
                        [s for s in range(self.nz) if s != place and not self.merged(place, s)],
                    )

    def ends(self, k, place):
        @pl.when(self.me == place)
        def _():
            order = range(1, self.nz - 1)
            self.start(k, place, reversed(order) if place == 0 else order)

    def merge(self, k, place):
        s = self.nz - 1 if place == 1 else 0

        @pl.when(self.me == place)
        def _():
            self.copy(k, 0, 0, place).wait_recv()
            for at in range(0, self.held.shape[2], 16):
                rows = slice(at, at + 16)
                self.held[k, s, rows] = (
                    self.held[k, s, rows].astype(f32) + self.came[k, place, rows].astype(f32)
                ).astype(bf16)
            self.start(k, place, [s])

    def total(self, k, put):
        last = self.nz - 1
        for place in range(self.nz):

            @pl.when(self.me == place)
            def _():
                senders = [p for p in range(self.nz) if p != place and abs(p - place) != last]
                for p in senders:
                    self.copy(k, 0, 0, p).wait_recv()
                for at in range(0, self.held.shape[2], 16):
                    rows = slice(at, at + 16)
                    value = self.held[k, place, rows].astype(f32)
                    for p in senders:
                        value = value + self.came[k, p, rows].astype(f32)
                    put(at, value)
                for s in range(self.nz):
                    if s != place:
                        self.copy(k, s, *self.route(place, s)).wait_send()


def experts_kernel(sizes, cap, defs, *refs):
    r = named(defs, refs)
    ne, nz, nd = sizes
    ex, dp, ctx = (lax.axis_index(a) for a in ("expert", "dp", "context"))
    local, width, hid = r.w_gate.shape
    tokens = r.rows_all.shape[1]
    gate_rows, down_rows = width // (nz * nd), hid // (nz * nd)
    line = Line(nz, r.held_s, *r.line)

    barrier = pltpu.get_barrier_semaphore()
    for axis, place, size in (("dp", dp, nd), ("context", ctx, nz)):
        for step in range(1, size):
            pl.semaphore_signal(
                barrier, inc=1, device_id={axis: lax.rem(place + step, size)}, device_id_type=MESH
            )

    def weights(e, slot):
        return [
            pltpu.make_async_copy(src, dst, r.weight_sem.at[slot, i])
            for i, (src, dst) in enumerate(
                (
                    (r.w_gate.at[e], r.both.at[slot, :, pl.ds(0, hid)]),
                    (r.w_up.at[e], r.both.at[slot, :, pl.ds(hid, hid)]),
                    (r.w_down.at[e], r.down.at[slot]),
                )
            )
        ]

    for copy in r.loads + weights(0, 0):
        copy.start()
    pl.semaphore_wait(barrier, nd + nz - 2)
    for copy in r.loads:
        copy.wait()

    def cores(k, step):
        other = lax.rem(dp + step, nd)
        return pltpu.make_async_remote_copy(
            src_ref=r.made.at[:, other],
            dst_ref=r.from_dp.at[step - 1, k],
            send_sem=r.dp_send.at[k, step],
            recv_sem=r.dp_recv.at[k, step],
            device_id={"dp": other},
            device_id_type=MESH,
        )

    def keep(k):
        return pltpu.make_async_copy(r.held_s.at[k], r.held.at[k], r.held_sem.at[k])

    def add_cores(k):
        for step in range(1, nd):
            cores(k, step).wait_recv()
            for z in range(nz):
                add_rows(r.held_s, (k, z), r.from_dp, (step - 1, k, z), gate_rows + down_rows)

        @pl.when(k > 0)
        def _():
            keep(k).start()

    row_id = lax.broadcasted_iota(jnp.int32, (cap, tokens), 0).astype(f32)

    @pl.loop(0, local)
    def _(e):
        slot = lax.rem(e, 2)
        own = pl.ds(pl.multiple_of(e * cap, 16), cap)
        for src in range(ne):
            at = pl.ds(src * cap, cap)
            hits = r.tables_all[src, 0, pl.ds(ex * local + e, 1), :] == row_id
            gate_row = r.tables_all[src, 1, pl.ds(ex * local + e, 1), :]
            gate = jnp.sum(jnp.where(hits, gate_row, 0.0), axis=1, keepdims=True)
            low = jnp.where(hits, 1.0, 0.0).astype(bf16)
            r.hits[src, own, :] = low
            r.gate_s[at, :] = jnp.broadcast_to(gate, (cap, 128))
            r.x_s[at, :] = nn(low, r.rows_all[src]).astype(bf16)
            og = nn(low, r.grad_all[src])
            r.og_s[at, :] = og.astype(bf16)
            r.sg_s[at, :] = (og * gate).astype(bf16)
        for copy in weights(e, slot):
            copy.wait()

        @pl.when(e < local - 1)
        def _():
            for copy in weights(e + 1, 1 - slot):
                copy.start()

        pre = nn(r.x_s[...], r.both[slot])

        @pl.when(e > 0)
        def _():
            add_cores(e - 1)

        @pl.when(e == 1)
        def _():
            line.first(0)

        @pl.when(e == 2)
        def _():
            line.ends(0, 0)
            line.ends(0, nz - 1)
            line.merge(0, 1)
            line.merge(0, nz - 2)

        gate_pre, up_pre = pre[:, :hid], pre[:, hid:]
        sig = jax.nn.sigmoid(gate_pre)
        silu = gate_pre * sig
        r.hidden[...] = (silu * up_pre).astype(bf16)
        hidden_back = nt(r.sg_s[...], r.down[slot])
        r.pre_back[:, :hid] = (
            hidden_back * up_pre * sig * (1.0 + gate_pre * (1.0 - sig))
        ).astype(bf16)
        r.pre_back[:, hid:] = (hidden_back * silu).astype(bf16)
        produced = nn(r.hidden[...], r.down[slot])
        pair = jnp.sum(r.og_s[...].astype(f32) * produced, axis=1, keepdims=True)
        weighed = (produced * r.gate_s[:, :1]).astype(bf16)
        for src in range(ne):
            a, b = src * cap, (src + 1) * cap
            r.weighed[src, own, :] = weighed[a:b]
            r.soft_part[src, pl.ds(e, 1), :] = jnp.sum(
                r.hits[src, own, :].astype(f32) * pair[a:b], axis=0, keepdims=True
            )
        back = nt(r.pre_back[...], r.both[slot]).astype(bf16)
        for src in range(ne):
            r.back_rows[src, own, :] = back[src * cap : (src + 1) * cap]

        @pl.when(e > 0)
        def _():
            for step in range(1, nd):
                cores(e - 1, step).wait_send()

        r.made[:, :, :gate_rows, :] = (
            tn(r.x_s[...], r.pre_back[...]).astype(bf16).reshape(nz, nd, gate_rows, 2 * hid)
        )
        r.made[:, :, gate_rows:, :] = (
            tn(r.hidden[...], r.sg_s[...]).astype(bf16).reshape(nz, nd, down_rows, width)
        )
        for step in range(1, nd):
            cores(e, step).start()
        r.held_s[e] = r.made[:, dp]

    stores = []
    for kind, (rows, out) in enumerate(((r.back_rows, r.back_part), (r.weighed, r.out_part))):
        for src in range(ne):
            r.sums[kind, src] = tn(r.hits[src], rows[src]).astype(bf16)
            stores.append(
                pltpu.make_async_copy(r.sums.at[kind, src], out.at[src], r.store_sem.at[kind, src])
            )
            stores[-1].start()
    add_cores(local - 1)

    def put(at, value):
        r.shard[at : at + 16, :] = value

    line.total(0, put)
    for step in range(1, nd):
        cores(local - 1, step).wait_send()
    for k in range(1, local):
        keep(k).wait()
    for copy in stores:
        copy.wait()


def experts(sizes, cid, cap, kept, read):
    ne, nz, nd = sizes
    local, width, hid = kept["w_gate"].shape
    tokens = read["rows_all"].shape[1]
    piece = width // (nz * nd) + hid // (nz * nd)
    shape, vmem, dma = jax.ShapeDtypeStruct, pltpu.VMEM, pltpu.SemaphoreType.DMA
    held, *line = Line.scratch(nz, local, piece, width)
    line[0] = vmem((1, nz, piece, width), bf16)
    outs = dict(
        held=shape((local, nz, piece, width), bf16),
        out_part=shape((ne, tokens, width), bf16),
        back_part=shape((ne, tokens, width), bf16),
        soft_part=shape((ne, local, tokens), f32),
        shard=shape((piece, width), f32),
    )
    rows = ne * cap
    scratch = dict(
        both=vmem((2, width, 2 * hid), bf16),
        down=vmem((2, hid, width), bf16),
        x_s=vmem((rows, width), bf16),
        og_s=vmem((rows, width), bf16),
        sg_s=vmem((rows, width), bf16),
        gate_s=vmem((rows, 128), f32),
        hidden=vmem((rows, hid), bf16),
        pre_back=vmem((rows, 2 * hid), bf16),
        hits=vmem((ne, local * cap, tokens), bf16),
        weighed=vmem((ne, local * cap, width), bf16),
        back_rows=vmem((ne, local * cap, width), bf16),
        sums=vmem((2, ne, tokens, width), bf16),
        made=vmem((nz, nd, piece, width), bf16),
        from_dp=vmem((nd - 1, local, nz, piece, width), bf16),
        held_s=held,
        line=line,
        weight_sem=dma((2, 3)),
        dp_send=dma((local, nd)),
        dp_recv=dma((local, nd)),
        held_sem=dma((local,)),
        store_sem=dma((2, ne)),
    )
    return call_named(
        functools.partial(experts_kernel, sizes, cap),
        kept, read, outs, scratch, cid, 62 << 20, ("held", "out_part", "back_part"),
    )


class Spread:
    def __init__(self, sizes, made, from_dp, held, from_ex, line, from_z, send, recv):
        self.sizes, self.made, self.from_dp, self.held = sizes, made, from_dp, held
        self.from_ex, self.line, self.from_z, self.send, self.recv = from_ex, line, from_z, send, recv
        self.places = tuple(lax.axis_index(a) for a in ("dp", "expert", "context"))

    @staticmethod
    def scratch(sizes, rows, width):
        ne, nz, nd = sizes
        most = max(sizes)
        return [
            pltpu.VMEM((nd - 1, ne, nz, rows, width), bf16),
            pltpu.VMEM((ne, nz, rows, width), bf16),
            pltpu.VMEM((ne - 1, nz, rows, width), bf16),
            pltpu.VMEM((nz, rows, width), bf16),
            pltpu.VMEM((nz - 1, rows, width), bf16),
            pltpu.SemaphoreType.DMA((3, most)),
            pltpu.SemaphoreType.DMA((3, most)),
        ]

    def copy(self, stage, step):
        ne, nz, nd = self.sizes
        axis, size = (("dp", nd), ("expert", ne), ("context", nz))[stage]
        other = lax.rem(self.places[stage] + step, size)
        src = (
            self.made.at[:, :, other]
            if stage == 0
            else self.held.at[other] if stage == 1 else self.line.at[other]
        )
        dst = (self.from_dp, self.from_ex, self.from_z)[stage].at[step - 1]
        return pltpu.make_async_remote_copy(
            src_ref=src,
            dst_ref=dst,
            send_sem=self.send.at[stage, step],
            recv_sem=self.recv.at[stage, step],
            device_id={axis: other},
            device_id_type=MESH,
        )

    def others(self, stage):
        ne, nz, nd = self.sizes
        return range(1, (nd, ne, nz)[stage])

    def over_dp(self):
        for step in self.others(0):
            self.copy(0, step).start()

    def made_free(self):
        for step in self.others(0):
            self.copy(0, step).wait_send()

    def over_expert(self):
        ne, nz, _ = self.sizes
        for step in self.others(0):
            self.copy(0, step).wait_recv()

        @pl.loop(0, ne * nz)
        def _(i):
            a = lax.div(i, nz)
            b = i - a * nz
            total = self.made[a, b, self.places[0]].astype(f32)
            for step in self.others(0):
                total = total + self.from_dp[step - 1, a, b].astype(f32)
            self.held[a, b] = total.astype(bf16)

        for step in self.others(1):
            self.copy(1, step).start()

    def over_context(self):
        nz = self.sizes[1]
        for step in self.others(1):
            self.copy(1, step).wait_recv()

        @pl.loop(0, nz)
        def _(b):
            total = self.held[self.places[1], b].astype(f32)
            for step in self.others(1):
                total = total + self.from_ex[step - 1, b].astype(f32)
            self.line[b] = total.astype(bf16)

        for step in self.others(2):
            self.copy(2, step).start()

    def finish(self, out):
        for step in self.others(2):
            self.copy(2, step).wait_recv()
        total = self.line[self.places[2]].astype(f32)
        for step in self.others(2):
            total = total + self.from_z[step - 1].astype(f32)
        out[...] = total
        for stage in (1, 2):
            for step in self.others(stage):
                self.copy(stage, step).wait_send()


def tail_kernel(sizes, defs, *refs):
    r = named(defs, refs)
    ne, nz, nd = sizes
    ex, me, dp = (lax.axis_index(a) for a in ("expert", "context", "dp"))
    tokens, width = r.tokens.shape
    kv_width = r.kv_all.shape[2] // 2
    slices = kv_width // 128
    group = width // ne

    barrier = pltpu.get_barrier_semaphore()
    for axis, place, size in (("expert", ex, ne), ("context", me, nz), ("dp", dp, nd)):
        for step in range(1, size):
            pl.semaphore_signal(
                barrier, inc=1, device_id={axis: lax.rem(place + step, size)}, device_id_type=MESH
            )
    for copy in r.loads:
        copy.start()
    pl.semaphore_wait(barrier, ne + nz + nd - 3)

    line = Line(nz, *r.line)
    proj = Spread(sizes, r.made, *r.proj)
    query = Spread(sizes, r.made, *r.query)
    kv = Spread(sizes, r.made, *r.kv)
    small = Spread(sizes, r.small_made, *r.small)

    chunks = range(r.held_in.shape[0] - 1)
    held_copies = [
        pltpu.make_async_copy(r.held_in.at[k + 1], line.held.at[k], r.held_sem.at[k])
        for k in chunks
    ]
    for copy in held_copies:
        copy.start()

    def rows_copy(kind, step):
        other = lax.rem(ex + step, ne)
        return pltpu.make_async_remote_copy(
            src_ref=(r.back_in, r.out_in, r.soft_in)[kind].at[other],
            dst_ref=r.soft_all.at[ex] if kind == 2 else (r.back_came, r.out_came)[kind].at[step - 1],
            send_sem=r.rows_send.at[kind, step],
            recv_sem=r.rows_recv.at[kind, step],
            device_id={"expert": other},
            device_id_type=MESH,
        )

    for kind in (2, 0):
        for step in range(1, ne):
            rows_copy(kind, step).start()
    loads = [
        pltpu.make_async_copy(r.back_in.at[ex], r.back_own, r.load_sem.at[0]),
        pltpu.make_async_copy(r.soft_in.at[ex], r.soft_all.at[ex], r.load_sem.at[1]),
        pltpu.make_async_copy(r.out_in.at[ex], r.out_own, r.load_sem.at[2]),
        pltpu.make_async_copy(r.w_out, r.w_out_v, r.load_sem.at[3]),
        pltpu.make_async_copy(r.w_query, r.w_query_v, r.load_sem.at[4]),
        pltpu.make_async_copy(r.w_key, r.w_key_v, r.load_sem.at[5]),
        pltpu.make_async_copy(r.w_value, r.w_value_v, r.load_sem.at[6]),
        pltpu.make_async_copy(r.tables_all.at[ex], r.tables_own, r.load_sem.at[7]),
    ]
    for copy in loads:
        copy.start()
    for k in chunks:
        held_copies[k].wait()
        line.first(k)
    for copy in r.loads + loads:
        copy.wait()
    for t in range(2 * slices):
        for ab in (0, 1):
            h = 2 * t + ab
            r.attn_turned[h * HEAD_DIM : (h + 1) * HEAD_DIM, :] = r.heads[
                t, :, ab * tokens : (ab + 1) * tokens
            ]

    for kind in (2, 0):
        for step in range(1, ne):
            rows_copy(kind, step).wait_recv()
    for step in range(1, ne):
        rows_copy(1, step).start()
    soft_back = jnp.concatenate([r.soft_all[i] for i in range(ne)], axis=0)
    router_soft = r.tables_own[1]
    logit_back = (
        router_soft * (soft_back - jnp.sum(router_soft * soft_back, axis=0, keepdims=True))
    ).astype(bf16)
    second_back = r.back_own[...].astype(f32) + tn(logit_back, r.w_router_turned[...])
    for step in range(1, ne):
        second_back = second_back + r.back_came[step - 1].astype(f32)
    middle = r.middle[...]
    inverse = lax.rsqrt(jnp.mean(middle * middle, axis=-1, keepdims=True) + epsilon)
    normed = middle * inverse
    scaled = second_back * r.gains[1:, :].astype(f32)
    moe_gain_grad = jnp.sum(second_back * normed, axis=0, keepdims=True)
    middle_grad = r.grad_top[...].astype(f32) + inverse * (
        scaled - normed * jnp.mean(scaled * normed, axis=-1, keepdims=True)
    )
    r.middle_grad[...] = middle_grad
    r.branch[...] = middle_grad.astype(bf16)
    experts_all = logit_back.shape[0]
    r.small_rows[...] = jnp.zeros_like(r.small_rows)
    r.small_rows[:experts_all, :] = nn(logit_back, r.second_low[...])
    r.small_rows[experts_all : experts_all + 1, :] = moe_gain_grad

    @pl.loop(0, slices)
    def _(t):
        at = pl.ds(pl.multiple_of(t * 256, 256), 256)
        turned = nt(r.w_out_v[at, :], r.branch[...]).astype(bf16)
        for half in (0, 1):
            a, b = half * HEAD_DIM, (half + 1) * HEAD_DIM
            for ab in (0, 1):
                c = (2 * half + ab) * HEAD_DIM
                r.do[t, a:b, ab * tokens : (ab + 1) * tokens] = turned[c : c + HEAD_DIM]
            r.delta[t, half : half + 1, :] = jnp.sum(
                r.do[t, a:b, :].astype(f32) * r.heads[2 * t + half].astype(f32),
                axis=0,
                keepdims=True,
            )

    @pl.loop(0, ne)
    def _(g):
        at = pl.ds(pl.multiple_of(g * group, group), group)
        grad = nn(r.attn_turned[at, :], r.branch[...])
        r.made[g] = grad.reshape((nz, nd, group // (nz * nd), width)).astype(bf16)

    proj.over_dp()
    for k in chunks:
        line.ends(k, 0)
        line.merge(k, 1)

    r.dq[...] = jnp.zeros_like(r.dq)
    bias_s = r.bias

    def block(j, store):
        bias = mask_bias(r.seg_all, j, me, tokens)
        bias_s[:, :tokens] = bias
        bias_s[:, tokens:] = bias

        @pl.loop(0, slices)
        def _(t):
            k_at = pl.ds(pl.multiple_of(t * 128, 128), 128)
            v_at = pl.ds(pl.multiple_of(kv_width + t * 128, 128), 128)
            keys = r.kv_all[j, :, k_at]
            vals = r.kv_all[j, :, v_at]
            dks, dvs = [], []
            for half in (0, 1):
                keep = lane_half((tokens, 128), half)
                zero = jnp.zeros_like(keys)
                keys_half = jnp.where(keep, keys, zero)
                scores = nt(keys_half, r.q[t]) + bias_s[...]
                soft = jnp.exp(scores - r.lse[t, half : half + 1, :])
                soft_grad = nn(jnp.where(keep, vals, zero), r.do[t])
                back = (soft * (soft_grad - r.delta[t, half : half + 1, :])).astype(bf16)
                dvs.append(nt(soft.astype(bf16), r.do[t]))
                dks.append(nn(back, r.q[t]))
                r.dq[t] += tn(keys_half, back)
            low = lane_half((tokens, 128), 0)
            store(k_at, jnp.where(low, dks[0], dks[1]))
            store(v_at, jnp.where(low, dvs[0], dvs[1]))

    def give(j):
        return pltpu.make_async_remote_copy(
            src_ref=r.kv_part.at[j],
            dst_ref=r.kv_came.at[j],
            send_sem=r.kv_send.at[j],
            recv_sem=r.kv_recv.at[j],
            device_id={"context": me - 1},
            device_id_type=MESH,
        )

    for j in range(nz - 1):

        @pl.when(j < me)
        def _():
            def store(at, value):
                r.kv_part[j, :, at] = value.astype(bf16)

            block(j, store)

            @pl.when(me == nz - 1)
            def _():
                give(j).start()

    def store_own(at, value):
        r.own_kv[:, at] = value

    block(me, store_own)
    proj.over_expert()
    for k in chunks:
        line.merge(k, nz - 2)

    quarter = HEAD_DIM // 2
    cos_q, sin_q = (
        jnp.concatenate([r.turn[i].T[:quarter]] * 2, axis=1) * HEAD_DIM ** (-0.5) for i in (0, 1)
    )
    for t in range(slices):
        for half in (0, 1):
            a = half * HEAD_DIM
            first = r.dq[t, a : a + quarter, :]
            second = r.dq[t, a + quarter : a + 2 * quarter, :]
            turned = jnp.concatenate(
                [first * cos_q + second * sin_q, second * cos_q - first * sin_q], axis=0
            )
            pair = jnp.concatenate([turned[:, :tokens], turned[:, tokens:]], axis=0)
            at = (2 * t + half) * 128
            r.back_s[:, at : at + 128] = pair.T.astype(bf16)

    def make(a, b):
        @pl.loop(0, ne)
        def _(g):
            at = pl.ds(pl.multiple_of(g * group, group), group)
            grad = tn(r.first_low[:, at], r.back_s[:, a:b])
            r.made[g] = grad.reshape((nz, nd, group // (nz * nd), b - a)).astype(bf16)

    proj.made_free()
    make(0, width)
    query.over_dp()
    query.over_expert()

    for j in range(nz - 1):

        @pl.when((j < me) & (me < nz - 1))
        def _():
            give(j).wait_recv()

            @pl.loop(0, tokens // 16)
            def _(i):
                at = pl.ds(pl.multiple_of(i * 16, 16), 16)
                r.kv_part[j, at, :] = (
                    r.kv_part[j, at, :].astype(f32) + r.kv_came[j, at, :].astype(f32)
                ).astype(bf16)

            give(j).start()

    @pl.when(me < nz - 1)
    def _():
        give(me).wait_recv()

        @pl.loop(0, tokens // 16)
        def _(i):
            at = pl.ds(pl.multiple_of(i * 16, 16), 16)
            r.own_kv[at, :] += r.kv_came[me, at, :].astype(f32)

    @pl.when(me == nz - 1)
    def _():
        for j in range(nz - 1):
            give(j).wait_send()

    for k in chunks:
        line.ends(k, nz - 1)
    cos_k, sin_k = r.turn[0], r.turn[1]
    first_lanes = lax.rem(lax.broadcasted_iota(jnp.int32, (tokens, 128), 1), HEAD_DIM) < quarter
    for t in range(slices):
        grad = r.own_kv[:, t * 128 : (t + 1) * 128]
        swapped = jnp.where(
            first_lanes, pltpu.roll(grad, 128 - quarter, 1), pltpu.roll(grad, quarter, 1)
        )
        r.back_s[:, width + t * 128 : width + (t + 1) * 128] = (
            grad * cos_k + swapped * sin_k
        ).astype(bf16)
    r.back_s[:, width + kv_width :] = r.own_kv[:, kv_width:].astype(bf16)
    query.made_free()
    make(width, width + 2 * kv_width)
    kv.over_dp()
    proj.over_context()

    first_back = nt(r.back_s[:, :width], r.w_query_v[...])
    first_back = first_back + nt(r.back_s[:, width : width + kv_width], r.w_key_v[...])
    first_back = first_back + nt(r.back_s[:, width + kv_width :], r.w_value_v[...])
    values = r.tokens[...].astype(f32)
    inverse = lax.rsqrt(jnp.mean(values * values, axis=-1, keepdims=True) + epsilon)
    normed = values * inverse
    scaled = first_back * r.gains[:1, :].astype(f32)
    r.small_rows[experts_all + 1 : experts_all + 2, :] = jnp.sum(
        first_back * normed, axis=0, keepdims=True
    )
    r.input_grad[...] = r.middle_grad[...] + inverse * (
        scaled - normed * jnp.mean(scaled * normed, axis=-1, keepdims=True)
    )
    small_turned = r.small_rows[...].T
    r.small_made[...] = small_turned.reshape(r.small_made.shape).astype(bf16)
    small.over_dp()
    kv.over_expert()
    small.over_expert()
    query.over_context()

    for step in range(1, ne):
        rows_copy(1, step).wait_recv()

    @pl.loop(0, tokens // 16)
    def _(i):
        at = pl.ds(pl.multiple_of(i * 16, 16), 16)
        total = r.middle[at, :] + r.out_own[at, :].astype(f32)
        for step in range(1, ne):
            total = total + r.out_came[step - 1, at, :].astype(f32)
        r.layer_out[at, :] = total

    kv.over_context()
    small.over_context()
    kv.made_free()
    small.made_free()
    for group_sum, out in zip((proj, query, kv, small), r.sums_out + [r.small_sum]):
        group_sum.finish(out)
    r.router_out[...] = r.small_sum[:, :experts_all]
    turned = r.small_sum[...].T
    r.gains_out[0] = turned[experts_all + 1 : experts_all + 2]
    r.gains_out[1] = turned[experts_all : experts_all + 1]
    gate_out, up_out, down_out = r.experts_out
    gate_rows, hid = gate_out.shape[1:]

    def put(k, at, value):
        if at < gate_rows:
            gate_out[k, at : at + 16, :] = value[:, :hid]
            up_out[k, at : at + 16, :] = value[:, hid:]
        else:
            down_out[k, at - gate_rows : at - gate_rows + 16, :] = value

    for at in range(0, r.first_shard.shape[0], 16):
        put(0, at, r.first_shard[at : at + 16, :])
    for k in chunks:
        line.total(k, functools.partial(put, k + 1))
    for kind in range(3):
        for step in range(1, ne):
            rows_copy(kind, step).wait_send()
    for j in range(nz - 1):

        @pl.when((j < me) & (me < nz - 1))
        def _():
            give(j).wait_send()


def tail(sizes, cid, hidden, hbm_ins, vmem_ins):
    ne, nz, nd = sizes
    ins = types.SimpleNamespace(**hbm_ins, **vmem_ins)
    tokens, width = ins.tokens.shape
    slices, wide, _ = ins.q.shape
    chunks, _, piece, _ = ins.held_in.shape
    kv_shape = ins.kv_all.shape
    rows = width // (ne * nz * nd)
    gate_rows = width // (nz * nd)
    shard = lambda *shape: jax.ShapeDtypeStruct(shape, f32)
    outs = dict(
        layer_out=shard(tokens, width),
        input_grad=shard(tokens, width),
        sums_out=[shard(rows, c) for c in (width, width, kv_shape[2])],
        router_out=shard(rows, ins.w_router_turned.shape[0]),
        gains_out=shard(2, 1, rows),
        experts_out=[
            shard(chunks, gate_rows, hidden),
            shard(chunks, gate_rows, hidden),
            shard(chunks, piece - gate_rows, width),
        ],
    )
    dma = pltpu.SemaphoreType.DMA
    vmem = pltpu.VMEM
    scratch = dict(
        back_own=vmem((tokens, width), bf16),
        back_came=vmem((ne - 1, tokens, width), bf16),
        out_own=vmem((tokens, width), bf16),
        out_came=vmem((ne - 1, tokens, width), bf16),
        soft_all=vmem(ins.soft_in.shape, f32),
        w_out_v=vmem(ins.w_out.shape, bf16),
        w_query_v=vmem(ins.w_query.shape, bf16),
        w_key_v=vmem(ins.w_key.shape, bf16),
        w_value_v=vmem(ins.w_value.shape, bf16),
        attn_turned=vmem((width, tokens), bf16),
        middle_grad=vmem((tokens, width), f32),
        branch=vmem((tokens, width), bf16),
        small_rows=vmem((128, width), f32),
        do=vmem((slices, 128, wide), bf16),
        delta=vmem((slices, 2, wide), f32),
        bias=vmem((tokens, wide), f32),
        dq=vmem((slices, 128, wide), f32),
        kv_part=vmem((nz - 1,) + kv_shape[1:], bf16),
        kv_came=vmem(kv_shape, bf16),
        own_kv=vmem(kv_shape[1:], f32),
        back_s=vmem((tokens, width + kv_shape[2]), bf16),
        made=vmem((ne, nz, nd, rows, width), bf16),
        small_made=vmem((ne, nz, nd, rows, 128), bf16),
        small_sum=vmem((rows, 128), f32),
        rows_send=dma((3, ne)),
        rows_recv=dma((3, ne)),
        load_sem=dma((8,)),
        tables_own=vmem(ins.tables_all.shape[1:], f32),
        held_sem=dma((chunks,)),
        kv_send=dma((nz,)),
        kv_recv=dma((nz,)),
        line=Line.scratch(nz, chunks - 1, piece, width),
        proj=Spread.scratch(sizes, rows, width),
        query=Spread.scratch(sizes, rows, width),
        kv=Spread.scratch(sizes, rows, kv_shape[2]),
        small=Spread.scratch(sizes, rows, 128),
    )
    return call_named(
        functools.partial(tail_kernel, sizes), hbm_ins, vmem_ins, outs, scratch, cid, 63 << 20, ()
    )


def deliver_kernel(parts, count, *refs):
    ins, outs, sem, held = refs[:count], refs[count : 2 * count], refs[2 * count], refs[2 * count + 1 :]
    reads = [
        pltpu.make_async_copy(
            ins[i] if part is None else ins[i].at[:, pl.ds(*part)], held[i], sem.at[0, i]
        )
        for i, part in enumerate(parts)
    ]
    writes = [pltpu.make_async_copy(held[i], outs[i], sem.at[1, i]) for i in range(count)]
    for copy in reads:
        copy.start()
    for read, write in zip(reads, writes):
        read.wait()
        write.start()
    for copy in writes:
        copy.wait()


def deliver(moved):
    arrays, parts = zip(*moved)
    hbm = pl.BlockSpec(memory_space=pl.ANY)
    shapes = [a.shape[:-1] + (part[1] if part else a.shape[-1],) for a, part in moved]
    return pl.pallas_call(
        functools.partial(deliver_kernel, parts, len(parts)),
        out_shape=[jax.ShapeDtypeStruct(shape, a.dtype) for shape, a in zip(shapes, arrays)],
        in_specs=[hbm] * len(parts),
        out_specs=[hbm] * len(parts),
        scratch_shapes=[pltpu.SemaphoreType.DMA((2, len(parts)))]
        + [pltpu.VMEM(shape, a.dtype) for shape, a in zip(shapes, arrays)],
        compiler_params=pltpu.CompilerParams(vmem_limit_bytes=60 << 20),
        name="deliver",
    )(*arrays)


def turn_tables(tokens, blocks):
    freq = rope_base ** (-2.0 * np.arange(HEAD_DIM // 2) / HEAD_DIM)
    freq = np.tile(freq, 128 // freq.size)
    inner = np.arange(tokens)[:, None] * freq
    base = tokens * np.arange(blocks)[:, None] * freq
    return tuple(
        jnp.asarray(np.stack([np.cos(a), np.sin(a)]), f32) for a in (inner, base)
    )


def body(
    sizes,
    tokens,
    attn_scale,
    w_query,
    w_key,
    w_value,
    w_out,
    moe_scale,
    w_router,
    w_gate,
    w_up,
    w_down,
    segment_ids,
    expert_choice,
    slot_order,
    out_grad,
):
    ne, nz, nd = sizes
    local_rows = tokens.shape[1]
    kv_width = w_key.shape[1]
    experts_all = w_router.shape[1]
    pair_count = local_rows * expert_choice.shape[2]
    capacity = (pair_count * 9 + 8 * experts_all - 1) // (8 * experts_all)
    inner, base = turn_tables(local_rows, nz)
    w_router_turned = w_router.T
    gains = jnp.stack([attn_scale, moe_scale])

    begun = front(
        sizes,
        1,
        capacity,
        dict(
            w_query=w_query, w_key=w_key, w_value=w_value, w_out=w_out, grad_top=out_grad[0]
        ),
        dict(
            tokens=tokens[0],
            gains=gains,
            w_router_turned=w_router_turned,
            seg=segment_ids,
            chosen=expert_choice[0].T,
            order=slot_order[0],
            inner=inner,
            base=base,
        ),
    )
    mixed = experts(
        sizes,
        2,
        capacity,
        dict(w_gate=w_gate, w_up=w_up, w_down=w_down),
        dict(rows_all=begun.rows_all, grad_all=begun.grad_all, tables_all=begun.tables_all),
    )
    ended = tail(
        sizes,
        3,
        w_gate.shape[2],
        dict(
            held_in=mixed.held,
            back_in=mixed.back_part,
            out_in=mixed.out_part,
            soft_in=mixed.soft_part,
            w_query=w_query,
            w_key=w_key,
            w_value=w_value,
            w_out=w_out,
            tables_all=begun.tables_all,
        ),
        dict(
            q=begun.q,
            kv_all=begun.kv_all,
            seg_all=begun.seg_all,
            lse=begun.lse,
            heads=begun.heads,
            middle=begun.middle,
            tokens=tokens[0],
            grad_top=out_grad[0],
            second_low=begun.second_low,
            first_low=begun.first_low,
            w_router_turned=w_router_turned,
            gains=gains,
            turn=begun.turn,
            first_shard=mixed.shard,
        ),
    )
    out_shard, query_shard, kv_shard = ended.sums_out
    moved = [
        (ended.layer_out, None),
        (ended.input_grad, None),
        (query_shard, None),
        (kv_shard, (0, kv_width)),
        (kv_shard, (kv_width, kv_width)),
        (out_shard, None),
        *((array, None) for array in ended.experts_out),
    ]
    layer_out, input_grad, *shards = deliver(moved)
    return (
        layer_out[None],
        input_grad[None],
        ended.gains_out[0, 0],
        ended.gains_out[1, 0],
        *shards[:4],
        ended.router_out,
        *shards[4:],
    )


def solution(mesh):
    sizes = (mesh.shape["expert"], mesh.shape["context"], mesh.shape["dp"])
    in_specs = (
        P(("expert", "dp"), "context", None),
        P(),
        P(),
        P(),
        P(),
        P(),
        P(),
        P(),
        P("expert", None, None),
        P("expert", None, None),
        P("expert", None, None),
        P(("expert", "dp"), "context"),
        P(("expert", "dp"), "context", None),
        P(("expert", "dp"), "context", None),
        P(("expert", "dp"), "context", None),
    )
    out_specs = (
        P(("expert", "dp"), "context", None),
        P(("expert", "dp"), "context", None),
        P(("expert", "context", "dp")),
        P(("expert", "context", "dp")),
        P(("expert", "context", "dp"), None),
        P(("expert", "context", "dp"), None),
        P(("expert", "context", "dp"), None),
        P(("expert", "context", "dp"), None),
        P(("expert", "context", "dp"), None),
        P("expert", ("context", "dp"), None),
        P("expert", ("context", "dp"), None),
        P("expert", ("context", "dp"), None),
    )
    return jax.shard_map(
        functools.partial(body, sizes),
        mesh=mesh,
        in_specs=in_specs,
        out_specs=out_specs,
        check_vma=False,
    )
```

```python
import functools
import types

import jax
import jax.numpy as jnp
import numpy as np
from jax import lax
from jax.experimental import pallas as pl
from jax.experimental.pallas import tpu as pltpu
from jax.sharding import PartitionSpec as P

HEAD_DIM = 64
MESH = pl.DeviceIdType.MESH

epsilon = 1e-06
rope_base = 10000.0
negative_large = -1e30
bf16 = jnp.bfloat16
f32 = jnp.float32


def nt(a, b):
    return lax.dot_general(a, b, (((1,), (1,)), ((), ())), preferred_element_type=f32)


def tn(a, b):
    return lax.dot_general(a, b, (((0,), (0,)), ((), ())), preferred_element_type=f32)


def nn(a, b):
    return jnp.dot(a, b, preferred_element_type=f32)


def add_rows(dst, dst_at, src, src_at, rows):
    step = 16

    @pl.loop(0, rows // step)
    def _(i):
        at = pl.ds(pl.multiple_of(i * step, step), step)
        dst[dst_at + (at, slice(None))] = (
            dst[dst_at + (at, slice(None))].astype(f32) + src[src_at + (at, slice(None))].astype(f32)
        ).astype(bf16)


def lane_half(shape, which):
    lanes = lax.broadcasted_iota(jnp.int32, shape, 1)
    return (lanes >= HEAD_DIM) if which else (lanes < HEAD_DIM)


def column_of(row):
    n = row.shape[1]
    rows = lax.broadcasted_iota(jnp.int32, (n, n), 0)
    cols = lax.broadcasted_iota(jnp.int32, (n, n), 1)
    return jnp.sum(jnp.where(rows == cols, row, 0.0), axis=1, keepdims=True)


def mask_bias(seg_ref, block, me, tokens):
    key_seg = column_of(seg_ref[block, :1, :])
    same = key_seg == seg_ref[me, :1, :]
    rows = lax.broadcasted_iota(jnp.int32, (tokens, tokens), 0) + block * tokens
    cols = lax.broadcasted_iota(jnp.int32, (tokens, tokens), 1) + me * tokens
    return jnp.where(same & (rows <= cols), 0.0, negative_large)


def named(defs, refs):
    counts = [d.num_leaves for d in defs]
    at = [sum(counts[:i]) for i in range(len(counts) + 1)]
    trees = [jax.tree.unflatten(d, refs[at[i] : at[i + 1]]) for i, d in enumerate(defs)]
    r = types.SimpleNamespace(**{k: v for tree in trees for k, v in tree.items()})
    read, (copies, sem) = trees[1], trees[3]["read"]
    r.loads = [
        pltpu.make_async_copy(read[k], copies[k], sem.at[i]) for i, k in enumerate(sorted(read))
    ]
    for k in read:
        setattr(r, k, copies[k])
    return r


def call_named(kernel, kept, read, outs, scratch, cid, limit, kept_outs):
    vm = pl.BlockSpec(memory_space=pltpu.VMEM)
    hbm = pl.BlockSpec(memory_space=pl.ANY)
    scratch["read"] = (
        {k: pltpu.VMEM(v.shape, v.dtype) for k, v in read.items()},
        pltpu.SemaphoreType.DMA((len(read),)),
    )
    flats, defs = zip(*(jax.tree.flatten(t) for t in (kept, read, outs, scratch)))
    out_specs = jax.tree.leaves(
        {k: jax.tree.map(lambda _: hbm if k in kept_outs else vm, v) for k, v in outs.items()}
    )
    results = pl.pallas_call(
        functools.partial(kernel, defs),
        out_shape=tuple(flats[2]),
        in_specs=[hbm] * (len(flats[0]) + len(flats[1])),
        out_specs=tuple(out_specs),
        scratch_shapes=flats[3],
        compiler_params=pltpu.CompilerParams(
            collective_id=cid, has_side_effects=True, vmem_limit_bytes=limit
        ),
        name=kernel.func.__name__,
    )(*flats[0], *flats[1])
    return types.SimpleNamespace(**jax.tree.unflatten(defs[2], results))


def slot_table(chosen, order, experts_all, capacity):
    top_count, tokens = chosen.shape
    pairs = order.shape[1]
    shift = top_count.bit_length() - 1
    if top_count != 1 << shift:
        raise ValueError("top count")
    owner = jnp.where(
        (order >> shift) == lax.broadcasted_iota(jnp.int32, (tokens, pairs), 0), 1.0, 0.0
    ).astype(bf16)
    which = (order & (top_count - 1)) == lax.broadcasted_iota(jnp.int32, (top_count, pairs), 0)
    turns = lax.broadcasted_iota(jnp.int32, (top_count, pairs), 1)
    high, low = (
        nt(jnp.where(which, part.astype(f32), 0.0).astype(bf16), owner)
        for part in (turns >> 8, turns & 255)
    )
    turn_of = high * 256.0 + low
    far = float(2 * pairs)
    ids = lax.broadcasted_iota(jnp.int32, (128, tokens), 0)
    turn_row = jnp.full((128, tokens), far, f32)
    for k in range(top_count):
        turn_row = jnp.where(chosen[k : k + 1, :] == ids, turn_of[k : k + 1, :], turn_row)
    turn_at = turn_row.T
    for e in range(experts_all):
        row = turn_row[e : e + 1, :]
        rank = jnp.sum(jnp.where(turn_at[:, e : e + 1] < row, 1.0, 0.0), axis=0, keepdims=True)
        yield jnp.where((row < far) & (rank < capacity), rank, -1.0)


def front_kernel(sizes, capacity, defs, *refs):
    r = named(defs, refs)
    ne, nz, nd = sizes
    ex, me = lax.axis_index("expert"), lax.axis_index("context")
    tokens, width = r.tokens.shape
    kv_width = r.w_key.shape[1]
    slices = kv_width // 128
    quarter = HEAD_DIM // 2

    barrier = pltpu.get_barrier_semaphore()
    for step in range(1, ne):
        pl.semaphore_signal(
            barrier, inc=1, device_id={"expert": lax.rem(ex + step, ne)}, device_id_type=MESH
        )

    @pl.when(me > 0)
    def _():
        pl.semaphore_signal(barrier, inc=1, device_id={"context": me - 1}, device_id_type=MESH)

    @pl.when(me < nz - 1)
    def _():
        pl.semaphore_signal(barrier, inc=1, device_id={"context": me + 1}, device_id_type=MESH)

    loads = [
        pltpu.make_async_copy(src, dst, r.load_sem.at[i])
        for i, (src, dst) in enumerate(
            (
                (r.w_key, r.w_key_v),
                (r.w_value, r.w_value_v),
                (r.w_query, r.w_query_v),
                (r.w_out, r.w_out_v),
                (r.grad_top, r.grad_all.at[ex]),
            )
        )
    ]
    for copy in r.loads + loads:
        copy.start()
    pl.semaphore_wait(
        barrier, ne - 1 + jnp.where(me > 0, 1, 0) + jnp.where(me < nz - 1, 1, 0)
    )

    def spread(kind, step):
        src = (r.grad_top, r.tables_s, r.second_s)[kind]
        dst = (r.grad_all, r.tables_all, r.rows_all)[kind]
        return pltpu.make_async_remote_copy(
            src_ref=src,
            dst_ref=dst.at[ex],
            send_sem=r.spread_send.at[kind, step],
            recv_sem=r.spread_recv.at[kind, step],
            device_id={"expert": lax.rem(ex + step, ne)},
            device_id_type=MESH,
        )

    last, helper = nz - 1, nz - 2

    def to(place, src, dst, send, recv):
        return pltpu.make_async_remote_copy(
            src_ref=src,
            dst_ref=dst,
            send_sem=send,
            recv_sem=recv,
            device_id={"context": place},
            device_id_type=MESH,
        )

    def up(j, t):
        at = r.kv_s.at[j, t]
        return to(me + 1, at, at, r.up_send.at[j, t], r.up_recv.at[j, t])

    def up_seg(j):
        at = r.seg_s.at[j]
        return to(me + 1, at, at, r.seg_send.at[j], r.seg_recv.at[j])

    ask = [
        to(helper, src, dst, r.ask_send.at[i], r.ask_recv.at[i])
        for i, (src, dst) in enumerate(
            ((r.q_s, r.q_far_s), (r.seg_s.at[last], r.seg_s.at[last]))
        )
    ]

    def answer(t):
        return [
            to(last, src.at[t], dst.at[t], r.answer_send.at[i, t], r.answer_recv.at[i, t])
            for i, (src, dst) in enumerate(
                ((r.far_head, r.far_head_in), (r.far_lse, r.far_lse_in))
            )
        ]

    for step in range(1, ne):
        spread(0, step).start()

    for copy in r.loads:
        copy.wait()

    values = r.tokens[...].astype(f32)
    inverse = lax.rsqrt(jnp.mean(values * values, axis=-1, keepdims=True) + epsilon)
    first = (values * inverse * r.gains[:1, :].astype(f32)).astype(bf16)
    r.first_s[...] = first
    cos_b, sin_b = r.base[0, pl.ds(me, 1), :], r.base[1, pl.ds(me, 1), :]
    cos_i, sin_i = r.inner[0], r.inner[1]
    cosine = cos_i * cos_b - sin_i * sin_b
    sine = sin_i * cos_b + cos_i * sin_b
    first_lanes = lax.rem(lax.broadcasted_iota(jnp.int32, (tokens, 128), 1), HEAD_DIM) < quarter
    sine = jnp.where(first_lanes, sine, -sine)
    r.turn_s[0] = cosine
    r.turn_s[1] = sine

    def rotate(x):
        swapped = jnp.where(
            first_lanes, pltpu.roll(x, 128 - quarter, 1), pltpu.roll(x, quarter, 1)
        )
        return x * cosine - swapped * sine

    loads[0].wait()
    keys = nn(first, r.w_key_v[...])
    for t in range(slices):
        at = slice(t * 128, (t + 1) * 128)
        r.kv_s[me, t, :, :128] = rotate(keys[:, at]).astype(bf16)
    loads[1].wait()
    vals = nn(first, r.w_value_v[...]).astype(bf16)
    for t in range(slices):
        r.kv_s[me, t, :, 128:] = vals[:, t * 128 : (t + 1) * 128]
    r.seg_s[me] = jnp.broadcast_to(r.seg[...].astype(f32), (8, tokens))

    @pl.when(me < helper)
    def _():
        up_seg(me).start()
        for t in range(slices):
            up(me, t).start()

    loads[2].wait()
    factor = HEAD_DIM ** (-0.5)
    low = lane_half((tokens, 128), 0)
    for t in range(slices):
        two = nn(first, r.w_query_v[:, t * 256 : (t + 1) * 256])
        left, right = rotate(two[:, :128]), rotate(two[:, 128:])
        even = jnp.where(low, left, pltpu.roll(right, HEAD_DIM, 1))
        odd = jnp.where(low, pltpu.roll(left, HEAD_DIM, 1), right)
        r.q_s[t, :tokens, :] = (even * factor).astype(bf16)
        r.q_s[t, tokens:, :] = (odd * factor).astype(bf16)

    @pl.when(me == last)
    def _():
        for copy in ask:
            copy.start()

    experts_all = r.tables_s.shape[1]
    for e, row in enumerate(slot_table(r.chosen[...], r.order[...], experts_all, capacity)):
        r.tables_s[0, e : e + 1, :] = row

    for ref in (r.acc, r.total, r.far_acc, r.far_total):
        ref[...] = jnp.zeros_like(ref)
    for ref in (r.top, r.far_top):
        ref[...] = jnp.full_like(ref, -3e38)

    def attend(j, t, queries, acc, top, total, bias):
        keys = r.kv_s[j, t, :, :128]
        vals = r.kv_s[j, t, :, 128:]
        for half in (0, 1):
            keep = lane_half((tokens, 128), half)
            zero = jnp.zeros_like(keys)
            scores = nt(jnp.where(keep, keys, zero), queries[t]) + jnp.concatenate(
                [bias[...]] * 2, axis=1
            )
            old = top[t, half : half + 1, :]
            new = jnp.maximum(old, jnp.max(scores, axis=0, keepdims=True))
            scale = jnp.exp(old - new)
            soft = jnp.exp(scores - new)
            top[t, half : half + 1, :] = new
            total[t, half : half + 1, :] = total[t, half : half + 1, :] * scale + jnp.sum(
                soft, axis=0, keepdims=True
            )
            mixed = tn(jnp.where(keep, vals, zero), soft.astype(bf16))
            a, b = half * HEAD_DIM, (half + 1) * HEAD_DIM
            acc[t, a:b, :] = acc[t, a:b, :] * scale + mixed[a:b]

    def own_slice(j, t):
        attend(j, t, r.q_s, r.acc, r.top, r.total, r.bias)

    def far_slice(j, t):
        attend(j, t, r.q_far_s, r.far_acc, r.far_top, r.far_total, r.far_bias)

    r.bias[...] = mask_bias(r.seg_s, me, me, tokens)

    @pl.loop(0, slices)
    def _(t):
        own_slice(me, t)

    @pl.when(me == helper)
    def _():
        for copy in ask:
            copy.wait_recv()
        r.far_bias[...] = mask_bias(r.seg_s, helper, last, tokens)

        @pl.loop(0, slices)
        def _(t):
            far_slice(helper, t)

    for step in range(1, nz - 1):
        j = me - step

        @pl.when((j >= 0) & (me < last))
        def _():
            up_seg(j).wait_recv()

            @pl.when(me < helper)
            def _():
                up_seg(j).start()

            r.bias[...] = mask_bias(r.seg_s, j, me, tokens)

            @pl.when(me == helper)
            def _():
                r.far_bias[...] = mask_bias(r.seg_s, j, last, tokens)

            @pl.loop(0, slices)
            def _(t):
                up(j, t).wait_recv()

                @pl.when(me < helper)
                def _():
                    up(j, t).start()

                @pl.when(me == helper)
                def _():
                    far_slice(j, t)
                    if step == nz - 2:
                        for half in (0, 1):
                            a, b = half * HEAD_DIM, (half + 1) * HEAD_DIM
                            r.far_head[t, a:b, :] = (
                                r.far_acc[t, a:b, :] / r.far_total[t, half : half + 1, :]
                            ).astype(bf16)
                        r.far_lse[t] = r.far_top[t] + jnp.log(r.far_total[t])
                        for copy in answer(t):
                            copy.start()

                own_slice(j, t)

    @pl.loop(0, slices)
    def _(t):
        r.lse_s[t] = r.top[t] + jnp.log(r.total[t])
        for half in (0, 1):
            a, b = half * HEAD_DIM, (half + 1) * HEAD_DIM
            r.acc[t, a:b, :] = r.acc[t, a:b, :] / r.total[t, half : half + 1, :]

        @pl.when(me == last)
        def _():
            for copy in answer(t):
                copy.wait_recv()
            near, far = r.lse_s[t], r.far_lse_in[t]
            top = jnp.maximum(near, far)
            both = top + jnp.log(jnp.exp(near - top) + jnp.exp(far - top))
            r.lse_s[t] = both
            near, far = jnp.exp(near - both), jnp.exp(far - both)
            for half in (0, 1):
                a, b = half * HEAD_DIM, (half + 1) * HEAD_DIM
                r.acc[t, a:b, :] = (
                    r.acc[t, a:b, :] * near[half : half + 1]
                    + r.far_head_in[t, a:b, :].astype(f32) * far[half : half + 1]
                )

    for t in range(slices):
        for half in (0, 1):
            a, b = half * HEAD_DIM, (half + 1) * HEAD_DIM
            head = r.acc[t, a:b, :].astype(bf16)
            r.heads_s[2 * t + half] = head
            for ab in (0, 1):
                h = (4 * t + 2 * half + ab) * HEAD_DIM
                r.attn_turned[h : h + HEAD_DIM, :] = head[:, ab * tokens : (ab + 1) * tokens]

    loads[3].wait()
    middle = r.tokens[...].astype(f32) + tn(r.attn_turned[...], r.w_out_v[...])
    r.middle_s[...] = middle
    inverse = lax.rsqrt(jnp.mean(middle * middle, axis=-1, keepdims=True) + epsilon)
    second = (middle * inverse * r.gains[1:, :].astype(f32)).astype(bf16)
    r.second_s[...] = second
    for step in range(1, ne):
        spread(2, step).start()
    logits = nt(r.w_router_turned[...], second)
    grown = jnp.exp(logits - jnp.max(logits, axis=0, keepdims=True))
    r.tables_s[1] = grown / jnp.sum(grown, axis=0, keepdims=True)
    for step in range(1, ne):
        spread(1, step).start()
    stores = [
        pltpu.make_async_copy(src, dst, r.store_sem.at[i])
        for i, (src, dst) in enumerate(
            (
                (r.second_s, r.rows_all.at[ex]),
                (r.tables_s, r.tables_all.at[ex]),
                (r.q_s, r.q),
                (r.q_far_s, r.q_far),
                (r.kv_s, r.kv_all),
                (r.seg_s, r.seg_all),
                (r.lse_s, r.lse),
                (r.heads_s, r.heads),
                (r.middle_s, r.middle),
                (r.second_s, r.second_low),
                (r.first_s, r.first_low),
                (r.turn_s, r.turn),
            )
        )
    ]
    for copy in stores:
        copy.start()
    for copy in stores:
        copy.wait()
    loads[4].wait()
    for kind in range(3):
        for step in range(1, ne):
            spread(kind, step).wait()
    for step in range(nz - 1):
        j = me - step

        @pl.when((j >= 0) & (me < helper))
        def _():
            up_seg(j).wait_send()
            for t in range(slices):
                up(j, t).wait_send()

    @pl.when(me == last)
    def _():
        for copy in ask:
            copy.wait_send()

    @pl.when(me == helper)
    def _():
        for t in range(slices):
            for copy in answer(t):
                copy.wait_send()


def front(sizes, cid, capacity, hbm_ins, vmem_ins):
    ne, nz, nd = sizes
    ins = types.SimpleNamespace(**hbm_ins, **vmem_ins)
    tokens, width = ins.tokens.shape
    kv_width = ins.w_key.shape[1]
    slices, wide = kv_width // 128, 2 * tokens
    experts_all = ins.w_router_turned.shape[0]
    shape = jax.ShapeDtypeStruct
    vmem, dma = pltpu.VMEM, pltpu.SemaphoreType.DMA
    sized = dict(
        q=((slices, wide, 128), bf16),
        q_far=((slices, wide, 128), bf16),
        kv=((nz, slices, tokens, 256), bf16),
        seg=((nz, 8, tokens), f32),
        lse=((slices, 2, wide), f32),
        heads=((2 * slices, HEAD_DIM, wide), bf16),
        middle=((tokens, width), f32),
        second=((tokens, width), bf16),
        first=((tokens, width), bf16),
        turn=((2, tokens, 128), f32),
        tables=((2, experts_all, tokens), f32),
    )
    outs = dict(
        rows_all=shape((ne, tokens, width), bf16),
        grad_all=shape((ne, tokens, width), bf16),
        tables_all=shape((ne, 2, experts_all, tokens), f32),
        q=shape(*sized["q"]),
        q_far=shape(*sized["q"]),
        kv_all=shape(*sized["kv"]),
        seg_all=shape(*sized["seg"]),
        lse=shape(*sized["lse"]),
        heads=shape(*sized["heads"]),
        middle=shape(*sized["middle"]),
        second_low=shape(*sized["second"]),
        first_low=shape(*sized["first"]),
        turn=shape(*sized["turn"]),
    )
    scratch = dict(
        w_query_v=vmem(ins.w_query.shape, bf16),
        w_key_v=vmem(ins.w_key.shape, bf16),
        w_value_v=vmem(ins.w_value.shape, bf16),
        w_out_v=vmem(ins.w_out.shape, bf16),
        attn_turned=vmem((width, tokens), bf16),
        acc=vmem((slices, 128, wide), f32),
        top=vmem((slices, 2, wide), f32),
        total=vmem((slices, 2, wide), f32),
        bias=vmem((tokens, tokens), f32),
        far_acc=vmem((slices, 128, wide), f32),
        far_top=vmem((slices, 2, wide), f32),
        far_total=vmem((slices, 2, wide), f32),
        far_bias=vmem((tokens, tokens), f32),
        far_head=vmem((slices, 128, wide), bf16),
        far_lse=vmem((slices, 2, wide), f32),
        far_head_in=vmem((slices, 128, wide), bf16),
        far_lse_in=vmem((slices, 2, wide), f32),
        load_sem=dma((5,)),
        store_sem=dma((12,)),
        spread_send=dma((3, ne)),
        spread_recv=dma((3, ne)),
        up_send=dma((nz, slices)),
        up_recv=dma((nz, slices)),
        seg_send=dma((nz,)),
        seg_recv=dma((nz,)),
        ask_send=dma((2,)),
        ask_recv=dma((2,)),
        answer_send=dma((2, slices)),
        answer_recv=dma((2, slices)),
        **{k + "_s": vmem(*v) for k, v in sized.items()},
    )
    return call_named(
        functools.partial(front_kernel, sizes, capacity),
        hbm_ins, vmem_ins, outs, scratch, cid, 60 << 20, tuple(outs),
    )


class Line:
    def __init__(self, nz, held, came, send, recv):
        if nz != 4:
            raise ValueError("context")
        self.nz, self.held, self.came, self.send, self.recv = nz, held, came, send, recv
        self.me = lax.axis_index("context")

    @staticmethod
    def scratch(nz, chunks, rows, width):
        return [
            pltpu.VMEM((chunks, nz, rows, width), bf16),
            pltpu.VMEM((chunks, nz, rows, width), bf16),
            pltpu.SemaphoreType.DMA((chunks, nz)),
            pltpu.SemaphoreType.DMA((chunks, nz)),
        ]

    routes = {
        (0, 3): (1, 3),
        (0, 2): (1, 2),
        (0, 1): (1, 0),
        (3, 0): (2, 0),
        (3, 1): (2, 1),
        (3, 2): (2, 3),
        (1, 0): (0, 1),
        (2, 3): (3, 2),
        (1, 3): (3, 1),
        (1, 2): (2, 2),
        (2, 0): (0, 2),
        (2, 1): (1, 1),
    }

    def copy(self, k, place, s):
        target, slot = self.routes[place, s]
        return pltpu.make_async_remote_copy(
            src_ref=self.held.at[k, s],
            dst_ref=self.came.at[k, slot],
            send_sem=self.send.at[k, s],
            recv_sem=self.recv.at[k, slot],
            device_id={"context": target},
            device_id_type=MESH,
        )

    def start(self, k, moves):
        for place in range(self.nz):
            pieces = [s for p, s in moves if p == place]
            if pieces:

                @pl.when(self.me == place)
                def _():
                    for s in pieces:
                        self.copy(k, place, s).start()

    def far_piece(self, place, which):
        return 3 - which if place < 2 else which

    def cross(self, k, which, place):
        self.start(k, [(place, self.far_piece(place, which))])

    def left(self, k, which, place):
        @pl.when(self.me == place)
        def _():
            self.copy(k, place, self.far_piece(place, which)).wait_send()

    def straight(self, k):
        self.start(k, [(1, 0), (2, 3)])

    def ends(self, k, place):
        self.start(k, [(place, 1 if place == 0 else 2)])

    def join(self, k, which, place):
        s = self.far_piece(place, which)

        @pl.when(self.me == place)
        def _():
            self.copy(k, 0 if place == 1 else 3, s).wait_recv()
            add_rows(self.held, (k, s), self.came, (k, s), self.held.shape[2])
            self.copy(k, place, s).start()

    def total(self, k, put):
        for place in range(self.nz):

            @pl.when(self.me == place)
            def _():
                senders = [(p, s) for (p, s), (t, _) in self.routes.items() if t == place == s]
                for p, s in senders:
                    self.copy(k, p, s).wait_recv()
                for at in range(0, self.held.shape[2], 16):
                    rows = slice(at, at + 16)
                    value = self.held[k, place, rows].astype(f32)
                    for move in senders:
                        value = value + self.came[k, self.routes[move][1], rows].astype(f32)
                    put(at, value)
                for s in range(self.nz):
                    if s != place and (place in (1, 2) or abs(s - place) == 1):
                        self.copy(k, place, s).wait_send()


def experts_kernel(sizes, cap, defs, *refs):
    r = named(defs, refs)
    ne, nz, nd = sizes
    ex, dp, ctx = (lax.axis_index(a) for a in ("expert", "dp", "context"))
    local, width, hid = r.w_gate.shape
    tokens = r.rows_all.shape[1]
    gate_rows, down_rows = width // (nz * nd), hid // (nz * nd)
    line = Line(nz, r.held_s, *r.line)

    barrier = pltpu.get_barrier_semaphore()
    for axis, place, size in (("dp", dp, nd), ("context", ctx, nz)):
        for step in range(1, size):
            pl.semaphore_signal(
                barrier, inc=1, device_id={axis: lax.rem(place + step, size)}, device_id_type=MESH
            )

    def weights(e, slot):
        return [
            pltpu.make_async_copy(src, dst, r.weight_sem.at[slot, i])
            for i, (src, dst) in enumerate(
                (
                    (r.w_gate.at[e], r.both.at[slot, :, pl.ds(0, hid)]),
                    (r.w_up.at[e], r.both.at[slot, :, pl.ds(hid, hid)]),
                    (r.w_down.at[e], r.down.at[slot]),
                )
            )
        ]

    for copy in r.loads + weights(0, 0):
        copy.start()
    pl.semaphore_wait(barrier, nd + nz - 2)
    for copy in r.loads:
        copy.wait()

    def cores(k, step):
        other = lax.rem(dp + step, nd)
        return pltpu.make_async_remote_copy(
            src_ref=r.made.at[:, other],
            dst_ref=r.from_dp.at[step - 1, k],
            send_sem=r.dp_send.at[k, step],
            recv_sem=r.dp_recv.at[k, step],
            device_id={"dp": other},
            device_id_type=MESH,
        )

    def keep(k):
        return pltpu.make_async_copy(r.held_s.at[k], r.held.at[k], r.held_sem.at[k])

    def add_cores(k):
        for step in range(1, nd):
            cores(k, step).wait_recv()
            for z in range(nz):
                add_rows(r.held_s, (k, z), r.from_dp, (step - 1, k, z), gate_rows + down_rows)

        @pl.when(k > 0)
        def _():
            keep(k).start()

    row_id = lax.broadcasted_iota(jnp.int32, (cap, tokens), 0).astype(f32)

    @pl.loop(0, local)
    def _(e):
        slot = lax.rem(e, 2)
        own = pl.ds(pl.multiple_of(e * cap, 16), cap)
        for src in range(ne):
            at = pl.ds(src * cap, cap)
            hits = r.tables_all[src, 0, pl.ds(ex * local + e, 1), :] == row_id
            gate_row = r.tables_all[src, 1, pl.ds(ex * local + e, 1), :]
            gate = jnp.sum(jnp.where(hits, gate_row, 0.0), axis=1, keepdims=True)
            low = jnp.where(hits, 1.0, 0.0).astype(bf16)
            r.hits[src, own, :] = low
            r.gate_s[at, :] = jnp.broadcast_to(gate, (cap, 128))
            r.x_s[at, :] = nn(low, r.rows_all[src]).astype(bf16)
            og = nn(low, r.grad_all[src])
            r.og_s[at, :] = og.astype(bf16)
            r.sg_s[at, :] = (og * gate).astype(bf16)
        for copy in weights(e, slot):
            copy.wait()

        @pl.when(e < local - 1)
        def _():
            for copy in weights(e + 1, 1 - slot):
                copy.start()

        pre = nn(r.x_s[...], r.both[slot])

        @pl.when(e > 0)
        def _():
            add_cores(e - 1)

        @pl.when(e == 1)
        def _():
            for place in (0, 3):
                line.cross(0, 0, place)
            line.straight(0)

        @pl.when(e == 2)
        def _():
            for place in (0, 3):
                line.ends(0, place)

        @pl.when(e == 3)
        def _():
            for place in (1, 2):
                line.join(0, 1, place)

        gate_pre, up_pre = pre[:, :hid], pre[:, hid:]
        sig = jax.nn.sigmoid(gate_pre)
        silu = gate_pre * sig
        r.hidden[...] = (silu * up_pre).astype(bf16)
        hidden_back = nt(r.sg_s[...], r.down[slot])
        r.pre_back[:, :hid] = (
            hidden_back * up_pre * sig * (1.0 + gate_pre * (1.0 - sig))
        ).astype(bf16)
        r.pre_back[:, hid:] = (hidden_back * silu).astype(bf16)
        produced = nn(r.hidden[...], r.down[slot])
        pair = jnp.sum(r.og_s[...].astype(f32) * produced, axis=1, keepdims=True)
        weighed = (produced * r.gate_s[:, :1]).astype(bf16)
        for src in range(ne):
            a, b = src * cap, (src + 1) * cap
            r.weighed[src, own, :] = weighed[a:b]
            r.soft_part[src, pl.ds(e, 1), :] = jnp.sum(
                r.hits[src, own, :].astype(f32) * pair[a:b], axis=0, keepdims=True
            )
        back = nt(r.pre_back[...], r.both[slot]).astype(bf16)
        for src in range(ne):
            r.back_rows[src, own, :] = back[src * cap : (src + 1) * cap]

        @pl.when(e == 1)
        def _():
            for place in (0, 3):
                line.cross(0, 1, place)

        @pl.when(e == 2)
        def _():
            for place in (1, 2):
                line.join(0, 0, place)

        @pl.when(e > 0)
        def _():
            for step in range(1, nd):
                cores(e - 1, step).wait_send()

        r.made[:, :, :gate_rows, :] = (
            tn(r.x_s[...], r.pre_back[...]).astype(bf16).reshape(nz, nd, gate_rows, 2 * hid)
        )
        r.made[:, :, gate_rows:, :] = (
            tn(r.hidden[...], r.sg_s[...]).astype(bf16).reshape(nz, nd, down_rows, width)
        )
        for step in range(1, nd):
            cores(e, step).start()
        r.held_s[e] = r.made[:, dp]

    stores = []
    for kind, (rows, out) in enumerate(((r.back_rows, r.back_part), (r.weighed, r.out_part))):
        for src in range(ne):
            r.sums[kind, src] = tn(r.hits[src], rows[src]).astype(bf16)
            stores.append(
                pltpu.make_async_copy(r.sums.at[kind, src], out.at[src], r.store_sem.at[kind, src])
            )
            stores[-1].start()
    add_cores(local - 1)

    def put(at, value):
        r.shard[at : at + 16, :] = value

    for place in (0, 3):
        for which in (0, 1):
            line.left(0, which, place)
    line.total(0, put)
    for step in range(1, nd):
        cores(local - 1, step).wait_send()
    for k in range(1, local):
        keep(k).wait()
    for copy in stores:
        copy.wait()


def experts(sizes, cid, cap, kept, read):
    ne, nz, nd = sizes
    local, width, hid = kept["w_gate"].shape
    tokens = read["rows_all"].shape[1]
    piece = width // (nz * nd) + hid // (nz * nd)
    shape, vmem, dma = jax.ShapeDtypeStruct, pltpu.VMEM, pltpu.SemaphoreType.DMA
    held, *line = Line.scratch(nz, local, piece, width)
    line[0] = vmem((1, nz, piece, width), bf16)
    outs = dict(
        held=shape((local, nz, piece, width), bf16),
        out_part=shape((ne, tokens, width), bf16),
        back_part=shape((ne, tokens, width), bf16),
        soft_part=shape((ne, local, tokens), f32),
        shard=shape((piece, width), f32),
    )
    rows = ne * cap
    scratch = dict(
        both=vmem((2, width, 2 * hid), bf16),
        down=vmem((2, hid, width), bf16),
        x_s=vmem((rows, width), bf16),
        og_s=vmem((rows, width), bf16),
        sg_s=vmem((rows, width), bf16),
        gate_s=vmem((rows, 128), f32),
        hidden=vmem((rows, hid), bf16),
        pre_back=vmem((rows, 2 * hid), bf16),
        hits=vmem((ne, local * cap, tokens), bf16),
        weighed=vmem((ne, local * cap, width), bf16),
        back_rows=vmem((ne, local * cap, width), bf16),
        sums=vmem((2, ne, tokens, width), bf16),
        made=vmem((nz, nd, piece, width), bf16),
        from_dp=vmem((nd - 1, local, nz, piece, width), bf16),
        held_s=held,
        line=line,
        weight_sem=dma((2, 3)),
        dp_send=dma((local, nd)),
        dp_recv=dma((local, nd)),
        held_sem=dma((local,)),
        store_sem=dma((2, ne)),
    )
    return call_named(
        functools.partial(experts_kernel, sizes, cap),
        kept, read, outs, scratch, cid, 62 << 20, ("held", "out_part", "back_part"),
    )


class Spread:
    def __init__(self, sizes, made, from_dp, held, from_ex, line, from_z, send, recv):
        self.sizes, self.made, self.from_dp, self.held = sizes, made, from_dp, held
        self.from_ex, self.line, self.from_z, self.send, self.recv = from_ex, line, from_z, send, recv
        self.places = tuple(lax.axis_index(a) for a in ("dp", "expert", "context"))

    @staticmethod
    def scratch(sizes, rows, width):
        ne, nz, nd = sizes
        most = max(sizes)
        return [
            pltpu.VMEM((nd - 1, ne, nz, rows, width), bf16),
            pltpu.VMEM((ne, nz, rows, width), bf16),
            pltpu.VMEM((ne - 1, nz, rows, width), bf16),
            pltpu.VMEM((nz, rows, width), bf16),
            pltpu.VMEM((nz - 1, rows, width), bf16),
            pltpu.SemaphoreType.DMA((3, most)),
            pltpu.SemaphoreType.DMA((3, most)),
        ]

    def copy(self, stage, step):
        ne, nz, nd = self.sizes
        axis, size = (("dp", nd), ("expert", ne), ("context", nz))[stage]
        other = lax.rem(self.places[stage] + step, size)
        src = (
            self.made.at[:, :, other]
            if stage == 0
            else self.held.at[other] if stage == 1 else self.line.at[other]
        )
        dst = (self.from_dp, self.from_ex, self.from_z)[stage].at[step - 1]
        return pltpu.make_async_remote_copy(
            src_ref=src,
            dst_ref=dst,
            send_sem=self.send.at[stage, step],
            recv_sem=self.recv.at[stage, step],
            device_id={axis: other},
            device_id_type=MESH,
        )

    def others(self, stage):
        ne, nz, nd = self.sizes
        return range(1, (nd, ne, nz)[stage])

    def over_dp(self):
        for step in self.others(0):
            self.copy(0, step).start()

    def made_free(self):
        for step in self.others(0):
            self.copy(0, step).wait_send()

    def over_expert(self):
        ne, nz, _ = self.sizes
        for step in self.others(0):
            self.copy(0, step).wait_recv()

        @pl.loop(0, ne * nz)
        def _(i):
            a = lax.div(i, nz)
            b = i - a * nz
            total = self.made[a, b, self.places[0]].astype(f32)
            for step in self.others(0):
                total = total + self.from_dp[step - 1, a, b].astype(f32)
            self.held[a, b] = total.astype(bf16)

        for step in self.others(1):
            self.copy(1, step).start()

    def over_context(self):
        nz = self.sizes[1]
        for step in self.others(1):
            self.copy(1, step).wait_recv()

        @pl.loop(0, nz)
        def _(b):
            total = self.held[self.places[1], b].astype(f32)
            for step in self.others(1):
                total = total + self.from_ex[step - 1, b].astype(f32)
            self.line[b] = total.astype(bf16)

        for step in self.others(2):
            self.copy(2, step).start()

    def finish(self, out):
        for step in self.others(2):
            self.copy(2, step).wait_recv()
        total = self.line[self.places[2]].astype(f32)
        for step in self.others(2):
            total = total + self.from_z[step - 1].astype(f32)
        out[...] = total
        for stage in (1, 2):
            for step in self.others(stage):
                self.copy(stage, step).wait_send()


def tail_kernel(sizes, defs, *refs):
    r = named(defs, refs)
    ne, nz, nd = sizes
    ex, me, dp = (lax.axis_index(a) for a in ("expert", "context", "dp"))
    tokens, width = r.tokens.shape
    slices = r.kv_all.shape[1]
    kv_width = slices * 128
    group = width // ne
    last, helper = nz - 1, nz - 2

    barrier = pltpu.get_barrier_semaphore()
    for axis, place, size in (("expert", ex, ne), ("context", me, nz), ("dp", dp, nd)):
        for step in range(1, size):
            pl.semaphore_signal(
                barrier, inc=1, device_id={axis: lax.rem(place + step, size)}, device_id_type=MESH
            )
    for copy in r.loads:
        copy.start()
    pl.semaphore_wait(barrier, ne + nz + nd - 3)

    line = Line(nz, *r.line)
    proj = Spread(sizes, r.made, *r.proj)
    query = Spread(sizes, r.made, *r.query)
    kv = Spread(sizes, r.made, *r.kv)
    small = Spread(sizes, r.small_made, *r.small)

    chunks = range(r.held_in.shape[0] - 1)
    held_copies = [
        pltpu.make_async_copy(r.held_in.at[k + 1], line.held.at[k], r.held_sem.at[k])
        for k in chunks
    ]
    for copy in held_copies:
        copy.start()

    def rows_copy(kind, step):
        other = lax.rem(ex + step, ne)
        return pltpu.make_async_remote_copy(
            src_ref=(r.back_in, r.out_in, r.soft_in)[kind].at[other],
            dst_ref=r.soft_all.at[ex] if kind == 2 else (r.back_came, r.out_came)[kind].at[step - 1],
            send_sem=r.rows_send.at[kind, step],
            recv_sem=r.rows_recv.at[kind, step],
            device_id={"expert": other},
            device_id_type=MESH,
        )

    for kind in (2, 0):
        for step in range(1, ne):
            rows_copy(kind, step).start()
    loads = [
        pltpu.make_async_copy(r.back_in.at[ex], r.back_own, r.load_sem.at[0]),
        pltpu.make_async_copy(r.soft_in.at[ex], r.soft_all.at[ex], r.load_sem.at[1]),
        pltpu.make_async_copy(r.out_in.at[ex], r.out_own, r.load_sem.at[2]),
        pltpu.make_async_copy(r.w_out, r.w_out_v, r.load_sem.at[3]),
        pltpu.make_async_copy(r.w_query, r.w_query_v, r.load_sem.at[4]),
        pltpu.make_async_copy(r.w_key, r.w_key_v, r.load_sem.at[5]),
        pltpu.make_async_copy(r.w_value, r.w_value_v, r.load_sem.at[6]),
        pltpu.make_async_copy(r.tables_all.at[ex], r.tables_own, r.load_sem.at[7]),
    ]
    for copy in loads:
        copy.start()
    for k in chunks:
        held_copies[k].wait()
        if k == 0:
            for place in (0, 3):
                line.cross(0, 0, place)
                line.cross(0, 1, place)
        line.straight(k)
    for copy in r.loads + loads:
        copy.wait()
    for t in range(2 * slices):
        for ab in (0, 1):
            h = 2 * t + ab
            r.attn_turned[h * HEAD_DIM : (h + 1) * HEAD_DIM, :] = r.heads[
                t, :, ab * tokens : (ab + 1) * tokens
            ]

    for place in (0, 3):
        for which in (0, 1):
            line.left(0, which, place)
        line.cross(1, 0, place)
    line.cross(1, 1, 0)
    for kind in (2, 0):
        for step in range(1, ne):
            rows_copy(kind, step).wait_recv()
    for which in (0, 1):
        line.join(0, which, 2)
    for step in range(1, ne):
        rows_copy(1, step).start()
    soft_back = jnp.concatenate([r.soft_all[i] for i in range(ne)], axis=0)
    router_soft = r.tables_own[1]
    logit_back = (
        router_soft * (soft_back - jnp.sum(router_soft * soft_back, axis=0, keepdims=True))
    ).astype(bf16)
    second_back = r.back_own[...].astype(f32) + tn(logit_back, r.w_router_turned[...])
    for step in range(1, ne):
        second_back = second_back + r.back_came[step - 1].astype(f32)
    middle = r.middle[...]
    inverse = lax.rsqrt(jnp.mean(middle * middle, axis=-1, keepdims=True) + epsilon)
    normed = middle * inverse
    scaled = second_back * r.gains[1:, :].astype(f32)
    moe_gain_grad = jnp.sum(second_back * normed, axis=0, keepdims=True)
    middle_grad = r.grad_top[...].astype(f32) + inverse * (
        scaled - normed * jnp.mean(scaled * normed, axis=-1, keepdims=True)
    )
    r.middle_grad[...] = middle_grad
    r.branch[...] = middle_grad.astype(bf16)
    experts_all = logit_back.shape[0]
    r.small_rows[...] = jnp.zeros_like(r.small_rows)
    r.small_rows[:experts_all, :] = nn(logit_back, r.second_low[...])
    r.small_rows[experts_all : experts_all + 1, :] = moe_gain_grad

    def to(place, src, dst, send, recv):
        return pltpu.make_async_remote_copy(
            src_ref=src,
            dst_ref=dst,
            send_sem=send,
            recv_sem=recv,
            device_id={"context": place},
            device_id_type=MESH,
        )

    def ask(t):
        return [
            to(helper, src.at[t], dst.at[t], r.ask_send.at[i, t], r.ask_recv.at[i, t])
            for i, (src, dst) in enumerate(((r.do, r.far_do), (r.stats, r.far_stats)))
        ]

    def answer(t):
        return to(
            last, r.far_dq_low.at[t], r.dq_came.at[t], r.answer_send.at[t], r.answer_recv.at[t]
        )

    @pl.loop(0, slices)
    def _(t):
        at = pl.ds(pl.multiple_of(t * 256, 256), 256)
        turned = nt(r.w_out_v[at, :], r.branch[...]).astype(bf16)
        r.stats[t, 0] = r.lse[t]
        for half in (0, 1):
            a, b = half * HEAD_DIM, (half + 1) * HEAD_DIM
            for ab in (0, 1):
                c = (2 * half + ab) * HEAD_DIM
                r.do[t, a:b, ab * tokens : (ab + 1) * tokens] = turned[c : c + HEAD_DIM]
            r.stats[t, 1, half : half + 1, :] = jnp.sum(
                r.do[t, a:b, :].astype(f32) * r.heads[2 * t + half].astype(f32),
                axis=0,
                keepdims=True,
            )

        @pl.when(me == last)
        def _():
            for copy in ask(t):
                copy.start()

    @pl.loop(0, ne)
    def _(g):
        at = pl.ds(pl.multiple_of(g * group, group), group)
        grad = nn(r.attn_turned[at, :], r.branch[...])
        r.made[g] = grad.reshape((nz, nd, group // (nz * nd), width)).astype(bf16)

    proj.over_dp()
    for which in (0, 1):
        line.join(0, which, 1)
    for which in (0, 1):
        line.left(1, which, 0)
        line.cross(2, which, 0)
    proj.over_expert()

    r.dq[...] = jnp.zeros_like(r.dq)
    r.far_dq[...] = jnp.zeros_like(r.far_dq)

    def mine(j):
        return me == last if j == last else (j <= me) & (me < last)

    for j in range(nz):

        @pl.when(mine(j))
        def _():
            r.bias[j] = mask_bias(r.seg_all, j, me, tokens)

    @pl.when(me == helper)
    def _():
        for j in range(last):
            r.far_bias[j] = mask_bias(r.seg_all, j, last, tokens)

    def back_slice(j, t, queries, do, stats, dq, bias):
        keys = r.kv_all[j, t, :, :128]
        vals = r.kv_all[j, t, :, 128:]
        dks, dvs = [], []
        for half in (0, 1):
            keep = lane_half((tokens, 128), half)
            zero = jnp.zeros_like(keys)
            keys_half = jnp.where(keep, keys, zero)
            scores = nt(keys_half, queries[t]) + jnp.concatenate([bias[j]] * 2, axis=1)
            soft = jnp.exp(scores - stats[t, 0, half : half + 1, :])
            soft_grad = nn(jnp.where(keep, vals, zero), do[t])
            back = (soft * (soft_grad - stats[t, 1, half : half + 1, :])).astype(bf16)
            dvs.append(nt(soft.astype(bf16), do[t]))
            dks.append(nn(back, queries[t]))
            dq[t] += tn(keys_half, back)
        low = lane_half((tokens, 128), 0)
        return jnp.concatenate(
            [jnp.where(low, dks[0], dks[1]), jnp.where(low, dvs[0], dvs[1])], axis=1
        )

    def give(j, t):
        return to(
            me - 1, r.kv_part.at[j, t], r.kv_came.at[j, t], r.kv_send.at[j, t], r.kv_recv.at[j, t]
        )

    @pl.loop(0, slices)
    def _(t):
        for j in range(nz):

            @pl.when(mine(j))
            def _():
                r.kv_sum[j] = back_slice(j, t, r.q, r.do, r.stats, r.dq, r.bias)

        @pl.when(me == helper)
        def _():
            for copy in ask(t):
                copy.wait_recv()
            for j in range(last):
                r.kv_sum[j] += back_slice(
                    j, t, r.q_far, r.far_do, r.far_stats, r.far_dq, r.far_bias
                )
                if j < helper:
                    r.kv_part[j, t] = r.kv_sum[j].astype(bf16)
                    give(j, t).start()
            r.far_dq_low[t] = r.far_dq[t].astype(bf16)
            answer(t).start()

        for j in range(helper):

            @pl.when((j < me) & (me < helper))
            def _():
                r.kv_part[j, t] = r.kv_sum[j].astype(bf16)

        r.own_kv[t] = r.kv_sum[me]

    line.left(1, 0, 3)
    line.cross(1, 1, 3)
    line.cross(2, 0, 3)

    @pl.when(me == last)
    def _():
        @pl.loop(0, slices)
        def _(t):
            answer(t).wait_recv()
            r.dq[t] += r.dq_came[t].astype(f32)

    quarter = HEAD_DIM // 2
    cos_q, sin_q = (
        jnp.concatenate([r.turn[i].T[:quarter]] * 2, axis=1) * HEAD_DIM ** (-0.5) for i in (0, 1)
    )
    for t in range(slices):
        for half in (0, 1):
            a = half * HEAD_DIM
            first = r.dq[t, a : a + quarter, :]
            second = r.dq[t, a + quarter : a + 2 * quarter, :]
            turned = jnp.concatenate(
                [first * cos_q + second * sin_q, second * cos_q - first * sin_q], axis=0
            )
            pair = jnp.concatenate([turned[:, :tokens], turned[:, tokens:]], axis=0)
            at = (2 * t + half) * 128
            r.back_s[:, at : at + 128] = pair.T.astype(bf16)

    def make(a, b):
        @pl.loop(0, ne)
        def _(g):
            at = pl.ds(pl.multiple_of(g * group, group), group)
            grad = tn(r.first_low[:, at], r.back_s[:, a:b])
            r.made[g] = grad.reshape((nz, nd, group // (nz * nd), b - a)).astype(bf16)

    proj.made_free()
    make(0, width)
    query.over_dp()
    for which in (0, 1):
        line.join(1, which, 1)
    line.join(1, 0, 2)
    for which in (0, 1):
        line.left(2, which, 0)
    for k in chunks:
        line.ends(k, 0)
    line.cross(2, 1, 3)
    line.ends(0, 3)
    query.over_expert()

    @pl.loop(0, slices)
    def _(t):
        for j in range(helper):

            @pl.when((j < me) & (me < helper))
            def _():
                give(j, t).wait_recv()
                r.kv_part[j, t] = (
                    r.kv_part[j, t].astype(f32) + r.kv_came[j, t].astype(f32)
                ).astype(bf16)
                give(j, t).start()

        @pl.when(me < helper)
        def _():
            give(me, t).wait_recv()
            r.own_kv[t] += r.kv_came[me, t].astype(f32)

    for which in (0, 1):
        line.join(2, which, 1)
    for k in chunks[1:]:
        line.ends(k, 3)
    cos_k, sin_k = r.turn[0], r.turn[1]
    first_lanes = lax.rem(lax.broadcasted_iota(jnp.int32, (tokens, 128), 1), HEAD_DIM) < quarter
    for t in range(slices):
        grad = r.own_kv[t, :, :128]
        swapped = jnp.where(
            first_lanes, pltpu.roll(grad, 128 - quarter, 1), pltpu.roll(grad, quarter, 1)
        )
        r.back_s[:, width + t * 128 : width + (t + 1) * 128] = (
            grad * cos_k + swapped * sin_k
        ).astype(bf16)
        at = width + kv_width + t * 128
        r.back_s[:, at : at + 128] = r.own_kv[t, :, 128:].astype(bf16)
    query.made_free()
    make(width, width + 2 * kv_width)
    kv.over_dp()
    proj.over_context()
    line.join(1, 1, 2)
    line.join(2, 0, 2)

    first_back = nt(r.back_s[:, :width], r.w_query_v[...])
    first_back = first_back + nt(r.back_s[:, width : width + kv_width], r.w_key_v[...])
    first_back = first_back + nt(r.back_s[:, width + kv_width :], r.w_value_v[...])
    values = r.tokens[...].astype(f32)
    inverse = lax.rsqrt(jnp.mean(values * values, axis=-1, keepdims=True) + epsilon)
    normed = values * inverse
    scaled = first_back * r.gains[:1, :].astype(f32)
    r.small_rows[experts_all + 1 : experts_all + 2, :] = jnp.sum(
        first_back * normed, axis=0, keepdims=True
    )
    r.input_grad[...] = r.middle_grad[...] + inverse * (
        scaled - normed * jnp.mean(scaled * normed, axis=-1, keepdims=True)
    )
    small_turned = r.small_rows[...].T
    r.small_made[...] = small_turned.reshape(r.small_made.shape).astype(bf16)
    small.over_dp()
    kv.over_expert()
    small.over_expert()
    query.over_context()
    line.join(2, 1, 2)

    for step in range(1, ne):
        rows_copy(1, step).wait_recv()

    @pl.loop(0, tokens // 16)
    def _(i):
        at = pl.ds(pl.multiple_of(i * 16, 16), 16)
        total = r.middle[at, :] + r.out_own[at, :].astype(f32)
        for step in range(1, ne):
            total = total + r.out_came[step - 1, at, :].astype(f32)
        r.layer_out[at, :] = total

    kv.over_context()
    small.over_context()
    kv.made_free()
    small.made_free()
    for group_sum, out in zip((proj, query, kv, small), r.sums_out + [r.small_sum]):
        group_sum.finish(out)
    r.router_out[...] = r.small_sum[:, :experts_all]
    turned = r.small_sum[...].T
    r.gains_out[0] = turned[experts_all + 1 : experts_all + 2]
    r.gains_out[1] = turned[experts_all : experts_all + 1]
    gate_out, up_out, down_out = r.experts_out
    gate_rows, hid = gate_out.shape[1:]

    def put(k, at, value):
        if at < gate_rows:
            gate_out[k, at : at + 16, :] = value[:, :hid]
            up_out[k, at : at + 16, :] = value[:, hid:]
        else:
            down_out[k, at - gate_rows : at - gate_rows + 16, :] = value

    for at in range(0, r.first_shard.shape[0], 16):
        put(0, at, r.first_shard[at : at + 16, :])
    for k, which in ((1, 1), (2, 0), (2, 1)):
        line.left(k, which, 3)
    for k in chunks:
        line.total(k, functools.partial(put, k + 1))
    for kind in range(3):
        for step in range(1, ne):
            rows_copy(kind, step).wait_send()
    for j in range(helper):

        @pl.when((j < me) & (me < last))
        def _():
            for t in range(slices):
                give(j, t).wait_send()

    @pl.when(me == last)
    def _():
        for t in range(slices):
            for copy in ask(t):
                copy.wait_send()

    @pl.when(me == helper)
    def _():
        for t in range(slices):
            answer(t).wait_send()


def tail(sizes, cid, hidden, hbm_ins, vmem_ins):
    ne, nz, nd = sizes
    ins = types.SimpleNamespace(**hbm_ins, **vmem_ins)
    tokens, width = ins.tokens.shape
    slices, wide, _ = ins.q.shape
    chunks, _, piece, _ = ins.held_in.shape
    kv_shape = ins.kv_all.shape[1:]
    kv_cols = slices * 256
    rows = width // (ne * nz * nd)
    gate_rows = width // (nz * nd)
    shard = lambda *shape: jax.ShapeDtypeStruct(shape, f32)
    outs = dict(
        layer_out=shard(tokens, width),
        input_grad=shard(tokens, width),
        sums_out=[shard(rows, c) for c in (width, width, kv_cols)],
        router_out=shard(rows, ins.w_router_turned.shape[0]),
        gains_out=shard(2, 1, rows),
        experts_out=[
            shard(chunks, gate_rows, hidden),
            shard(chunks, gate_rows, hidden),
            shard(chunks, piece - gate_rows, width),
        ],
    )
    dma = pltpu.SemaphoreType.DMA
    vmem = pltpu.VMEM
    scratch = dict(
        back_own=vmem((tokens, width), bf16),
        back_came=vmem((ne - 1, tokens, width), bf16),
        out_own=vmem((tokens, width), bf16),
        out_came=vmem((ne - 1, tokens, width), bf16),
        soft_all=vmem(ins.soft_in.shape, f32),
        w_out_v=vmem(ins.w_out.shape, bf16),
        w_query_v=vmem(ins.w_query.shape, bf16),
        w_key_v=vmem(ins.w_key.shape, bf16),
        w_value_v=vmem(ins.w_value.shape, bf16),
        attn_turned=vmem((width, tokens), bf16),
        middle_grad=vmem((tokens, width), f32),
        branch=vmem((tokens, width), bf16),
        small_rows=vmem((128, width), f32),
        do=vmem((slices, 128, wide), bf16),
        stats=vmem((slices, 2, 2, wide), f32),
        bias=vmem((nz, tokens, tokens), f32),
        dq=vmem((slices, 128, wide), f32),
        dq_came=vmem((slices, 128, wide), bf16),
        far_do=vmem((slices, 128, wide), bf16),
        far_stats=vmem((slices, 2, 2, wide), f32),
        far_bias=vmem((nz - 1, tokens, tokens), f32),
        far_dq=vmem((slices, 128, wide), f32),
        far_dq_low=vmem((slices, 128, wide), bf16),
        kv_sum=vmem((nz, tokens, 256), f32),
        kv_part=vmem((nz - 2,) + kv_shape, bf16),
        kv_came=vmem((nz - 2,) + kv_shape, bf16),
        own_kv=vmem(kv_shape, f32),
        back_s=vmem((tokens, width + kv_cols), bf16),
        made=vmem((ne, nz, nd, rows, width), bf16),
        small_made=vmem((ne, nz, nd, rows, 128), bf16),
        small_sum=vmem((rows, 128), f32),
        rows_send=dma((3, ne)),
        rows_recv=dma((3, ne)),
        load_sem=dma((8,)),
        tables_own=vmem(ins.tables_all.shape[1:], f32),
        held_sem=dma((chunks,)),
        kv_send=dma((nz, slices)),
        kv_recv=dma((nz, slices)),
        ask_send=dma((2, slices)),
        ask_recv=dma((2, slices)),
        answer_send=dma((slices,)),
        answer_recv=dma((slices,)),
        line=Line.scratch(nz, chunks - 1, piece, width),
        proj=Spread.scratch(sizes, rows, width),
        query=Spread.scratch(sizes, rows, width),
        kv=Spread.scratch(sizes, rows, kv_cols),
        small=Spread.scratch(sizes, rows, 128),
    )
    return call_named(
        functools.partial(tail_kernel, sizes), hbm_ins, vmem_ins, outs, scratch, cid, 63 << 20, ()
    )


def deliver_kernel(parts, count, *refs):
    ins, outs, sem, held = refs[:count], refs[count : 2 * count], refs[2 * count], refs[2 * count + 1 :]
    reads = [
        pltpu.make_async_copy(
            ins[i] if part is None else ins[i].at[:, pl.ds(*part)], held[i], sem.at[0, i]
        )
        for i, part in enumerate(parts)
    ]
    writes = [pltpu.make_async_copy(held[i], outs[i], sem.at[1, i]) for i in range(count)]
    for copy in reads:
        copy.start()
    for read, write in zip(reads, writes):
        read.wait()
        write.start()
    for copy in writes:
        copy.wait()


def deliver(moved):
    arrays, parts = zip(*moved)
    hbm = pl.BlockSpec(memory_space=pl.ANY)
    shapes = [a.shape[:-1] + (part[1] if part else a.shape[-1],) for a, part in moved]
    return pl.pallas_call(
        functools.partial(deliver_kernel, parts, len(parts)),
        out_shape=[jax.ShapeDtypeStruct(shape, a.dtype) for shape, a in zip(shapes, arrays)],
        in_specs=[hbm] * len(parts),
        out_specs=[hbm] * len(parts),
        scratch_shapes=[pltpu.SemaphoreType.DMA((2, len(parts)))]
        + [pltpu.VMEM(shape, a.dtype) for shape, a in zip(shapes, arrays)],
        compiler_params=pltpu.CompilerParams(vmem_limit_bytes=60 << 20),
        name="deliver",
    )(*arrays)


def turn_tables(tokens, blocks):
    freq = rope_base ** (-2.0 * np.arange(HEAD_DIM // 2) / HEAD_DIM)
    freq = np.tile(freq, 128 // freq.size)
    inner = np.arange(tokens)[:, None] * freq
    base = tokens * np.arange(blocks)[:, None] * freq
    return tuple(
        jnp.asarray(np.stack([np.cos(a), np.sin(a)]), f32) for a in (inner, base)
    )


def body(
    sizes,
    tokens,
    attn_scale,
    w_query,
    w_key,
    w_value,
    w_out,
    moe_scale,
    w_router,
    w_gate,
    w_up,
    w_down,
    segment_ids,
    expert_choice,
    slot_order,
    out_grad,
):
    ne, nz, nd = sizes
    local_rows = tokens.shape[1]
    kv_width = w_key.shape[1]
    experts_all = w_router.shape[1]
    pair_count = local_rows * expert_choice.shape[2]
    capacity = (pair_count * 9 + 8 * experts_all - 1) // (8 * experts_all)
    inner, base = turn_tables(local_rows, nz)
    w_router_turned = w_router.T
    gains = jnp.stack([attn_scale, moe_scale])

    begun = front(
        sizes,
        1,
        capacity,
        dict(
            w_query=w_query, w_key=w_key, w_value=w_value, w_out=w_out, grad_top=out_grad[0]
        ),
        dict(
            tokens=tokens[0],
            gains=gains,
            w_router_turned=w_router_turned,
            seg=segment_ids,
            chosen=expert_choice[0].T,
            order=slot_order[0],
            inner=inner,
            base=base,
        ),
    )
    mixed = experts(
        sizes,
        2,
        capacity,
        dict(w_gate=w_gate, w_up=w_up, w_down=w_down),
        dict(rows_all=begun.rows_all, grad_all=begun.grad_all, tables_all=begun.tables_all),
    )
    ended = tail(
        sizes,
        3,
        w_gate.shape[2],
        dict(
            held_in=mixed.held,
            back_in=mixed.back_part,
            out_in=mixed.out_part,
            soft_in=mixed.soft_part,
            w_query=w_query,
            w_key=w_key,
            w_value=w_value,
            w_out=w_out,
            tables_all=begun.tables_all,
        ),
        dict(
            q=begun.q,
            q_far=begun.q_far,
            kv_all=begun.kv_all,
            seg_all=begun.seg_all,
            lse=begun.lse,
            heads=begun.heads,
            middle=begun.middle,
            tokens=tokens[0],
            grad_top=out_grad[0],
            second_low=begun.second_low,
            first_low=begun.first_low,
            w_router_turned=w_router_turned,
            gains=gains,
            turn=begun.turn,
            first_shard=mixed.shard,
        ),
    )
    out_shard, query_shard, kv_shard = ended.sums_out
    moved = [
        (ended.layer_out, None),
        (ended.input_grad, None),
        (query_shard, None),
        (kv_shard, (0, kv_width)),
        (kv_shard, (kv_width, kv_width)),
        (out_shard, None),
        *((array, None) for array in ended.experts_out),
    ]
    layer_out, input_grad, *shards = deliver(moved)
    return (
        layer_out[None],
        input_grad[None],
        ended.gains_out[0, 0],
        ended.gains_out[1, 0],
        *shards[:4],
        ended.router_out,
        *shards[4:],
    )


def solution(mesh):
    sizes = (mesh.shape["expert"], mesh.shape["context"], mesh.shape["dp"])
    in_specs = (
        P(("expert", "dp"), "context", None),
        P(),
        P(),
        P(),
        P(),
        P(),
        P(),
        P(),
        P("expert", None, None),
        P("expert", None, None),
        P("expert", None, None),
        P(("expert", "dp"), "context"),
        P(("expert", "dp"), "context", None),
        P(("expert", "dp"), "context", None),
        P(("expert", "dp"), "context", None),
    )
    out_specs = (
        P(("expert", "dp"), "context", None),
        P(("expert", "dp"), "context", None),
        P(("expert", "context", "dp")),
        P(("expert", "context", "dp")),
        P(("expert", "context", "dp"), None),
        P(("expert", "context", "dp"), None),
        P(("expert", "context", "dp"), None),
        P(("expert", "context", "dp"), None),
        P(("expert", "context", "dp"), None),
        P("expert", ("context", "dp"), None),
        P("expert", ("context", "dp"), None),
        P("expert", ("context", "dp"), None),
    )
    return jax.shard_map(
        functools.partial(body, sizes),
        mesh=mesh,
        in_specs=in_specs,
        out_specs=out_specs,
        check_vma=False,
    )
```

```python
import functools
import types

import jax
import jax.numpy as jnp
import numpy as np
from jax import lax
from jax.experimental import pallas as pl
from jax.experimental.pallas import tpu as pltpu
from jax.sharding import PartitionSpec as P

HEAD_DIM = 64
MESH = pl.DeviceIdType.MESH

epsilon = 1e-06
rope_base = 10000.0
negative_large = -1e30
bf16 = jnp.bfloat16
f32 = jnp.float32


def nt(a, b):
    return lax.dot_general(a, b, (((1,), (1,)), ((), ())), preferred_element_type=f32)


def tn(a, b):
    return lax.dot_general(a, b, (((0,), (0,)), ((), ())), preferred_element_type=f32)


def nn(a, b):
    return jnp.dot(a, b, preferred_element_type=f32)


def add_rows(dst, dst_at, src, src_at, rows):
    step = 16

    @pl.loop(0, rows // step)
    def _(i):
        at = pl.ds(pl.multiple_of(i * step, step), step)
        dst[dst_at + (at, slice(None))] = (
            dst[dst_at + (at, slice(None))].astype(f32) + src[src_at + (at, slice(None))].astype(f32)
        ).astype(bf16)


def lane_half(shape, which):
    lanes = lax.broadcasted_iota(jnp.int32, shape, 1)
    return (lanes >= HEAD_DIM) if which else (lanes < HEAD_DIM)


def column_of(row):
    n = row.shape[1]
    rows = lax.broadcasted_iota(jnp.int32, (n, n), 0)
    cols = lax.broadcasted_iota(jnp.int32, (n, n), 1)
    return jnp.sum(jnp.where(rows == cols, row, 0.0), axis=1, keepdims=True)


def mask_bias(seg_ref, block, me, tokens):
    key_seg = column_of(seg_ref[block, :1, :])
    same = key_seg == seg_ref[me, :1, :]
    rows = lax.broadcasted_iota(jnp.int32, (tokens, tokens), 0) + block * tokens
    cols = lax.broadcasted_iota(jnp.int32, (tokens, tokens), 1) + me * tokens
    return jnp.where(same & (rows <= cols), 0.0, negative_large)


def named(defs, refs):
    counts = [d.num_leaves for d in defs]
    at = [sum(counts[:i]) for i in range(len(counts) + 1)]
    trees = [jax.tree.unflatten(d, refs[at[i] : at[i + 1]]) for i, d in enumerate(defs)]
    r = types.SimpleNamespace(**{k: v for tree in trees for k, v in tree.items()})
    read, (copies, sem) = trees[1], trees[3]["read"]
    r.loads = [
        pltpu.make_async_copy(read[k], copies[k], sem.at[i]) for i, k in enumerate(sorted(read))
    ]
    for k in read:
        setattr(r, k, copies[k])
    return r


def call_named(kernel, kept, read, outs, scratch, cid, limit, kept_outs):
    vm = pl.BlockSpec(memory_space=pltpu.VMEM)
    hbm = pl.BlockSpec(memory_space=pl.ANY)
    scratch["read"] = (
        {k: pltpu.VMEM(v.shape, v.dtype) for k, v in read.items()},
        pltpu.SemaphoreType.DMA((len(read),)),
    )
    flats, defs = zip(*(jax.tree.flatten(t) for t in (kept, read, outs, scratch)))
    out_specs = jax.tree.leaves(
        {k: jax.tree.map(lambda _: hbm if k in kept_outs else vm, v) for k, v in outs.items()}
    )
    results = pl.pallas_call(
        functools.partial(kernel, defs),
        out_shape=tuple(flats[2]),
        in_specs=[hbm] * (len(flats[0]) + len(flats[1])),
        out_specs=tuple(out_specs),
        scratch_shapes=flats[3],
        compiler_params=pltpu.CompilerParams(
            collective_id=cid, has_side_effects=True, vmem_limit_bytes=limit
        ),
        name=kernel.func.__name__,
    )(*flats[0], *flats[1])
    return types.SimpleNamespace(**jax.tree.unflatten(defs[2], results))


def slot_table(chosen, order, experts_all, capacity):
    top_count, tokens = chosen.shape
    pairs = order.shape[1]
    shift = top_count.bit_length() - 1
    if top_count != 1 << shift:
        raise ValueError("top count")
    owner = jnp.where(
        (order >> shift) == lax.broadcasted_iota(jnp.int32, (tokens, pairs), 0), 1.0, 0.0
    ).astype(bf16)
    which = (order & (top_count - 1)) == lax.broadcasted_iota(jnp.int32, (top_count, pairs), 0)
    turns = lax.broadcasted_iota(jnp.int32, (top_count, pairs), 1)
    high, low = (
        nt(jnp.where(which, part.astype(f32), 0.0).astype(bf16), owner)
        for part in (turns >> 8, turns & 255)
    )
    turn_of = high * 256.0 + low
    far = float(2 * pairs)
    ids = lax.broadcasted_iota(jnp.int32, (128, tokens), 0)
    turn_row = jnp.full((128, tokens), far, f32)
    for k in range(top_count):
        turn_row = jnp.where(chosen[k : k + 1, :] == ids, turn_of[k : k + 1, :], turn_row)
    turn_at = turn_row.T
    for e in range(experts_all):
        row = turn_row[e : e + 1, :]
        rank = jnp.sum(jnp.where(turn_at[:, e : e + 1] < row, 1.0, 0.0), axis=0, keepdims=True)
        yield jnp.where((row < far) & (rank < capacity), rank, -1.0)


def partners(ex, ne):
    if ne != 4:
        raise ValueError("expert")
    return ex + 1 - 2 * lax.rem(ex, 2), lax.rem(ex + 2, 4)


def front_kernel(sizes, capacity, defs, *refs):
    r = named(defs, refs)
    ne, nz, nd = sizes
    ex, me = lax.axis_index("expert"), lax.axis_index("context")
    tokens, width = r.tokens.shape
    kv_width = r.w_key.shape[1]
    slices = kv_width // 128
    quarter = HEAD_DIM // 2

    barrier = pltpu.get_barrier_semaphore()
    for step in range(1, ne):
        pl.semaphore_signal(
            barrier, inc=1, device_id={"expert": lax.rem(ex + step, ne)}, device_id_type=MESH
        )

    @pl.when(me > 0)
    def _():
        pl.semaphore_signal(barrier, inc=1, device_id={"context": me - 1}, device_id_type=MESH)

    @pl.when(me < nz - 1)
    def _():
        pl.semaphore_signal(barrier, inc=1, device_id={"context": me + 1}, device_id_type=MESH)

    loads = [
        pltpu.make_async_copy(src, dst, r.load_sem.at[i])
        for i, (src, dst) in enumerate(
            (
                (r.w_key, r.w_key_v),
                (r.w_value, r.w_value_v),
                (r.w_query, r.w_query_v),
                (r.w_out, r.w_out_v),
                (r.grad_top, r.grad_all.at[ex]),
            )
        )
    ]
    for copy in r.loads + loads:
        copy.start()
    pl.semaphore_wait(
        barrier, ne - 1 + jnp.where(me > 0, 1, 0) + jnp.where(me < nz - 1, 1, 0)
    )

    def spread(kind, step):
        src = (r.grad_top, r.tables_s)[kind]
        dst = (r.grad_all, r.tables_all)[kind]
        return pltpu.make_async_remote_copy(
            src_ref=src,
            dst_ref=dst.at[ex],
            send_sem=r.spread_send.at[kind, step],
            recv_sem=r.spread_recv.at[kind, step],
            device_id={"expert": lax.rem(ex + step, ne)},
            device_id_type=MESH,
        )

    pair = partners(ex, ne)
    halves = (pl.ds(0, tokens // 2), pl.ds(tokens // 2, tokens // 2))

    def hand(i, half, onward):
        at = halves[half]
        src = r.rows_all.at[pair[1 - i], at] if onward else r.second_s.at[at]
        dst = r.rows_all.at[pair[1 - i] if onward else ex, at]
        return pltpu.make_async_remote_copy(
            src_ref=src,
            dst_ref=dst,
            send_sem=r.hand_send.at[i, half, int(onward)],
            recv_sem=r.hand_recv.at[i, half, int(onward)],
            device_id={"expert": pair[i]},
            device_id_type=MESH,
        )

    last, helper = nz - 1, nz - 2

    def to(place, src, dst, send, recv):
        return pltpu.make_async_remote_copy(
            src_ref=src,
            dst_ref=dst,
            send_sem=send,
            recv_sem=recv,
            device_id={"context": place},
            device_id_type=MESH,
        )

    def up(j, t):
        at = r.kv_s.at[j, t]
        return to(me + 1, at, at, r.up_send.at[j, t], r.up_recv.at[j, t])

    def up_seg(j):
        at = r.seg_s.at[j]
        return to(me + 1, at, at, r.seg_send.at[j], r.seg_recv.at[j])

    ask = [
        to(helper, src, dst, r.ask_send.at[i], r.ask_recv.at[i])
        for i, (src, dst) in enumerate(
            ((r.q_s, r.q_far_s), (r.seg_s.at[last], r.seg_s.at[last]))
        )
    ]

    def answer(t):
        return [
            to(last, src.at[t], dst.at[t], r.answer_send.at[i, t], r.answer_recv.at[i, t])
            for i, (src, dst) in enumerate(
                ((r.far_head, r.far_head_in), (r.far_lse, r.far_lse_in))
            )
        ]

    for step in range(1, ne):
        spread(0, step).start()

    for copy in r.loads:
        copy.wait()

    values = r.tokens[...].astype(f32)
    inverse = lax.rsqrt(jnp.mean(values * values, axis=-1, keepdims=True) + epsilon)
    first = (values * inverse * r.gains[:1, :].astype(f32)).astype(bf16)
    r.first_s[...] = first
    cos_b, sin_b = r.base[0, pl.ds(me, 1), :], r.base[1, pl.ds(me, 1), :]
    cos_i, sin_i = r.inner[0], r.inner[1]
    cosine = cos_i * cos_b - sin_i * sin_b
    sine = sin_i * cos_b + cos_i * sin_b
    first_lanes = lax.rem(lax.broadcasted_iota(jnp.int32, (tokens, 128), 1), HEAD_DIM) < quarter
    sine = jnp.where(first_lanes, sine, -sine)
    r.turn_s[0] = cosine
    r.turn_s[1] = sine

    def rotate(x):
        swapped = jnp.where(
            first_lanes, pltpu.roll(x, 128 - quarter, 1), pltpu.roll(x, quarter, 1)
        )
        return x * cosine - swapped * sine

    loads[0].wait()
    keys = nn(first, r.w_key_v[...])
    for t in range(slices):
        at = slice(t * 128, (t + 1) * 128)
        r.kv_s[me, t, :, :128] = rotate(keys[:, at]).astype(bf16)
    loads[1].wait()
    vals = nn(first, r.w_value_v[...]).astype(bf16)
    for t in range(slices):
        r.kv_s[me, t, :, 128:] = vals[:, t * 128 : (t + 1) * 128]
    r.seg_s[me] = jnp.broadcast_to(r.seg[...].astype(f32), (8, tokens))

    @pl.when(me < helper)
    def _():
        up_seg(me).start()
        for t in range(slices):
            up(me, t).start()

    loads[2].wait()
    factor = HEAD_DIM ** (-0.5)
    low = lane_half((tokens, 128), 0)
    for t in range(slices):
        two = nn(first, r.w_query_v[:, t * 256 : (t + 1) * 256])
        left, right = rotate(two[:, :128]), rotate(two[:, 128:])
        even = jnp.where(low, left, pltpu.roll(right, HEAD_DIM, 1))
        odd = jnp.where(low, pltpu.roll(left, HEAD_DIM, 1), right)
        r.q_s[t, :tokens, :] = (even * factor).astype(bf16)
        r.q_s[t, tokens:, :] = (odd * factor).astype(bf16)

    @pl.when(me == last)
    def _():
        for copy in ask:
            copy.start()

    experts_all = r.tables_s.shape[1]
    for e, row in enumerate(slot_table(r.chosen[...], r.order[...], experts_all, capacity)):
        r.tables_s[0, e : e + 1, :] = row

    for ref in (r.acc, r.total, r.far_acc, r.far_total):
        ref[...] = jnp.zeros_like(ref)
    for ref in (r.top, r.far_top):
        ref[...] = jnp.full_like(ref, -3e38)

    def attend(j, t, queries, acc, top, total, bias):
        keys = r.kv_s[j, t, :, :128]
        vals = r.kv_s[j, t, :, 128:]
        for half in (0, 1):
            keep = lane_half((tokens, 128), half)
            zero = jnp.zeros_like(keys)
            scores = nt(jnp.where(keep, keys, zero), queries[t]) + jnp.concatenate(
                [bias[...]] * 2, axis=1
            )
            old = top[t, half : half + 1, :]
            new = jnp.maximum(old, jnp.max(scores, axis=0, keepdims=True))
            scale = jnp.exp(old - new)
            soft = jnp.exp(scores - new)
            top[t, half : half + 1, :] = new
            total[t, half : half + 1, :] = total[t, half : half + 1, :] * scale + jnp.sum(
                soft, axis=0, keepdims=True
            )
            mixed = tn(jnp.where(keep, vals, zero), soft.astype(bf16))
            a, b = half * HEAD_DIM, (half + 1) * HEAD_DIM
            acc[t, a:b, :] = acc[t, a:b, :] * scale + mixed[a:b]

    def own_slice(j, t):
        attend(j, t, r.q_s, r.acc, r.top, r.total, r.bias)

    def far_slice(j, t):
        attend(j, t, r.q_far_s, r.far_acc, r.far_top, r.far_total, r.far_bias)

    r.bias[...] = mask_bias(r.seg_s, me, me, tokens)

    @pl.loop(0, slices)
    def _(t):
        own_slice(me, t)

    @pl.when(me == helper)
    def _():
        for copy in ask:
            copy.wait_recv()
        r.far_bias[...] = mask_bias(r.seg_s, helper, last, tokens)

        @pl.loop(0, slices)
        def _(t):
            far_slice(helper, t)

    for step in range(1, nz - 1):
        j = me - step

        @pl.when((j >= 0) & (me < last))
        def _():
            up_seg(j).wait_recv()

            @pl.when(me < helper)
            def _():
                up_seg(j).start()

            r.bias[...] = mask_bias(r.seg_s, j, me, tokens)

            @pl.when(me == helper)
            def _():
                r.far_bias[...] = mask_bias(r.seg_s, j, last, tokens)

            @pl.loop(0, slices)
            def _(t):
                up(j, t).wait_recv()

                @pl.when(me < helper)
                def _():
                    up(j, t).start()

                @pl.when(me == helper)
                def _():
                    far_slice(j, t)
                    if step == nz - 2:
                        for half in (0, 1):
                            a, b = half * HEAD_DIM, (half + 1) * HEAD_DIM
                            r.far_head[t, a:b, :] = (
                                r.far_acc[t, a:b, :] / r.far_total[t, half : half + 1, :]
                            ).astype(bf16)
                        r.far_lse[t] = r.far_top[t] + jnp.log(r.far_total[t])
                        for copy in answer(t):
                            copy.start()

                own_slice(j, t)

    @pl.loop(0, slices)
    def _(t):
        r.lse_s[t] = r.top[t] + jnp.log(r.total[t])
        for half in (0, 1):
            a, b = half * HEAD_DIM, (half + 1) * HEAD_DIM
            r.acc[t, a:b, :] = r.acc[t, a:b, :] / r.total[t, half : half + 1, :]

        @pl.when(me == last)
        def _():
            for copy in answer(t):
                copy.wait_recv()
            near, far = r.lse_s[t], r.far_lse_in[t]
            top = jnp.maximum(near, far)
            both = top + jnp.log(jnp.exp(near - top) + jnp.exp(far - top))
            r.lse_s[t] = both
            near, far = jnp.exp(near - both), jnp.exp(far - both)
            for half in (0, 1):
                a, b = half * HEAD_DIM, (half + 1) * HEAD_DIM
                r.acc[t, a:b, :] = (
                    r.acc[t, a:b, :] * near[half : half + 1]
                    + r.far_head_in[t, a:b, :].astype(f32) * far[half : half + 1]
                )

    for t in range(slices):
        for half in (0, 1):
            a, b = half * HEAD_DIM, (half + 1) * HEAD_DIM
            head = r.acc[t, a:b, :].astype(bf16)
            r.heads_s[2 * t + half] = head
            for ab in (0, 1):
                h = (4 * t + 2 * half + ab) * HEAD_DIM
                r.attn_turned[h : h + HEAD_DIM, :] = head[:, ab * tokens : (ab + 1) * tokens]

    loads[3].wait()
    middle = r.tokens[...].astype(f32) + tn(r.attn_turned[...], r.w_out_v[...])
    r.middle_s[...] = middle
    inverse = lax.rsqrt(jnp.mean(middle * middle, axis=-1, keepdims=True) + epsilon)
    second = (middle * inverse * r.gains[1:, :].astype(f32)).astype(bf16)
    r.second_s[...] = second
    for i, half in ((0, 0), (1, 1), (0, 1), (1, 0)):
        hand(i, half, False).start()
    logits = nt(r.w_router_turned[...], second)
    grown = jnp.exp(logits - jnp.max(logits, axis=0, keepdims=True))
    r.tables_s[1] = grown / jnp.sum(grown, axis=0, keepdims=True)
    for step in range(1, ne):
        spread(1, step).start()
    stores = [
        pltpu.make_async_copy(src, dst, r.store_sem.at[i])
        for i, (src, dst) in enumerate(
            (
                (r.second_s, r.rows_all.at[ex]),
                (r.tables_s, r.tables_all.at[ex]),
                (r.q_s, r.q),
                (r.q_far_s, r.q_far),
                (r.kv_s, r.kv_all),
                (r.seg_s, r.seg_all),
                (r.lse_s, r.lse),
                (r.heads_s, r.heads),
                (r.middle_s, r.middle),
                (r.second_s, r.second_low),
                (r.first_s, r.first_low),
                (r.turn_s, r.turn),
            )
        )
    ]
    for copy in stores:
        copy.start()
    for copy in stores:
        copy.wait()
    for i in (0, 1):
        hand(i, i, False).wait_recv()
        hand(1 - i, i, True).start()
    loads[4].wait()
    for kind in range(2):
        for step in range(1, ne):
            spread(kind, step).wait()
    for i in (0, 1):
        hand(i, i, False).wait_send()
        hand(i, 1 - i, False).wait()
        hand(1 - i, i, True).wait()
    for step in range(nz - 1):
        j = me - step

        @pl.when((j >= 0) & (me < helper))
        def _():
            up_seg(j).wait_send()
            for t in range(slices):
                up(j, t).wait_send()

    @pl.when(me == last)
    def _():
        for copy in ask:
            copy.wait_send()

    @pl.when(me == helper)
    def _():
        for t in range(slices):
            for copy in answer(t):
                copy.wait_send()


def front(sizes, cid, capacity, hbm_ins, vmem_ins):
    ne, nz, nd = sizes
    ins = types.SimpleNamespace(**hbm_ins, **vmem_ins)
    tokens, width = ins.tokens.shape
    kv_width = ins.w_key.shape[1]
    slices, wide = kv_width // 128, 2 * tokens
    experts_all = ins.w_router_turned.shape[0]
    shape = jax.ShapeDtypeStruct
    vmem, dma = pltpu.VMEM, pltpu.SemaphoreType.DMA
    sized = dict(
        q=((slices, wide, 128), bf16),
        q_far=((slices, wide, 128), bf16),
        kv=((nz, slices, tokens, 256), bf16),
        seg=((nz, 8, tokens), f32),
        lse=((slices, 2, wide), f32),
        heads=((2 * slices, HEAD_DIM, wide), bf16),
        middle=((tokens, width), f32),
        second=((tokens, width), bf16),
        first=((tokens, width), bf16),
        turn=((2, tokens, 128), f32),
        tables=((2, experts_all, tokens), f32),
    )
    outs = dict(
        rows_all=shape((ne, tokens, width), bf16),
        grad_all=shape((ne, tokens, width), bf16),
        tables_all=shape((ne, 2, experts_all, tokens), f32),
        q=shape(*sized["q"]),
        q_far=shape(*sized["q"]),
        kv_all=shape(*sized["kv"]),
        seg_all=shape(*sized["seg"]),
        lse=shape(*sized["lse"]),
        heads=shape(*sized["heads"]),
        middle=shape(*sized["middle"]),
        second_low=shape(*sized["second"]),
        first_low=shape(*sized["first"]),
        turn=shape(*sized["turn"]),
    )
    scratch = dict(
        w_query_v=vmem(ins.w_query.shape, bf16),
        w_key_v=vmem(ins.w_key.shape, bf16),
        w_value_v=vmem(ins.w_value.shape, bf16),
        w_out_v=vmem(ins.w_out.shape, bf16),
        attn_turned=vmem((width, tokens), bf16),
        acc=vmem((slices, 128, wide), f32),
        top=vmem((slices, 2, wide), f32),
        total=vmem((slices, 2, wide), f32),
        bias=vmem((tokens, tokens), f32),
        far_acc=vmem((slices, 128, wide), f32),
        far_top=vmem((slices, 2, wide), f32),
        far_total=vmem((slices, 2, wide), f32),
        far_bias=vmem((tokens, tokens), f32),
        far_head=vmem((slices, 128, wide), bf16),
        far_lse=vmem((slices, 2, wide), f32),
        far_head_in=vmem((slices, 128, wide), bf16),
        far_lse_in=vmem((slices, 2, wide), f32),
        load_sem=dma((5,)),
        store_sem=dma((12,)),
        spread_send=dma((2, ne)),
        spread_recv=dma((2, ne)),
        hand_send=dma((2, 2, 2)),
        hand_recv=dma((2, 2, 2)),
        up_send=dma((nz, slices)),
        up_recv=dma((nz, slices)),
        seg_send=dma((nz,)),
        seg_recv=dma((nz,)),
        ask_send=dma((2,)),
        ask_recv=dma((2,)),
        answer_send=dma((2, slices)),
        answer_recv=dma((2, slices)),
        **{k + "_s": vmem(*v) for k, v in sized.items()},
    )
    return call_named(
        functools.partial(front_kernel, sizes, capacity),
        hbm_ins, vmem_ins, outs, scratch, cid, 60 << 20, tuple(outs),
    )


class Line:
    def __init__(self, nz, held, came, send, recv):
        if nz != 4:
            raise ValueError("context")
        self.nz, self.held, self.came, self.send, self.recv = nz, held, came, send, recv
        self.me = lax.axis_index("context")

    @staticmethod
    def scratch(nz, chunks, rows, width):
        return [
            pltpu.VMEM((chunks, nz, rows, width), bf16),
            pltpu.VMEM((chunks, nz, rows, width), bf16),
            pltpu.SemaphoreType.DMA((chunks, nz)),
            pltpu.SemaphoreType.DMA((chunks, nz)),
        ]

    routes = {
        (0, 3): (1, 3),
        (0, 2): (1, 2),
        (0, 1): (1, 0),
        (3, 0): (2, 0),
        (3, 1): (2, 1),
        (3, 2): (2, 3),
        (1, 0): (0, 1),
        (2, 3): (3, 2),
        (1, 3): (3, 1),
        (1, 2): (2, 2),
        (2, 0): (0, 2),
        (2, 1): (1, 1),
    }

    def copy(self, k, place, s):
        target, slot = self.routes[place, s]
        return pltpu.make_async_remote_copy(
            src_ref=self.held.at[k, s],
            dst_ref=self.came.at[k, slot],
            send_sem=self.send.at[k, s],
            recv_sem=self.recv.at[k, slot],
            device_id={"context": target},
            device_id_type=MESH,
        )

    def start(self, k, moves):
        for place in range(self.nz):
            pieces = [s for p, s in moves if p == place]
            if pieces:

                @pl.when(self.me == place)
                def _():
                    for s in pieces:
                        self.copy(k, place, s).start()

    def far_piece(self, place, which):
        return 3 - which if place < 2 else which

    def cross(self, k, which, place):
        self.start(k, [(place, self.far_piece(place, which))])

    def left(self, k, which, place):
        @pl.when(self.me == place)
        def _():
            self.copy(k, place, self.far_piece(place, which)).wait_send()

    def straight(self, k):
        self.start(k, [(1, 0), (2, 3)])

    def ends(self, k, place):
        self.start(k, [(place, 1 if place == 0 else 2)])

    def join(self, k, which, place):
        s = self.far_piece(place, which)

        @pl.when(self.me == place)
        def _():
            self.copy(k, 0 if place == 1 else 3, s).wait_recv()
            add_rows(self.held, (k, s), self.came, (k, s), self.held.shape[2])
            self.copy(k, place, s).start()

    def total(self, k, put):
        for place in range(self.nz):

            @pl.when(self.me == place)
            def _():
                senders = [(p, s) for (p, s), (t, _) in self.routes.items() if t == place == s]
                for p, s in senders:
                    self.copy(k, p, s).wait_recv()
                for at in range(0, self.held.shape[2], 16):
                    rows = slice(at, at + 16)
                    value = self.held[k, place, rows].astype(f32)
                    for move in senders:
                        value = value + self.came[k, self.routes[move][1], rows].astype(f32)
                    put(at, value)
                for s in range(self.nz):
                    if s != place and (place in (1, 2) or abs(s - place) == 1):
                        self.copy(k, place, s).wait_send()


def experts_kernel(sizes, cap, defs, *refs):
    r = named(defs, refs)
    ne, nz, nd = sizes
    ex, dp, ctx = (lax.axis_index(a) for a in ("expert", "dp", "context"))
    local, width, hid = r.w_gate.shape
    tokens = r.rows_all.shape[1]
    gate_rows, down_rows = width // (nz * nd), hid // (nz * nd)
    line = Line(nz, r.held_s, *r.line)

    barrier = pltpu.get_barrier_semaphore()
    for axis, place, size in (("dp", dp, nd), ("context", ctx, nz)):
        for step in range(1, size):
            pl.semaphore_signal(
                barrier, inc=1, device_id={axis: lax.rem(place + step, size)}, device_id_type=MESH
            )

    def weights(e, slot):
        return [
            pltpu.make_async_copy(src, dst, r.weight_sem.at[slot, i])
            for i, (src, dst) in enumerate(
                (
                    (r.w_gate.at[e], r.both.at[slot, :, pl.ds(0, hid)]),
                    (r.w_up.at[e], r.both.at[slot, :, pl.ds(hid, hid)]),
                    (r.w_down.at[e], r.down.at[slot]),
                )
            )
        ]

    for copy in r.loads + weights(0, 0):
        copy.start()
    pl.semaphore_wait(barrier, nd + nz - 2)
    for copy in r.loads:
        copy.wait()

    def cores(k, step):
        other = lax.rem(dp + step, nd)
        return pltpu.make_async_remote_copy(
            src_ref=r.made.at[:, other],
            dst_ref=r.from_dp.at[step - 1, k],
            send_sem=r.dp_send.at[k, step],
            recv_sem=r.dp_recv.at[k, step],
            device_id={"dp": other},
            device_id_type=MESH,
        )

    def keep(k):
        return pltpu.make_async_copy(r.held_s.at[k], r.held.at[k], r.held_sem.at[k])

    def add_cores(k):
        for step in range(1, nd):
            cores(k, step).wait_recv()
            for z in range(nz):
                add_rows(r.held_s, (k, z), r.from_dp, (step - 1, k, z), gate_rows + down_rows)

        @pl.when(k > 0)
        def _():
            keep(k).start()

    row_id = lax.broadcasted_iota(jnp.int32, (cap, tokens), 0).astype(f32)

    @pl.loop(0, local)
    def _(e):
        slot = lax.rem(e, 2)
        own = pl.ds(pl.multiple_of(e * cap, 16), cap)
        for src in range(ne):
            at = pl.ds(src * cap, cap)
            hits = r.tables_all[src, 0, pl.ds(ex * local + e, 1), :] == row_id
            gate_row = r.tables_all[src, 1, pl.ds(ex * local + e, 1), :]
            gate = jnp.sum(jnp.where(hits, gate_row, 0.0), axis=1, keepdims=True)
            low = jnp.where(hits, 1.0, 0.0).astype(bf16)
            r.hits[src, own, :] = low
            r.gate_s[at, :] = jnp.broadcast_to(gate, (cap, 128))
            r.x_s[at, :] = nn(low, r.rows_all[src]).astype(bf16)
            og = nn(low, r.grad_all[src])
            r.og_s[at, :] = og.astype(bf16)
            r.sg_s[at, :] = (og * gate).astype(bf16)
        for copy in weights(e, slot):
            copy.wait()

        @pl.when(e < local - 1)
        def _():
            for copy in weights(e + 1, 1 - slot):
                copy.start()

        pre = nn(r.x_s[...], r.both[slot])

        @pl.when(e > 0)
        def _():
            add_cores(e - 1)

        @pl.when(e == 1)
        def _():
            for place in (0, 3):
                line.cross(0, 0, place)
            line.straight(0)

        @pl.when(e == 2)
        def _():
            for place in (0, 3):
                line.ends(0, place)

        @pl.when(e == 3)
        def _():
            for place in (1, 2):
                line.join(0, 1, place)

        gate_pre, up_pre = pre[:, :hid], pre[:, hid:]
        sig = jax.nn.sigmoid(gate_pre)
        silu = gate_pre * sig
        r.hidden[...] = (silu * up_pre).astype(bf16)
        hidden_back = nt(r.sg_s[...], r.down[slot])
        r.pre_back[:, :hid] = (
            hidden_back * up_pre * sig * (1.0 + gate_pre * (1.0 - sig))
        ).astype(bf16)
        r.pre_back[:, hid:] = (hidden_back * silu).astype(bf16)
        produced = nn(r.hidden[...], r.down[slot])
        pair = jnp.sum(r.og_s[...].astype(f32) * produced, axis=1, keepdims=True)
        weighed = (produced * r.gate_s[:, :1]).astype(bf16)
        for src in range(ne):
            a, b = src * cap, (src + 1) * cap
            r.weighed[src, own, :] = weighed[a:b]
            r.soft_part[src, pl.ds(e, 1), :] = jnp.sum(
                r.hits[src, own, :].astype(f32) * pair[a:b], axis=0, keepdims=True
            )
        back = nt(r.pre_back[...], r.both[slot]).astype(bf16)
        for src in range(ne):
            r.back_rows[src, own, :] = back[src * cap : (src + 1) * cap]

        @pl.when(e == 1)
        def _():
            for place in (0, 3):
                line.cross(0, 1, place)

        @pl.when(e == 2)
        def _():
            for place in (1, 2):
                line.join(0, 0, place)

        @pl.when(e > 0)
        def _():
            for step in range(1, nd):
                cores(e - 1, step).wait_send()

        r.made[:, :, :gate_rows, :] = (
            tn(r.x_s[...], r.pre_back[...]).astype(bf16).reshape(nz, nd, gate_rows, 2 * hid)
        )
        r.made[:, :, gate_rows:, :] = (
            tn(r.hidden[...], r.sg_s[...]).astype(bf16).reshape(nz, nd, down_rows, width)
        )
        for step in range(1, nd):
            cores(e, step).start()
        r.held_s[e] = r.made[:, dp]

    stores = []
    for kind, (rows, out) in enumerate(((r.back_rows, r.back_part), (r.weighed, r.out_part))):
        for src in range(ne):
            r.sums[kind, src] = tn(r.hits[src], rows[src]).astype(bf16)
            stores.append(
                pltpu.make_async_copy(r.sums.at[kind, src], out.at[src], r.store_sem.at[kind, src])
            )
            stores[-1].start()
    add_cores(local - 1)

    def put(at, value):
        r.shard[at : at + 16, :] = value

    for place in (0, 3):
        for which in (0, 1):
            line.left(0, which, place)
    line.total(0, put)
    for step in range(1, nd):
        cores(local - 1, step).wait_send()
    for k in range(1, local):
        keep(k).wait()
    for copy in stores:
        copy.wait()


def experts(sizes, cid, cap, kept, read):
    ne, nz, nd = sizes
    local, width, hid = kept["w_gate"].shape
    tokens = read["rows_all"].shape[1]
    piece = width // (nz * nd) + hid // (nz * nd)
    shape, vmem, dma = jax.ShapeDtypeStruct, pltpu.VMEM, pltpu.SemaphoreType.DMA
    held, *line = Line.scratch(nz, local, piece, width)
    line[0] = vmem((1, nz, piece, width), bf16)
    outs = dict(
        held=shape((local, nz, piece, width), bf16),
        out_part=shape((ne, tokens, width), bf16),
        back_part=shape((ne, tokens, width), bf16),
        soft_part=shape((ne, local, tokens), f32),
        shard=shape((piece, width), f32),
    )
    rows = ne * cap
    scratch = dict(
        both=vmem((2, width, 2 * hid), bf16),
        down=vmem((2, hid, width), bf16),
        x_s=vmem((rows, width), bf16),
        og_s=vmem((rows, width), bf16),
        sg_s=vmem((rows, width), bf16),
        gate_s=vmem((rows, 128), f32),
        hidden=vmem((rows, hid), bf16),
        pre_back=vmem((rows, 2 * hid), bf16),
        hits=vmem((ne, local * cap, tokens), bf16),
        weighed=vmem((ne, local * cap, width), bf16),
        back_rows=vmem((ne, local * cap, width), bf16),
        sums=vmem((2, ne, tokens, width), bf16),
        made=vmem((nz, nd, piece, width), bf16),
        from_dp=vmem((nd - 1, local, nz, piece, width), bf16),
        held_s=held,
        line=line,
        weight_sem=dma((2, 3)),
        dp_send=dma((local, nd)),
        dp_recv=dma((local, nd)),
        held_sem=dma((local,)),
        store_sem=dma((2, ne)),
    )
    return call_named(
        functools.partial(experts_kernel, sizes, cap),
        kept, read, outs, scratch, cid, 62 << 20, ("held", "out_part", "back_part"),
    )


class Spread:
    def __init__(self, sizes, made, from_dp, held, from_ex, line, from_z, send, recv):
        self.sizes, self.made, self.from_dp, self.held = sizes, made, from_dp, held
        self.from_ex, self.line, self.from_z, self.send, self.recv = from_ex, line, from_z, send, recv
        self.places = tuple(lax.axis_index(a) for a in ("dp", "expert", "context"))

    @staticmethod
    def scratch(sizes, rows, width):
        ne, nz, nd = sizes
        most = max(sizes)
        return [
            pltpu.VMEM((nd - 1, ne, nz, rows, width), bf16),
            pltpu.VMEM((ne, nz, rows, width), bf16),
            pltpu.VMEM((ne - 1, nz, rows, width), bf16),
            pltpu.VMEM((nz, rows, width), bf16),
            pltpu.VMEM((nz - 1, rows, width), bf16),
            pltpu.SemaphoreType.DMA((3, most)),
            pltpu.SemaphoreType.DMA((3, most)),
        ]

    def copy(self, stage, step):
        ne, nz, nd = self.sizes
        axis, size = (("dp", nd), ("expert", ne), ("context", nz))[stage]
        other = lax.rem(self.places[stage] + step, size)
        src = (
            self.made.at[:, :, other]
            if stage == 0
            else self.held.at[other] if stage == 1 else self.line.at[other]
        )
        dst = (self.from_dp, self.from_ex, self.from_z)[stage].at[step - 1]
        return pltpu.make_async_remote_copy(
            src_ref=src,
            dst_ref=dst,
            send_sem=self.send.at[stage, step],
            recv_sem=self.recv.at[stage, step],
            device_id={axis: other},
            device_id_type=MESH,
        )

    def others(self, stage):
        ne, nz, nd = self.sizes
        return range(1, (nd, ne, nz)[stage])

    def over_dp(self):
        for step in self.others(0):
            self.copy(0, step).start()

    def made_free(self):
        for step in self.others(0):
            self.copy(0, step).wait_send()

    def over_expert(self):
        ne, nz, _ = self.sizes
        for step in self.others(0):
            self.copy(0, step).wait_recv()

        @pl.loop(0, ne * nz)
        def _(i):
            a = lax.div(i, nz)
            b = i - a * nz
            total = self.made[a, b, self.places[0]].astype(f32)
            for step in self.others(0):
                total = total + self.from_dp[step - 1, a, b].astype(f32)
            self.held[a, b] = total.astype(bf16)

        for step in self.others(1):
            self.copy(1, step).start()

    def over_context(self):
        nz = self.sizes[1]
        for step in self.others(1):
            self.copy(1, step).wait_recv()

        @pl.loop(0, nz)
        def _(b):
            total = self.held[self.places[1], b].astype(f32)
            for step in self.others(1):
                total = total + self.from_ex[step - 1, b].astype(f32)
            self.line[b] = total.astype(bf16)

        for step in self.others(2):
            self.copy(2, step).start()

    def finish(self, out):
        for step in self.others(2):
            self.copy(2, step).wait_recv()
        total = self.line[self.places[2]].astype(f32)
        for step in self.others(2):
            total = total + self.from_z[step - 1].astype(f32)
        out[...] = total
        for stage in (1, 2):
            for step in self.others(stage):
                self.copy(stage, step).wait_send()


class Fold:
    def __init__(self, ex, parts, own, mine, passing, came, load, send, recv):
        self.ex, self.parts, self.own, self.mine, self.passing, self.came = (
            ex, parts, own, mine, passing, came,
        )
        self.load, self.send, self.recv = load, send, recv
        self.pair = partners(ex, 4)
        half = parts.shape[1] // 2
        self.halves = (pl.ds(0, half), pl.ds(half, half))

    @staticmethod
    def scratch(rows, width):
        half = (2, rows // 2, width)
        return [
            pltpu.VMEM((rows, width), bf16),
            pltpu.VMEM(half, bf16),
            pltpu.VMEM(half, bf16),
            pltpu.VMEM((2, rows, width), bf16),
            pltpu.SemaphoreType.DMA((3,)),
            pltpu.SemaphoreType.DMA((3, 2)),
            pltpu.SemaphoreType.DMA((3, 2)),
        ]

    def copy(self, stage, i):
        src, dst = (
            (self.parts.at[3 - self.ex, self.halves[i]], self.passing.at[i]),
            (self.parts.at[self.pair[i], self.halves[i]], self.came.at[i, self.halves[i]]),
            (self.mine.at[i], self.came.at[i, self.halves[1 - i]]),
        )[stage]
        return pltpu.make_async_remote_copy(
            src_ref=src,
            dst_ref=dst,
            send_sem=self.send.at[stage, i],
            recv_sem=self.recv.at[stage, i],
            device_id={"expert": self.pair[i]},
            device_id_type=MESH,
        )

    def loads(self):
        return [
            pltpu.make_async_copy(self.parts.at[self.ex], self.own, self.load.at[2])
        ] + [
            pltpu.make_async_copy(
                self.parts.at[self.pair[i], self.halves[1 - i]], self.mine.at[i], self.load.at[i]
            )
            for i in (0, 1)
        ]

    def begin(self):
        for stage in (0, 1):
            for i in (0, 1):
                self.copy(stage, i).start()
        for copy in self.loads():
            copy.start()

    def onward(self):
        for copy in self.loads():
            copy.wait()
        for i in (0, 1):
            self.copy(0, 1 - i).wait_recv()
            add_rows(self.mine, (i,), self.passing, (1 - i,), self.mine.shape[1])
            self.copy(2, i).start()

    def arrive(self):
        for stage in (1, 2):
            for i in (0, 1):
                self.copy(stage, i).wait_recv()

    def finish(self):
        for stage in range(3):
            for i in (0, 1):
                self.copy(stage, i).wait_send()


def tail_kernel(sizes, defs, *refs):
    r = named(defs, refs)
    ne, nz, nd = sizes
    ex, me, dp = (lax.axis_index(a) for a in ("expert", "context", "dp"))
    tokens, width = r.tokens.shape
    slices = r.kv_all.shape[1]
    kv_width = slices * 128
    group = width // ne
    last, helper = nz - 1, nz - 2

    barrier = pltpu.get_barrier_semaphore()
    for axis, place, size in (("expert", ex, ne), ("context", me, nz), ("dp", dp, nd)):
        for step in range(1, size):
            pl.semaphore_signal(
                barrier, inc=1, device_id={axis: lax.rem(place + step, size)}, device_id_type=MESH
            )
    for copy in r.loads:
        copy.start()
    pl.semaphore_wait(barrier, ne + nz + nd - 3)

    line = Line(nz, *r.line)
    proj = Spread(sizes, r.made, *r.proj)
    query = Spread(sizes, r.made, *r.query)
    kv = Spread(sizes, r.made, *r.kv)
    small = Spread(sizes, r.small_made, *r.small)

    chunks = range(r.held_in.shape[0] - 1)
    held_copies = [
        pltpu.make_async_copy(r.held_in.at[k + 1], line.held.at[k], r.held_sem.at[k])
        for k in chunks
    ]
    for copy in held_copies:
        copy.start()

    back = Fold(ex, r.back_in, *r.back)
    out = Fold(ex, r.out_in, *r.out)

    def gates_copy(step):
        other = lax.rem(ex + step, ne)
        return pltpu.make_async_remote_copy(
            src_ref=r.soft_in.at[other],
            dst_ref=r.soft_all.at[ex],
            send_sem=r.gates_send.at[step],
            recv_sem=r.gates_recv.at[step],
            device_id={"expert": other},
            device_id_type=MESH,
        )

    back.begin()
    for step in range(1, ne):
        gates_copy(step).start()
    loads = [
        pltpu.make_async_copy(src, dst, r.load_sem.at[i])
        for i, (src, dst) in enumerate(
            (
                (r.soft_in.at[ex], r.soft_all.at[ex]),
                (r.w_out, r.w_out_v),
                (r.w_query, r.w_query_v),
                (r.w_key, r.w_key_v),
                (r.w_value, r.w_value_v),
                (r.tables_all.at[ex], r.tables_own),
            )
        )
    ]
    for copy in loads:
        copy.start()
    for k in chunks:
        held_copies[k].wait()
        if k == 0:
            for place in (0, 3):
                line.cross(0, 0, place)
                line.cross(0, 1, place)
        line.straight(k)
    for copy in r.loads + loads:
        copy.wait()
    for t in range(2 * slices):
        for ab in (0, 1):
            h = 2 * t + ab
            r.attn_turned[h * HEAD_DIM : (h + 1) * HEAD_DIM, :] = r.heads[
                t, :, ab * tokens : (ab + 1) * tokens
            ]

    back.onward()
    for place in (0, 3):
        for which in (0, 1):
            line.left(0, which, place)
        for which in (0, 1):
            line.cross(1, which, place)
    for which in (0, 1):
        line.join(0, which, 2)
    for step in range(1, ne):
        gates_copy(step).wait_recv()
    back.arrive()
    out.begin()
    soft_back = jnp.concatenate([r.soft_all[i] for i in range(ne)], axis=0)
    router_soft = r.tables_own[1]
    logit_back = (
        router_soft * (soft_back - jnp.sum(router_soft * soft_back, axis=0, keepdims=True))
    ).astype(bf16)
    second_back = back.own[...].astype(f32) + tn(logit_back, r.w_router_turned[...])
    for i in (0, 1):
        second_back = second_back + back.came[i].astype(f32)
    middle = r.middle[...]
    inverse = lax.rsqrt(jnp.mean(middle * middle, axis=-1, keepdims=True) + epsilon)
    normed = middle * inverse
    scaled = second_back * r.gains[1:, :].astype(f32)
    moe_gain_grad = jnp.sum(second_back * normed, axis=0, keepdims=True)
    middle_grad = r.grad_top[...].astype(f32) + inverse * (
        scaled - normed * jnp.mean(scaled * normed, axis=-1, keepdims=True)
    )
    r.middle_grad[...] = middle_grad
    r.branch[...] = middle_grad.astype(bf16)
    experts_all = logit_back.shape[0]
    r.small_rows[...] = jnp.zeros_like(r.small_rows)
    r.small_rows[:experts_all, :] = nn(logit_back, r.second_low[...])
    r.small_rows[experts_all : experts_all + 1, :] = moe_gain_grad

    def to(place, src, dst, send, recv):
        return pltpu.make_async_remote_copy(
            src_ref=src,
            dst_ref=dst,
            send_sem=send,
            recv_sem=recv,
            device_id={"context": place},
            device_id_type=MESH,
        )

    def ask(t):
        return [
            to(helper, src.at[t], dst.at[t], r.ask_send.at[i, t], r.ask_recv.at[i, t])
            for i, (src, dst) in enumerate(((r.do, r.far_do), (r.stats, r.far_stats)))
        ]

    def answer(t):
        return to(
            last, r.far_dq_low.at[t], r.dq_came.at[t], r.answer_send.at[t], r.answer_recv.at[t]
        )

    @pl.loop(0, slices)
    def _(t):
        at = pl.ds(pl.multiple_of(t * 256, 256), 256)
        turned = nt(r.w_out_v[at, :], r.branch[...]).astype(bf16)
        r.stats[t, 0] = r.lse[t]
        for half in (0, 1):
            a, b = half * HEAD_DIM, (half + 1) * HEAD_DIM
            for ab in (0, 1):
                c = (2 * half + ab) * HEAD_DIM
                r.do[t, a:b, ab * tokens : (ab + 1) * tokens] = turned[c : c + HEAD_DIM]
            r.stats[t, 1, half : half + 1, :] = jnp.sum(
                r.do[t, a:b, :].astype(f32) * r.heads[2 * t + half].astype(f32),
                axis=0,
                keepdims=True,
            )

        @pl.when(me == last)
        def _():
            for copy in ask(t):
                copy.start()

    @pl.loop(0, ne)
    def _(g):
        at = pl.ds(pl.multiple_of(g * group, group), group)
        grad = nn(r.attn_turned[at, :], r.branch[...])
        r.made[g] = grad.reshape((nz, nd, group // (nz * nd), width)).astype(bf16)

    proj.over_dp()
    for which in (0, 1):
        line.join(0, which, 1)
    for which in (0, 1):
        line.left(1, which, 0)
        line.cross(2, which, 0)
    proj.over_expert()
    out.onward()

    r.dq[...] = jnp.zeros_like(r.dq)
    r.far_dq[...] = jnp.zeros_like(r.far_dq)

    def mine(j):
        return me == last if j == last else (j <= me) & (me < last)

    for j in range(nz):

        @pl.when(mine(j))
        def _():
            r.bias[j] = mask_bias(r.seg_all, j, me, tokens)

    @pl.when(me == helper)
    def _():
        for j in range(last):
            r.far_bias[j] = mask_bias(r.seg_all, j, last, tokens)

    def back_slice(j, t, queries, do, stats, dq, bias):
        keys = r.kv_all[j, t, :, :128]
        vals = r.kv_all[j, t, :, 128:]
        dks, dvs = [], []
        for half in (0, 1):
            keep = lane_half((tokens, 128), half)
            zero = jnp.zeros_like(keys)
            keys_half = jnp.where(keep, keys, zero)
            scores = nt(keys_half, queries[t]) + jnp.concatenate([bias[j]] * 2, axis=1)
            soft = jnp.exp(scores - stats[t, 0, half : half + 1, :])
            soft_grad = nn(jnp.where(keep, vals, zero), do[t])
            back = (soft * (soft_grad - stats[t, 1, half : half + 1, :])).astype(bf16)
            dvs.append(nt(soft.astype(bf16), do[t]))
            dks.append(nn(back, queries[t]))
            dq[t] += tn(keys_half, back)
        low = lane_half((tokens, 128), 0)
        return jnp.concatenate(
            [jnp.where(low, dks[0], dks[1]), jnp.where(low, dvs[0], dvs[1])], axis=1
        )

    def give(j, t):
        return to(
            me - 1, r.kv_part.at[j, t], r.kv_came.at[j, t], r.kv_send.at[j, t], r.kv_recv.at[j, t]
        )

    @pl.loop(0, slices)
    def _(t):
        for j in range(nz):

            @pl.when(mine(j))
            def _():
                r.kv_sum[j] = back_slice(j, t, r.q, r.do, r.stats, r.dq, r.bias)

        @pl.when(me == helper)
        def _():
            for copy in ask(t):
                copy.wait_recv()
            for j in range(last):
                r.kv_sum[j] += back_slice(
                    j, t, r.q_far, r.far_do, r.far_stats, r.far_dq, r.far_bias
                )
                if j < helper:
                    r.kv_part[j, t] = r.kv_sum[j].astype(bf16)
                    give(j, t).start()
            r.far_dq_low[t] = r.far_dq[t].astype(bf16)
            answer(t).start()

        for j in range(helper):

            @pl.when((j < me) & (me < helper))
            def _():
                r.kv_part[j, t] = r.kv_sum[j].astype(bf16)

        r.own_kv[t] = r.kv_sum[me]

    for which in (0, 1):
        line.cross(2, which, 3)
        line.join(1, which, 2)

    @pl.when(me == last)
    def _():
        @pl.loop(0, slices)
        def _(t):
            answer(t).wait_recv()
            r.dq[t] += r.dq_came[t].astype(f32)

    quarter = HEAD_DIM // 2
    cos_q, sin_q = (
        jnp.concatenate([r.turn[i].T[:quarter]] * 2, axis=1) * HEAD_DIM ** (-0.5) for i in (0, 1)
    )
    for t in range(slices):
        for half in (0, 1):
            a = half * HEAD_DIM
            first = r.dq[t, a : a + quarter, :]
            second = r.dq[t, a + quarter : a + 2 * quarter, :]
            turned = jnp.concatenate(
                [first * cos_q + second * sin_q, second * cos_q - first * sin_q], axis=0
            )
            pair = jnp.concatenate([turned[:, :tokens], turned[:, tokens:]], axis=0)
            at = (2 * t + half) * 128
            r.back_s[:, at : at + 128] = pair.T.astype(bf16)

    def make(a, b):
        @pl.loop(0, ne)
        def _(g):
            at = pl.ds(pl.multiple_of(g * group, group), group)
            grad = tn(r.first_low[:, at], r.back_s[:, a:b])
            r.made[g] = grad.reshape((nz, nd, group // (nz * nd), b - a)).astype(bf16)

    proj.made_free()
    make(0, width)
    query.over_dp()
    for which in (0, 1):
        line.join(1, which, 1)
    for k in chunks:
        line.ends(k, 0)
    line.ends(0, 3)
    query.over_expert()

    @pl.loop(0, slices)
    def _(t):
        for j in range(helper):

            @pl.when((j < me) & (me < helper))
            def _():
                give(j, t).wait_recv()
                r.kv_part[j, t] = (
                    r.kv_part[j, t].astype(f32) + r.kv_came[j, t].astype(f32)
                ).astype(bf16)
                give(j, t).start()

        @pl.when(me < helper)
        def _():
            give(me, t).wait_recv()
            r.own_kv[t] += r.kv_came[me, t].astype(f32)

    for which in (0, 1):
        line.join(2, which, 1)
    for k in chunks[1:]:
        line.ends(k, 3)
    cos_k, sin_k = r.turn[0], r.turn[1]
    first_lanes = lax.rem(lax.broadcasted_iota(jnp.int32, (tokens, 128), 1), HEAD_DIM) < quarter
    for t in range(slices):
        grad = r.own_kv[t, :, :128]
        swapped = jnp.where(
            first_lanes, pltpu.roll(grad, 128 - quarter, 1), pltpu.roll(grad, quarter, 1)
        )
        r.back_s[:, width + t * 128 : width + (t + 1) * 128] = (
            grad * cos_k + swapped * sin_k
        ).astype(bf16)
        at = width + kv_width + t * 128
        r.back_s[:, at : at + 128] = r.own_kv[t, :, 128:].astype(bf16)
    query.made_free()
    make(width, width + 2 * kv_width)
    kv.over_dp()
    proj.over_context()

    first_back = nt(r.back_s[:, :width], r.w_query_v[...])
    first_back = first_back + nt(r.back_s[:, width : width + kv_width], r.w_key_v[...])
    first_back = first_back + nt(r.back_s[:, width + kv_width :], r.w_value_v[...])
    values = r.tokens[...].astype(f32)
    inverse = lax.rsqrt(jnp.mean(values * values, axis=-1, keepdims=True) + epsilon)
    normed = values * inverse
    scaled = first_back * r.gains[:1, :].astype(f32)
    r.small_rows[experts_all + 1 : experts_all + 2, :] = jnp.sum(
        first_back * normed, axis=0, keepdims=True
    )
    r.input_grad[...] = r.middle_grad[...] + inverse * (
        scaled - normed * jnp.mean(scaled * normed, axis=-1, keepdims=True)
    )
    for which in (0, 1):
        line.join(2, which, 2)
    small_turned = r.small_rows[...].T
    r.small_made[...] = small_turned.reshape(r.small_made.shape).astype(bf16)
    small.over_dp()
    kv.over_expert()
    small.over_expert()
    query.over_context()

    out.arrive()

    @pl.loop(0, tokens // 16)
    def _(i):
        at = pl.ds(pl.multiple_of(i * 16, 16), 16)
        total = r.middle[at, :] + out.own[at, :].astype(f32)
        for i in (0, 1):
            total = total + out.came[i, at, :].astype(f32)
        r.layer_out[at, :] = total

    kv.over_context()
    small.over_context()
    kv.made_free()
    small.made_free()
    for group_sum, target in zip((proj, query, kv, small), r.sums_out + [r.small_sum]):
        group_sum.finish(target)
    r.router_out[...] = r.small_sum[:, :experts_all]
    turned = r.small_sum[...].T
    r.gains_out[0] = turned[experts_all + 1 : experts_all + 2]
    r.gains_out[1] = turned[experts_all : experts_all + 1]
    gate_out, up_out, down_out = r.experts_out
    gate_rows, hid = gate_out.shape[1:]

    def put(k, at, value):
        if at < gate_rows:
            gate_out[k, at : at + 16, :] = value[:, :hid]
            up_out[k, at : at + 16, :] = value[:, hid:]
        else:
            down_out[k, at - gate_rows : at - gate_rows + 16, :] = value

    for at in range(0, r.first_shard.shape[0], 16):
        put(0, at, r.first_shard[at : at + 16, :])
    for which in (0, 1):
        line.left(1, which, 3)
        line.left(2, which, 3)
        line.left(2, which, 0)
    for k in chunks:
        line.total(k, functools.partial(put, k + 1))
    back.finish()
    out.finish()
    for step in range(1, ne):
        gates_copy(step).wait_send()
    for j in range(helper):

        @pl.when((j < me) & (me < last))
        def _():
            for t in range(slices):
                give(j, t).wait_send()

    @pl.when(me == last)
    def _():
        for t in range(slices):
            for copy in ask(t):
                copy.wait_send()

    @pl.when(me == helper)
    def _():
        for t in range(slices):
            answer(t).wait_send()


def tail(sizes, cid, hidden, hbm_ins, vmem_ins):
    ne, nz, nd = sizes
    ins = types.SimpleNamespace(**hbm_ins, **vmem_ins)
    tokens, width = ins.tokens.shape
    slices, wide, _ = ins.q.shape
    chunks, _, piece, _ = ins.held_in.shape
    kv_shape = ins.kv_all.shape[1:]
    kv_cols = slices * 256
    rows = width // (ne * nz * nd)
    gate_rows = width // (nz * nd)
    shard = lambda *shape: jax.ShapeDtypeStruct(shape, f32)
    outs = dict(
        layer_out=shard(tokens, width),
        input_grad=shard(tokens, width),
        sums_out=[shard(rows, c) for c in (width, width, kv_cols)],
        router_out=shard(rows, ins.w_router_turned.shape[0]),
        gains_out=shard(2, 1, rows),
        experts_out=[
            shard(chunks, gate_rows, hidden),
            shard(chunks, gate_rows, hidden),
            shard(chunks, piece - gate_rows, width),
        ],
    )
    dma = pltpu.SemaphoreType.DMA
    vmem = pltpu.VMEM
    scratch = dict(
        back=Fold.scratch(tokens, width),
        out=Fold.scratch(tokens, width),
        soft_all=vmem(ins.soft_in.shape, f32),
        w_out_v=vmem(ins.w_out.shape, bf16),
        w_query_v=vmem(ins.w_query.shape, bf16),
        w_key_v=vmem(ins.w_key.shape, bf16),
        w_value_v=vmem(ins.w_value.shape, bf16),
        attn_turned=vmem((width, tokens), bf16),
        middle_grad=vmem((tokens, width), f32),
        branch=vmem((tokens, width), bf16),
        small_rows=vmem((128, width), f32),
        do=vmem((slices, 128, wide), bf16),
        stats=vmem((slices, 2, 2, wide), f32),
        bias=vmem((nz, tokens, tokens), f32),
        dq=vmem((slices, 128, wide), f32),
        dq_came=vmem((slices, 128, wide), bf16),
        far_do=vmem((slices, 128, wide), bf16),
        far_stats=vmem((slices, 2, 2, wide), f32),
        far_bias=vmem((nz - 1, tokens, tokens), f32),
        far_dq=vmem((slices, 128, wide), f32),
        far_dq_low=vmem((slices, 128, wide), bf16),
        kv_sum=vmem((nz, tokens, 256), f32),
        kv_part=vmem((nz - 2,) + kv_shape, bf16),
        kv_came=vmem((nz - 2,) + kv_shape, bf16),
        own_kv=vmem(kv_shape, f32),
        back_s=vmem((tokens, width + kv_cols), bf16),
        made=vmem((ne, nz, nd, rows, width), bf16),
        small_made=vmem((ne, nz, nd, rows, 128), bf16),
        small_sum=vmem((rows, 128), f32),
        gates_send=dma((ne,)),
        gates_recv=dma((ne,)),
        load_sem=dma((6,)),
        tables_own=vmem(ins.tables_all.shape[1:], f32),
        held_sem=dma((chunks,)),
        kv_send=dma((nz, slices)),
        kv_recv=dma((nz, slices)),
        ask_send=dma((2, slices)),
        ask_recv=dma((2, slices)),
        answer_send=dma((slices,)),
        answer_recv=dma((slices,)),
        line=Line.scratch(nz, chunks - 1, piece, width),
        proj=Spread.scratch(sizes, rows, width),
        query=Spread.scratch(sizes, rows, width),
        kv=Spread.scratch(sizes, rows, kv_cols),
        small=Spread.scratch(sizes, rows, 128),
    )
    return call_named(
        functools.partial(tail_kernel, sizes), hbm_ins, vmem_ins, outs, scratch, cid, 63 << 20, ()
    )


def deliver_kernel(parts, count, *refs):
    ins, outs, sem, held = refs[:count], refs[count : 2 * count], refs[2 * count], refs[2 * count + 1 :]
    reads = [
        pltpu.make_async_copy(
            ins[i] if part is None else ins[i].at[:, pl.ds(*part)], held[i], sem.at[0, i]
        )
        for i, part in enumerate(parts)
    ]
    writes = [pltpu.make_async_copy(held[i], outs[i], sem.at[1, i]) for i in range(count)]
    for copy in reads:
        copy.start()
    for read, write in zip(reads, writes):
        read.wait()
        write.start()
    for copy in writes:
        copy.wait()


def deliver(moved):
    arrays, parts = zip(*moved)
    hbm = pl.BlockSpec(memory_space=pl.ANY)
    shapes = [a.shape[:-1] + (part[1] if part else a.shape[-1],) for a, part in moved]
    return pl.pallas_call(
        functools.partial(deliver_kernel, parts, len(parts)),
        out_shape=[jax.ShapeDtypeStruct(shape, a.dtype) for shape, a in zip(shapes, arrays)],
        in_specs=[hbm] * len(parts),
        out_specs=[hbm] * len(parts),
        scratch_shapes=[pltpu.SemaphoreType.DMA((2, len(parts)))]
        + [pltpu.VMEM(shape, a.dtype) for shape, a in zip(shapes, arrays)],
        compiler_params=pltpu.CompilerParams(vmem_limit_bytes=60 << 20),
        name="deliver",
    )(*arrays)


def turn_tables(tokens, blocks):
    freq = rope_base ** (-2.0 * np.arange(HEAD_DIM // 2) / HEAD_DIM)
    freq = np.tile(freq, 128 // freq.size)
    inner = np.arange(tokens)[:, None] * freq
    base = tokens * np.arange(blocks)[:, None] * freq
    return tuple(
        jnp.asarray(np.stack([np.cos(a), np.sin(a)]), f32) for a in (inner, base)
    )


def body(
    sizes,
    tokens,
    attn_scale,
    w_query,
    w_key,
    w_value,
    w_out,
    moe_scale,
    w_router,
    w_gate,
    w_up,
    w_down,
    segment_ids,
    expert_choice,
    slot_order,
    out_grad,
):
    ne, nz, nd = sizes
    local_rows = tokens.shape[1]
    kv_width = w_key.shape[1]
    experts_all = w_router.shape[1]
    pair_count = local_rows * expert_choice.shape[2]
    capacity = (pair_count * 9 + 8 * experts_all - 1) // (8 * experts_all)
    inner, base = turn_tables(local_rows, nz)
    w_router_turned = w_router.T
    gains = jnp.stack([attn_scale, moe_scale])

    begun = front(
        sizes,
        1,
        capacity,
        dict(
            w_query=w_query, w_key=w_key, w_value=w_value, w_out=w_out, grad_top=out_grad[0]
        ),
        dict(
            tokens=tokens[0],
            gains=gains,
            w_router_turned=w_router_turned,
            seg=segment_ids,
            chosen=expert_choice[0].T,
            order=slot_order[0],
            inner=inner,
            base=base,
        ),
    )
    mixed = experts(
        sizes,
        2,
        capacity,
        dict(w_gate=w_gate, w_up=w_up, w_down=w_down),
        dict(rows_all=begun.rows_all, grad_all=begun.grad_all, tables_all=begun.tables_all),
    )
    ended = tail(
        sizes,
        3,
        w_gate.shape[2],
        dict(
            held_in=mixed.held,
            back_in=mixed.back_part,
            out_in=mixed.out_part,
            soft_in=mixed.soft_part,
            w_query=w_query,
            w_key=w_key,
            w_value=w_value,
            w_out=w_out,
            tables_all=begun.tables_all,
        ),
        dict(
            q=begun.q,
            q_far=begun.q_far,
            kv_all=begun.kv_all,
            seg_all=begun.seg_all,
            lse=begun.lse,
            heads=begun.heads,
            middle=begun.middle,
            tokens=tokens[0],
            grad_top=out_grad[0],
            second_low=begun.second_low,
            first_low=begun.first_low,
            w_router_turned=w_router_turned,
            gains=gains,
            turn=begun.turn,
            first_shard=mixed.shard,
        ),
    )
    out_shard, query_shard, kv_shard = ended.sums_out
    moved = [
        (ended.layer_out, None),
        (ended.input_grad, None),
        (query_shard, None),
        (kv_shard, (0, kv_width)),
        (kv_shard, (kv_width, kv_width)),
        (out_shard, None),
        *((array, None) for array in ended.experts_out),
    ]
    layer_out, input_grad, *shards = deliver(moved)
    return (
        layer_out[None],
        input_grad[None],
        ended.gains_out[0, 0],
        ended.gains_out[1, 0],
        *shards[:4],
        ended.router_out,
        *shards[4:],
    )


def solution(mesh):
    sizes = (mesh.shape["expert"], mesh.shape["context"], mesh.shape["dp"])
    in_specs = (
        P(("expert", "dp"), "context", None),
        P(),
        P(),
        P(),
        P(),
        P(),
        P(),
        P(),
        P("expert", None, None),
        P("expert", None, None),
        P("expert", None, None),
        P(("expert", "dp"), "context"),
        P(("expert", "dp"), "context", None),
        P(("expert", "dp"), "context", None),
        P(("expert", "dp"), "context", None),
    )
    out_specs = (
        P(("expert", "dp"), "context", None),
        P(("expert", "dp"), "context", None),
        P(("expert", "context", "dp")),
        P(("expert", "context", "dp")),
        P(("expert", "context", "dp"), None),
        P(("expert", "context", "dp"), None),
        P(("expert", "context", "dp"), None),
        P(("expert", "context", "dp"), None),
        P(("expert", "context", "dp"), None),
        P("expert", ("context", "dp"), None),
        P("expert", ("context", "dp"), None),
        P("expert", ("context", "dp"), None),
    )
    return jax.shard_map(
        functools.partial(body, sizes),
        mesh=mesh,
        in_specs=in_specs,
        out_specs=out_specs,
        check_vma=False,
    )
```

```python
import functools
import types

import jax
import jax.numpy as jnp
import numpy as np
from jax import lax
from jax.experimental import pallas as pl
from jax.experimental.pallas import tpu as pltpu
from jax.sharding import PartitionSpec as P

HEAD_DIM = 64
MESH = pl.DeviceIdType.MESH

epsilon = 1e-06
rope_base = 10000.0
negative_large = -1e30
bf16 = jnp.bfloat16
f32 = jnp.float32


def nt(a, b):
    return lax.dot_general(a, b, (((1,), (1,)), ((), ())), preferred_element_type=f32)


def tn(a, b):
    return lax.dot_general(a, b, (((0,), (0,)), ((), ())), preferred_element_type=f32)


def nn(a, b):
    return jnp.dot(a, b, preferred_element_type=f32)


def add_rows(dst, dst_at, src, src_at, rows):
    step = 16

    @pl.loop(0, rows // step)
    def _(i):
        at = pl.ds(pl.multiple_of(i * step, step), step)
        dst[dst_at + (at, slice(None))] = (
            dst[dst_at + (at, slice(None))].astype(f32) + src[src_at + (at, slice(None))].astype(f32)
        ).astype(bf16)


def lane_half(shape, which):
    lanes = lax.broadcasted_iota(jnp.int32, shape, 1)
    return (lanes >= HEAD_DIM) if which else (lanes < HEAD_DIM)


def column_of(row):
    n = row.shape[1]
    rows = lax.broadcasted_iota(jnp.int32, (n, n), 0)
    cols = lax.broadcasted_iota(jnp.int32, (n, n), 1)
    return jnp.sum(jnp.where(rows == cols, row, 0.0), axis=1, keepdims=True)


def mask_bias(seg_ref, block, me, tokens):
    key_seg = column_of(seg_ref[block, :1, :])
    same = key_seg == seg_ref[me, :1, :]
    rows = lax.broadcasted_iota(jnp.int32, (tokens, tokens), 0) + block * tokens
    cols = lax.broadcasted_iota(jnp.int32, (tokens, tokens), 1) + me * tokens
    return jnp.where(same & (rows <= cols), 0.0, negative_large)


def named(defs, refs):
    counts = [d.num_leaves for d in defs]
    at = [sum(counts[:i]) for i in range(len(counts) + 1)]
    trees = [jax.tree.unflatten(d, refs[at[i] : at[i + 1]]) for i, d in enumerate(defs)]
    r = types.SimpleNamespace(**{k: v for tree in trees for k, v in tree.items()})
    read, (copies, sem) = trees[1], trees[3]["read"]
    r.loads = [
        pltpu.make_async_copy(read[k], copies[k], sem.at[i]) for i, k in enumerate(sorted(read))
    ]
    for k in read:
        setattr(r, k, copies[k])
    return r


def call_named(kernel, kept, read, outs, scratch, cid, limit, kept_outs):
    vm = pl.BlockSpec(memory_space=pltpu.VMEM)
    hbm = pl.BlockSpec(memory_space=pl.ANY)
    scratch["read"] = (
        {k: pltpu.VMEM(v.shape, v.dtype) for k, v in read.items()},
        pltpu.SemaphoreType.DMA((len(read),)),
    )
    flats, defs = zip(*(jax.tree.flatten(t) for t in (kept, read, outs, scratch)))
    out_specs = jax.tree.leaves(
        {k: jax.tree.map(lambda _: hbm if k in kept_outs else vm, v) for k, v in outs.items()}
    )
    results = pl.pallas_call(
        functools.partial(kernel, defs),
        out_shape=tuple(flats[2]),
        in_specs=[hbm] * (len(flats[0]) + len(flats[1])),
        out_specs=tuple(out_specs),
        scratch_shapes=flats[3],
        compiler_params=pltpu.CompilerParams(
            collective_id=cid, has_side_effects=True, vmem_limit_bytes=limit
        ),
        name=kernel.func.__name__,
    )(*flats[0], *flats[1])
    return types.SimpleNamespace(**jax.tree.unflatten(defs[2], results))


def slot_table(chosen, order, experts_all, capacity):
    top_count, tokens = chosen.shape
    pairs = order.shape[1]
    shift = top_count.bit_length() - 1
    if top_count != 1 << shift:
        raise ValueError("top count")
    owner = jnp.where(
        (order >> shift) == lax.broadcasted_iota(jnp.int32, (tokens, pairs), 0), 1.0, 0.0
    ).astype(bf16)
    which = (order & (top_count - 1)) == lax.broadcasted_iota(jnp.int32, (top_count, pairs), 0)
    turns = lax.broadcasted_iota(jnp.int32, (top_count, pairs), 1)
    high, low = (
        nt(jnp.where(which, part.astype(f32), 0.0).astype(bf16), owner)
        for part in (turns >> 8, turns & 255)
    )
    turn_of = high * 256.0 + low
    far = float(2 * pairs)
    ids = lax.broadcasted_iota(jnp.int32, (128, tokens), 0)
    turn_row = jnp.full((128, tokens), far, f32)
    for k in range(top_count):
        turn_row = jnp.where(chosen[k : k + 1, :] == ids, turn_of[k : k + 1, :], turn_row)
    turn_at = turn_row.T
    for e in range(experts_all):
        row = turn_row[e : e + 1, :]
        rank = jnp.sum(jnp.where(turn_at[:, e : e + 1] < row, 1.0, 0.0), axis=0, keepdims=True)
        yield jnp.where((row < far) & (rank < capacity), rank, -1.0)


def partners(ex, ne):
    if ne != 4:
        raise ValueError("expert")
    return ex + 1 - 2 * lax.rem(ex, 2), lax.rem(ex + 2, 4)


def front_kernel(sizes, capacity, defs, *refs):
    r = named(defs, refs)
    ne, nz, nd = sizes
    ex, me = lax.axis_index("expert"), lax.axis_index("context")
    tokens, width = r.tokens.shape
    kv_width = r.w_key.shape[1]
    slices = kv_width // 128
    quarter = HEAD_DIM // 2

    barrier = pltpu.get_barrier_semaphore()
    for step in range(1, ne):
        pl.semaphore_signal(
            barrier, inc=1, device_id={"expert": lax.rem(ex + step, ne)}, device_id_type=MESH
        )

    @pl.when(me > 0)
    def _():
        pl.semaphore_signal(barrier, inc=1, device_id={"context": me - 1}, device_id_type=MESH)

    @pl.when(me < nz - 1)
    def _():
        pl.semaphore_signal(barrier, inc=1, device_id={"context": me + 1}, device_id_type=MESH)

    loads = [
        pltpu.make_async_copy(src, dst, r.load_sem.at[i])
        for i, (src, dst) in enumerate(
            (
                (r.w_key, r.w_key_v),
                (r.w_value, r.w_value_v),
                (r.w_query, r.w_query_v),
                (r.w_out, r.w_out_v),
                (r.grad_top, r.grad_all.at[ex]),
            )
        )
    ]
    for copy in r.loads + loads:
        copy.start()
    pl.semaphore_wait(
        barrier, ne - 1 + jnp.where(me > 0, 1, 0) + jnp.where(me < nz - 1, 1, 0)
    )

    def spread(kind, step):
        src = (r.grad_top, r.tables_s)[kind]
        dst = (r.grad_all, r.tables_all)[kind]
        return pltpu.make_async_remote_copy(
            src_ref=src,
            dst_ref=dst.at[ex],
            send_sem=r.spread_send.at[kind, step],
            recv_sem=r.spread_recv.at[kind, step],
            device_id={"expert": lax.rem(ex + step, ne)},
            device_id_type=MESH,
        )

    pair = partners(ex, ne)
    halves = (pl.ds(0, tokens // 2), pl.ds(tokens // 2, tokens // 2))

    def hand(i, half, onward):
        at = halves[half]
        src = r.rows_all.at[pair[1 - i], at] if onward else r.second_s.at[at]
        dst = r.rows_all.at[pair[1 - i] if onward else ex, at]
        return pltpu.make_async_remote_copy(
            src_ref=src,
            dst_ref=dst,
            send_sem=r.hand_send.at[i, half, int(onward)],
            recv_sem=r.hand_recv.at[i, half, int(onward)],
            device_id={"expert": pair[i]},
            device_id_type=MESH,
        )

    last, helper = nz - 1, nz - 2

    def to(place, src, dst, send, recv):
        return pltpu.make_async_remote_copy(
            src_ref=src,
            dst_ref=dst,
            send_sem=send,
            recv_sem=recv,
            device_id={"context": place},
            device_id_type=MESH,
        )

    def up(j, t):
        at = r.kv_s.at[j, t]
        return to(me + 1, at, at, r.up_send.at[j, t], r.up_recv.at[j, t])

    def up_seg(j):
        at = r.seg_s.at[j]
        return to(me + 1, at, at, r.seg_send.at[j], r.seg_recv.at[j])

    ask = [
        to(helper, src, dst, r.ask_send.at[i], r.ask_recv.at[i])
        for i, (src, dst) in enumerate(
            ((r.q_s, r.q_far_s), (r.seg_s.at[last], r.seg_s.at[last]))
        )
    ]

    def answer(t):
        return [
            to(last, src.at[t], dst.at[t], r.answer_send.at[i, t], r.answer_recv.at[i, t])
            for i, (src, dst) in enumerate(
                ((r.far_head, r.far_head_in), (r.far_lse, r.far_lse_in))
            )
        ]

    for step in range(1, ne):
        spread(0, step).start()

    for copy in r.loads:
        copy.wait()

    values = r.tokens[...].astype(f32)
    inverse = lax.rsqrt(jnp.mean(values * values, axis=-1, keepdims=True) + epsilon)
    first = (values * inverse * r.gains[:1, :].astype(f32)).astype(bf16)
    r.first_s[...] = first
    cos_b, sin_b = r.base[0, pl.ds(me, 1), :], r.base[1, pl.ds(me, 1), :]
    cos_i, sin_i = r.inner[0], r.inner[1]
    cosine = cos_i * cos_b - sin_i * sin_b
    sine = sin_i * cos_b + cos_i * sin_b
    first_lanes = lax.rem(lax.broadcasted_iota(jnp.int32, (tokens, 128), 1), HEAD_DIM) < quarter
    sine = jnp.where(first_lanes, sine, -sine)
    r.turn_s[0] = cosine
    r.turn_s[1] = sine

    def rotate(x):
        swapped = jnp.where(
            first_lanes, pltpu.roll(x, 128 - quarter, 1), pltpu.roll(x, quarter, 1)
        )
        return x * cosine - swapped * sine

    loads[0].wait()
    keys = nn(first, r.w_key_v[...])
    for t in range(slices):
        at = slice(t * 128, (t + 1) * 128)
        r.kv_s[me, t, :, :128] = rotate(keys[:, at]).astype(bf16)
    loads[1].wait()
    vals = nn(first, r.w_value_v[...]).astype(bf16)
    for t in range(slices):
        r.kv_s[me, t, :, 128:] = vals[:, t * 128 : (t + 1) * 128]
    r.seg_s[me] = jnp.broadcast_to(r.seg[...].astype(f32), (8, tokens))

    @pl.when(me < helper)
    def _():
        up_seg(me).start()
        for t in range(slices):
            up(me, t).start()

    loads[2].wait()
    factor = HEAD_DIM ** (-0.5)
    low = lane_half((tokens, 128), 0)
    for t in range(slices):
        two = nn(first, r.w_query_v[:, t * 256 : (t + 1) * 256])
        left, right = rotate(two[:, :128]), rotate(two[:, 128:])
        even = jnp.where(low, left, pltpu.roll(right, HEAD_DIM, 1))
        odd = jnp.where(low, pltpu.roll(left, HEAD_DIM, 1), right)
        r.q_s[t, :tokens, :] = (even * factor).astype(bf16)
        r.q_s[t, tokens:, :] = (odd * factor).astype(bf16)

    @pl.when(me == last)
    def _():
        for copy in ask:
            copy.start()

    experts_all = r.tables_s.shape[1]
    for e, row in enumerate(slot_table(r.chosen[...], r.order[...], experts_all, capacity)):
        r.tables_s[0, e : e + 1, :] = row

    for ref in (r.acc, r.total, r.far_acc, r.far_total):
        ref[...] = jnp.zeros_like(ref)
    for ref in (r.top, r.far_top):
        ref[...] = jnp.full_like(ref, -3e38)

    def attend(j, t, queries, acc, top, total, bias):
        keys = r.kv_s[j, t, :, :128]
        vals = r.kv_s[j, t, :, 128:]
        for half in (0, 1):
            keep = lane_half((tokens, 128), half)
            zero = jnp.zeros_like(keys)
            scores = nt(jnp.where(keep, keys, zero), queries[t]) + jnp.concatenate(
                [bias[...]] * 2, axis=1
            )
            old = top[t, half : half + 1, :]
            new = jnp.maximum(old, jnp.max(scores, axis=0, keepdims=True))
            scale = jnp.exp(old - new)
            soft = jnp.exp(scores - new)
            top[t, half : half + 1, :] = new
            total[t, half : half + 1, :] = total[t, half : half + 1, :] * scale + jnp.sum(
                soft, axis=0, keepdims=True
            )
            mixed = tn(jnp.where(keep, vals, zero), soft.astype(bf16))
            a, b = half * HEAD_DIM, (half + 1) * HEAD_DIM
            acc[t, a:b, :] = acc[t, a:b, :] * scale + mixed[a:b]

    def own_slice(j, t):
        attend(j, t, r.q_s, r.acc, r.top, r.total, r.bias)

    def far_slice(j, t):
        attend(j, t, r.q_far_s, r.far_acc, r.far_top, r.far_total, r.far_bias)

    r.bias[...] = mask_bias(r.seg_s, me, me, tokens)

    @pl.loop(0, slices)
    def _(t):
        own_slice(me, t)

    @pl.when(me == helper)
    def _():
        for copy in ask:
            copy.wait_recv()
        r.far_bias[...] = mask_bias(r.seg_s, helper, last, tokens)

        @pl.loop(0, slices)
        def _(t):
            far_slice(helper, t)

    for step in range(1, nz - 1):
        j = me - step

        @pl.when((j >= 0) & (me < last))
        def _():
            up_seg(j).wait_recv()

            @pl.when(me < helper)
            def _():
                up_seg(j).start()

            r.bias[...] = mask_bias(r.seg_s, j, me, tokens)

            @pl.when(me == helper)
            def _():
                r.far_bias[...] = mask_bias(r.seg_s, j, last, tokens)

            @pl.loop(0, slices)
            def _(t):
                up(j, t).wait_recv()

                @pl.when(me < helper)
                def _():
                    up(j, t).start()

                @pl.when(me == helper)
                def _():
                    far_slice(j, t)
                    if step == nz - 2:
                        for half in (0, 1):
                            a, b = half * HEAD_DIM, (half + 1) * HEAD_DIM
                            r.far_head[t, a:b, :] = (
                                r.far_acc[t, a:b, :] / r.far_total[t, half : half + 1, :]
                            ).astype(bf16)
                        r.far_lse[t] = r.far_top[t] + jnp.log(r.far_total[t])
                        for copy in answer(t):
                            copy.start()

                own_slice(j, t)

    @pl.loop(0, slices)
    def _(t):
        r.lse_s[t] = r.top[t] + jnp.log(r.total[t])
        for half in (0, 1):
            a, b = half * HEAD_DIM, (half + 1) * HEAD_DIM
            r.acc[t, a:b, :] = r.acc[t, a:b, :] / r.total[t, half : half + 1, :]

        @pl.when(me == last)
        def _():
            for copy in answer(t):
                copy.wait_recv()
            near, far = r.lse_s[t], r.far_lse_in[t]
            top = jnp.maximum(near, far)
            both = top + jnp.log(jnp.exp(near - top) + jnp.exp(far - top))
            r.lse_s[t] = both
            near, far = jnp.exp(near - both), jnp.exp(far - both)
            for half in (0, 1):
                a, b = half * HEAD_DIM, (half + 1) * HEAD_DIM
                r.acc[t, a:b, :] = (
                    r.acc[t, a:b, :] * near[half : half + 1]
                    + r.far_head_in[t, a:b, :].astype(f32) * far[half : half + 1]
                )

    for t in range(slices):
        for half in (0, 1):
            a, b = half * HEAD_DIM, (half + 1) * HEAD_DIM
            head = r.acc[t, a:b, :].astype(bf16)
            r.heads_s[2 * t + half] = head
            for ab in (0, 1):
                h = (4 * t + 2 * half + ab) * HEAD_DIM
                r.attn_turned[h : h + HEAD_DIM, :] = head[:, ab * tokens : (ab + 1) * tokens]

    loads[3].wait()
    middle = r.tokens[...].astype(f32) + tn(r.attn_turned[...], r.w_out_v[...])
    r.middle_s[...] = middle
    inverse = lax.rsqrt(jnp.mean(middle * middle, axis=-1, keepdims=True) + epsilon)
    second = (middle * inverse * r.gains[1:, :].astype(f32)).astype(bf16)
    r.second_s[...] = second
    for i, half in ((0, 0), (1, 1), (0, 1), (1, 0)):
        hand(i, half, False).start()
    logits = nt(r.w_router_turned[...], second)
    grown = jnp.exp(logits - jnp.max(logits, axis=0, keepdims=True))
    r.tables_s[1] = grown / jnp.sum(grown, axis=0, keepdims=True)
    for step in range(1, ne):
        spread(1, step).start()
    stores = [
        pltpu.make_async_copy(src, dst, r.store_sem.at[i])
        for i, (src, dst) in enumerate(
            (
                (r.second_s, r.rows_all.at[ex]),
                (r.tables_s, r.tables_all.at[ex]),
                (r.q_s, r.q),
                (r.q_far_s, r.q_far),
                (r.kv_s, r.kv_all),
                (r.seg_s, r.seg_all),
                (r.lse_s, r.lse),
                (r.heads_s, r.heads),
                (r.middle_s, r.middle),
                (r.second_s, r.second_low),
                (r.first_s, r.first_low),
                (r.turn_s, r.turn),
            )
        )
    ]
    for copy in stores:
        copy.start()
    for copy in stores:
        copy.wait()
    for i in (0, 1):
        hand(i, i, False).wait_recv()
        hand(1 - i, i, True).start()
    loads[4].wait()
    for kind in range(2):
        for step in range(1, ne):
            spread(kind, step).wait()
    for i in (0, 1):
        hand(i, i, False).wait_send()
        hand(i, 1 - i, False).wait()
        hand(1 - i, i, True).wait()
    for step in range(nz - 1):
        j = me - step

        @pl.when((j >= 0) & (me < helper))
        def _():
            up_seg(j).wait_send()
            for t in range(slices):
                up(j, t).wait_send()

    @pl.when(me == last)
    def _():
        for copy in ask:
            copy.wait_send()

    @pl.when(me == helper)
    def _():
        for t in range(slices):
            for copy in answer(t):
                copy.wait_send()


def front(sizes, cid, capacity, hbm_ins, vmem_ins):
    ne, nz, nd = sizes
    ins = types.SimpleNamespace(**hbm_ins, **vmem_ins)
    tokens, width = ins.tokens.shape
    kv_width = ins.w_key.shape[1]
    slices, wide = kv_width // 128, 2 * tokens
    experts_all = ins.w_router_turned.shape[0]
    shape = jax.ShapeDtypeStruct
    vmem, dma = pltpu.VMEM, pltpu.SemaphoreType.DMA
    sized = dict(
        q=((slices, wide, 128), bf16),
        q_far=((slices, wide, 128), bf16),
        kv=((nz, slices, tokens, 256), bf16),
        seg=((nz, 8, tokens), f32),
        lse=((slices, 2, wide), f32),
        heads=((2 * slices, HEAD_DIM, wide), bf16),
        middle=((tokens, width), f32),
        second=((tokens, width), bf16),
        first=((tokens, width), bf16),
        turn=((2, tokens, 128), f32),
        tables=((2, experts_all, tokens), f32),
    )
    outs = dict(
        rows_all=shape((ne, tokens, width), bf16),
        grad_all=shape((ne, tokens, width), bf16),
        tables_all=shape((ne, 2, experts_all, tokens), f32),
        q=shape(*sized["q"]),
        q_far=shape(*sized["q"]),
        kv_all=shape(*sized["kv"]),
        seg_all=shape(*sized["seg"]),
        lse=shape(*sized["lse"]),
        heads=shape(*sized["heads"]),
        middle=shape(*sized["middle"]),
        second_low=shape(*sized["second"]),
        first_low=shape(*sized["first"]),
        turn=shape(*sized["turn"]),
    )
    scratch = dict(
        w_query_v=vmem(ins.w_query.shape, bf16),
        w_key_v=vmem(ins.w_key.shape, bf16),
        w_value_v=vmem(ins.w_value.shape, bf16),
        w_out_v=vmem(ins.w_out.shape, bf16),
        attn_turned=vmem((width, tokens), bf16),
        acc=vmem((slices, 128, wide), f32),
        top=vmem((slices, 2, wide), f32),
        total=vmem((slices, 2, wide), f32),
        bias=vmem((tokens, tokens), f32),
        far_acc=vmem((slices, 128, wide), f32),
        far_top=vmem((slices, 2, wide), f32),
        far_total=vmem((slices, 2, wide), f32),
        far_bias=vmem((tokens, tokens), f32),
        far_head=vmem((slices, 128, wide), bf16),
        far_lse=vmem((slices, 2, wide), f32),
        far_head_in=vmem((slices, 128, wide), bf16),
        far_lse_in=vmem((slices, 2, wide), f32),
        load_sem=dma((5,)),
        store_sem=dma((12,)),
        spread_send=dma((2, ne)),
        spread_recv=dma((2, ne)),
        hand_send=dma((2, 2, 2)),
        hand_recv=dma((2, 2, 2)),
        up_send=dma((nz, slices)),
        up_recv=dma((nz, slices)),
        seg_send=dma((nz,)),
        seg_recv=dma((nz,)),
        ask_send=dma((2,)),
        ask_recv=dma((2,)),
        answer_send=dma((2, slices)),
        answer_recv=dma((2, slices)),
        **{k + "_s": vmem(*v) for k, v in sized.items()},
    )
    return call_named(
        functools.partial(front_kernel, sizes, capacity),
        hbm_ins, vmem_ins, outs, scratch, cid, 60 << 20, tuple(outs),
    )


class Line:
    def __init__(self, nz, held, came, send, recv):
        if nz != 4:
            raise ValueError("context")
        self.nz, self.held, self.came, self.send, self.recv = nz, held, came, send, recv
        self.me = lax.axis_index("context")

    @staticmethod
    def scratch(nz, chunks, rows, width):
        return [
            pltpu.VMEM((chunks, nz, rows, width), bf16),
            pltpu.VMEM((chunks, nz, rows, width), bf16),
            pltpu.SemaphoreType.DMA((chunks, nz)),
            pltpu.SemaphoreType.DMA((chunks, nz)),
        ]

    routes = {
        (0, 3): (1, 3),
        (0, 2): (1, 2),
        (0, 1): (1, 0),
        (3, 0): (2, 0),
        (3, 1): (2, 1),
        (3, 2): (2, 3),
        (1, 0): (0, 1),
        (2, 3): (3, 2),
        (1, 3): (3, 1),
        (1, 2): (2, 2),
        (2, 0): (0, 2),
        (2, 1): (1, 1),
    }

    def copy(self, k, place, s):
        target, slot = self.routes[place, s]
        return pltpu.make_async_remote_copy(
            src_ref=self.held.at[k, s],
            dst_ref=self.came.at[k, slot],
            send_sem=self.send.at[k, s],
            recv_sem=self.recv.at[k, slot],
            device_id={"context": target},
            device_id_type=MESH,
        )

    def start(self, k, moves):
        for place in range(self.nz):
            pieces = [s for p, s in moves if p == place]
            if pieces:

                @pl.when(self.me == place)
                def _():
                    for s in pieces:
                        self.copy(k, place, s).start()

    def far_piece(self, place, which):
        return 3 - which if place < 2 else which

    def cross(self, k, which, place):
        self.start(k, [(place, self.far_piece(place, which))])

    def left(self, k, which, place):
        @pl.when(self.me == place)
        def _():
            self.copy(k, place, self.far_piece(place, which)).wait_send()

    def straight(self, k):
        self.start(k, [(1, 0), (2, 3)])

    def ends(self, k, place):
        self.start(k, [(place, 1 if place == 0 else 2)])

    def join(self, k, which, place):
        s = self.far_piece(place, which)

        @pl.when(self.me == place)
        def _():
            self.copy(k, 0 if place == 1 else 3, s).wait_recv()
            add_rows(self.held, (k, s), self.came, (k, s), self.held.shape[2])
            self.copy(k, place, s).start()

    def total(self, k, put):
        for place in range(self.nz):

            @pl.when(self.me == place)
            def _():
                senders = [(p, s) for (p, s), (t, _) in self.routes.items() if t == place == s]
                for p, s in senders:
                    self.copy(k, p, s).wait_recv()
                for at in range(0, self.held.shape[2], 16):
                    rows = slice(at, at + 16)
                    value = self.held[k, place, rows].astype(f32)
                    for move in senders:
                        value = value + self.came[k, self.routes[move][1], rows].astype(f32)
                    put(at, value)
                for s in range(self.nz):
                    if s != place and (place in (1, 2) or abs(s - place) == 1):
                        self.copy(k, place, s).wait_send()


def experts_kernel(sizes, cap, defs, *refs):
    r = named(defs, refs)
    ne, nz, nd = sizes
    ex, dp, ctx = (lax.axis_index(a) for a in ("expert", "dp", "context"))
    local, width, hid = r.w_gate.shape
    tokens = r.rows_all.shape[1]
    gate_rows, down_rows = width // (nz * nd), hid // (nz * nd)
    line = Line(nz, r.held_s, *r.line)

    barrier = pltpu.get_barrier_semaphore()
    for axis, place, size in (("dp", dp, nd), ("context", ctx, nz)):
        for step in range(1, size):
            pl.semaphore_signal(
                barrier, inc=1, device_id={axis: lax.rem(place + step, size)}, device_id_type=MESH
            )

    def weights(e, slot):
        return [
            pltpu.make_async_copy(src, dst, r.weight_sem.at[slot, i])
            for i, (src, dst) in enumerate(
                (
                    (r.w_gate.at[e], r.both.at[slot, :, pl.ds(0, hid)]),
                    (r.w_up.at[e], r.both.at[slot, :, pl.ds(hid, hid)]),
                    (r.w_down.at[e], r.down.at[slot]),
                )
            )
        ]

    for copy in r.loads + weights(0, 0):
        copy.start()
    pl.semaphore_wait(barrier, nd + nz - 2)
    for copy in r.loads:
        copy.wait()

    def cores(k, step):
        other = lax.rem(dp + step, nd)
        return pltpu.make_async_remote_copy(
            src_ref=r.made.at[:, other],
            dst_ref=r.from_dp.at[step - 1, k],
            send_sem=r.dp_send.at[k, step],
            recv_sem=r.dp_recv.at[k, step],
            device_id={"dp": other},
            device_id_type=MESH,
        )

    def keep(k):
        return pltpu.make_async_copy(r.held_s.at[k], r.held.at[k], r.held_sem.at[k])

    def add_cores(k):
        for step in range(1, nd):
            cores(k, step).wait_recv()
            for z in range(nz):
                add_rows(r.held_s, (k, z), r.from_dp, (step - 1, k, z), gate_rows + down_rows)

        @pl.when(k > 0)
        def _():
            keep(k).start()

    row_id = lax.broadcasted_iota(jnp.int32, (cap, tokens), 0).astype(f32)

    @pl.loop(0, local)
    def _(e):
        slot = lax.rem(e, 2)
        own = pl.ds(pl.multiple_of(e * cap, 16), cap)
        for src in range(ne):
            at = pl.ds(src * cap, cap)
            hits = r.tables_all[src, 0, pl.ds(ex * local + e, 1), :] == row_id
            gate_row = r.tables_all[src, 1, pl.ds(ex * local + e, 1), :]
            gate = jnp.sum(jnp.where(hits, gate_row, 0.0), axis=1, keepdims=True)
            low = jnp.where(hits, 1.0, 0.0).astype(bf16)
            r.hits[src, own, :] = low
            r.gate_s[at, :] = jnp.broadcast_to(gate, (cap, 128))
            r.x_s[at, :] = nn(low, r.rows_all[src]).astype(bf16)
            og = nn(low, r.grad_all[src])
            r.og_s[at, :] = og.astype(bf16)
            r.sg_s[at, :] = (og * gate).astype(bf16)
        for copy in weights(e, slot):
            copy.wait()

        @pl.when(e < local - 1)
        def _():
            for copy in weights(e + 1, 1 - slot):
                copy.start()

        pre = nn(r.x_s[...], r.both[slot])

        @pl.when(e > 0)
        def _():
            add_cores(e - 1)

        @pl.when(e == 1)
        def _():
            for place in (0, 3):
                line.cross(0, 0, place)
            line.straight(0)

        @pl.when(e == 2)
        def _():
            for place in (0, 3):
                line.ends(0, place)

        @pl.when(e == 3)
        def _():
            for place in (1, 2):
                line.join(0, 1, place)

        gate_pre, up_pre = pre[:, :hid], pre[:, hid:]
        sig = jax.nn.sigmoid(gate_pre)
        silu = gate_pre * sig
        r.hidden[...] = (silu * up_pre).astype(bf16)
        hidden_back = nt(r.sg_s[...], r.down[slot])
        r.pre_back[:, :hid] = (
            hidden_back * up_pre * sig * (1.0 + gate_pre * (1.0 - sig))
        ).astype(bf16)
        r.pre_back[:, hid:] = (hidden_back * silu).astype(bf16)
        produced = nn(r.hidden[...], r.down[slot])
        pair = jnp.sum(r.og_s[...].astype(f32) * produced, axis=1, keepdims=True)
        weighed = (produced * r.gate_s[:, :1]).astype(bf16)
        for src in range(ne):
            a, b = src * cap, (src + 1) * cap
            r.weighed[src, own, :] = weighed[a:b]
            r.soft_part[src, pl.ds(e, 1), :] = jnp.sum(
                r.hits[src, own, :].astype(f32) * pair[a:b], axis=0, keepdims=True
            )
        back = nt(r.pre_back[...], r.both[slot]).astype(bf16)
        for src in range(ne):
            r.back_rows[src, own, :] = back[src * cap : (src + 1) * cap]

        @pl.when(e == 1)
        def _():
            for place in (0, 3):
                line.cross(0, 1, place)

        @pl.when(e == 2)
        def _():
            for place in (1, 2):
                line.join(0, 0, place)

        @pl.when(e > 0)
        def _():
            for step in range(1, nd):
                cores(e - 1, step).wait_send()

        r.made[:, :, :gate_rows, :] = (
            tn(r.x_s[...], r.pre_back[...]).astype(bf16).reshape(nz, nd, gate_rows, 2 * hid)
        )
        r.made[:, :, gate_rows:, :] = (
            tn(r.hidden[...], r.sg_s[...]).astype(bf16).reshape(nz, nd, down_rows, width)
        )
        for step in range(1, nd):
            cores(e, step).start()
        r.held_s[e] = r.made[:, dp]

    stores = []
    for kind, (rows, out) in enumerate(((r.back_rows, r.back_part), (r.weighed, r.out_part))):
        for src in range(ne):
            r.sums[kind, src] = tn(r.hits[src], rows[src]).astype(bf16)
            stores.append(
                pltpu.make_async_copy(r.sums.at[kind, src], out.at[src], r.store_sem.at[kind, src])
            )
            stores[-1].start()
    add_cores(local - 1)

    def put(at, value):
        r.shard[at : at + 16, :] = value

    for place in (0, 3):
        for which in (0, 1):
            line.left(0, which, place)
    line.total(0, put)
    for step in range(1, nd):
        cores(local - 1, step).wait_send()
    for k in range(1, local):
        keep(k).wait()
    for copy in stores:
        copy.wait()


def experts(sizes, cid, cap, kept, read):
    ne, nz, nd = sizes
    local, width, hid = kept["w_gate"].shape
    tokens = read["rows_all"].shape[1]
    piece = width // (nz * nd) + hid // (nz * nd)
    shape, vmem, dma = jax.ShapeDtypeStruct, pltpu.VMEM, pltpu.SemaphoreType.DMA
    held, *line = Line.scratch(nz, local, piece, width)
    line[0] = vmem((1, nz, piece, width), bf16)
    outs = dict(
        held=shape((local, nz, piece, width), bf16),
        out_part=shape((ne, tokens, width), bf16),
        back_part=shape((ne, tokens, width), bf16),
        soft_part=shape((ne, local, tokens), f32),
        shard=shape((piece, width), f32),
    )
    rows = ne * cap
    scratch = dict(
        both=vmem((2, width, 2 * hid), bf16),
        down=vmem((2, hid, width), bf16),
        x_s=vmem((rows, width), bf16),
        og_s=vmem((rows, width), bf16),
        sg_s=vmem((rows, width), bf16),
        gate_s=vmem((rows, 128), f32),
        hidden=vmem((rows, hid), bf16),
        pre_back=vmem((rows, 2 * hid), bf16),
        hits=vmem((ne, local * cap, tokens), bf16),
        weighed=vmem((ne, local * cap, width), bf16),
        back_rows=vmem((ne, local * cap, width), bf16),
        sums=vmem((2, ne, tokens, width), bf16),
        made=vmem((nz, nd, piece, width), bf16),
        from_dp=vmem((nd - 1, local, nz, piece, width), bf16),
        held_s=held,
        line=line,
        weight_sem=dma((2, 3)),
        dp_send=dma((local, nd)),
        dp_recv=dma((local, nd)),
        held_sem=dma((local,)),
        store_sem=dma((2, ne)),
    )
    return call_named(
        functools.partial(experts_kernel, sizes, cap),
        kept, read, outs, scratch, cid, 62 << 20, ("held", "out_part", "back_part"),
    )


class Spread:
    def __init__(self, sizes, made, from_dp, held, from_ex, line, from_z, send, recv):
        self.sizes, self.made, self.from_dp, self.held = sizes, made, from_dp, held
        self.from_ex, self.line, self.from_z, self.send, self.recv = from_ex, line, from_z, send, recv
        self.places = tuple(lax.axis_index(a) for a in ("dp", "expert", "context"))

    @staticmethod
    def scratch(sizes, rows, width):
        ne, nz, nd = sizes
        most = max(sizes)
        return [
            pltpu.VMEM((nd - 1, ne, nz, rows, width), bf16),
            pltpu.VMEM((ne, nz, rows, width), bf16),
            pltpu.VMEM((ne - 1, nz, rows, width), bf16),
            pltpu.VMEM((nz, rows, width), bf16),
            pltpu.VMEM((nz - 1, rows, width), bf16),
            pltpu.SemaphoreType.DMA((3, most)),
            pltpu.SemaphoreType.DMA((3, most)),
        ]

    def copy(self, stage, step):
        ne, nz, nd = self.sizes
        axis, size = (("dp", nd), ("expert", ne), ("context", nz))[stage]
        other = lax.rem(self.places[stage] + step, size)
        src = (
            self.made.at[:, :, other]
            if stage == 0
            else self.held.at[other] if stage == 1 else self.line.at[other]
        )
        dst = (self.from_dp, self.from_ex, self.from_z)[stage].at[step - 1]
        return pltpu.make_async_remote_copy(
            src_ref=src,
            dst_ref=dst,
            send_sem=self.send.at[stage, step],
            recv_sem=self.recv.at[stage, step],
            device_id={axis: other},
            device_id_type=MESH,
        )

    def others(self, stage):
        ne, nz, nd = self.sizes
        return range(1, (nd, ne, nz)[stage])

    def over_dp(self):
        for step in self.others(0):
            self.copy(0, step).start()

    def made_free(self):
        for step in self.others(0):
            self.copy(0, step).wait_send()

    def over_expert(self):
        ne, nz, _ = self.sizes
        for step in self.others(0):
            self.copy(0, step).wait_recv()

        @pl.loop(0, ne * nz)
        def _(i):
            a = lax.div(i, nz)
            b = i - a * nz
            total = self.made[a, b, self.places[0]].astype(f32)
            for step in self.others(0):
                total = total + self.from_dp[step - 1, a, b].astype(f32)
            self.held[a, b] = total.astype(bf16)

        for step in self.others(1):
            self.copy(1, step).start()

    def over_context(self):
        nz = self.sizes[1]
        for step in self.others(1):
            self.copy(1, step).wait_recv()

        @pl.loop(0, nz)
        def _(b):
            total = self.held[self.places[1], b].astype(f32)
            for step in self.others(1):
                total = total + self.from_ex[step - 1, b].astype(f32)
            self.line[b] = total.astype(bf16)

        for step in self.others(2):
            self.copy(2, step).start()

    def finish(self, out):
        for step in self.others(2):
            self.copy(2, step).wait_recv()
        total = self.line[self.places[2]].astype(f32)
        for step in self.others(2):
            total = total + self.from_z[step - 1].astype(f32)
        out[...] = total
        for stage in (1, 2):
            for step in self.others(stage):
                self.copy(stage, step).wait_send()


class Fold:
    def __init__(self, ex, parts, own, mine, passing, came, load, send, recv):
        self.ex, self.parts, self.own, self.mine, self.passing, self.came = (
            ex, parts, own, mine, passing, came,
        )
        self.load, self.send, self.recv = load, send, recv
        self.pair = partners(ex, 4)
        half = parts.shape[1] // 2
        self.halves = (pl.ds(0, half), pl.ds(half, half))

    @staticmethod
    def scratch(rows, width):
        half = (2, rows // 2, width)
        return [
            pltpu.VMEM((rows, width), bf16),
            pltpu.VMEM(half, bf16),
            pltpu.VMEM(half, bf16),
            pltpu.VMEM((2, rows, width), bf16),
            pltpu.SemaphoreType.DMA((3,)),
            pltpu.SemaphoreType.DMA((3, 2)),
            pltpu.SemaphoreType.DMA((3, 2)),
        ]

    def copy(self, stage, i):
        src, dst = (
            (self.parts.at[3 - self.ex, self.halves[i]], self.passing.at[i]),
            (self.parts.at[self.pair[i], self.halves[i]], self.came.at[i, self.halves[i]]),
            (self.mine.at[i], self.came.at[i, self.halves[1 - i]]),
        )[stage]
        return pltpu.make_async_remote_copy(
            src_ref=src,
            dst_ref=dst,
            send_sem=self.send.at[stage, i],
            recv_sem=self.recv.at[stage, i],
            device_id={"expert": self.pair[i]},
            device_id_type=MESH,
        )

    def loads(self):
        return [
            pltpu.make_async_copy(self.parts.at[self.ex], self.own, self.load.at[2])
        ] + [
            pltpu.make_async_copy(
                self.parts.at[self.pair[i], self.halves[1 - i]], self.mine.at[i], self.load.at[i]
            )
            for i in (0, 1)
        ]

    def begin(self):
        for stage in (0, 1):
            for i in (0, 1):
                self.copy(stage, i).start()
        for copy in self.loads():
            copy.start()

    def onward(self):
        for copy in self.loads():
            copy.wait()
        for i in (0, 1):
            self.copy(0, 1 - i).wait_recv()
            add_rows(self.mine, (i,), self.passing, (1 - i,), self.mine.shape[1])
            self.copy(2, i).start()

    def arrive(self):
        for stage in (1, 2):
            for i in (0, 1):
                self.copy(stage, i).wait_recv()

    def finish(self):
        for stage in range(3):
            for i in (0, 1):
                self.copy(stage, i).wait_send()


def tail_kernel(sizes, defs, *refs):
    r = named(defs, refs)
    ne, nz, nd = sizes
    ex, me, dp = (lax.axis_index(a) for a in ("expert", "context", "dp"))
    tokens, width = r.tokens.shape
    slices = r.kv_all.shape[1]
    kv_width = slices * 128
    group = width // ne
    last, helper = nz - 1, nz - 2

    barrier = pltpu.get_barrier_semaphore()
    for axis, place, size in (("expert", ex, ne), ("context", me, nz), ("dp", dp, nd)):
        for step in range(1, size):
            pl.semaphore_signal(
                barrier, inc=1, device_id={axis: lax.rem(place + step, size)}, device_id_type=MESH
            )
    for copy in r.loads:
        copy.start()
    pl.semaphore_wait(barrier, ne + nz + nd - 3)

    line = Line(nz, *r.line)
    proj = Spread(sizes, r.made, *r.proj)
    query = Spread(sizes, r.made, *r.query)
    kv = Spread(sizes, r.made, *r.kv)
    small = Spread(sizes, r.small_made, *r.small)

    chunks = range(r.held_in.shape[0] - 1)
    held_copies = [
        pltpu.make_async_copy(r.held_in.at[k + 1], line.held.at[k], r.held_sem.at[k])
        for k in chunks
    ]
    for copy in held_copies:
        copy.start()

    back = Fold(ex, r.back_in, *r.back)
    out = Fold(ex, r.out_in, *r.out)

    def gates_copy(step):
        other = lax.rem(ex + step, ne)
        return pltpu.make_async_remote_copy(
            src_ref=r.soft_in.at[other],
            dst_ref=r.soft_all.at[ex],
            send_sem=r.gates_send.at[step],
            recv_sem=r.gates_recv.at[step],
            device_id={"expert": other},
            device_id_type=MESH,
        )

    back.begin()
    for step in range(1, ne):
        gates_copy(step).start()
    loads = [
        pltpu.make_async_copy(src, dst, r.load_sem.at[i])
        for i, (src, dst) in enumerate(
            (
                (r.soft_in.at[ex], r.soft_all.at[ex]),
                (r.w_out, r.w_out_v),
                (r.w_query, r.w_query_v),
                (r.w_key, r.w_key_v),
                (r.w_value, r.w_value_v),
                (r.tables_all.at[ex], r.tables_own),
            )
        )
    ]
    for copy in loads:
        copy.start()
    for k in chunks:
        held_copies[k].wait()
        if k == 0:
            for place in (0, 3):
                line.cross(0, 0, place)
    for k in chunks:
        line.straight(k)
    for copy in r.loads + loads:
        copy.wait()
    for t in range(2 * slices):
        for ab in (0, 1):
            h = 2 * t + ab
            r.attn_turned[h * HEAD_DIM : (h + 1) * HEAD_DIM, :] = r.heads[
                t, :, ab * tokens : (ab + 1) * tokens
            ]

    back.onward()
    for place in (0, 3):
        line.cross(0, 1, place)
    for place in (1, 2):
        line.join(0, 0, place)
    for place in (0, 3):
        line.left(0, 0, place)
        line.cross(1, 0, place)
    for place in (1, 2):
        line.join(0, 1, place)
    for place in (0, 3):
        line.left(0, 1, place)
        line.cross(1, 1, place)
    for step in range(1, ne):
        gates_copy(step).wait_recv()
    back.arrive()
    out.begin()
    soft_back = jnp.concatenate([r.soft_all[i] for i in range(ne)], axis=0)
    router_soft = r.tables_own[1]
    logit_back = (
        router_soft * (soft_back - jnp.sum(router_soft * soft_back, axis=0, keepdims=True))
    ).astype(bf16)
    second_back = back.own[...].astype(f32) + tn(logit_back, r.w_router_turned[...])
    for i in (0, 1):
        second_back = second_back + back.came[i].astype(f32)
    middle = r.middle[...]
    inverse = lax.rsqrt(jnp.mean(middle * middle, axis=-1, keepdims=True) + epsilon)
    normed = middle * inverse
    scaled = second_back * r.gains[1:, :].astype(f32)
    moe_gain_grad = jnp.sum(second_back * normed, axis=0, keepdims=True)
    middle_grad = r.grad_top[...].astype(f32) + inverse * (
        scaled - normed * jnp.mean(scaled * normed, axis=-1, keepdims=True)
    )
    r.middle_grad[...] = middle_grad
    r.branch[...] = middle_grad.astype(bf16)
    experts_all = logit_back.shape[0]
    r.small_rows[...] = jnp.zeros_like(r.small_rows)
    r.small_rows[:experts_all, :] = nn(logit_back, r.second_low[...])
    r.small_rows[experts_all : experts_all + 1, :] = moe_gain_grad

    def to(place, src, dst, send, recv):
        return pltpu.make_async_remote_copy(
            src_ref=src,
            dst_ref=dst,
            send_sem=send,
            recv_sem=recv,
            device_id={"context": place},
            device_id_type=MESH,
        )

    def ask(t):
        return [
            to(helper, src.at[t], dst.at[t], r.ask_send.at[i, t], r.ask_recv.at[i, t])
            for i, (src, dst) in enumerate(((r.do, r.far_do), (r.stats, r.far_stats)))
        ]

    def answer(t):
        return to(
            last, r.far_dq_low.at[t], r.dq_came.at[t], r.answer_send.at[t], r.answer_recv.at[t]
        )

    @pl.loop(0, slices)
    def _(t):
        at = pl.ds(pl.multiple_of(t * 256, 256), 256)
        turned = nt(r.w_out_v[at, :], r.branch[...]).astype(bf16)
        r.stats[t, 0] = r.lse[t]
        for half in (0, 1):
            a, b = half * HEAD_DIM, (half + 1) * HEAD_DIM
            for ab in (0, 1):
                c = (2 * half + ab) * HEAD_DIM
                r.do[t, a:b, ab * tokens : (ab + 1) * tokens] = turned[c : c + HEAD_DIM]
            r.stats[t, 1, half : half + 1, :] = jnp.sum(
                r.do[t, a:b, :].astype(f32) * r.heads[2 * t + half].astype(f32),
                axis=0,
                keepdims=True,
            )

        @pl.when(me == last)
        def _():
            for copy in ask(t):
                copy.start()

    @pl.loop(0, ne)
    def _(g):
        at = pl.ds(pl.multiple_of(g * group, group), group)
        grad = nn(r.attn_turned[at, :], r.branch[...])
        r.made[g] = grad.reshape((nz, nd, group // (nz * nd), width)).astype(bf16)

    proj.over_dp()
    for which in (0, 1):
        line.left(1, which, 0)
        line.cross(2, which, 0)
    proj.over_expert()
    out.onward()
    line.join(1, 0, 2)

    r.dq[...] = jnp.zeros_like(r.dq)
    r.far_dq[...] = jnp.zeros_like(r.far_dq)

    def mine(j):
        return me == last if j == last else (j <= me) & (me < last)

    for j in range(nz):

        @pl.when(mine(j))
        def _():
            r.bias[j] = mask_bias(r.seg_all, j, me, tokens)

    @pl.when(me == helper)
    def _():
        for j in range(last):
            r.far_bias[j] = mask_bias(r.seg_all, j, last, tokens)

    def back_slice(j, t, queries, do, stats, dq, bias):
        keys = r.kv_all[j, t, :, :128]
        vals = r.kv_all[j, t, :, 128:]
        dks, dvs = [], []
        for half in (0, 1):
            keep = lane_half((tokens, 128), half)
            zero = jnp.zeros_like(keys)
            keys_half = jnp.where(keep, keys, zero)
            scores = nt(keys_half, queries[t]) + jnp.concatenate([bias[j]] * 2, axis=1)
            soft = jnp.exp(scores - stats[t, 0, half : half + 1, :])
            soft_grad = nn(jnp.where(keep, vals, zero), do[t])
            back = (soft * (soft_grad - stats[t, 1, half : half + 1, :])).astype(bf16)
            dvs.append(nt(soft.astype(bf16), do[t]))
            dks.append(nn(back, queries[t]))
            dq[t] += tn(keys_half, back)
        low = lane_half((tokens, 128), 0)
        return jnp.concatenate(
            [jnp.where(low, dks[0], dks[1]), jnp.where(low, dvs[0], dvs[1])], axis=1
        )

    def give(j, t):
        return to(
            me - 1, r.kv_part.at[j, t], r.kv_came.at[j, t], r.kv_send.at[j, t], r.kv_recv.at[j, t]
        )

    @pl.loop(0, slices)
    def _(t):
        for j in range(nz):

            @pl.when(mine(j))
            def _():
                r.kv_sum[j] = back_slice(j, t, r.q, r.do, r.stats, r.dq, r.bias)

        @pl.when(me == helper)
        def _():
            for copy in ask(t):
                copy.wait_recv()
            for j in range(last):
                r.kv_sum[j] += back_slice(
                    j, t, r.q_far, r.far_do, r.far_stats, r.far_dq, r.far_bias
                )
                if j < helper:
                    r.kv_part[j, t] = r.kv_sum[j].astype(bf16)
                    give(j, t).start()
            r.far_dq_low[t] = r.far_dq[t].astype(bf16)
            answer(t).start()

        for j in range(helper):

            @pl.when((j < me) & (me < helper))
            def _():
                r.kv_part[j, t] = r.kv_sum[j].astype(bf16)

        r.own_kv[t] = r.kv_sum[me]

        @pl.when(t == 0)
        def _():
            line.join(1, 1, 2)

    for which in (0, 1):
        line.cross(2, which, 3)

    @pl.when(me == last)
    def _():
        @pl.loop(0, slices)
        def _(t):
            answer(t).wait_recv()
            r.dq[t] += r.dq_came[t].astype(f32)

    quarter = HEAD_DIM // 2
    cos_q, sin_q = (
        jnp.concatenate([r.turn[i].T[:quarter]] * 2, axis=1) * HEAD_DIM ** (-0.5) for i in (0, 1)
    )
    for t in range(slices):
        for half in (0, 1):
            a = half * HEAD_DIM
            first = r.dq[t, a : a + quarter, :]
            second = r.dq[t, a + quarter : a + 2 * quarter, :]
            turned = jnp.concatenate(
                [first * cos_q + second * sin_q, second * cos_q - first * sin_q], axis=0
            )
            pair = jnp.concatenate([turned[:, :tokens], turned[:, tokens:]], axis=0)
            at = (2 * t + half) * 128
            r.back_s[:, at : at + 128] = pair.T.astype(bf16)

    def make(a, b):
        @pl.loop(0, ne)
        def _(g):
            at = pl.ds(pl.multiple_of(g * group, group), group)
            grad = tn(r.first_low[:, at], r.back_s[:, a:b])
            r.made[g] = grad.reshape((nz, nd, group // (nz * nd), b - a)).astype(bf16)

    proj.made_free()
    make(0, width)
    query.over_dp()
    for which in (0, 1):
        line.join(1, which, 1)
    for which in (0, 1):
        line.join(2, which, 2)
    for k in chunks:
        line.ends(k, 0)
    line.ends(0, 3)
    query.over_expert()

    @pl.loop(0, slices)
    def _(t):
        for j in range(helper):

            @pl.when((j < me) & (me < helper))
            def _():
                give(j, t).wait_recv()
                r.kv_part[j, t] = (
                    r.kv_part[j, t].astype(f32) + r.kv_came[j, t].astype(f32)
                ).astype(bf16)
                give(j, t).start()

        @pl.when(me < helper)
        def _():
            give(me, t).wait_recv()
            r.own_kv[t] += r.kv_came[me, t].astype(f32)

    for which in (0, 1):
        line.join(2, which, 1)
    for k in chunks[1:]:
        line.ends(k, 3)
    cos_k, sin_k = r.turn[0], r.turn[1]
    first_lanes = lax.rem(lax.broadcasted_iota(jnp.int32, (tokens, 128), 1), HEAD_DIM) < quarter
    for t in range(slices):
        grad = r.own_kv[t, :, :128]
        swapped = jnp.where(
            first_lanes, pltpu.roll(grad, 128 - quarter, 1), pltpu.roll(grad, quarter, 1)
        )
        r.back_s[:, width + t * 128 : width + (t + 1) * 128] = (
            grad * cos_k + swapped * sin_k
        ).astype(bf16)
        at = width + kv_width + t * 128
        r.back_s[:, at : at + 128] = r.own_kv[t, :, 128:].astype(bf16)
    query.made_free()
    make(width, width + 2 * kv_width)
    kv.over_dp()
    proj.over_context()

    first_back = nt(r.back_s[:, :width], r.w_query_v[...])
    first_back = first_back + nt(r.back_s[:, width : width + kv_width], r.w_key_v[...])
    first_back = first_back + nt(r.back_s[:, width + kv_width :], r.w_value_v[...])
    values = r.tokens[...].astype(f32)
    inverse = lax.rsqrt(jnp.mean(values * values, axis=-1, keepdims=True) + epsilon)
    normed = values * inverse
    scaled = first_back * r.gains[:1, :].astype(f32)
    r.small_rows[experts_all + 1 : experts_all + 2, :] = jnp.sum(
        first_back * normed, axis=0, keepdims=True
    )
    r.input_grad[...] = r.middle_grad[...] + inverse * (
        scaled - normed * jnp.mean(scaled * normed, axis=-1, keepdims=True)
    )
    small_turned = r.small_rows[...].T
    r.small_made[...] = small_turned.reshape(r.small_made.shape).astype(bf16)
    small.over_dp()
    kv.over_expert()
    small.over_expert()
    query.over_context()

    out.arrive()

    @pl.loop(0, tokens // 16)
    def _(i):
        at = pl.ds(pl.multiple_of(i * 16, 16), 16)
        total = r.middle[at, :] + out.own[at, :].astype(f32)
        for i in (0, 1):
            total = total + out.came[i, at, :].astype(f32)
        r.layer_out[at, :] = total

    kv.over_context()
    small.over_context()
    kv.made_free()
    small.made_free()
    for group_sum, target in zip((proj, query, kv, small), r.sums_out + [r.small_sum]):
        group_sum.finish(target)
    r.router_out[...] = r.small_sum[:, :experts_all]
    turned = r.small_sum[...].T
    r.gains_out[0] = turned[experts_all + 1 : experts_all + 2]
    r.gains_out[1] = turned[experts_all : experts_all + 1]
    gate_out, up_out, down_out = r.experts_out
    gate_rows, hid = gate_out.shape[1:]

    def put(k, at, value):
        if at < gate_rows:
            gate_out[k, at : at + 16, :] = value[:, :hid]
            up_out[k, at : at + 16, :] = value[:, hid:]
        else:
            down_out[k, at - gate_rows : at - gate_rows + 16, :] = value

    for at in range(0, r.first_shard.shape[0], 16):
        put(0, at, r.first_shard[at : at + 16, :])
    for which in (0, 1):
        line.left(1, which, 3)
        line.left(2, which, 3)
        line.left(2, which, 0)
    for k in chunks:
        line.total(k, functools.partial(put, k + 1))
    back.finish()
    out.finish()
    for step in range(1, ne):
        gates_copy(step).wait_send()
    for j in range(helper):

        @pl.when((j < me) & (me < last))
        def _():
            for t in range(slices):
                give(j, t).wait_send()

    @pl.when(me == last)
    def _():
        for t in range(slices):
            for copy in ask(t):
                copy.wait_send()

    @pl.when(me == helper)
    def _():
        for t in range(slices):
            answer(t).wait_send()


def tail(sizes, cid, hidden, hbm_ins, vmem_ins):
    ne, nz, nd = sizes
    ins = types.SimpleNamespace(**hbm_ins, **vmem_ins)
    tokens, width = ins.tokens.shape
    slices, wide, _ = ins.q.shape
    chunks, _, piece, _ = ins.held_in.shape
    kv_shape = ins.kv_all.shape[1:]
    kv_cols = slices * 256
    rows = width // (ne * nz * nd)
    gate_rows = width // (nz * nd)
    shard = lambda *shape: jax.ShapeDtypeStruct(shape, f32)
    outs = dict(
        layer_out=shard(tokens, width),
        input_grad=shard(tokens, width),
        sums_out=[shard(rows, c) for c in (width, width, kv_cols)],
        router_out=shard(rows, ins.w_router_turned.shape[0]),
        gains_out=shard(2, 1, rows),
        experts_out=[
            shard(chunks, gate_rows, hidden),
            shard(chunks, gate_rows, hidden),
            shard(chunks, piece - gate_rows, width),
        ],
    )
    dma = pltpu.SemaphoreType.DMA
    vmem = pltpu.VMEM
    scratch = dict(
        back=Fold.scratch(tokens, width),
        out=Fold.scratch(tokens, width),
        soft_all=vmem(ins.soft_in.shape, f32),
        w_out_v=vmem(ins.w_out.shape, bf16),
        w_query_v=vmem(ins.w_query.shape, bf16),
        w_key_v=vmem(ins.w_key.shape, bf16),
        w_value_v=vmem(ins.w_value.shape, bf16),
        attn_turned=vmem((width, tokens), bf16),
        middle_grad=vmem((tokens, width), f32),
        branch=vmem((tokens, width), bf16),
        small_rows=vmem((128, width), f32),
        do=vmem((slices, 128, wide), bf16),
        stats=vmem((slices, 2, 2, wide), f32),
        bias=vmem((nz, tokens, tokens), f32),
        dq=vmem((slices, 128, wide), f32),
        dq_came=vmem((slices, 128, wide), bf16),
        far_do=vmem((slices, 128, wide), bf16),
        far_stats=vmem((slices, 2, 2, wide), f32),
        far_bias=vmem((nz - 1, tokens, tokens), f32),
        far_dq=vmem((slices, 128, wide), f32),
        far_dq_low=vmem((slices, 128, wide), bf16),
        kv_sum=vmem((nz, tokens, 256), f32),
        kv_part=vmem((nz - 2,) + kv_shape, bf16),
        kv_came=vmem((nz - 2,) + kv_shape, bf16),
        own_kv=vmem(kv_shape, f32),
        back_s=vmem((tokens, width + kv_cols), bf16),
        made=vmem((ne, nz, nd, rows, width), bf16),
        small_made=vmem((ne, nz, nd, rows, 128), bf16),
        small_sum=vmem((rows, 128), f32),
        gates_send=dma((ne,)),
        gates_recv=dma((ne,)),
        load_sem=dma((6,)),
        tables_own=vmem(ins.tables_all.shape[1:], f32),
        held_sem=dma((chunks,)),
        kv_send=dma((nz, slices)),
        kv_recv=dma((nz, slices)),
        ask_send=dma((2, slices)),
        ask_recv=dma((2, slices)),
        answer_send=dma((slices,)),
        answer_recv=dma((slices,)),
        line=Line.scratch(nz, chunks - 1, piece, width),
        proj=Spread.scratch(sizes, rows, width),
        query=Spread.scratch(sizes, rows, width),
        kv=Spread.scratch(sizes, rows, kv_cols),
        small=Spread.scratch(sizes, rows, 128),
    )
    return call_named(
        functools.partial(tail_kernel, sizes), hbm_ins, vmem_ins, outs, scratch, cid, 63 << 20, ()
    )


def deliver_kernel(parts, count, *refs):
    ins, outs, sem, held = refs[:count], refs[count : 2 * count], refs[2 * count], refs[2 * count + 1 :]
    reads = [
        pltpu.make_async_copy(
            ins[i] if part is None else ins[i].at[:, pl.ds(*part)], held[i], sem.at[0, i]
        )
        for i, part in enumerate(parts)
    ]
    writes = [pltpu.make_async_copy(held[i], outs[i], sem.at[1, i]) for i in range(count)]
    for copy in reads:
        copy.start()
    for read, write in zip(reads, writes):
        read.wait()
        write.start()
    for copy in writes:
        copy.wait()


def deliver(moved):
    arrays, parts = zip(*moved)
    hbm = pl.BlockSpec(memory_space=pl.ANY)
    shapes = [a.shape[:-1] + (part[1] if part else a.shape[-1],) for a, part in moved]
    return pl.pallas_call(
        functools.partial(deliver_kernel, parts, len(parts)),
        out_shape=[jax.ShapeDtypeStruct(shape, a.dtype) for shape, a in zip(shapes, arrays)],
        in_specs=[hbm] * len(parts),
        out_specs=[hbm] * len(parts),
        scratch_shapes=[pltpu.SemaphoreType.DMA((2, len(parts)))]
        + [pltpu.VMEM(shape, a.dtype) for shape, a in zip(shapes, arrays)],
        compiler_params=pltpu.CompilerParams(vmem_limit_bytes=60 << 20),
        name="deliver",
    )(*arrays)


def turn_tables(tokens, blocks):
    freq = rope_base ** (-2.0 * np.arange(HEAD_DIM // 2) / HEAD_DIM)
    freq = np.tile(freq, 128 // freq.size)
    inner = np.arange(tokens)[:, None] * freq
    base = tokens * np.arange(blocks)[:, None] * freq
    return tuple(
        jnp.asarray(np.stack([np.cos(a), np.sin(a)]), f32) for a in (inner, base)
    )


def body(
    sizes,
    tokens,
    attn_scale,
    w_query,
    w_key,
    w_value,
    w_out,
    moe_scale,
    w_router,
    w_gate,
    w_up,
    w_down,
    segment_ids,
    expert_choice,
    slot_order,
    out_grad,
):
    ne, nz, nd = sizes
    local_rows = tokens.shape[1]
    kv_width = w_key.shape[1]
    experts_all = w_router.shape[1]
    pair_count = local_rows * expert_choice.shape[2]
    capacity = (pair_count * 9 + 8 * experts_all - 1) // (8 * experts_all)
    inner, base = turn_tables(local_rows, nz)
    w_router_turned = w_router.T
    gains = jnp.stack([attn_scale, moe_scale])

    begun = front(
        sizes,
        1,
        capacity,
        dict(
            w_query=w_query, w_key=w_key, w_value=w_value, w_out=w_out, grad_top=out_grad[0]
        ),
        dict(
            tokens=tokens[0],
            gains=gains,
            w_router_turned=w_router_turned,
            seg=segment_ids,
            chosen=expert_choice[0].T,
            order=slot_order[0],
            inner=inner,
            base=base,
        ),
    )
    mixed = experts(
        sizes,
        2,
        capacity,
        dict(w_gate=w_gate, w_up=w_up, w_down=w_down),
        dict(rows_all=begun.rows_all, grad_all=begun.grad_all, tables_all=begun.tables_all),
    )
    ended = tail(
        sizes,
        3,
        w_gate.shape[2],
        dict(
            held_in=mixed.held,
            back_in=mixed.back_part,
            out_in=mixed.out_part,
            soft_in=mixed.soft_part,
            w_query=w_query,
            w_key=w_key,
            w_value=w_value,
            w_out=w_out,
            tables_all=begun.tables_all,
        ),
        dict(
            q=begun.q,
            q_far=begun.q_far,
            kv_all=begun.kv_all,
            seg_all=begun.seg_all,
            lse=begun.lse,
            heads=begun.heads,
            middle=begun.middle,
            tokens=tokens[0],
            grad_top=out_grad[0],
            second_low=begun.second_low,
            first_low=begun.first_low,
            w_router_turned=w_router_turned,
            gains=gains,
            turn=begun.turn,
            first_shard=mixed.shard,
        ),
    )
    out_shard, query_shard, kv_shard = ended.sums_out
    moved = [
        (ended.layer_out, None),
        (ended.input_grad, None),
        (query_shard, None),
        (kv_shard, (0, kv_width)),
        (kv_shard, (kv_width, kv_width)),
        (out_shard, None),
        *((array, None) for array in ended.experts_out),
    ]
    layer_out, input_grad, *shards = deliver(moved)
    return (
        layer_out[None],
        input_grad[None],
        ended.gains_out[0, 0],
        ended.gains_out[1, 0],
        *shards[:4],
        ended.router_out,
        *shards[4:],
    )


def solution(mesh):
    sizes = (mesh.shape["expert"], mesh.shape["context"], mesh.shape["dp"])
    in_specs = (
        P(("expert", "dp"), "context", None),
        P(),
        P(),
        P(),
        P(),
        P(),
        P(),
        P(),
        P("expert", None, None),
        P("expert", None, None),
        P("expert", None, None),
        P(("expert", "dp"), "context"),
        P(("expert", "dp"), "context", None),
        P(("expert", "dp"), "context", None),
        P(("expert", "dp"), "context", None),
    )
    out_specs = (
        P(("expert", "dp"), "context", None),
        P(("expert", "dp"), "context", None),
        P(("expert", "context", "dp")),
        P(("expert", "context", "dp")),
        P(("expert", "context", "dp"), None),
        P(("expert", "context", "dp"), None),
        P(("expert", "context", "dp"), None),
        P(("expert", "context", "dp"), None),
        P(("expert", "context", "dp"), None),
        P("expert", ("context", "dp"), None),
        P("expert", ("context", "dp"), None),
        P("expert", ("context", "dp"), None),
    )
    return jax.shard_map(
        functools.partial(body, sizes),
        mesh=mesh,
        in_specs=in_specs,
        out_specs=out_specs,
        check_vma=False,
    )
```

```python
import functools
import types

import jax
import jax.numpy as jnp
import numpy as np
from jax import lax
from jax.experimental import pallas as pl
from jax.experimental.pallas import tpu as pltpu
from jax.sharding import PartitionSpec as P

HEAD_DIM = 64
MESH = pl.DeviceIdType.MESH

epsilon = 1e-06
rope_base = 10000.0
negative_large = -1e30
bf16 = jnp.bfloat16
f32 = jnp.float32


def nt(a, b):
    return lax.dot_general(a, b, (((1,), (1,)), ((), ())), preferred_element_type=f32)


def tn(a, b):
    return lax.dot_general(a, b, (((0,), (0,)), ((), ())), preferred_element_type=f32)


def nn(a, b):
    return jnp.dot(a, b, preferred_element_type=f32)


def add_rows(dst, dst_at, src, src_at, rows):
    step = 16

    @pl.loop(0, rows // step)
    def _(i):
        at = pl.ds(pl.multiple_of(i * step, step), step)
        dst[dst_at + (at, slice(None))] = (
            dst[dst_at + (at, slice(None))].astype(f32) + src[src_at + (at, slice(None))].astype(f32)
        ).astype(bf16)


def lane_half(shape, which):
    lanes = lax.broadcasted_iota(jnp.int32, shape, 1)
    return (lanes >= HEAD_DIM) if which else (lanes < HEAD_DIM)


def column_of(row):
    n = row.shape[1]
    rows = lax.broadcasted_iota(jnp.int32, (n, n), 0)
    cols = lax.broadcasted_iota(jnp.int32, (n, n), 1)
    return jnp.sum(jnp.where(rows == cols, row, 0.0), axis=1, keepdims=True)


def mask_bias(seg_ref, block, me, tokens):
    key_seg = column_of(seg_ref[block, :1, :])
    same = key_seg == seg_ref[me, :1, :]
    rows = lax.broadcasted_iota(jnp.int32, (tokens, tokens), 0) + block * tokens
    cols = lax.broadcasted_iota(jnp.int32, (tokens, tokens), 1) + me * tokens
    return jnp.where(same & (rows <= cols), 0.0, negative_large)


def named(defs, refs):
    counts = [d.num_leaves for d in defs]
    at = [sum(counts[:i]) for i in range(len(counts) + 1)]
    trees = [jax.tree.unflatten(d, refs[at[i] : at[i + 1]]) for i, d in enumerate(defs)]
    r = types.SimpleNamespace(**{k: v for tree in trees for k, v in tree.items()})
    read, (copies, sem) = trees[1], trees[3]["read"]
    r.loads = [
        pltpu.make_async_copy(read[k], copies[k], sem.at[i]) for i, k in enumerate(sorted(read))
    ]
    for k in read:
        setattr(r, k, copies[k])
    return r


def call_named(kernel, kept, read, outs, scratch, cid, limit, kept_outs):
    vm = pl.BlockSpec(memory_space=pltpu.VMEM)
    hbm = pl.BlockSpec(memory_space=pl.ANY)
    scratch["read"] = (
        {k: pltpu.VMEM(v.shape, v.dtype) for k, v in read.items()},
        pltpu.SemaphoreType.DMA((len(read),)),
    )
    flats, defs = zip(*(jax.tree.flatten(t) for t in (kept, read, outs, scratch)))
    out_specs = jax.tree.leaves(
        {k: jax.tree.map(lambda _: hbm if k in kept_outs else vm, v) for k, v in outs.items()}
    )
    results = pl.pallas_call(
        functools.partial(kernel, defs),
        out_shape=tuple(flats[2]),
        in_specs=[hbm] * (len(flats[0]) + len(flats[1])),
        out_specs=tuple(out_specs),
        scratch_shapes=flats[3],
        compiler_params=pltpu.CompilerParams(
            collective_id=cid, has_side_effects=True, vmem_limit_bytes=limit
        ),
        name=kernel.func.__name__,
    )(*flats[0], *flats[1])
    return types.SimpleNamespace(**jax.tree.unflatten(defs[2], results))


def slot_table(chosen, order, experts_all, capacity):
    top_count, tokens = chosen.shape
    pairs = order.shape[1]
    shift = top_count.bit_length() - 1
    if top_count != 1 << shift:
        raise ValueError("top count")
    owner = jnp.where(
        (order >> shift) == lax.broadcasted_iota(jnp.int32, (tokens, pairs), 0), 1.0, 0.0
    ).astype(bf16)
    which = (order & (top_count - 1)) == lax.broadcasted_iota(jnp.int32, (top_count, pairs), 0)
    turns = lax.broadcasted_iota(jnp.int32, (top_count, pairs), 1)
    high, low = (
        nt(jnp.where(which, part.astype(f32), 0.0).astype(bf16), owner)
        for part in (turns >> 8, turns & 255)
    )
    turn_of = high * 256.0 + low
    far = float(2 * pairs)
    ids = lax.broadcasted_iota(jnp.int32, (128, tokens), 0)
    turn_row = jnp.full((128, tokens), far, f32)
    for k in range(top_count):
        turn_row = jnp.where(chosen[k : k + 1, :] == ids, turn_of[k : k + 1, :], turn_row)
    turn_at = turn_row.T
    for e in range(experts_all):
        row = turn_row[e : e + 1, :]
        rank = jnp.sum(jnp.where(turn_at[:, e : e + 1] < row, 1.0, 0.0), axis=0, keepdims=True)
        yield jnp.where((row < far) & (rank < capacity), rank, -1.0)


def partners(ex, ne):
    if ne != 4:
        raise ValueError("expert")
    return ex + 1 - 2 * lax.rem(ex, 2), lax.rem(ex + 2, 4)


def front_kernel(sizes, capacity, defs, *refs):
    r = named(defs, refs)
    ne, nz, nd = sizes
    ex, me = lax.axis_index("expert"), lax.axis_index("context")
    tokens, width = r.tokens.shape
    kv_width = r.w_key.shape[1]
    slices = kv_width // 128
    quarter = HEAD_DIM // 2

    barrier = pltpu.get_barrier_semaphore()
    for step in range(1, ne):
        pl.semaphore_signal(
            barrier, inc=1, device_id={"expert": lax.rem(ex + step, ne)}, device_id_type=MESH
        )

    @pl.when(me > 0)
    def _():
        pl.semaphore_signal(barrier, inc=1, device_id={"context": me - 1}, device_id_type=MESH)

    @pl.when(me < nz - 1)
    def _():
        pl.semaphore_signal(barrier, inc=1, device_id={"context": me + 1}, device_id_type=MESH)

    loads = [
        pltpu.make_async_copy(src, dst, r.load_sem.at[i])
        for i, (src, dst) in enumerate(
            (
                (r.w_key, r.w_key_v),
                (r.w_value, r.w_value_v),
                (r.w_query, r.w_query_v),
                (r.w_out, r.w_out_v),
                (r.grad_top, r.grad_all.at[ex]),
            )
        )
    ]
    for copy in r.loads + loads:
        copy.start()
    pl.semaphore_wait(
        barrier, ne - 1 + jnp.where(me > 0, 1, 0) + jnp.where(me < nz - 1, 1, 0)
    )

    def spread(kind, step):
        src = (r.grad_top, r.tables_s)[kind]
        dst = (r.grad_all, r.tables_all)[kind]
        return pltpu.make_async_remote_copy(
            src_ref=src,
            dst_ref=dst.at[ex],
            send_sem=r.spread_send.at[kind, step],
            recv_sem=r.spread_recv.at[kind, step],
            device_id={"expert": lax.rem(ex + step, ne)},
            device_id_type=MESH,
        )

    pair = partners(ex, ne)
    halves = (pl.ds(0, tokens // 2), pl.ds(tokens // 2, tokens // 2))

    def hand(i, half, onward):
        at = halves[half]
        src = r.rows_all.at[pair[1 - i], at] if onward else r.second_s.at[at]
        dst = r.rows_all.at[pair[1 - i] if onward else ex, at]
        return pltpu.make_async_remote_copy(
            src_ref=src,
            dst_ref=dst,
            send_sem=r.hand_send.at[i, half, int(onward)],
            recv_sem=r.hand_recv.at[i, half, int(onward)],
            device_id={"expert": pair[i]},
            device_id_type=MESH,
        )

    last, helper = nz - 1, nz - 2

    def to(place, src, dst, send, recv):
        return pltpu.make_async_remote_copy(
            src_ref=src,
            dst_ref=dst,
            send_sem=send,
            recv_sem=recv,
            device_id={"context": place},
            device_id_type=MESH,
        )

    def up(j, t):
        at = r.kv_s.at[j, t]
        return to(me + 1, at, at, r.up_send.at[j, t], r.up_recv.at[j, t])

    def up_seg(j):
        at = r.seg_s.at[j]
        return to(me + 1, at, at, r.seg_send.at[j], r.seg_recv.at[j])

    ask = [
        to(helper, src, dst, r.ask_send.at[i], r.ask_recv.at[i])
        for i, (src, dst) in enumerate(
            ((r.q_s, r.q_far_s), (r.seg_s.at[last], r.seg_s.at[last]))
        )
    ]

    def answer(t):
        return [
            to(last, src.at[t], dst.at[t], r.answer_send.at[i, t], r.answer_recv.at[i, t])
            for i, (src, dst) in enumerate(
                ((r.far_head, r.far_head_in), (r.far_lse, r.far_lse_in))
            )
        ]

    for step in range(1, ne):
        spread(0, step).start()

    for copy in r.loads:
        copy.wait()

    values = r.tokens[...].astype(f32)
    inverse = lax.rsqrt(jnp.mean(values * values, axis=-1, keepdims=True) + epsilon)
    first = (values * inverse * r.gains[:1, :].astype(f32)).astype(bf16)
    r.first_s[...] = first
    cos_b, sin_b = r.base[0, pl.ds(me, 1), :], r.base[1, pl.ds(me, 1), :]
    cos_i, sin_i = r.inner[0], r.inner[1]
    cosine = cos_i * cos_b - sin_i * sin_b
    sine = sin_i * cos_b + cos_i * sin_b
    first_lanes = lax.rem(lax.broadcasted_iota(jnp.int32, (tokens, 128), 1), HEAD_DIM) < quarter
    sine = jnp.where(first_lanes, sine, -sine)
    r.turn_s[0] = cosine
    r.turn_s[1] = sine

    def rotate(x):
        swapped = jnp.where(
            first_lanes, pltpu.roll(x, 128 - quarter, 1), pltpu.roll(x, quarter, 1)
        )
        return x * cosine - swapped * sine

    loads[0].wait()
    keys = nn(first, r.w_key_v[...])
    for t in range(slices):
        at = slice(t * 128, (t + 1) * 128)
        r.kv_s[me, t, :, :128] = rotate(keys[:, at]).astype(bf16)
    loads[1].wait()
    vals = nn(first, r.w_value_v[...]).astype(bf16)
    for t in range(slices):
        r.kv_s[me, t, :, 128:] = vals[:, t * 128 : (t + 1) * 128]
    r.seg_s[me] = jnp.broadcast_to(r.seg[...].astype(f32), (8, tokens))

    @pl.when(me < helper)
    def _():
        up_seg(me).start()
        for t in range(slices):
            up(me, t).start()

    loads[2].wait()
    factor = HEAD_DIM ** (-0.5)
    low = lane_half((tokens, 128), 0)
    for t in range(slices):
        two = nn(first, r.w_query_v[:, t * 256 : (t + 1) * 256])
        left, right = rotate(two[:, :128]), rotate(two[:, 128:])
        even = jnp.where(low, left, pltpu.roll(right, HEAD_DIM, 1))
        odd = jnp.where(low, pltpu.roll(left, HEAD_DIM, 1), right)
        r.q_s[t, :tokens, :] = (even * factor).astype(bf16)
        r.q_s[t, tokens:, :] = (odd * factor).astype(bf16)

    @pl.when(me == last)
    def _():
        for copy in ask:
            copy.start()

    experts_all = r.tables_s.shape[1]
    for e, row in enumerate(slot_table(r.chosen[...], r.order[...], experts_all, capacity)):
        r.tables_s[0, e : e + 1, :] = row

    for ref in (r.acc, r.total, r.far_acc, r.far_total):
        ref[...] = jnp.zeros_like(ref)
    for ref in (r.top, r.far_top):
        ref[...] = jnp.full_like(ref, -3e38)

    def attend(j, t, queries, acc, top, total, bias):
        keys = r.kv_s[j, t, :, :128]
        vals = r.kv_s[j, t, :, 128:]
        for half in (0, 1):
            keep = lane_half((tokens, 128), half)
            zero = jnp.zeros_like(keys)
            scores = nt(jnp.where(keep, keys, zero), queries[t]) + jnp.concatenate(
                [bias[...]] * 2, axis=1
            )
            old = top[t, half : half + 1, :]
            new = jnp.maximum(old, jnp.max(scores, axis=0, keepdims=True))
            scale = jnp.exp(old - new)
            soft = jnp.exp(scores - new)
            top[t, half : half + 1, :] = new
            total[t, half : half + 1, :] = total[t, half : half + 1, :] * scale + jnp.sum(
                soft, axis=0, keepdims=True
            )
            mixed = tn(jnp.where(keep, vals, zero), soft.astype(bf16))
            a, b = half * HEAD_DIM, (half + 1) * HEAD_DIM
            acc[t, a:b, :] = acc[t, a:b, :] * scale + mixed[a:b]

    def own_slice(j, t):
        attend(j, t, r.q_s, r.acc, r.top, r.total, r.bias)

    def far_slice(j, t):
        attend(j, t, r.q_far_s, r.far_acc, r.far_top, r.far_total, r.far_bias)

    r.bias[...] = mask_bias(r.seg_s, me, me, tokens)

    @pl.loop(0, slices)
    def _(t):
        own_slice(me, t)

    @pl.when(me == helper)
    def _():
        for copy in ask:
            copy.wait_recv()
        r.far_bias[...] = mask_bias(r.seg_s, helper, last, tokens)

        @pl.loop(0, slices)
        def _(t):
            far_slice(helper, t)

    for step in range(1, nz - 1):
        j = me - step

        @pl.when((j >= 0) & (me < last))
        def _():
            up_seg(j).wait_recv()

            @pl.when(me < helper)
            def _():
                up_seg(j).start()

            r.bias[...] = mask_bias(r.seg_s, j, me, tokens)

            @pl.when(me == helper)
            def _():
                r.far_bias[...] = mask_bias(r.seg_s, j, last, tokens)

            @pl.loop(0, slices)
            def _(t):
                up(j, t).wait_recv()

                @pl.when(me < helper)
                def _():
                    up(j, t).start()

                @pl.when(me == helper)
                def _():
                    far_slice(j, t)
                    if step == nz - 2:
                        for half in (0, 1):
                            a, b = half * HEAD_DIM, (half + 1) * HEAD_DIM
                            r.far_head[t, a:b, :] = (
                                r.far_acc[t, a:b, :] / r.far_total[t, half : half + 1, :]
                            ).astype(bf16)
                        r.far_lse[t] = r.far_top[t] + jnp.log(r.far_total[t])
                        for copy in answer(t):
                            copy.start()

                own_slice(j, t)

    @pl.loop(0, slices)
    def _(t):
        r.lse_s[t] = r.top[t] + jnp.log(r.total[t])
        for half in (0, 1):
            a, b = half * HEAD_DIM, (half + 1) * HEAD_DIM
            r.acc[t, a:b, :] = r.acc[t, a:b, :] / r.total[t, half : half + 1, :]

        @pl.when(me == last)
        def _():
            for copy in answer(t):
                copy.wait_recv()
            near, far = r.lse_s[t], r.far_lse_in[t]
            top = jnp.maximum(near, far)
            both = top + jnp.log(jnp.exp(near - top) + jnp.exp(far - top))
            r.lse_s[t] = both
            near, far = jnp.exp(near - both), jnp.exp(far - both)
            for half in (0, 1):
                a, b = half * HEAD_DIM, (half + 1) * HEAD_DIM
                r.acc[t, a:b, :] = (
                    r.acc[t, a:b, :] * near[half : half + 1]
                    + r.far_head_in[t, a:b, :].astype(f32) * far[half : half + 1]
                )

    for t in range(slices):
        for half in (0, 1):
            a, b = half * HEAD_DIM, (half + 1) * HEAD_DIM
            head = r.acc[t, a:b, :].astype(bf16)
            r.heads_s[2 * t + half] = head
            for ab in (0, 1):
                h = (4 * t + 2 * half + ab) * HEAD_DIM
                r.attn_turned[h : h + HEAD_DIM, :] = head[:, ab * tokens : (ab + 1) * tokens]

    loads[3].wait()
    middle = r.tokens[...].astype(f32) + tn(r.attn_turned[...], r.w_out_v[...])
    r.middle_s[...] = middle
    inverse = lax.rsqrt(jnp.mean(middle * middle, axis=-1, keepdims=True) + epsilon)
    second = (middle * inverse * r.gains[1:, :].astype(f32)).astype(bf16)
    r.second_s[...] = second
    for i, half in ((0, 0), (1, 1), (0, 1), (1, 0)):
        hand(i, half, False).start()
    logits = nt(r.w_router_turned[...], second)
    grown = jnp.exp(logits - jnp.max(logits, axis=0, keepdims=True))
    r.tables_s[1] = grown / jnp.sum(grown, axis=0, keepdims=True)
    for step in range(1, ne):
        spread(1, step).start()
    stores = [
        pltpu.make_async_copy(src, dst, r.store_sem.at[i])
        for i, (src, dst) in enumerate(
            (
                (r.second_s, r.rows_all.at[ex]),
                (r.tables_s, r.tables_all.at[ex]),
                (r.q_s, r.q),
                (r.q_far_s, r.q_far),
                (r.kv_s, r.kv_all),
                (r.seg_s, r.seg_all),
                (r.lse_s, r.lse),
                (r.heads_s, r.heads),
                (r.middle_s, r.middle),
                (r.second_s, r.second_low),
                (r.first_s, r.first_low),
                (r.turn_s, r.turn),
            )
        )
    ]
    for copy in stores:
        copy.start()
    for copy in stores:
        copy.wait()
    for i in (0, 1):
        hand(i, i, False).wait_recv()
        hand(1 - i, i, True).start()
    loads[4].wait()
    for kind in range(2):
        for step in range(1, ne):
            spread(kind, step).wait()
    for i in (0, 1):
        hand(i, i, False).wait_send()
        hand(i, 1 - i, False).wait()
        hand(1 - i, i, True).wait()
    for step in range(nz - 1):
        j = me - step

        @pl.when((j >= 0) & (me < helper))
        def _():
            up_seg(j).wait_send()
            for t in range(slices):
                up(j, t).wait_send()

    @pl.when(me == last)
    def _():
        for copy in ask:
            copy.wait_send()

    @pl.when(me == helper)
    def _():
        for t in range(slices):
            for copy in answer(t):
                copy.wait_send()


def front(sizes, cid, capacity, hbm_ins, vmem_ins):
    ne, nz, nd = sizes
    ins = types.SimpleNamespace(**hbm_ins, **vmem_ins)
    tokens, width = ins.tokens.shape
    kv_width = ins.w_key.shape[1]
    slices, wide = kv_width // 128, 2 * tokens
    experts_all = ins.w_router_turned.shape[0]
    shape = jax.ShapeDtypeStruct
    vmem, dma = pltpu.VMEM, pltpu.SemaphoreType.DMA
    sized = dict(
        q=((slices, wide, 128), bf16),
        q_far=((slices, wide, 128), bf16),
        kv=((nz, slices, tokens, 256), bf16),
        seg=((nz, 8, tokens), f32),
        lse=((slices, 2, wide), f32),
        heads=((2 * slices, HEAD_DIM, wide), bf16),
        middle=((tokens, width), f32),
        second=((tokens, width), bf16),
        first=((tokens, width), bf16),
        turn=((2, tokens, 128), f32),
        tables=((2, experts_all, tokens), f32),
    )
    outs = dict(
        rows_all=shape((ne, tokens, width), bf16),
        grad_all=shape((ne, tokens, width), bf16),
        tables_all=shape((ne, 2, experts_all, tokens), f32),
        q=shape(*sized["q"]),
        q_far=shape(*sized["q"]),
        kv_all=shape(*sized["kv"]),
        seg_all=shape(*sized["seg"]),
        lse=shape(*sized["lse"]),
        heads=shape(*sized["heads"]),
        middle=shape(*sized["middle"]),
        second_low=shape(*sized["second"]),
        first_low=shape(*sized["first"]),
        turn=shape(*sized["turn"]),
    )
    scratch = dict(
        w_query_v=vmem(ins.w_query.shape, bf16),
        w_key_v=vmem(ins.w_key.shape, bf16),
        w_value_v=vmem(ins.w_value.shape, bf16),
        w_out_v=vmem(ins.w_out.shape, bf16),
        attn_turned=vmem((width, tokens), bf16),
        acc=vmem((slices, 128, wide), f32),
        top=vmem((slices, 2, wide), f32),
        total=vmem((slices, 2, wide), f32),
        bias=vmem((tokens, tokens), f32),
        far_acc=vmem((slices, 128, wide), f32),
        far_top=vmem((slices, 2, wide), f32),
        far_total=vmem((slices, 2, wide), f32),
        far_bias=vmem((tokens, tokens), f32),
        far_head=vmem((slices, 128, wide), bf16),
        far_lse=vmem((slices, 2, wide), f32),
        far_head_in=vmem((slices, 128, wide), bf16),
        far_lse_in=vmem((slices, 2, wide), f32),
        load_sem=dma((5,)),
        store_sem=dma((12,)),
        spread_send=dma((2, ne)),
        spread_recv=dma((2, ne)),
        hand_send=dma((2, 2, 2)),
        hand_recv=dma((2, 2, 2)),
        up_send=dma((nz, slices)),
        up_recv=dma((nz, slices)),
        seg_send=dma((nz,)),
        seg_recv=dma((nz,)),
        ask_send=dma((2,)),
        ask_recv=dma((2,)),
        answer_send=dma((2, slices)),
        answer_recv=dma((2, slices)),
        **{k + "_s": vmem(*v) for k, v in sized.items()},
    )
    return call_named(
        functools.partial(front_kernel, sizes, capacity),
        hbm_ins, vmem_ins, outs, scratch, cid, 60 << 20, tuple(outs),
    )


class Line:
    def __init__(self, nz, held, came, send, recv):
        if nz != 4:
            raise ValueError("context")
        self.nz, self.held, self.came, self.send, self.recv = nz, held, came, send, recv
        self.me = lax.axis_index("context")

    @staticmethod
    def scratch(nz, chunks, rows, width):
        return [
            pltpu.VMEM((chunks, nz, rows, width), bf16),
            pltpu.VMEM((chunks, nz, rows, width), bf16),
            pltpu.SemaphoreType.DMA((chunks, nz)),
            pltpu.SemaphoreType.DMA((chunks, nz)),
        ]

    routes = {
        (0, 3): (1, 3),
        (0, 2): (1, 2),
        (0, 1): (1, 0),
        (3, 0): (2, 0),
        (3, 1): (2, 1),
        (3, 2): (2, 3),
        (1, 0): (0, 1),
        (2, 3): (3, 2),
        (1, 3): (3, 1),
        (1, 2): (2, 2),
        (2, 0): (0, 2),
        (2, 1): (1, 1),
    }

    def copy(self, k, place, s):
        target, slot = self.routes[place, s]
        return pltpu.make_async_remote_copy(
            src_ref=self.held.at[k, s],
            dst_ref=self.came.at[k, slot],
            send_sem=self.send.at[k, s],
            recv_sem=self.recv.at[k, slot],
            device_id={"context": target},
            device_id_type=MESH,
        )

    def start(self, k, moves):
        for place in range(self.nz):
            pieces = [s for p, s in moves if p == place]
            if pieces:

                @pl.when(self.me == place)
                def _():
                    for s in pieces:
                        self.copy(k, place, s).start()

    def far_piece(self, place, which):
        return 3 - which if place < 2 else which

    def cross(self, k, which, place):
        self.start(k, [(place, self.far_piece(place, which))])

    def left(self, k, which, place):
        @pl.when(self.me == place)
        def _():
            self.copy(k, place, self.far_piece(place, which)).wait_send()

    def straight(self, k):
        self.start(k, [(1, 0), (2, 3)])

    def ends(self, k, place):
        self.start(k, [(place, 1 if place == 0 else 2)])

    def join(self, k, which, place):
        s = self.far_piece(place, which)

        @pl.when(self.me == place)
        def _():
            self.copy(k, 0 if place == 1 else 3, s).wait_recv()
            add_rows(self.held, (k, s), self.came, (k, s), self.held.shape[2])
            self.copy(k, place, s).start()

    def total(self, k, put):
        for place in range(self.nz):

            @pl.when(self.me == place)
            def _():
                senders = [(p, s) for (p, s), (t, _) in self.routes.items() if t == place == s]
                for p, s in senders:
                    self.copy(k, p, s).wait_recv()
                for at in range(0, self.held.shape[2], 16):
                    rows = slice(at, at + 16)
                    value = self.held[k, place, rows].astype(f32)
                    for move in senders:
                        value = value + self.came[k, self.routes[move][1], rows].astype(f32)
                    put(at, value)
                for s in range(self.nz):
                    if s != place and (place in (1, 2) or abs(s - place) == 1):
                        self.copy(k, place, s).wait_send()


def experts_kernel(sizes, cap, defs, *refs):
    r = named(defs, refs)
    ne, nz, nd = sizes
    ex, dp, ctx = (lax.axis_index(a) for a in ("expert", "dp", "context"))
    local, width, hid = r.w_gate.shape
    tokens = r.rows_all.shape[1]
    gate_rows, down_rows = width // (nz * nd), hid // (nz * nd)
    line = Line(nz, r.held_s, *r.line)

    barrier = pltpu.get_barrier_semaphore()
    for axis, place, size in (("dp", dp, nd), ("context", ctx, nz)):
        for step in range(1, size):
            pl.semaphore_signal(
                barrier, inc=1, device_id={axis: lax.rem(place + step, size)}, device_id_type=MESH
            )

    def weights(e, slot):
        return [
            pltpu.make_async_copy(src, dst, r.weight_sem.at[slot, i])
            for i, (src, dst) in enumerate(
                (
                    (r.w_gate.at[e], r.both.at[slot, :, pl.ds(0, hid)]),
                    (r.w_up.at[e], r.both.at[slot, :, pl.ds(hid, hid)]),
                    (r.w_down.at[e], r.down.at[slot]),
                )
            )
        ]

    for copy in r.loads + weights(0, 0):
        copy.start()
    pl.semaphore_wait(barrier, nd + nz - 2)
    for copy in r.loads:
        copy.wait()

    def cores(k, step):
        other = lax.rem(dp + step, nd)
        return pltpu.make_async_remote_copy(
            src_ref=r.made.at[:, other],
            dst_ref=r.from_dp.at[step - 1, k],
            send_sem=r.dp_send.at[k, step],
            recv_sem=r.dp_recv.at[k, step],
            device_id={"dp": other},
            device_id_type=MESH,
        )

    def keep(k):
        return pltpu.make_async_copy(r.held_s.at[k], r.held.at[k], r.held_sem.at[k])

    def add_cores(k):
        for step in range(1, nd):
            cores(k, step).wait_recv()
            for z in range(nz):
                add_rows(r.held_s, (k, z), r.from_dp, (step - 1, k, z), gate_rows + down_rows)

        @pl.when(k > 0)
        def _():
            keep(k).start()

    row_id = lax.broadcasted_iota(jnp.int32, (cap, tokens), 0).astype(f32)

    @pl.loop(0, local)
    def _(e):
        slot = lax.rem(e, 2)
        own = pl.ds(pl.multiple_of(e * cap, 16), cap)
        for src in range(ne):
            at = pl.ds(src * cap, cap)
            hits = r.tables_all[src, 0, pl.ds(ex * local + e, 1), :] == row_id
            gate_row = r.tables_all[src, 1, pl.ds(ex * local + e, 1), :]
            gate = jnp.sum(jnp.where(hits, gate_row, 0.0), axis=1, keepdims=True)
            low = jnp.where(hits, 1.0, 0.0).astype(bf16)
            r.hits[src, own, :] = low
            r.gate_s[at, :] = jnp.broadcast_to(gate, (cap, 128))
            r.x_s[at, :] = nn(low, r.rows_all[src]).astype(bf16)
            og = nn(low, r.grad_all[src])
            r.og_s[at, :] = og.astype(bf16)
            r.sg_s[at, :] = (og * gate).astype(bf16)
        for copy in weights(e, slot):
            copy.wait()

        @pl.when(e < local - 1)
        def _():
            for copy in weights(e + 1, 1 - slot):
                copy.start()

        pre = nn(r.x_s[...], r.both[slot])

        @pl.when(e > 0)
        def _():
            add_cores(e - 1)

        @pl.when(e == 1)
        def _():
            for place in (0, 3):
                line.cross(0, 0, place)
            line.straight(0)

        @pl.when(e == 2)
        def _():
            for place in (0, 3):
                line.ends(0, place)

        @pl.when(e == 3)
        def _():
            for place in (1, 2):
                line.join(0, 1, place)

        gate_pre, up_pre = pre[:, :hid], pre[:, hid:]
        sig = jax.nn.sigmoid(gate_pre)
        silu = gate_pre * sig
        r.hidden[...] = (silu * up_pre).astype(bf16)
        hidden_back = nt(r.sg_s[...], r.down[slot])
        r.pre_back[:, :hid] = (
            hidden_back * up_pre * sig * (1.0 + gate_pre * (1.0 - sig))
        ).astype(bf16)
        r.pre_back[:, hid:] = (hidden_back * silu).astype(bf16)
        produced = nn(r.hidden[...], r.down[slot])
        pair = jnp.sum(r.og_s[...].astype(f32) * produced, axis=1, keepdims=True)
        weighed = (produced * r.gate_s[:, :1]).astype(bf16)
        for src in range(ne):
            a, b = src * cap, (src + 1) * cap
            r.weighed[src, own, :] = weighed[a:b]
            r.soft_part[src, pl.ds(e, 1), :] = jnp.sum(
                r.hits[src, own, :].astype(f32) * pair[a:b], axis=0, keepdims=True
            )
        back = nt(r.pre_back[...], r.both[slot]).astype(bf16)
        for src in range(ne):
            r.back_rows[src, own, :] = back[src * cap : (src + 1) * cap]

        @pl.when(e == 1)
        def _():
            for place in (0, 3):
                line.cross(0, 1, place)

        @pl.when(e == 2)
        def _():
            for place in (1, 2):
                line.join(0, 0, place)

        @pl.when(e > 0)
        def _():
            for step in range(1, nd):
                cores(e - 1, step).wait_send()

        r.made[:, :, :gate_rows, :] = (
            tn(r.x_s[...], r.pre_back[...]).astype(bf16).reshape(nz, nd, gate_rows, 2 * hid)
        )
        r.made[:, :, gate_rows:, :] = (
            tn(r.hidden[...], r.sg_s[...]).astype(bf16).reshape(nz, nd, down_rows, width)
        )
        for step in range(1, nd):
            cores(e, step).start()
        r.held_s[e] = r.made[:, dp]

    stores = []
    for kind, (rows, out) in enumerate(((r.back_rows, r.back_part), (r.weighed, r.out_part))):
        for src in range(ne):
            r.sums[kind, src] = tn(r.hits[src], rows[src]).astype(bf16)
            stores.append(
                pltpu.make_async_copy(r.sums.at[kind, src], out.at[src], r.store_sem.at[kind, src])
            )
            stores[-1].start()
    add_cores(local - 1)

    def put(at, value):
        r.shard[at : at + 16, :] = value

    for place in (0, 3):
        for which in (0, 1):
            line.left(0, which, place)
    line.total(0, put)
    for step in range(1, nd):
        cores(local - 1, step).wait_send()
    for k in range(1, local):
        keep(k).wait()
    for copy in stores:
        copy.wait()


def experts(sizes, cid, cap, kept, read):
    ne, nz, nd = sizes
    local, width, hid = kept["w_gate"].shape
    tokens = read["rows_all"].shape[1]
    piece = width // (nz * nd) + hid // (nz * nd)
    shape, vmem, dma = jax.ShapeDtypeStruct, pltpu.VMEM, pltpu.SemaphoreType.DMA
    held, *line = Line.scratch(nz, local, piece, width)
    line[0] = vmem((1, nz, piece, width), bf16)
    outs = dict(
        held=shape((local, nz, piece, width), bf16),
        out_part=shape((ne, tokens, width), bf16),
        back_part=shape((ne, tokens, width), bf16),
        soft_part=shape((ne, local, tokens), f32),
        shard=shape((piece, width), f32),
    )
    rows = ne * cap
    scratch = dict(
        both=vmem((2, width, 2 * hid), bf16),
        down=vmem((2, hid, width), bf16),
        x_s=vmem((rows, width), bf16),
        og_s=vmem((rows, width), bf16),
        sg_s=vmem((rows, width), bf16),
        gate_s=vmem((rows, 128), f32),
        hidden=vmem((rows, hid), bf16),
        pre_back=vmem((rows, 2 * hid), bf16),
        hits=vmem((ne, local * cap, tokens), bf16),
        weighed=vmem((ne, local * cap, width), bf16),
        back_rows=vmem((ne, local * cap, width), bf16),
        sums=vmem((2, ne, tokens, width), bf16),
        made=vmem((nz, nd, piece, width), bf16),
        from_dp=vmem((nd - 1, local, nz, piece, width), bf16),
        held_s=held,
        line=line,
        weight_sem=dma((2, 3)),
        dp_send=dma((local, nd)),
        dp_recv=dma((local, nd)),
        held_sem=dma((local,)),
        store_sem=dma((2, ne)),
    )
    return call_named(
        functools.partial(experts_kernel, sizes, cap),
        kept, read, outs, scratch, cid, 62 << 20, ("held", "out_part", "back_part"),
    )


class Spread:
    def __init__(self, sizes, made, from_dp, held, from_ex, line, from_z, send, recv):
        self.sizes, self.made, self.from_dp, self.held = sizes, made, from_dp, held
        self.from_ex, self.line, self.from_z, self.send, self.recv = from_ex, line, from_z, send, recv
        self.places = tuple(lax.axis_index(a) for a in ("dp", "expert", "context"))

    @staticmethod
    def scratch(sizes, rows, width):
        ne, nz, nd = sizes
        most = max(sizes)
        return [
            pltpu.VMEM((nd - 1, ne, nz, rows, width), bf16),
            pltpu.VMEM((ne, nz, rows, width), bf16),
            pltpu.VMEM((ne - 1, nz, rows, width), bf16),
            pltpu.VMEM((nz, rows, width), bf16),
            pltpu.VMEM((nz - 1, rows, width), bf16),
            pltpu.SemaphoreType.DMA((3, most)),
            pltpu.SemaphoreType.DMA((3, most)),
        ]

    def copy(self, stage, step):
        ne, nz, nd = self.sizes
        axis, size = (("dp", nd), ("expert", ne), ("context", nz))[stage]
        other = lax.rem(self.places[stage] + step, size)
        src = (
            self.made.at[:, :, other]
            if stage == 0
            else self.held.at[other] if stage == 1 else self.line.at[other]
        )
        dst = (self.from_dp, self.from_ex, self.from_z)[stage].at[step - 1]
        return pltpu.make_async_remote_copy(
            src_ref=src,
            dst_ref=dst,
            send_sem=self.send.at[stage, step],
            recv_sem=self.recv.at[stage, step],
            device_id={axis: other},
            device_id_type=MESH,
        )

    def others(self, stage):
        ne, nz, nd = self.sizes
        return range(1, (nd, ne, nz)[stage])

    def over_dp(self):
        for step in self.others(0):
            self.copy(0, step).start()

    def made_free(self):
        for step in self.others(0):
            self.copy(0, step).wait_send()

    def over_expert(self):
        ne, nz, _ = self.sizes
        for step in self.others(0):
            self.copy(0, step).wait_recv()

        @pl.loop(0, ne * nz)
        def _(i):
            a = lax.div(i, nz)
            b = i - a * nz
            total = self.made[a, b, self.places[0]].astype(f32)
            for step in self.others(0):
                total = total + self.from_dp[step - 1, a, b].astype(f32)
            self.held[a, b] = total.astype(bf16)

        for step in self.others(1):
            self.copy(1, step).start()

    def over_context(self):
        nz = self.sizes[1]
        for step in self.others(1):
            self.copy(1, step).wait_recv()

        @pl.loop(0, nz)
        def _(b):
            total = self.held[self.places[1], b].astype(f32)
            for step in self.others(1):
                total = total + self.from_ex[step - 1, b].astype(f32)
            self.line[b] = total.astype(bf16)

        for step in self.others(2):
            self.copy(2, step).start()

    def finish(self, out):
        for step in self.others(2):
            self.copy(2, step).wait_recv()
        total = self.line[self.places[2]].astype(f32)
        for step in self.others(2):
            total = total + self.from_z[step - 1].astype(f32)
        out[...] = total
        for stage in (1, 2):
            for step in self.others(stage):
                self.copy(stage, step).wait_send()


class Fold:
    def __init__(self, ex, parts, own, mine, passing, came, load, send, recv):
        self.ex, self.parts, self.own, self.mine, self.passing, self.came = (
            ex, parts, own, mine, passing, came,
        )
        self.load, self.send, self.recv = load, send, recv
        self.pair = partners(ex, 4)
        half = parts.shape[1] // 2
        self.halves = (pl.ds(0, half), pl.ds(half, half))

    @staticmethod
    def scratch(rows, width):
        half = (2, rows // 2, width)
        return [
            pltpu.VMEM((rows, width), bf16),
            pltpu.VMEM(half, bf16),
            pltpu.VMEM(half, bf16),
            pltpu.VMEM((2, rows, width), bf16),
            pltpu.SemaphoreType.DMA((3,)),
            pltpu.SemaphoreType.DMA((3, 2)),
            pltpu.SemaphoreType.DMA((3, 2)),
        ]

    def copy(self, stage, i):
        src, dst = (
            (self.parts.at[3 - self.ex, self.halves[i]], self.passing.at[i]),
            (self.parts.at[self.pair[i], self.halves[i]], self.came.at[i, self.halves[i]]),
            (self.mine.at[i], self.came.at[i, self.halves[1 - i]]),
        )[stage]
        return pltpu.make_async_remote_copy(
            src_ref=src,
            dst_ref=dst,
            send_sem=self.send.at[stage, i],
            recv_sem=self.recv.at[stage, i],
            device_id={"expert": self.pair[i]},
            device_id_type=MESH,
        )

    def loads(self):
        return [
            pltpu.make_async_copy(self.parts.at[self.ex], self.own, self.load.at[2])
        ] + [
            pltpu.make_async_copy(
                self.parts.at[self.pair[i], self.halves[1 - i]], self.mine.at[i], self.load.at[i]
            )
            for i in (0, 1)
        ]

    def begin(self):
        for stage in (0, 1):
            for i in (0, 1):
                self.copy(stage, i).start()
        for copy in self.loads():
            copy.start()

    def onward(self):
        for copy in self.loads():
            copy.wait()
        for i in (0, 1):
            self.copy(0, 1 - i).wait_recv()
            add_rows(self.mine, (i,), self.passing, (1 - i,), self.mine.shape[1])
            self.copy(2, i).start()

    def arrive(self):
        for stage in (1, 2):
            for i in (0, 1):
                self.copy(stage, i).wait_recv()

    def finish(self):
        for stage in range(3):
            for i in (0, 1):
                self.copy(stage, i).wait_send()


def tail_kernel(sizes, defs, *refs):
    r = named(defs, refs)
    ne, nz, nd = sizes
    ex, me, dp = (lax.axis_index(a) for a in ("expert", "context", "dp"))
    tokens, width = r.tokens.shape
    slices = r.kv_all.shape[1]
    kv_width = slices * 128
    group = width // ne
    last, helper = nz - 1, nz - 2

    barrier = pltpu.get_barrier_semaphore()
    for axis, place, size in (("expert", ex, ne), ("context", me, nz), ("dp", dp, nd)):
        for step in range(1, size):
            pl.semaphore_signal(
                barrier, inc=1, device_id={axis: lax.rem(place + step, size)}, device_id_type=MESH
            )
    for copy in r.loads:
        copy.start()
    pl.semaphore_wait(barrier, ne + nz + nd - 3)

    line = Line(nz, *r.line)
    proj = Spread(sizes, r.made, *r.proj)
    query = Spread(sizes, r.made, *r.query)
    kv = Spread(sizes, r.made, *r.kv)
    small = Spread(sizes, r.small_made, *r.small)

    chunks = range(r.held_in.shape[0] - 1)
    held_copies = [
        pltpu.make_async_copy(r.held_in.at[k + 1], line.held.at[k], r.held_sem.at[k])
        for k in chunks
    ]
    for copy in held_copies:
        copy.start()

    back = Fold(ex, r.back_in, *r.back)
    out = Fold(ex, r.out_in, *r.out)

    def gates_copy(step):
        other = lax.rem(ex + step, ne)
        return pltpu.make_async_remote_copy(
            src_ref=r.soft_in.at[other],
            dst_ref=r.soft_all.at[ex],
            send_sem=r.gates_send.at[step],
            recv_sem=r.gates_recv.at[step],
            device_id={"expert": other},
            device_id_type=MESH,
        )

    back.begin()
    for step in range(1, ne):
        gates_copy(step).start()
    loads = [
        pltpu.make_async_copy(src, dst, r.load_sem.at[i])
        for i, (src, dst) in enumerate(
            (
                (r.soft_in.at[ex], r.soft_all.at[ex]),
                (r.w_out, r.w_out_v),
                (r.w_query, r.w_query_v),
                (r.w_key, r.w_key_v),
                (r.w_value, r.w_value_v),
                (r.tables_all.at[ex], r.tables_own),
            )
        )
    ]
    for copy in loads:
        copy.start()
    for k in chunks:
        held_copies[k].wait()
        if k == 0:
            for place in (0, 3):
                line.cross(0, 0, place)
    for k in chunks:
        line.straight(k)
    for copy in r.loads + loads:
        copy.wait()
    for t in range(2 * slices):
        for ab in (0, 1):
            h = 2 * t + ab
            r.attn_turned[h * HEAD_DIM : (h + 1) * HEAD_DIM, :] = r.heads[
                t, :, ab * tokens : (ab + 1) * tokens
            ]

    back.onward()
    for place in (0, 3):
        line.cross(0, 1, place)
    for place in (1, 2):
        line.join(0, 0, place)
    for place in (0, 3):
        line.left(0, 0, place)
        line.cross(1, 0, place)
    for place in (1, 2):
        line.join(0, 1, place)
    for place in (0, 3):
        line.left(0, 1, place)
        line.cross(1, 1, place)
    for step in range(1, ne):
        gates_copy(step).wait_recv()
    back.arrive()
    out.begin()
    soft_back = jnp.concatenate([r.soft_all[i] for i in range(ne)], axis=0)
    router_soft = r.tables_own[1]
    logit_back = (
        router_soft * (soft_back - jnp.sum(router_soft * soft_back, axis=0, keepdims=True))
    ).astype(bf16)
    second_back = back.own[...].astype(f32) + tn(logit_back, r.w_router_turned[...])
    for i in (0, 1):
        second_back = second_back + back.came[i].astype(f32)
    middle = r.middle[...]
    inverse = lax.rsqrt(jnp.mean(middle * middle, axis=-1, keepdims=True) + epsilon)
    normed = middle * inverse
    scaled = second_back * r.gains[1:, :].astype(f32)
    moe_gain_grad = jnp.sum(second_back * normed, axis=0, keepdims=True)
    middle_grad = r.grad_top[...].astype(f32) + inverse * (
        scaled - normed * jnp.mean(scaled * normed, axis=-1, keepdims=True)
    )
    r.middle_grad[...] = middle_grad
    r.branch[...] = middle_grad.astype(bf16)
    experts_all = logit_back.shape[0]
    r.small_rows[...] = jnp.zeros_like(r.small_rows)
    r.small_rows[:experts_all, :] = nn(logit_back, r.second_low[...])
    r.small_rows[experts_all : experts_all + 1, :] = moe_gain_grad

    def to(place, src, dst, send, recv):
        return pltpu.make_async_remote_copy(
            src_ref=src,
            dst_ref=dst,
            send_sem=send,
            recv_sem=recv,
            device_id={"context": place},
            device_id_type=MESH,
        )

    def ask(t):
        return [
            to(helper, src.at[t], dst.at[t], r.ask_send.at[i, t], r.ask_recv.at[i, t])
            for i, (src, dst) in enumerate(((r.do, r.far_do), (r.stats, r.far_stats)))
        ]

    def answer(t):
        return to(
            last, r.far_dq_low.at[t], r.dq_came.at[t], r.answer_send.at[t], r.answer_recv.at[t]
        )

    @pl.loop(0, slices)
    def _(t):
        at = pl.ds(pl.multiple_of(t * 256, 256), 256)
        turned = nt(r.w_out_v[at, :], r.branch[...]).astype(bf16)
        r.stats[t, 0] = r.lse[t]
        for half in (0, 1):
            a, b = half * HEAD_DIM, (half + 1) * HEAD_DIM
            for ab in (0, 1):
                c = (2 * half + ab) * HEAD_DIM
                r.do[t, a:b, ab * tokens : (ab + 1) * tokens] = turned[c : c + HEAD_DIM]
            r.stats[t, 1, half : half + 1, :] = jnp.sum(
                r.do[t, a:b, :].astype(f32) * r.heads[2 * t + half].astype(f32),
                axis=0,
                keepdims=True,
            )

        @pl.when(me == last)
        def _():
            for copy in ask(t):
                copy.start()

    @pl.loop(0, ne)
    def _(g):
        at = pl.ds(pl.multiple_of(g * group, group), group)
        grad = nn(r.attn_turned[at, :], r.branch[...])
        r.made[g] = grad.reshape((nz, nd, group // (nz * nd), width)).astype(bf16)

    proj.over_dp()
    for which in (0, 1):
        line.left(1, which, 0)
        line.cross(2, which, 0)
    proj.over_expert()
    out.onward()
    line.join(1, 0, 2)

    r.dq[...] = jnp.zeros_like(r.dq)
    r.far_dq[...] = jnp.zeros_like(r.far_dq)

    def mine(j):
        return me == last if j == last else (j <= me) & (me < last)

    for j in range(nz):

        @pl.when(mine(j))
        def _():
            r.bias[j] = mask_bias(r.seg_all, j, me, tokens)

    @pl.when(me == helper)
    def _():
        for j in range(last):
            r.far_bias[j] = mask_bias(r.seg_all, j, last, tokens)

    def back_slice(j, t, queries, do, stats, dq, bias):
        keys = r.kv_all[j, t, :, :128]
        vals = r.kv_all[j, t, :, 128:]
        dks, dvs = [], []
        for half in (0, 1):
            keep = lane_half((tokens, 128), half)
            zero = jnp.zeros_like(keys)
            keys_half = jnp.where(keep, keys, zero)
            scores = nt(keys_half, queries[t]) + jnp.concatenate([bias[j]] * 2, axis=1)
            soft = jnp.exp(scores - stats[t, 0, half : half + 1, :])
            soft_grad = nn(jnp.where(keep, vals, zero), do[t])
            back = (soft * (soft_grad - stats[t, 1, half : half + 1, :])).astype(bf16)
            dvs.append(nt(soft.astype(bf16), do[t]))
            dks.append(nn(back, queries[t]))
            dq[t] += tn(keys_half, back)
        low = lane_half((tokens, 128), 0)
        return jnp.concatenate(
            [jnp.where(low, dks[0], dks[1]), jnp.where(low, dvs[0], dvs[1])], axis=1
        )

    def give(j, t):
        return to(
            me - 1, r.kv_part.at[j, t], r.kv_came.at[j, t], r.kv_send.at[j, t], r.kv_recv.at[j, t]
        )

    @pl.loop(0, slices)
    def _(t):
        for j in range(nz):

            @pl.when(mine(j))
            def _():
                r.kv_sum[j] = back_slice(j, t, r.q, r.do, r.stats, r.dq, r.bias)

        @pl.when(me == helper)
        def _():
            for copy in ask(t):
                copy.wait_recv()
            for j in range(last):
                r.kv_sum[j] += back_slice(
                    j, t, r.q_far, r.far_do, r.far_stats, r.far_dq, r.far_bias
                )
                if j < helper:
                    r.kv_part[j, t] = r.kv_sum[j].astype(bf16)
                    give(j, t).start()
            r.far_dq_low[t] = r.far_dq[t].astype(bf16)
            answer(t).start()

        for j in range(helper):

            @pl.when((j < me) & (me < helper))
            def _():
                r.kv_part[j, t] = r.kv_sum[j].astype(bf16)

        r.own_kv[t] = r.kv_sum[me]

        @pl.when(t == 0)
        def _():
            line.join(1, 1, 2)
            for which in (0, 1):
                line.cross(2, which, 3)


    line.ends(0, 3)
    line.join(2, 0, 2)

    @pl.when(me == last)
    def _():
        @pl.loop(0, slices)
        def _(t):
            answer(t).wait_recv()
            r.dq[t] += r.dq_came[t].astype(f32)

    quarter = HEAD_DIM // 2
    cos_q, sin_q = (
        jnp.concatenate([r.turn[i].T[:quarter]] * 2, axis=1) * HEAD_DIM ** (-0.5) for i in (0, 1)
    )
    for t in range(slices):
        for half in (0, 1):
            a = half * HEAD_DIM
            first = r.dq[t, a : a + quarter, :]
            second = r.dq[t, a + quarter : a + 2 * quarter, :]
            turned = jnp.concatenate(
                [first * cos_q + second * sin_q, second * cos_q - first * sin_q], axis=0
            )
            pair = jnp.concatenate([turned[:, :tokens], turned[:, tokens:]], axis=0)
            at = (2 * t + half) * 128
            r.back_s[:, at : at + 128] = pair.T.astype(bf16)

    def make(a, b):
        @pl.loop(0, ne)
        def _(g):
            at = pl.ds(pl.multiple_of(g * group, group), group)
            grad = tn(r.first_low[:, at], r.back_s[:, a:b])
            r.made[g] = grad.reshape((nz, nd, group // (nz * nd), b - a)).astype(bf16)

    proj.made_free()
    make(0, width)
    query.over_dp()
    for which in (0, 1):
        line.join(1, which, 1)
    line.join(2, 1, 2)
    for k in chunks:
        line.ends(k, 0)
    query.over_expert()

    @pl.loop(0, slices)
    def _(t):
        for j in range(helper):

            @pl.when((j < me) & (me < helper))
            def _():
                give(j, t).wait_recv()
                r.kv_part[j, t] = (
                    r.kv_part[j, t].astype(f32) + r.kv_came[j, t].astype(f32)
                ).astype(bf16)
                give(j, t).start()

        @pl.when(me < helper)
        def _():
            give(me, t).wait_recv()
            r.own_kv[t] += r.kv_came[me, t].astype(f32)

    for which in (0, 1):
        line.join(2, which, 1)
    for k in chunks[1:]:
        line.ends(k, 3)
    cos_k, sin_k = r.turn[0], r.turn[1]
    first_lanes = lax.rem(lax.broadcasted_iota(jnp.int32, (tokens, 128), 1), HEAD_DIM) < quarter
    for t in range(slices):
        grad = r.own_kv[t, :, :128]
        swapped = jnp.where(
            first_lanes, pltpu.roll(grad, 128 - quarter, 1), pltpu.roll(grad, quarter, 1)
        )
        r.back_s[:, width + t * 128 : width + (t + 1) * 128] = (
            grad * cos_k + swapped * sin_k
        ).astype(bf16)
        at = width + kv_width + t * 128
        r.back_s[:, at : at + 128] = r.own_kv[t, :, 128:].astype(bf16)
    query.made_free()
    make(width, width + 2 * kv_width)
    kv.over_dp()
    proj.over_context()

    first_back = nt(r.back_s[:, :width], r.w_query_v[...])
    first_back = first_back + nt(r.back_s[:, width : width + kv_width], r.w_key_v[...])
    first_back = first_back + nt(r.back_s[:, width + kv_width :], r.w_value_v[...])
    values = r.tokens[...].astype(f32)
    inverse = lax.rsqrt(jnp.mean(values * values, axis=-1, keepdims=True) + epsilon)
    normed = values * inverse
    scaled = first_back * r.gains[:1, :].astype(f32)
    r.small_rows[experts_all + 1 : experts_all + 2, :] = jnp.sum(
        first_back * normed, axis=0, keepdims=True
    )
    r.input_grad[...] = r.middle_grad[...] + inverse * (
        scaled - normed * jnp.mean(scaled * normed, axis=-1, keepdims=True)
    )
    small_turned = r.small_rows[...].T
    r.small_made[...] = small_turned.reshape(r.small_made.shape).astype(bf16)
    small.over_dp()
    kv.over_expert()
    small.over_expert()
    query.over_context()

    out.arrive()

    @pl.loop(0, tokens // 16)
    def _(i):
        at = pl.ds(pl.multiple_of(i * 16, 16), 16)
        total = r.middle[at, :] + out.own[at, :].astype(f32)
        for i in (0, 1):
            total = total + out.came[i, at, :].astype(f32)
        r.layer_out[at, :] = total

    gate_out, up_out, down_out = r.experts_out
    gate_rows, hid = gate_out.shape[1:]

    def put(k, at, value):
        if at < gate_rows:
            gate_out[k, at : at + 16, :] = value[:, :hid]
            up_out[k, at : at + 16, :] = value[:, hid:]
        else:
            down_out[k, at - gate_rows : at - gate_rows + 16, :] = value

    for at in range(0, r.first_shard.shape[0], 16):
        put(0, at, r.first_shard[at : at + 16, :])
    line.total(0, functools.partial(put, 1))
    kv.over_context()
    small.over_context()
    line.total(1, functools.partial(put, 2))
    kv.made_free()
    small.made_free()
    for group_sum, target in zip((proj, query, kv, small), r.sums_out + [r.small_sum]):
        group_sum.finish(target)
    r.router_out[...] = r.small_sum[:, :experts_all]
    turned = r.small_sum[...].T
    r.gains_out[0] = turned[experts_all + 1 : experts_all + 2]
    r.gains_out[1] = turned[experts_all : experts_all + 1]
    for which in (0, 1):
        line.left(1, which, 3)
        line.left(2, which, 3)
        line.left(2, which, 0)
    line.total(2, functools.partial(put, 3))
    back.finish()
    out.finish()
    for step in range(1, ne):
        gates_copy(step).wait_send()
    for j in range(helper):

        @pl.when((j < me) & (me < last))
        def _():
            for t in range(slices):
                give(j, t).wait_send()

    @pl.when(me == last)
    def _():
        for t in range(slices):
            for copy in ask(t):
                copy.wait_send()

    @pl.when(me == helper)
    def _():
        for t in range(slices):
            answer(t).wait_send()


def tail(sizes, cid, hidden, hbm_ins, vmem_ins):
    ne, nz, nd = sizes
    ins = types.SimpleNamespace(**hbm_ins, **vmem_ins)
    tokens, width = ins.tokens.shape
    slices, wide, _ = ins.q.shape
    chunks, _, piece, _ = ins.held_in.shape
    kv_shape = ins.kv_all.shape[1:]
    kv_cols = slices * 256
    rows = width // (ne * nz * nd)
    gate_rows = width // (nz * nd)
    shard = lambda *shape: jax.ShapeDtypeStruct(shape, f32)
    outs = dict(
        layer_out=shard(tokens, width),
        input_grad=shard(tokens, width),
        sums_out=[shard(rows, c) for c in (width, width, kv_cols)],
        router_out=shard(rows, ins.w_router_turned.shape[0]),
        gains_out=shard(2, 1, rows),
        experts_out=[
            shard(chunks, gate_rows, hidden),
            shard(chunks, gate_rows, hidden),
            shard(chunks, piece - gate_rows, width),
        ],
    )
    dma = pltpu.SemaphoreType.DMA
    vmem = pltpu.VMEM
    scratch = dict(
        back=Fold.scratch(tokens, width),
        out=Fold.scratch(tokens, width),
        soft_all=vmem(ins.soft_in.shape, f32),
        w_out_v=vmem(ins.w_out.shape, bf16),
        w_query_v=vmem(ins.w_query.shape, bf16),
        w_key_v=vmem(ins.w_key.shape, bf16),
        w_value_v=vmem(ins.w_value.shape, bf16),
        attn_turned=vmem((width, tokens), bf16),
        middle_grad=vmem((tokens, width), f32),
        branch=vmem((tokens, width), bf16),
        small_rows=vmem((128, width), f32),
        do=vmem((slices, 128, wide), bf16),
        stats=vmem((slices, 2, 2, wide), f32),
        bias=vmem((nz, tokens, tokens), f32),
        dq=vmem((slices, 128, wide), f32),
        dq_came=vmem((slices, 128, wide), bf16),
        far_do=vmem((slices, 128, wide), bf16),
        far_stats=vmem((slices, 2, 2, wide), f32),
        far_bias=vmem((nz - 1, tokens, tokens), f32),
        far_dq=vmem((slices, 128, wide), f32),
        far_dq_low=vmem((slices, 128, wide), bf16),
        kv_sum=vmem((nz, tokens, 256), f32),
        kv_part=vmem((nz - 2,) + kv_shape, bf16),
        kv_came=vmem((nz - 2,) + kv_shape, bf16),
        own_kv=vmem(kv_shape, f32),
        back_s=vmem((tokens, width + kv_cols), bf16),
        made=vmem((ne, nz, nd, rows, width), bf16),
        small_made=vmem((ne, nz, nd, rows, 128), bf16),
        small_sum=vmem((rows, 128), f32),
        gates_send=dma((ne,)),
        gates_recv=dma((ne,)),
        load_sem=dma((6,)),
        tables_own=vmem(ins.tables_all.shape[1:], f32),
        held_sem=dma((chunks,)),
        kv_send=dma((nz, slices)),
        kv_recv=dma((nz, slices)),
        ask_send=dma((2, slices)),
        ask_recv=dma((2, slices)),
        answer_send=dma((slices,)),
        answer_recv=dma((slices,)),
        line=Line.scratch(nz, chunks - 1, piece, width),
        proj=Spread.scratch(sizes, rows, width),
        query=Spread.scratch(sizes, rows, width),
        kv=Spread.scratch(sizes, rows, kv_cols),
        small=Spread.scratch(sizes, rows, 128),
    )
    return call_named(
        functools.partial(tail_kernel, sizes), hbm_ins, vmem_ins, outs, scratch, cid, 63 << 20, ()
    )


def deliver_kernel(parts, count, *refs):
    ins, outs, sem, held = refs[:count], refs[count : 2 * count], refs[2 * count], refs[2 * count + 1 :]
    reads = [
        pltpu.make_async_copy(
            ins[i] if part is None else ins[i].at[:, pl.ds(*part)], held[i], sem.at[0, i]
        )
        for i, part in enumerate(parts)
    ]
    writes = [pltpu.make_async_copy(held[i], outs[i], sem.at[1, i]) for i in range(count)]
    for copy in reads:
        copy.start()
    for read, write in zip(reads, writes):
        read.wait()
        write.start()
    for copy in writes:
        copy.wait()


def deliver(moved):
    arrays, parts = zip(*moved)
    hbm = pl.BlockSpec(memory_space=pl.ANY)
    shapes = [a.shape[:-1] + (part[1] if part else a.shape[-1],) for a, part in moved]
    return pl.pallas_call(
        functools.partial(deliver_kernel, parts, len(parts)),
        out_shape=[jax.ShapeDtypeStruct(shape, a.dtype) for shape, a in zip(shapes, arrays)],
        in_specs=[hbm] * len(parts),
        out_specs=[hbm] * len(parts),
        scratch_shapes=[pltpu.SemaphoreType.DMA((2, len(parts)))]
        + [pltpu.VMEM(shape, a.dtype) for shape, a in zip(shapes, arrays)],
        compiler_params=pltpu.CompilerParams(vmem_limit_bytes=60 << 20),
        name="deliver",
    )(*arrays)


def turn_tables(tokens, blocks):
    freq = rope_base ** (-2.0 * np.arange(HEAD_DIM // 2) / HEAD_DIM)
    freq = np.tile(freq, 128 // freq.size)
    inner = np.arange(tokens)[:, None] * freq
    base = tokens * np.arange(blocks)[:, None] * freq
    return tuple(
        jnp.asarray(np.stack([np.cos(a), np.sin(a)]), f32) for a in (inner, base)
    )


def body(
    sizes,
    tokens,
    attn_scale,
    w_query,
    w_key,
    w_value,
    w_out,
    moe_scale,
    w_router,
    w_gate,
    w_up,
    w_down,
    segment_ids,
    expert_choice,
    slot_order,
    out_grad,
):
    ne, nz, nd = sizes
    local_rows = tokens.shape[1]
    kv_width = w_key.shape[1]
    experts_all = w_router.shape[1]
    pair_count = local_rows * expert_choice.shape[2]
    capacity = (pair_count * 9 + 8 * experts_all - 1) // (8 * experts_all)
    inner, base = turn_tables(local_rows, nz)
    w_router_turned = w_router.T
    gains = jnp.stack([attn_scale, moe_scale])

    begun = front(
        sizes,
        1,
        capacity,
        dict(
            w_query=w_query, w_key=w_key, w_value=w_value, w_out=w_out, grad_top=out_grad[0]
        ),
        dict(
            tokens=tokens[0],
            gains=gains,
            w_router_turned=w_router_turned,
            seg=segment_ids,
            chosen=expert_choice[0].T,
            order=slot_order[0],
            inner=inner,
            base=base,
        ),
    )
    mixed = experts(
        sizes,
        2,
        capacity,
        dict(w_gate=w_gate, w_up=w_up, w_down=w_down),
        dict(rows_all=begun.rows_all, grad_all=begun.grad_all, tables_all=begun.tables_all),
    )
    ended = tail(
        sizes,
        3,
        w_gate.shape[2],
        dict(
            held_in=mixed.held,
            back_in=mixed.back_part,
            out_in=mixed.out_part,
            soft_in=mixed.soft_part,
            w_query=w_query,
            w_key=w_key,
            w_value=w_value,
            w_out=w_out,
            tables_all=begun.tables_all,
        ),
        dict(
            q=begun.q,
            q_far=begun.q_far,
            kv_all=begun.kv_all,
            seg_all=begun.seg_all,
            lse=begun.lse,
            heads=begun.heads,
            middle=begun.middle,
            tokens=tokens[0],
            grad_top=out_grad[0],
            second_low=begun.second_low,
            first_low=begun.first_low,
            w_router_turned=w_router_turned,
            gains=gains,
            turn=begun.turn,
            first_shard=mixed.shard,
        ),
    )
    out_shard, query_shard, kv_shard = ended.sums_out
    moved = [
        (ended.layer_out, None),
        (ended.input_grad, None),
        (query_shard, None),
        (kv_shard, (0, kv_width)),
        (kv_shard, (kv_width, kv_width)),
        (out_shard, None),
        *((array, None) for array in ended.experts_out),
    ]
    layer_out, input_grad, *shards = deliver(moved)
    return (
        layer_out[None],
        input_grad[None],
        ended.gains_out[0, 0],
        ended.gains_out[1, 0],
        *shards[:4],
        ended.router_out,
        *shards[4:],
    )


def solution(mesh):
    sizes = (mesh.shape["expert"], mesh.shape["context"], mesh.shape["dp"])
    in_specs = (
        P(("expert", "dp"), "context", None),
        P(),
        P(),
        P(),
        P(),
        P(),
        P(),
        P(),
        P("expert", None, None),
        P("expert", None, None),
        P("expert", None, None),
        P(("expert", "dp"), "context"),
        P(("expert", "dp"), "context", None),
        P(("expert", "dp"), "context", None),
        P(("expert", "dp"), "context", None),
    )
    out_specs = (
        P(("expert", "dp"), "context", None),
        P(("expert", "dp"), "context", None),
        P(("expert", "context", "dp")),
        P(("expert", "context", "dp")),
        P(("expert", "context", "dp"), None),
        P(("expert", "context", "dp"), None),
        P(("expert", "context", "dp"), None),
        P(("expert", "context", "dp"), None),
        P(("expert", "context", "dp"), None),
        P("expert", ("context", "dp"), None),
        P("expert", ("context", "dp"), None),
        P("expert", ("context", "dp"), None),
    )
    return jax.shard_map(
        functools.partial(body, sizes),
        mesh=mesh,
        in_specs=in_specs,
        out_specs=out_specs,
        check_vma=False,
    )
```

```python
import functools
import types

import jax
import jax.numpy as jnp
import numpy as np
from jax import lax
from jax.experimental import pallas as pl
from jax.experimental.pallas import tpu as pltpu
from jax.sharding import PartitionSpec as P

HEAD_DIM = 64
MESH = pl.DeviceIdType.MESH

epsilon = 1e-06
rope_base = 10000.0
negative_large = -1e30
bf16 = jnp.bfloat16
f32 = jnp.float32


def nt(a, b):
    return lax.dot_general(a, b, (((1,), (1,)), ((), ())), preferred_element_type=f32)


def tn(a, b):
    return lax.dot_general(a, b, (((0,), (0,)), ((), ())), preferred_element_type=f32)


def nn(a, b):
    return jnp.dot(a, b, preferred_element_type=f32)


def add_rows(dst, dst_at, src, src_at, rows):
    step = 16

    @pl.loop(0, rows // step)
    def _(i):
        at = pl.ds(pl.multiple_of(i * step, step), step)
        dst[dst_at + (at, slice(None))] = (
            dst[dst_at + (at, slice(None))].astype(f32) + src[src_at + (at, slice(None))].astype(f32)
        ).astype(bf16)


def lane_half(shape, which):
    lanes = lax.broadcasted_iota(jnp.int32, shape, 1)
    return (lanes >= HEAD_DIM) if which else (lanes < HEAD_DIM)


def column_of(row):
    n = row.shape[1]
    rows = lax.broadcasted_iota(jnp.int32, (n, n), 0)
    cols = lax.broadcasted_iota(jnp.int32, (n, n), 1)
    return jnp.sum(jnp.where(rows == cols, row, 0.0), axis=1, keepdims=True)


def mask_bias(seg_ref, block, me, tokens):
    key_seg = column_of(seg_ref[block, :1, :])
    same = key_seg == seg_ref[me, :1, :]
    rows = lax.broadcasted_iota(jnp.int32, (tokens, tokens), 0) + block * tokens
    cols = lax.broadcasted_iota(jnp.int32, (tokens, tokens), 1) + me * tokens
    return jnp.where(same & (rows <= cols), 0.0, negative_large)


def named(defs, refs):
    counts = [d.num_leaves for d in defs]
    at = [sum(counts[:i]) for i in range(len(counts) + 1)]
    trees = [jax.tree.unflatten(d, refs[at[i] : at[i + 1]]) for i, d in enumerate(defs)]
    r = types.SimpleNamespace(**{k: v for tree in trees for k, v in tree.items()})
    read, (copies, sem) = trees[1], trees[3]["read"]
    r.loads = [
        pltpu.make_async_copy(read[k], copies[k], sem.at[i]) for i, k in enumerate(sorted(read))
    ]
    for k in read:
        setattr(r, k, copies[k])
    return r


def call_named(kernel, kept, read, outs, scratch, cid, limit, kept_outs):
    vm = pl.BlockSpec(memory_space=pltpu.VMEM)
    hbm = pl.BlockSpec(memory_space=pl.ANY)
    scratch["read"] = (
        {k: pltpu.VMEM(v.shape, v.dtype) for k, v in read.items()},
        pltpu.SemaphoreType.DMA((len(read),)),
    )
    flats, defs = zip(*(jax.tree.flatten(t) for t in (kept, read, outs, scratch)))
    out_specs = jax.tree.leaves(
        {k: jax.tree.map(lambda _: hbm if k in kept_outs else vm, v) for k, v in outs.items()}
    )
    results = pl.pallas_call(
        functools.partial(kernel, defs),
        out_shape=tuple(flats[2]),
        in_specs=[hbm] * (len(flats[0]) + len(flats[1])),
        out_specs=tuple(out_specs),
        scratch_shapes=flats[3],
        compiler_params=pltpu.CompilerParams(
            collective_id=cid, has_side_effects=True, vmem_limit_bytes=limit
        ),
        name=kernel.func.__name__,
    )(*flats[0], *flats[1])
    return types.SimpleNamespace(**jax.tree.unflatten(defs[2], results))


def slot_table(chosen, order, experts_all, capacity):
    top_count, tokens = chosen.shape
    pairs = order.shape[1]
    shift = top_count.bit_length() - 1
    if top_count != 1 << shift:
        raise ValueError("top count")
    owner = jnp.where(
        (order >> shift) == lax.broadcasted_iota(jnp.int32, (tokens, pairs), 0), 1.0, 0.0
    ).astype(bf16)
    which = (order & (top_count - 1)) == lax.broadcasted_iota(jnp.int32, (top_count, pairs), 0)
    turns = lax.broadcasted_iota(jnp.int32, (top_count, pairs), 1)
    high, low = (
        nt(jnp.where(which, part.astype(f32), 0.0).astype(bf16), owner)
        for part in (turns >> 8, turns & 255)
    )
    turn_of = high * 256.0 + low
    far = float(2 * pairs)
    ids = lax.broadcasted_iota(jnp.int32, (128, tokens), 0)
    turn_row = jnp.full((128, tokens), far, f32)
    for k in range(top_count):
        turn_row = jnp.where(chosen[k : k + 1, :] == ids, turn_of[k : k + 1, :], turn_row)
    turn_at = turn_row.T
    for e in range(experts_all):
        row = turn_row[e : e + 1, :]
        rank = jnp.sum(jnp.where(turn_at[:, e : e + 1] < row, 1.0, 0.0), axis=0, keepdims=True)
        yield jnp.where((row < far) & (rank < capacity), rank, -1.0)


def partners(ex, ne):
    if ne != 4:
        raise ValueError("expert")
    return ex + 1 - 2 * lax.rem(ex, 2), lax.rem(ex + 2, 4)


def front_kernel(sizes, capacity, defs, *refs):
    r = named(defs, refs)
    ne, nz, nd = sizes
    ex, me = lax.axis_index("expert"), lax.axis_index("context")
    tokens, width = r.tokens.shape
    kv_width = r.w_key.shape[1]
    slices = kv_width // 128
    quarter = HEAD_DIM // 2

    barrier = pltpu.get_barrier_semaphore()
    for step in range(1, ne):
        pl.semaphore_signal(
            barrier, inc=1, device_id={"expert": lax.rem(ex + step, ne)}, device_id_type=MESH
        )

    @pl.when(me > 0)
    def _():
        pl.semaphore_signal(barrier, inc=1, device_id={"context": me - 1}, device_id_type=MESH)

    @pl.when(me < nz - 1)
    def _():
        pl.semaphore_signal(barrier, inc=1, device_id={"context": me + 1}, device_id_type=MESH)

    loads = [
        pltpu.make_async_copy(src, dst, r.load_sem.at[i])
        for i, (src, dst) in enumerate(
            (
                (r.w_key, r.w_key_v),
                (r.w_value, r.w_value_v),
                (r.w_query, r.w_query_v),
                (r.w_out, r.w_out_v),
                (r.grad_top, r.grad_all.at[ex]),
            )
        )
    ]
    for copy in r.loads + loads:
        copy.start()
    pl.semaphore_wait(
        barrier, ne - 1 + jnp.where(me > 0, 1, 0) + jnp.where(me < nz - 1, 1, 0)
    )

    def spread(kind, step):
        src = (r.grad_top, r.tables_s)[kind]
        dst = (r.grad_all, r.tables_all)[kind]
        return pltpu.make_async_remote_copy(
            src_ref=src,
            dst_ref=dst.at[ex],
            send_sem=r.spread_send.at[kind, step],
            recv_sem=r.spread_recv.at[kind, step],
            device_id={"expert": lax.rem(ex + step, ne)},
            device_id_type=MESH,
        )

    pair = partners(ex, ne)
    halves = (pl.ds(0, tokens // 2), pl.ds(tokens // 2, tokens // 2))

    def hand(i, half, onward):
        at = halves[half]
        src = r.rows_all.at[pair[1 - i], at] if onward else r.second_s.at[at]
        dst = r.rows_all.at[pair[1 - i] if onward else ex, at]
        return pltpu.make_async_remote_copy(
            src_ref=src,
            dst_ref=dst,
            send_sem=r.hand_send.at[i, half, int(onward)],
            recv_sem=r.hand_recv.at[i, half, int(onward)],
            device_id={"expert": pair[i]},
            device_id_type=MESH,
        )

    last, helper = nz - 1, nz - 2

    def to(place, src, dst, send, recv):
        return pltpu.make_async_remote_copy(
            src_ref=src,
            dst_ref=dst,
            send_sem=send,
            recv_sem=recv,
            device_id={"context": place},
            device_id_type=MESH,
        )

    def up(j, t):
        at = r.kv_s.at[j, t]
        return to(me + 1, at, at, r.up_send.at[j, t], r.up_recv.at[j, t])

    def up_seg(j):
        at = r.seg_s.at[j]
        return to(me + 1, at, at, r.seg_send.at[j], r.seg_recv.at[j])

    ask = [
        to(helper, src, dst, r.ask_send.at[i], r.ask_recv.at[i])
        for i, (src, dst) in enumerate(
            ((r.q_s, r.q_far_s), (r.seg_s.at[last], r.seg_s.at[last]))
        )
    ]

    def answer(t):
        return [
            to(last, src.at[t], dst.at[t], r.answer_send.at[i, t], r.answer_recv.at[i, t])
            for i, (src, dst) in enumerate(
                ((r.far_head, r.far_head_in), (r.far_lse, r.far_lse_in))
            )
        ]

    for step in range(1, ne):
        spread(0, step).start()

    for copy in r.loads:
        copy.wait()

    values = r.tokens[...].astype(f32)
    inverse = lax.rsqrt(jnp.mean(values * values, axis=-1, keepdims=True) + epsilon)
    first = (values * inverse * r.gains[:1, :].astype(f32)).astype(bf16)
    r.first_s[...] = first
    cos_b, sin_b = r.base[0, pl.ds(me, 1), :], r.base[1, pl.ds(me, 1), :]
    cos_i, sin_i = r.inner[0], r.inner[1]
    cosine = cos_i * cos_b - sin_i * sin_b
    sine = sin_i * cos_b + cos_i * sin_b
    first_lanes = lax.rem(lax.broadcasted_iota(jnp.int32, (tokens, 128), 1), HEAD_DIM) < quarter
    sine = jnp.where(first_lanes, sine, -sine)
    r.turn_s[0] = cosine
    r.turn_s[1] = sine

    def rotate(x):
        swapped = jnp.where(
            first_lanes, pltpu.roll(x, 128 - quarter, 1), pltpu.roll(x, quarter, 1)
        )
        return x * cosine - swapped * sine

    loads[0].wait()
    keys = nn(first, r.w_key_v[...])
    for t in range(slices):
        at = slice(t * 128, (t + 1) * 128)
        r.kv_s[me, t, :, :128] = rotate(keys[:, at]).astype(bf16)
    loads[1].wait()
    vals = nn(first, r.w_value_v[...]).astype(bf16)
    for t in range(slices):
        r.kv_s[me, t, :, 128:] = vals[:, t * 128 : (t + 1) * 128]
    r.seg_s[me] = jnp.broadcast_to(r.seg[...].astype(f32), (8, tokens))

    @pl.when(me < helper)
    def _():
        up_seg(me).start()
        for t in range(slices):
            up(me, t).start()

    loads[2].wait()
    factor = HEAD_DIM ** (-0.5)
    low = lane_half((tokens, 128), 0)
    for t in range(slices):
        two = nn(first, r.w_query_v[:, t * 256 : (t + 1) * 256])
        left, right = rotate(two[:, :128]), rotate(two[:, 128:])
        even = jnp.where(low, left, pltpu.roll(right, HEAD_DIM, 1))
        odd = jnp.where(low, pltpu.roll(left, HEAD_DIM, 1), right)
        r.q_s[t, :tokens, :] = (even * factor).astype(bf16)
        r.q_s[t, tokens:, :] = (odd * factor).astype(bf16)

    @pl.when(me == last)
    def _():
        for copy in ask:
            copy.start()

    experts_all = r.tables_s.shape[1]
    for e, row in enumerate(slot_table(r.chosen[...], r.order[...], experts_all, capacity)):
        r.tables_s[0, e : e + 1, :] = row

    for ref in (r.acc, r.total, r.far_acc, r.far_total):
        ref[...] = jnp.zeros_like(ref)
    for ref in (r.top, r.far_top):
        ref[...] = jnp.full_like(ref, -3e38)

    def attend(j, t, queries, acc, top, total, bias):
        keys = r.kv_s[j, t, :, :128]
        vals = r.kv_s[j, t, :, 128:]
        for half in (0, 1):
            keep = lane_half((tokens, 128), half)
            zero = jnp.zeros_like(keys)
            scores = nt(jnp.where(keep, keys, zero), queries[t]) + jnp.concatenate(
                [bias[...]] * 2, axis=1
            )
            old = top[t, half : half + 1, :]
            new = jnp.maximum(old, jnp.max(scores, axis=0, keepdims=True))
            scale = jnp.exp(old - new)
            soft = jnp.exp(scores - new)
            top[t, half : half + 1, :] = new
            total[t, half : half + 1, :] = total[t, half : half + 1, :] * scale + jnp.sum(
                soft, axis=0, keepdims=True
            )
            mixed = tn(jnp.where(keep, vals, zero), soft.astype(bf16))
            a, b = half * HEAD_DIM, (half + 1) * HEAD_DIM
            acc[t, a:b, :] = acc[t, a:b, :] * scale + mixed[a:b]

    def own_slice(j, t):
        attend(j, t, r.q_s, r.acc, r.top, r.total, r.bias)

    def far_slice(j, t):
        attend(j, t, r.q_far_s, r.far_acc, r.far_top, r.far_total, r.far_bias)

    r.bias[...] = mask_bias(r.seg_s, me, me, tokens)

    @pl.loop(0, slices)
    def _(t):
        own_slice(me, t)

    @pl.when(me == helper)
    def _():
        for copy in ask:
            copy.wait_recv()
        r.far_bias[...] = mask_bias(r.seg_s, helper, last, tokens)

        @pl.loop(0, slices)
        def _(t):
            far_slice(helper, t)

    for step in range(1, nz - 1):
        j = me - step

        @pl.when((j >= 0) & (me < last))
        def _():
            up_seg(j).wait_recv()

            @pl.when(me < helper)
            def _():
                up_seg(j).start()

            r.bias[...] = mask_bias(r.seg_s, j, me, tokens)

            @pl.when(me == helper)
            def _():
                r.far_bias[...] = mask_bias(r.seg_s, j, last, tokens)

            @pl.loop(0, slices)
            def _(t):
                up(j, t).wait_recv()

                @pl.when(me < helper)
                def _():
                    up(j, t).start()

                @pl.when(me == helper)
                def _():
                    far_slice(j, t)
                    if step == nz - 2:
                        for half in (0, 1):
                            a, b = half * HEAD_DIM, (half + 1) * HEAD_DIM
                            r.far_head[t, a:b, :] = (
                                r.far_acc[t, a:b, :] / r.far_total[t, half : half + 1, :]
                            ).astype(bf16)
                        r.far_lse[t] = r.far_top[t] + jnp.log(r.far_total[t])
                        for copy in answer(t):
                            copy.start()

                own_slice(j, t)

    @pl.loop(0, slices)
    def _(t):
        r.lse_s[t] = r.top[t] + jnp.log(r.total[t])
        for half in (0, 1):
            a, b = half * HEAD_DIM, (half + 1) * HEAD_DIM
            r.acc[t, a:b, :] = r.acc[t, a:b, :] / r.total[t, half : half + 1, :]

        @pl.when(me == last)
        def _():
            for copy in answer(t):
                copy.wait_recv()
            near, far = r.lse_s[t], r.far_lse_in[t]
            top = jnp.maximum(near, far)
            both = top + jnp.log(jnp.exp(near - top) + jnp.exp(far - top))
            r.lse_s[t] = both
            near, far = jnp.exp(near - both), jnp.exp(far - both)
            for half in (0, 1):
                a, b = half * HEAD_DIM, (half + 1) * HEAD_DIM
                r.acc[t, a:b, :] = (
                    r.acc[t, a:b, :] * near[half : half + 1]
                    + r.far_head_in[t, a:b, :].astype(f32) * far[half : half + 1]
                )

    for t in range(slices):
        for half in (0, 1):
            a, b = half * HEAD_DIM, (half + 1) * HEAD_DIM
            head = r.acc[t, a:b, :].astype(bf16)
            r.heads_s[2 * t + half] = head
            for ab in (0, 1):
                h = (4 * t + 2 * half + ab) * HEAD_DIM
                r.attn_turned[h : h + HEAD_DIM, :] = head[:, ab * tokens : (ab + 1) * tokens]

    loads[3].wait()
    middle = r.tokens[...].astype(f32) + tn(r.attn_turned[...], r.w_out_v[...])
    r.middle_s[...] = middle
    inverse = lax.rsqrt(jnp.mean(middle * middle, axis=-1, keepdims=True) + epsilon)
    second = (middle * inverse * r.gains[1:, :].astype(f32)).astype(bf16)
    r.second_s[...] = second
    for i, half in ((0, 0), (1, 1), (0, 1), (1, 0)):
        hand(i, half, False).start()
    logits = nt(r.w_router_turned[...], second)
    grown = jnp.exp(logits - jnp.max(logits, axis=0, keepdims=True))
    r.tables_s[1] = grown / jnp.sum(grown, axis=0, keepdims=True)
    for step in range(1, ne):
        spread(1, step).start()
    stores = [
        pltpu.make_async_copy(src, dst, r.store_sem.at[i])
        for i, (src, dst) in enumerate(
            (
                (r.second_s, r.rows_all.at[ex]),
                (r.tables_s, r.tables_all.at[ex]),
                (r.q_s, r.q),
                (r.q_far_s, r.q_far),
                (r.kv_s, r.kv_all),
                (r.seg_s, r.seg_all),
                (r.lse_s, r.lse),
                (r.heads_s, r.heads),
                (r.middle_s, r.middle),
                (r.second_s, r.second_low),
                (r.first_s, r.first_low),
                (r.turn_s, r.turn),
            )
        )
    ]
    for copy in stores:
        copy.start()
    for copy in stores:
        copy.wait()
    for i in (0, 1):
        hand(i, i, False).wait_recv()
        hand(1 - i, i, True).start()
    loads[4].wait()
    for kind in range(2):
        for step in range(1, ne):
            spread(kind, step).wait()
    for i in (0, 1):
        hand(i, i, False).wait_send()
        hand(i, 1 - i, False).wait()
        hand(1 - i, i, True).wait()
    for step in range(nz - 1):
        j = me - step

        @pl.when((j >= 0) & (me < helper))
        def _():
            up_seg(j).wait_send()
            for t in range(slices):
                up(j, t).wait_send()

    @pl.when(me == last)
    def _():
        for copy in ask:
            copy.wait_send()

    @pl.when(me == helper)
    def _():
        for t in range(slices):
            for copy in answer(t):
                copy.wait_send()


def front(sizes, cid, capacity, hbm_ins, vmem_ins):
    ne, nz, nd = sizes
    ins = types.SimpleNamespace(**hbm_ins, **vmem_ins)
    tokens, width = ins.tokens.shape
    kv_width = ins.w_key.shape[1]
    slices, wide = kv_width // 128, 2 * tokens
    experts_all = ins.w_router_turned.shape[0]
    shape = jax.ShapeDtypeStruct
    vmem, dma = pltpu.VMEM, pltpu.SemaphoreType.DMA
    sized = dict(
        q=((slices, wide, 128), bf16),
        q_far=((slices, wide, 128), bf16),
        kv=((nz, slices, tokens, 256), bf16),
        seg=((nz, 8, tokens), f32),
        lse=((slices, 2, wide), f32),
        heads=((2 * slices, HEAD_DIM, wide), bf16),
        middle=((tokens, width), f32),
        second=((tokens, width), bf16),
        first=((tokens, width), bf16),
        turn=((2, tokens, 128), f32),
        tables=((2, experts_all, tokens), f32),
    )
    outs = dict(
        rows_all=shape((ne, tokens, width), bf16),
        grad_all=shape((ne, tokens, width), bf16),
        tables_all=shape((ne, 2, experts_all, tokens), f32),
        q=shape(*sized["q"]),
        q_far=shape(*sized["q"]),
        kv_all=shape(*sized["kv"]),
        seg_all=shape(*sized["seg"]),
        lse=shape(*sized["lse"]),
        heads=shape(*sized["heads"]),
        middle=shape(*sized["middle"]),
        second_low=shape(*sized["second"]),
        first_low=shape(*sized["first"]),
        turn=shape(*sized["turn"]),
    )
    scratch = dict(
        w_query_v=vmem(ins.w_query.shape, bf16),
        w_key_v=vmem(ins.w_key.shape, bf16),
        w_value_v=vmem(ins.w_value.shape, bf16),
        w_out_v=vmem(ins.w_out.shape, bf16),
        attn_turned=vmem((width, tokens), bf16),
        acc=vmem((slices, 128, wide), f32),
        top=vmem((slices, 2, wide), f32),
        total=vmem((slices, 2, wide), f32),
        bias=vmem((tokens, tokens), f32),
        far_acc=vmem((slices, 128, wide), f32),
        far_top=vmem((slices, 2, wide), f32),
        far_total=vmem((slices, 2, wide), f32),
        far_bias=vmem((tokens, tokens), f32),
        far_head=vmem((slices, 128, wide), bf16),
        far_lse=vmem((slices, 2, wide), f32),
        far_head_in=vmem((slices, 128, wide), bf16),
        far_lse_in=vmem((slices, 2, wide), f32),
        load_sem=dma((5,)),
        store_sem=dma((12,)),
        spread_send=dma((2, ne)),
        spread_recv=dma((2, ne)),
        hand_send=dma((2, 2, 2)),
        hand_recv=dma((2, 2, 2)),
        up_send=dma((nz, slices)),
        up_recv=dma((nz, slices)),
        seg_send=dma((nz,)),
        seg_recv=dma((nz,)),
        ask_send=dma((2,)),
        ask_recv=dma((2,)),
        answer_send=dma((2, slices)),
        answer_recv=dma((2, slices)),
        **{k + "_s": vmem(*v) for k, v in sized.items()},
    )
    return call_named(
        functools.partial(front_kernel, sizes, capacity),
        hbm_ins, vmem_ins, outs, scratch, cid, 60 << 20, tuple(outs),
    )


class Line:
    def __init__(self, nz, held, came, send, recv):
        if nz != 4:
            raise ValueError("context")
        self.nz, self.held, self.came, self.send, self.recv = nz, held, came, send, recv
        self.me = lax.axis_index("context")

    @staticmethod
    def scratch(nz, chunks, rows, width):
        return [
            pltpu.VMEM((chunks, nz, rows, width), bf16),
            pltpu.VMEM((chunks, nz, rows, width), bf16),
            pltpu.SemaphoreType.DMA((chunks, nz)),
            pltpu.SemaphoreType.DMA((chunks, nz)),
        ]

    routes = {
        (0, 3): (1, 3),
        (0, 2): (1, 2),
        (0, 1): (1, 0),
        (3, 0): (2, 0),
        (3, 1): (2, 1),
        (3, 2): (2, 3),
        (1, 0): (0, 1),
        (2, 3): (3, 2),
        (1, 3): (3, 1),
        (1, 2): (2, 2),
        (2, 0): (0, 2),
        (2, 1): (1, 1),
    }

    def copy(self, k, place, s):
        target, slot = self.routes[place, s]
        return pltpu.make_async_remote_copy(
            src_ref=self.held.at[k, s],
            dst_ref=self.came.at[k, slot],
            send_sem=self.send.at[k, s],
            recv_sem=self.recv.at[k, slot],
            device_id={"context": target},
            device_id_type=MESH,
        )

    def start(self, k, moves):
        for place in range(self.nz):
            pieces = [s for p, s in moves if p == place]
            if pieces:

                @pl.when(self.me == place)
                def _():
                    for s in pieces:
                        self.copy(k, place, s).start()

    def far_piece(self, place, which):
        return 3 - which if place < 2 else which

    def cross(self, k, which, place):
        self.start(k, [(place, self.far_piece(place, which))])

    def left(self, k, which, place):
        @pl.when(self.me == place)
        def _():
            self.copy(k, place, self.far_piece(place, which)).wait_send()

    def straight(self, k):
        self.start(k, [(1, 0), (2, 3)])

    def ends(self, k, place):
        self.start(k, [(place, 1 if place == 0 else 2)])

    def join(self, k, which, place):
        s = self.far_piece(place, which)

        @pl.when(self.me == place)
        def _():
            self.copy(k, 0 if place == 1 else 3, s).wait_recv()
            add_rows(self.held, (k, s), self.came, (k, s), self.held.shape[2])
            self.copy(k, place, s).start()

    def total(self, k, put):
        for place in range(self.nz):

            @pl.when(self.me == place)
            def _():
                senders = [(p, s) for (p, s), (t, _) in self.routes.items() if t == place == s]
                for p, s in senders:
                    self.copy(k, p, s).wait_recv()
                for at in range(0, self.held.shape[2], 16):
                    rows = slice(at, at + 16)
                    value = self.held[k, place, rows].astype(f32)
                    for move in senders:
                        value = value + self.came[k, self.routes[move][1], rows].astype(f32)
                    put(at, value)
                for s in range(self.nz):
                    if s != place and (place in (1, 2) or abs(s - place) == 1):
                        self.copy(k, place, s).wait_send()


def experts_kernel(sizes, cap, defs, *refs):
    r = named(defs, refs)
    ne, nz, nd = sizes
    ex, dp, ctx = (lax.axis_index(a) for a in ("expert", "dp", "context"))
    local, width, hid = r.w_gate.shape
    tokens = r.rows_all.shape[1]
    gate_rows, down_rows = width // (nz * nd), hid // (nz * nd)
    line = Line(nz, r.held_s, *r.line)

    barrier = pltpu.get_barrier_semaphore()
    for axis, place, size in (("dp", dp, nd), ("context", ctx, nz)):
        for step in range(1, size):
            pl.semaphore_signal(
                barrier, inc=1, device_id={axis: lax.rem(place + step, size)}, device_id_type=MESH
            )

    def weights(e, slot):
        return [
            pltpu.make_async_copy(src, dst, r.weight_sem.at[slot, i])
            for i, (src, dst) in enumerate(
                (
                    (r.w_gate.at[e], r.both.at[slot, :, pl.ds(0, hid)]),
                    (r.w_up.at[e], r.both.at[slot, :, pl.ds(hid, hid)]),
                    (r.w_down.at[e], r.down.at[slot]),
                )
            )
        ]

    for copy in r.loads + weights(0, 0):
        copy.start()
    pl.semaphore_wait(barrier, nd + nz - 2)
    for copy in r.loads:
        copy.wait()

    def cores(k, step):
        other = lax.rem(dp + step, nd)
        return pltpu.make_async_remote_copy(
            src_ref=r.made.at[:, other],
            dst_ref=r.from_dp.at[step - 1, k],
            send_sem=r.dp_send.at[k, step],
            recv_sem=r.dp_recv.at[k, step],
            device_id={"dp": other},
            device_id_type=MESH,
        )

    def keep(k):
        return pltpu.make_async_copy(r.held_s.at[k], r.held.at[k], r.held_sem.at[k])

    def add_cores(k):
        for step in range(1, nd):
            cores(k, step).wait_recv()
            for z in range(nz):
                add_rows(r.held_s, (k, z), r.from_dp, (step - 1, k, z), gate_rows + down_rows)

        @pl.when(k > 0)
        def _():
            keep(k).start()

    row_id = lax.broadcasted_iota(jnp.int32, (cap, tokens), 0).astype(f32)

    @pl.loop(0, local)
    def _(e):
        slot = lax.rem(e, 2)
        own = pl.ds(pl.multiple_of(e * cap, 16), cap)
        for src in range(ne):
            at = pl.ds(src * cap, cap)
            hits = r.tables_all[src, 0, pl.ds(ex * local + e, 1), :] == row_id
            gate_row = r.tables_all[src, 1, pl.ds(ex * local + e, 1), :]
            gate = jnp.sum(jnp.where(hits, gate_row, 0.0), axis=1, keepdims=True)
            low = jnp.where(hits, 1.0, 0.0).astype(bf16)
            r.hits[src, own, :] = low
            r.gate_s[at, :] = jnp.broadcast_to(gate, (cap, 128))
            r.x_s[at, :] = nn(low, r.rows_all[src]).astype(bf16)
            og = nn(low, r.grad_all[src])
            r.og_s[at, :] = og.astype(bf16)
            r.sg_s[at, :] = (og * gate).astype(bf16)
        for copy in weights(e, slot):
            copy.wait()

        @pl.when(e < local - 1)
        def _():
            for copy in weights(e + 1, 1 - slot):
                copy.start()

        pre = nn(r.x_s[...], r.both[slot])

        @pl.when(e > 0)
        def _():
            add_cores(e - 1)

        @pl.when(e == 1)
        def _():
            for place in (0, 3):
                line.cross(0, 0, place)
            line.straight(0)

        @pl.when(e == 2)
        def _():
            for place in (0, 3):
                line.ends(0, place)

        @pl.when(e == 3)
        def _():
            for place in (1, 2):
                line.join(0, 1, place)

        gate_pre, up_pre = pre[:, :hid], pre[:, hid:]
        sig = jax.nn.sigmoid(gate_pre)
        silu = gate_pre * sig
        r.hidden[...] = (silu * up_pre).astype(bf16)
        hidden_back = nt(r.sg_s[...], r.down[slot])
        r.pre_back[:, :hid] = (
            hidden_back * up_pre * sig * (1.0 + gate_pre * (1.0 - sig))
        ).astype(bf16)
        r.pre_back[:, hid:] = (hidden_back * silu).astype(bf16)
        produced = nn(r.hidden[...], r.down[slot])
        pair = jnp.sum(r.og_s[...].astype(f32) * produced, axis=1, keepdims=True)
        weighed = (produced * r.gate_s[:, :1]).astype(bf16)
        for src in range(ne):
            a, b = src * cap, (src + 1) * cap
            r.weighed[src, own, :] = weighed[a:b]
            r.soft_part[src, pl.ds(e, 1), :] = jnp.sum(
                r.hits[src, own, :].astype(f32) * pair[a:b], axis=0, keepdims=True
            )
        back = nt(r.pre_back[...], r.both[slot]).astype(bf16)
        for src in range(ne):
            r.back_rows[src, own, :] = back[src * cap : (src + 1) * cap]

        @pl.when(e == 1)
        def _():
            for place in (0, 3):
                line.cross(0, 1, place)

        @pl.when(e == 2)
        def _():
            for place in (1, 2):
                line.join(0, 0, place)

        @pl.when(e > 0)
        def _():
            for step in range(1, nd):
                cores(e - 1, step).wait_send()

        r.made[:, :, :gate_rows, :] = (
            tn(r.x_s[...], r.pre_back[...]).astype(bf16).reshape(nz, nd, gate_rows, 2 * hid)
        )
        r.made[:, :, gate_rows:, :] = (
            tn(r.hidden[...], r.sg_s[...]).astype(bf16).reshape(nz, nd, down_rows, width)
        )
        for step in range(1, nd):
            cores(e, step).start()
        r.held_s[e] = r.made[:, dp]

    stores = []
    for kind, (rows, out) in enumerate(((r.back_rows, r.back_part), (r.weighed, r.out_part))):
        for src in range(ne):
            r.sums[kind, src] = tn(r.hits[src], rows[src]).astype(bf16)
            stores.append(
                pltpu.make_async_copy(r.sums.at[kind, src], out.at[src], r.store_sem.at[kind, src])
            )
            stores[-1].start()
    add_cores(local - 1)

    def put(at, value):
        r.shard[at : at + 16, :] = value

    for place in (0, 3):
        for which in (0, 1):
            line.left(0, which, place)
    line.total(0, put)
    for step in range(1, nd):
        cores(local - 1, step).wait_send()
    for k in range(1, local):
        keep(k).wait()
    for copy in stores:
        copy.wait()


def experts(sizes, cid, cap, kept, read):
    ne, nz, nd = sizes
    local, width, hid = kept["w_gate"].shape
    tokens = read["rows_all"].shape[1]
    piece = width // (nz * nd) + hid // (nz * nd)
    shape, vmem, dma = jax.ShapeDtypeStruct, pltpu.VMEM, pltpu.SemaphoreType.DMA
    held, *line = Line.scratch(nz, local, piece, width)
    line[0] = vmem((1, nz, piece, width), bf16)
    outs = dict(
        held=shape((local, nz, piece, width), bf16),
        out_part=shape((ne, tokens, width), bf16),
        back_part=shape((ne, tokens, width), bf16),
        soft_part=shape((ne, local, tokens), f32),
        shard=shape((piece, width), f32),
    )
    rows = ne * cap
    scratch = dict(
        both=vmem((2, width, 2 * hid), bf16),
        down=vmem((2, hid, width), bf16),
        x_s=vmem((rows, width), bf16),
        og_s=vmem((rows, width), bf16),
        sg_s=vmem((rows, width), bf16),
        gate_s=vmem((rows, 128), f32),
        hidden=vmem((rows, hid), bf16),
        pre_back=vmem((rows, 2 * hid), bf16),
        hits=vmem((ne, local * cap, tokens), bf16),
        weighed=vmem((ne, local * cap, width), bf16),
        back_rows=vmem((ne, local * cap, width), bf16),
        sums=vmem((2, ne, tokens, width), bf16),
        made=vmem((nz, nd, piece, width), bf16),
        from_dp=vmem((nd - 1, local, nz, piece, width), bf16),
        held_s=held,
        line=line,
        weight_sem=dma((2, 3)),
        dp_send=dma((local, nd)),
        dp_recv=dma((local, nd)),
        held_sem=dma((local,)),
        store_sem=dma((2, ne)),
    )
    return call_named(
        functools.partial(experts_kernel, sizes, cap),
        kept, read, outs, scratch, cid, 62 << 20, ("held", "out_part", "back_part"),
    )


class Spread:
    def __init__(self, sizes, made, from_dp, held, from_ex, line, from_z, send, recv):
        self.sizes, self.made, self.from_dp, self.held = sizes, made, from_dp, held
        self.from_ex, self.line, self.from_z, self.send, self.recv = from_ex, line, from_z, send, recv
        self.places = tuple(lax.axis_index(a) for a in ("dp", "expert", "context"))

    @staticmethod
    def scratch(sizes, rows, width):
        ne, nz, nd = sizes
        most = max(sizes)
        return [
            pltpu.VMEM((nd - 1, ne, nz, rows, width), bf16),
            pltpu.VMEM((ne, nz, rows, width), bf16),
            pltpu.VMEM((ne - 1, nz, rows, width), bf16),
            pltpu.VMEM((nz, rows, width), bf16),
            pltpu.VMEM((nz - 1, rows, width), bf16),
            pltpu.SemaphoreType.DMA((3, most)),
            pltpu.SemaphoreType.DMA((3, most)),
        ]

    def copy(self, stage, step):
        ne, nz, nd = self.sizes
        axis, size = (("dp", nd), ("expert", ne), ("context", nz))[stage]
        other = lax.rem(self.places[stage] + step, size)
        src = (
            self.made.at[:, :, other]
            if stage == 0
            else self.held.at[other] if stage == 1 else self.line.at[other]
        )
        dst = (self.from_dp, self.from_ex, self.from_z)[stage].at[step - 1]
        return pltpu.make_async_remote_copy(
            src_ref=src,
            dst_ref=dst,
            send_sem=self.send.at[stage, step],
            recv_sem=self.recv.at[stage, step],
            device_id={axis: other},
            device_id_type=MESH,
        )

    def others(self, stage):
        ne, nz, nd = self.sizes
        return range(1, (nd, ne, nz)[stage])

    def over_dp(self):
        for step in self.others(0):
            self.copy(0, step).start()

    def made_free(self):
        for step in self.others(0):
            self.copy(0, step).wait_send()

    def over_expert(self):
        ne, nz, _ = self.sizes
        for step in self.others(0):
            self.copy(0, step).wait_recv()

        @pl.loop(0, ne * nz)
        def _(i):
            a = lax.div(i, nz)
            b = i - a * nz
            total = self.made[a, b, self.places[0]].astype(f32)
            for step in self.others(0):
                total = total + self.from_dp[step - 1, a, b].astype(f32)
            self.held[a, b] = total.astype(bf16)

        for step in self.others(1):
            self.copy(1, step).start()

    def over_context(self):
        nz = self.sizes[1]
        for step in self.others(1):
            self.copy(1, step).wait_recv()

        @pl.loop(0, nz)
        def _(b):
            total = self.held[self.places[1], b].astype(f32)
            for step in self.others(1):
                total = total + self.from_ex[step - 1, b].astype(f32)
            self.line[b] = total.astype(bf16)

        for step in self.others(2):
            self.copy(2, step).start()

    def finish(self, out):
        for step in self.others(2):
            self.copy(2, step).wait_recv()
        total = self.line[self.places[2]].astype(f32)
        for step in self.others(2):
            total = total + self.from_z[step - 1].astype(f32)
        out[...] = total
        for stage in (1, 2):
            for step in self.others(stage):
                self.copy(stage, step).wait_send()


class Fold:
    def __init__(self, ex, parts, own, mine, passing, came, load, send, recv):
        self.ex, self.parts, self.own, self.mine, self.passing, self.came = (
            ex, parts, own, mine, passing, came,
        )
        self.load, self.send, self.recv = load, send, recv
        self.pair = partners(ex, 4)
        half = parts.shape[1] // 2
        self.halves = (pl.ds(0, half), pl.ds(half, half))

    @staticmethod
    def scratch(rows, width):
        half = (2, rows // 2, width)
        return [
            pltpu.VMEM((rows, width), bf16),
            pltpu.VMEM(half, bf16),
            pltpu.VMEM(half, bf16),
            pltpu.VMEM((2, rows, width), bf16),
            pltpu.SemaphoreType.DMA((3,)),
            pltpu.SemaphoreType.DMA((3, 2)),
            pltpu.SemaphoreType.DMA((3, 2)),
        ]

    def copy(self, stage, i):
        src, dst = (
            (self.parts.at[3 - self.ex, self.halves[i]], self.passing.at[i]),
            (self.parts.at[self.pair[i], self.halves[i]], self.came.at[i, self.halves[i]]),
            (self.mine.at[i], self.came.at[i, self.halves[1 - i]]),
        )[stage]
        return pltpu.make_async_remote_copy(
            src_ref=src,
            dst_ref=dst,
            send_sem=self.send.at[stage, i],
            recv_sem=self.recv.at[stage, i],
            device_id={"expert": self.pair[i]},
            device_id_type=MESH,
        )

    def loads(self):
        return [
            pltpu.make_async_copy(self.parts.at[self.ex], self.own, self.load.at[2])
        ] + [
            pltpu.make_async_copy(
                self.parts.at[self.pair[i], self.halves[1 - i]], self.mine.at[i], self.load.at[i]
            )
            for i in (0, 1)
        ]

    def begin(self):
        for stage in (0, 1):
            for i in (0, 1):
                self.copy(stage, i).start()
        for copy in self.loads():
            copy.start()

    def onward(self):
        for copy in self.loads():
            copy.wait()
        for i in (0, 1):
            self.copy(0, 1 - i).wait_recv()
            add_rows(self.mine, (i,), self.passing, (1 - i,), self.mine.shape[1])
            self.copy(2, i).start()

    def arrive(self):
        for stage in (1, 2):
            for i in (0, 1):
                self.copy(stage, i).wait_recv()

    def finish(self):
        for stage in range(3):
            for i in (0, 1):
                self.copy(stage, i).wait_send()


def tail_kernel(sizes, defs, *refs):
    r = named(defs, refs)
    ne, nz, nd = sizes
    ex, me, dp = (lax.axis_index(a) for a in ("expert", "context", "dp"))
    tokens, width = r.tokens.shape
    slices = r.kv_all.shape[1]
    kv_width = slices * 128
    group = width // ne
    last, helper = nz - 1, nz - 2

    barrier = pltpu.get_barrier_semaphore()
    for axis, place, size in (("expert", ex, ne), ("context", me, nz), ("dp", dp, nd)):
        for step in range(1, size):
            pl.semaphore_signal(
                barrier, inc=1, device_id={axis: lax.rem(place + step, size)}, device_id_type=MESH
            )
    for copy in r.loads:
        copy.start()
    pl.semaphore_wait(barrier, ne + nz + nd - 3)

    line = Line(nz, *r.line)
    proj = Spread(sizes, r.made, *r.proj)
    query = Spread(sizes, r.made, *r.query)
    kv = Spread(sizes, r.made, *r.kv)
    small = Spread(sizes, r.small_made, *r.small)

    chunks = range(r.held_in.shape[0] - 1)
    held_copies = [
        pltpu.make_async_copy(r.held_in.at[k + 1], line.held.at[k], r.held_sem.at[k])
        for k in chunks
    ]
    for copy in held_copies:
        copy.start()

    back = Fold(ex, r.back_in, *r.back)
    out = Fold(ex, r.out_in, *r.out)

    def gates_copy(step):
        other = lax.rem(ex + step, ne)
        return pltpu.make_async_remote_copy(
            src_ref=r.soft_in.at[other],
            dst_ref=r.soft_all.at[ex],
            send_sem=r.gates_send.at[step],
            recv_sem=r.gates_recv.at[step],
            device_id={"expert": other},
            device_id_type=MESH,
        )

    back.begin()
    for step in range(1, ne):
        gates_copy(step).start()
    loads = [
        pltpu.make_async_copy(src, dst, r.load_sem.at[i])
        for i, (src, dst) in enumerate(
            (
                (r.soft_in.at[ex], r.soft_all.at[ex]),
                (r.w_out, r.w_out_v),
                (r.w_query, r.w_query_v),
                (r.w_key, r.w_key_v),
                (r.w_value, r.w_value_v),
                (r.tables_all.at[ex], r.tables_own),
            )
        )
    ]
    for copy in loads:
        copy.start()
    for k in chunks:
        held_copies[k].wait()
        if k == 0:
            for place in (0, 3):
                line.cross(0, 0, place)
    for k in chunks:
        line.straight(k)
    for copy in r.loads + loads:
        copy.wait()
    for t in range(2 * slices):
        for ab in (0, 1):
            h = 2 * t + ab
            r.attn_turned[h * HEAD_DIM : (h + 1) * HEAD_DIM, :] = r.heads[
                t, :, ab * tokens : (ab + 1) * tokens
            ]

    back.onward()
    for place in (0, 3):
        line.cross(0, 1, place)
    for place in (1, 2):
        line.join(0, 0, place)
    for place in (0, 3):
        line.left(0, 0, place)
        line.cross(1, 0, place)
    for place in (1, 2):
        line.join(0, 1, place)
    for place in (0, 3):
        line.left(0, 1, place)
        line.cross(1, 1, place)
    gate_out, up_out, down_out = r.experts_out
    gate_rows, hid = gate_out.shape[1:]

    def put(k, at, value):
        if at < gate_rows:
            gate_out[k, at : at + 16, :] = value[:, :hid]
            up_out[k, at : at + 16, :] = value[:, hid:]
        else:
            down_out[k, at - gate_rows : at - gate_rows + 16, :] = value

    for at in range(0, r.first_shard.shape[0], 16):
        put(0, at, r.first_shard[at : at + 16, :])
    for step in range(1, ne):
        gates_copy(step).wait_recv()
    back.arrive()
    out.begin()
    soft_back = jnp.concatenate([r.soft_all[i] for i in range(ne)], axis=0)
    router_soft = r.tables_own[1]
    logit_back = (
        router_soft * (soft_back - jnp.sum(router_soft * soft_back, axis=0, keepdims=True))
    ).astype(bf16)
    second_back = back.own[...].astype(f32) + tn(logit_back, r.w_router_turned[...])
    for i in (0, 1):
        second_back = second_back + back.came[i].astype(f32)
    middle = r.middle[...]
    inverse = lax.rsqrt(jnp.mean(middle * middle, axis=-1, keepdims=True) + epsilon)
    normed = middle * inverse
    scaled = second_back * r.gains[1:, :].astype(f32)
    moe_gain_grad = jnp.sum(second_back * normed, axis=0, keepdims=True)
    middle_grad = r.grad_top[...].astype(f32) + inverse * (
        scaled - normed * jnp.mean(scaled * normed, axis=-1, keepdims=True)
    )
    r.middle_grad[...] = middle_grad
    r.branch[...] = middle_grad.astype(bf16)
    experts_all = logit_back.shape[0]
    r.small_rows[...] = jnp.zeros_like(r.small_rows)
    r.small_rows[:experts_all, :] = nn(logit_back, r.second_low[...])
    r.small_rows[experts_all : experts_all + 1, :] = moe_gain_grad

    def to(place, src, dst, send, recv):
        return pltpu.make_async_remote_copy(
            src_ref=src,
            dst_ref=dst,
            send_sem=send,
            recv_sem=recv,
            device_id={"context": place},
            device_id_type=MESH,
        )

    def ask(t):
        return [
            to(helper, src.at[t], dst.at[t], r.ask_send.at[i, t], r.ask_recv.at[i, t])
            for i, (src, dst) in enumerate(((r.do, r.far_do), (r.stats, r.far_stats)))
        ]

    def answer(t):
        return to(
            last, r.far_dq_low.at[t], r.dq_came.at[t], r.answer_send.at[t], r.answer_recv.at[t]
        )

    @pl.loop(0, slices)
    def _(t):
        at = pl.ds(pl.multiple_of(t * 256, 256), 256)
        turned = nt(r.w_out_v[at, :], r.branch[...]).astype(bf16)
        r.stats[t, 0] = r.lse[t]
        for half in (0, 1):
            a, b = half * HEAD_DIM, (half + 1) * HEAD_DIM
            for ab in (0, 1):
                c = (2 * half + ab) * HEAD_DIM
                r.do[t, a:b, ab * tokens : (ab + 1) * tokens] = turned[c : c + HEAD_DIM]
            r.stats[t, 1, half : half + 1, :] = jnp.sum(
                r.do[t, a:b, :].astype(f32) * r.heads[2 * t + half].astype(f32),
                axis=0,
                keepdims=True,
            )

        @pl.when(me == last)
        def _():
            for copy in ask(t):
                copy.start()

    @pl.loop(0, ne)
    def _(g):
        at = pl.ds(pl.multiple_of(g * group, group), group)
        grad = nn(r.attn_turned[at, :], r.branch[...])
        r.made[g] = grad.reshape((nz, nd, group // (nz * nd), width)).astype(bf16)

    proj.over_dp()
    for which in (0, 1):
        line.left(1, which, 0)
        line.cross(2, which, 0)
    proj.over_expert()
    out.onward()
    line.join(1, 0, 2)

    r.dq[...] = jnp.zeros_like(r.dq)
    r.far_dq[...] = jnp.zeros_like(r.far_dq)

    def mine(j):
        return me == last if j == last else (j <= me) & (me < last)

    for j in range(nz):

        @pl.when(mine(j))
        def _():
            r.bias[j] = mask_bias(r.seg_all, j, me, tokens)

    @pl.when(me == helper)
    def _():
        for j in range(last):
            r.far_bias[j] = mask_bias(r.seg_all, j, last, tokens)

    def back_slice(j, t, queries, do, stats, dq, bias):
        keys = r.kv_all[j, t, :, :128]
        vals = r.kv_all[j, t, :, 128:]
        dks, dvs = [], []
        for half in (0, 1):
            keep = lane_half((tokens, 128), half)
            zero = jnp.zeros_like(keys)
            keys_half = jnp.where(keep, keys, zero)
            scores = nt(keys_half, queries[t]) + jnp.concatenate([bias[j]] * 2, axis=1)
            soft = jnp.exp(scores - stats[t, 0, half : half + 1, :])
            soft_grad = nn(jnp.where(keep, vals, zero), do[t])
            back = (soft * (soft_grad - stats[t, 1, half : half + 1, :])).astype(bf16)
            dvs.append(nt(soft.astype(bf16), do[t]))
            dks.append(nn(back, queries[t]))
            dq[t] += tn(keys_half, back)
        low = lane_half((tokens, 128), 0)
        return jnp.concatenate(
            [jnp.where(low, dks[0], dks[1]), jnp.where(low, dvs[0], dvs[1])], axis=1
        )

    def give(j, t):
        return to(
            me - 1, r.kv_part.at[j, t], r.kv_came.at[j, t], r.kv_send.at[j, t], r.kv_recv.at[j, t]
        )

    @pl.loop(0, slices)
    def _(t):
        for j in range(nz):

            @pl.when(mine(j))
            def _():
                r.kv_sum[j] = back_slice(j, t, r.q, r.do, r.stats, r.dq, r.bias)

        @pl.when(me == helper)
        def _():
            for copy in ask(t):
                copy.wait_recv()
            for j in range(last):
                r.kv_sum[j] += back_slice(
                    j, t, r.q_far, r.far_do, r.far_stats, r.far_dq, r.far_bias
                )
                if j < helper:
                    r.kv_part[j, t] = r.kv_sum[j].astype(bf16)
                    give(j, t).start()
            r.far_dq_low[t] = r.far_dq[t].astype(bf16)
            answer(t).start()

        for j in range(helper):

            @pl.when((j < me) & (me < helper))
            def _():
                r.kv_part[j, t] = r.kv_sum[j].astype(bf16)

        r.own_kv[t] = r.kv_sum[me]

        @pl.when(t == 0)
        def _():
            line.join(1, 1, 2)
            for which in (0, 1):
                line.cross(2, which, 3)


    line.ends(0, 3)
    line.join(2, 0, 2)

    @pl.when(me == last)
    def _():
        @pl.loop(0, slices)
        def _(t):
            answer(t).wait_recv()
            r.dq[t] += r.dq_came[t].astype(f32)

    quarter = HEAD_DIM // 2
    cos_q, sin_q = (
        jnp.concatenate([r.turn[i].T[:quarter]] * 2, axis=1) * HEAD_DIM ** (-0.5) for i in (0, 1)
    )
    for t in range(slices):
        for half in (0, 1):
            a = half * HEAD_DIM
            first = r.dq[t, a : a + quarter, :]
            second = r.dq[t, a + quarter : a + 2 * quarter, :]
            turned = jnp.concatenate(
                [first * cos_q + second * sin_q, second * cos_q - first * sin_q], axis=0
            )
            pair = jnp.concatenate([turned[:, :tokens], turned[:, tokens:]], axis=0)
            at = (2 * t + half) * 128
            r.back_s[:, at : at + 128] = pair.T.astype(bf16)

    def make(a, b):
        @pl.loop(0, ne)
        def _(g):
            at = pl.ds(pl.multiple_of(g * group, group), group)
            grad = tn(r.first_low[:, at], r.back_s[:, a:b])
            r.made[g] = grad.reshape((nz, nd, group // (nz * nd), b - a)).astype(bf16)

    proj.made_free()
    make(0, width)
    query.over_dp()
    for which in (0, 1):
        line.join(1, which, 1)
    line.join(2, 1, 2)
    for k in chunks:
        line.ends(k, 0)
    query.over_expert()

    @pl.loop(0, slices)
    def _(t):
        for j in range(helper):

            @pl.when((j < me) & (me < helper))
            def _():
                give(j, t).wait_recv()
                r.kv_part[j, t] = (
                    r.kv_part[j, t].astype(f32) + r.kv_came[j, t].astype(f32)
                ).astype(bf16)
                give(j, t).start()

        @pl.when(me < helper)
        def _():
            give(me, t).wait_recv()
            r.own_kv[t] += r.kv_came[me, t].astype(f32)

    for which in (0, 1):
        line.join(2, which, 1)
    for k in chunks[1:]:
        line.ends(k, 3)
    cos_k, sin_k = r.turn[0], r.turn[1]
    first_lanes = lax.rem(lax.broadcasted_iota(jnp.int32, (tokens, 128), 1), HEAD_DIM) < quarter
    for t in range(slices):
        grad = r.own_kv[t, :, :128]
        swapped = jnp.where(
            first_lanes, pltpu.roll(grad, 128 - quarter, 1), pltpu.roll(grad, quarter, 1)
        )
        r.back_s[:, width + t * 128 : width + (t + 1) * 128] = (
            grad * cos_k + swapped * sin_k
        ).astype(bf16)
        at = width + kv_width + t * 128
        r.back_s[:, at : at + 128] = r.own_kv[t, :, 128:].astype(bf16)
    query.made_free()
    make(width, width + 2 * kv_width)
    kv.over_dp()
    proj.over_context()

    first_back = nt(r.back_s[:, :width], r.w_query_v[...])
    first_back = first_back + nt(r.back_s[:, width : width + kv_width], r.w_key_v[...])
    first_back = first_back + nt(r.back_s[:, width + kv_width :], r.w_value_v[...])
    values = r.tokens[...].astype(f32)
    inverse = lax.rsqrt(jnp.mean(values * values, axis=-1, keepdims=True) + epsilon)
    normed = values * inverse
    scaled = first_back * r.gains[:1, :].astype(f32)
    r.small_rows[experts_all + 1 : experts_all + 2, :] = jnp.sum(
        first_back * normed, axis=0, keepdims=True
    )
    r.input_grad[...] = r.middle_grad[...] + inverse * (
        scaled - normed * jnp.mean(scaled * normed, axis=-1, keepdims=True)
    )
    small_turned = r.small_rows[...].T
    r.small_made[...] = small_turned.reshape(r.small_made.shape).astype(bf16)
    small.over_dp()
    kv.over_expert()
    small.over_expert()
    query.over_context()

    out.arrive()

    @pl.loop(0, tokens // 16)
    def _(i):
        at = pl.ds(pl.multiple_of(i * 16, 16), 16)
        total = r.middle[at, :] + out.own[at, :].astype(f32)
        for i in (0, 1):
            total = total + out.came[i, at, :].astype(f32)
        r.layer_out[at, :] = total

    line.total(0, functools.partial(put, 1))
    kv.over_context()
    small.over_context()
    line.total(1, functools.partial(put, 2))
    kv.made_free()
    small.made_free()
    for group_sum, target in zip((proj, query, kv, small), r.sums_out + [r.small_sum]):
        group_sum.finish(target)
    r.router_out[...] = r.small_sum[:, :experts_all]
    turned = r.small_sum[...].T
    r.gains_out[0] = turned[experts_all + 1 : experts_all + 2]
    r.gains_out[1] = turned[experts_all : experts_all + 1]
    for which in (0, 1):
        line.left(1, which, 3)
        line.left(2, which, 3)
        line.left(2, which, 0)
    line.total(2, functools.partial(put, 3))
    back.finish()
    out.finish()
    for step in range(1, ne):
        gates_copy(step).wait_send()
    for j in range(helper):

        @pl.when((j < me) & (me < last))
        def _():
            for t in range(slices):
                give(j, t).wait_send()

    @pl.when(me == last)
    def _():
        for t in range(slices):
            for copy in ask(t):
                copy.wait_send()

    @pl.when(me == helper)
    def _():
        for t in range(slices):
            answer(t).wait_send()


def tail(sizes, cid, hidden, hbm_ins, vmem_ins):
    ne, nz, nd = sizes
    ins = types.SimpleNamespace(**hbm_ins, **vmem_ins)
    tokens, width = ins.tokens.shape
    slices, wide, _ = ins.q.shape
    chunks, _, piece, _ = ins.held_in.shape
    kv_shape = ins.kv_all.shape[1:]
    kv_cols = slices * 256
    rows = width // (ne * nz * nd)
    gate_rows = width // (nz * nd)
    shard = lambda *shape: jax.ShapeDtypeStruct(shape, f32)
    outs = dict(
        layer_out=shard(tokens, width),
        input_grad=shard(tokens, width),
        sums_out=[shard(rows, c) for c in (width, width, kv_cols)],
        router_out=shard(rows, ins.w_router_turned.shape[0]),
        gains_out=shard(2, 1, rows),
        experts_out=[
            shard(chunks, gate_rows, hidden),
            shard(chunks, gate_rows, hidden),
            shard(chunks, piece - gate_rows, width),
        ],
    )
    dma = pltpu.SemaphoreType.DMA
    vmem = pltpu.VMEM
    scratch = dict(
        back=Fold.scratch(tokens, width),
        out=Fold.scratch(tokens, width),
        soft_all=vmem(ins.soft_in.shape, f32),
        w_out_v=vmem(ins.w_out.shape, bf16),
        w_query_v=vmem(ins.w_query.shape, bf16),
        w_key_v=vmem(ins.w_key.shape, bf16),
        w_value_v=vmem(ins.w_value.shape, bf16),
        attn_turned=vmem((width, tokens), bf16),
        middle_grad=vmem((tokens, width), f32),
        branch=vmem((tokens, width), bf16),
        small_rows=vmem((128, width), f32),
        do=vmem((slices, 128, wide), bf16),
        stats=vmem((slices, 2, 2, wide), f32),
        bias=vmem((nz, tokens, tokens), f32),
        dq=vmem((slices, 128, wide), f32),
        dq_came=vmem((slices, 128, wide), bf16),
        far_do=vmem((slices, 128, wide), bf16),
        far_stats=vmem((slices, 2, 2, wide), f32),
        far_bias=vmem((nz - 1, tokens, tokens), f32),
        far_dq=vmem((slices, 128, wide), f32),
        far_dq_low=vmem((slices, 128, wide), bf16),
        kv_sum=vmem((nz, tokens, 256), f32),
        kv_part=vmem((nz - 2,) + kv_shape, bf16),
        kv_came=vmem((nz - 2,) + kv_shape, bf16),
        own_kv=vmem(kv_shape, f32),
        back_s=vmem((tokens, width + kv_cols), bf16),
        made=vmem((ne, nz, nd, rows, width), bf16),
        small_made=vmem((ne, nz, nd, rows, 128), bf16),
        small_sum=vmem((rows, 128), f32),
        gates_send=dma((ne,)),
        gates_recv=dma((ne,)),
        load_sem=dma((6,)),
        tables_own=vmem(ins.tables_all.shape[1:], f32),
        held_sem=dma((chunks,)),
        kv_send=dma((nz, slices)),
        kv_recv=dma((nz, slices)),
        ask_send=dma((2, slices)),
        ask_recv=dma((2, slices)),
        answer_send=dma((slices,)),
        answer_recv=dma((slices,)),
        line=Line.scratch(nz, chunks - 1, piece, width),
        proj=Spread.scratch(sizes, rows, width),
        query=Spread.scratch(sizes, rows, width),
        kv=Spread.scratch(sizes, rows, kv_cols),
        small=Spread.scratch(sizes, rows, 128),
    )
    return call_named(
        functools.partial(tail_kernel, sizes), hbm_ins, vmem_ins, outs, scratch, cid, 63 << 20, ()
    )


def deliver_kernel(parts, count, *refs):
    ins, outs, sem, held = refs[:count], refs[count : 2 * count], refs[2 * count], refs[2 * count + 1 :]
    reads = [
        pltpu.make_async_copy(
            ins[i] if part is None else ins[i].at[:, pl.ds(*part)], held[i], sem.at[0, i]
        )
        for i, part in enumerate(parts)
    ]
    writes = [pltpu.make_async_copy(held[i], outs[i], sem.at[1, i]) for i in range(count)]
    for copy in reads:
        copy.start()
    for read, write in zip(reads, writes):
        read.wait()
        write.start()
    for copy in writes:
        copy.wait()


def deliver(moved):
    arrays, parts = zip(*moved)
    hbm = pl.BlockSpec(memory_space=pl.ANY)
    shapes = [a.shape[:-1] + (part[1] if part else a.shape[-1],) for a, part in moved]
    return pl.pallas_call(
        functools.partial(deliver_kernel, parts, len(parts)),
        out_shape=[jax.ShapeDtypeStruct(shape, a.dtype) for shape, a in zip(shapes, arrays)],
        in_specs=[hbm] * len(parts),
        out_specs=[hbm] * len(parts),
        scratch_shapes=[pltpu.SemaphoreType.DMA((2, len(parts)))]
        + [pltpu.VMEM(shape, a.dtype) for shape, a in zip(shapes, arrays)],
        compiler_params=pltpu.CompilerParams(vmem_limit_bytes=60 << 20),
        name="deliver",
    )(*arrays)


def turn_tables(tokens, blocks):
    freq = rope_base ** (-2.0 * np.arange(HEAD_DIM // 2) / HEAD_DIM)
    freq = np.tile(freq, 128 // freq.size)
    inner = np.arange(tokens)[:, None] * freq
    base = tokens * np.arange(blocks)[:, None] * freq
    return tuple(
        jnp.asarray(np.stack([np.cos(a), np.sin(a)]), f32) for a in (inner, base)
    )


def body(
    sizes,
    tokens,
    attn_scale,
    w_query,
    w_key,
    w_value,
    w_out,
    moe_scale,
    w_router,
    w_gate,
    w_up,
    w_down,
    segment_ids,
    expert_choice,
    slot_order,
    out_grad,
):
    ne, nz, nd = sizes
    local_rows = tokens.shape[1]
    kv_width = w_key.shape[1]
    experts_all = w_router.shape[1]
    pair_count = local_rows * expert_choice.shape[2]
    capacity = (pair_count * 9 + 8 * experts_all - 1) // (8 * experts_all)
    inner, base = turn_tables(local_rows, nz)
    w_router_turned = w_router.T
    gains = jnp.stack([attn_scale, moe_scale])

    begun = front(
        sizes,
        1,
        capacity,
        dict(
            w_query=w_query, w_key=w_key, w_value=w_value, w_out=w_out, grad_top=out_grad[0]
        ),
        dict(
            tokens=tokens[0],
            gains=gains,
            w_router_turned=w_router_turned,
            seg=segment_ids,
            chosen=expert_choice[0].T,
            order=slot_order[0],
            inner=inner,
            base=base,
        ),
    )
    mixed = experts(
        sizes,
        2,
        capacity,
        dict(w_gate=w_gate, w_up=w_up, w_down=w_down),
        dict(rows_all=begun.rows_all, grad_all=begun.grad_all, tables_all=begun.tables_all),
    )
    ended = tail(
        sizes,
        3,
        w_gate.shape[2],
        dict(
            held_in=mixed.held,
            back_in=mixed.back_part,
            out_in=mixed.out_part,
            soft_in=mixed.soft_part,
            w_query=w_query,
            w_key=w_key,
            w_value=w_value,
            w_out=w_out,
            tables_all=begun.tables_all,
        ),
        dict(
            q=begun.q,
            q_far=begun.q_far,
            kv_all=begun.kv_all,
            seg_all=begun.seg_all,
            lse=begun.lse,
            heads=begun.heads,
            middle=begun.middle,
            tokens=tokens[0],
            grad_top=out_grad[0],
            second_low=begun.second_low,
            first_low=begun.first_low,
            w_router_turned=w_router_turned,
            gains=gains,
            turn=begun.turn,
            first_shard=mixed.shard,
        ),
    )
    out_shard, query_shard, kv_shard = ended.sums_out
    moved = [
        (ended.layer_out, None),
        (ended.input_grad, None),
        (query_shard, None),
        (kv_shard, (0, kv_width)),
        (kv_shard, (kv_width, kv_width)),
        (out_shard, None),
        *((array, None) for array in ended.experts_out),
    ]
    layer_out, input_grad, *shards = deliver(moved)
    return (
        layer_out[None],
        input_grad[None],
        ended.gains_out[0, 0],
        ended.gains_out[1, 0],
        *shards[:4],
        ended.router_out,
        *shards[4:],
    )


def solution(mesh):
    sizes = (mesh.shape["expert"], mesh.shape["context"], mesh.shape["dp"])
    in_specs = (
        P(("expert", "dp"), "context", None),
        P(),
        P(),
        P(),
        P(),
        P(),
        P(),
        P(),
        P("expert", None, None),
        P("expert", None, None),
        P("expert", None, None),
        P(("expert", "dp"), "context"),
        P(("expert", "dp"), "context", None),
        P(("expert", "dp"), "context", None),
        P(("expert", "dp"), "context", None),
    )
    out_specs = (
        P(("expert", "dp"), "context", None),
        P(("expert", "dp"), "context", None),
        P(("expert", "context", "dp")),
        P(("expert", "context", "dp")),
        P(("expert", "context", "dp"), None),
        P(("expert", "context", "dp"), None),
        P(("expert", "context", "dp"), None),
        P(("expert", "context", "dp"), None),
        P(("expert", "context", "dp"), None),
        P("expert", ("context", "dp"), None),
        P("expert", ("context", "dp"), None),
        P("expert", ("context", "dp"), None),
    )
    return jax.shard_map(
        functools.partial(body, sizes),
        mesh=mesh,
        in_specs=in_specs,
        out_specs=out_specs,
        check_vma=False,
    )
```
